32 devices in a mesh: wide: 8 (over z, y), narrow: 4 (over x, core).
Axes of the slice: x: 2, y: 2, z: 4, core: 2. Of those that a mesh axis runs over, the one named last changes fastest.
Arguments:
- inputs: bfloat16 [160, 197, 768], P(('wide', 'narrow')), may hold values from -6 to 6
- cotangent: bfloat16 [160, 197, 768], P(('wide', 'narrow')), may hold values from -6 to 6
- group_sizes: int32 [4], replicated, may hold values from 5 to 80, as said below
- mask_patterns: int32 [4, 196], replicated, may hold values 0 or 1
- mask_token: float32 [768], replicated, may hold values from -6 to 6
- norm1_gain: float32 [768], replicated, may hold values from 0.25 to 1.75
- norm1_bias: float32 [768], replicated, may hold values from -4 to 4
- qkv_weight: bfloat16 [768, 2304], P('wide', 'narrow'), may hold values from -0.21875 to 0.21875
- query_bias: float32 [768], replicated, may hold values from -4 to 4
- value_bias: float32 [768], replicated, may hold values from -1.5 to 1.5
- bias_table: float32 [732, 12], replicated, may hold values from -6 to 6
- proj_weight: bfloat16 [768, 768], P('wide', 'narrow'), may hold values from -1 to 1
- proj_bias: float32 [768], replicated, may hold values from -1.5 to 1.5
- gamma_attn: float32 [768], replicated, may hold values from 0.5 to 1.5
- norm2_gain: float32 [768], replicated, may hold values from 0.25 to 1.75
- norm2_bias: float32 [768], replicated, may hold values from -4 to 4
- fc1_weight: bfloat16 [768, 3072], P('wide', 'narrow'), may hold values from -0.21875 to 0.21875
- fc1_bias: float32 [3072], replicated, may hold values from -4 to 4
- fc2_weight: bfloat16 [3072, 768], P('wide', 'narrow'), may hold values from -0.109375 to 0.109375
- fc2_bias: float32 [768], replicated, may hold values from -1.5 to 1.5
- gamma_mlp: float32 [768], replicated, may hold values from 0.5 to 1.5
Outputs:
- layer_out: bfloat16 [160, 197, 768], P(('wide', 'narrow'))
- input_grad: float32 [160, 197, 768], P(('wide', 'narrow'))
- grad_mask_token: float32 [768], replicated
- grad_norm1_gain: float32 [768], replicated
- grad_norm1_bias: float32 [768], replicated
- grad_qkv: float32 [768, 2304], P('wide', 'narrow')
- grad_query_bias: float32 [768], replicated
- grad_value_bias: float32 [768], replicated
- grad_bias_table: float32 [732, 12], replicated
- grad_proj: float32 [768, 768], P('wide', 'narrow')
- grad_proj_bias: float32 [768], replicated
- grad_gamma_attn: float32 [768], replicated
- grad_norm2_gain: float32 [768], replicated
- grad_norm2_bias: float32 [768], replicated
- grad_fc1: float32 [768, 3072], P('wide', 'narrow')
- grad_fc1_bias: float32 [3072], replicated
- grad_fc2: float32 [3072, 768], P('wide', 'narrow')
- grad_fc2_bias: float32 [768], replicated
- grad_gamma_mlp: float32 [768], replicated
The draws below stay inside these ranges and needn't reach their ends.
Inputs may be any that keep to these rules, and one draw needn't show every extreme that they name: `group_sizes`: the sizes add up to 160; one group, at a place drawn from the seed, holds exactly 80 images, and another exactly 5.
All inputs are finite; a program needn't handle non-finite values.
Results may differ from the reference program's by a relative error of at most 0.018.
Values may be sent and summed in bfloat16 or wider, within the bound.
No kernel may reach another device: no remote copies, remote signals or barrier semaphores. Data moves between devices by JAX's collectives and lax.ppermute only.
A program may use at most 192 MiB of HBM per device.

```python
import math
import jax
import jax.numpy as jnp
from jax import lax

D = 768
HEADS = 12
HEAD_DIM = 64
FF = 3072
GRID = 14
GROUPS = 4
IMG_DEV = 5
PATCHES = 196
SEQ = 197
TABLE = 732
IMAGES = 160


def draw_group_sizes(key, part):
    largest = IMAGES // 2
    remain = IMAGES - largest - 3 * IMG_DEV
    cut = jax.random.randint(jax.random.fold_in(key, 11), (), 0, remain + 1)
    others = jnp.stack([IMG_DEV + cut, jnp.asarray(IMG_DEV, jnp.int32) + 0 * cut, IMG_DEV + remain - cut]).astype(jnp.int32)
    place = jax.random.randint(jax.random.fold_in(key, 12), (), 0, GROUPS)
    slots = jnp.arange(GROUPS, dtype=jnp.int32)
    before = slots - (slots > place).astype(jnp.int32)
    picked = others[jnp.clip(before, 0, 2)]
    return jnp.where(slots == place, largest, picked).astype(jnp.int32)


def place_ends(values, rng, low, top_value):
    extent = values.shape
    spot = [jax.random.randint(jax.random.fold_in(rng, axis), (), 0, extent[axis]) for axis in range(len(extent))]
    values = values.at[tuple(spot)].set(low)
    longest = extent.index(max(extent))
    spot[longest] = (spot[longest] + 1) % extent[longest]
    return values.at[tuple(spot)].set(top_value)


def raised(array, own_key, source, target, blocks, factor):
    def block_of(dim):
        return (jnp.arange(array.shape[dim]) // (array.shape[dim] // blocks)).reshape((-1,) + (1,) * (array.ndim - 1 - dim))

    near = jax.random.permutation(own_key, blocks)[block_of(target)]
    far = (block_of(target) + blocks // 2) % blocks
    return jnp.where((block_of(source) == near) | (block_of(source) == far), factor * array, array)


def steps_of(key, shape, cuts, least, high):
    level, own = 1.0, jax.random.fold_in(key, 6)
    for axis_at, blocks in cuts:
        heights = jnp.exp(jax.random.uniform(jax.random.fold_in(own, axis_at), (blocks,), jnp.float32, least / len(cuts), high / len(cuts)))
        level = level * jnp.repeat(heights, shape[axis_at] // blocks).reshape([-1 if axis == axis_at else 1 for axis in range(len(shape))])
    return level


def noise(key, extent, scale, bound, cuts=(), kind=jnp.bfloat16):
    drawn = jax.random.normal(key, extent, jnp.float32) * scale
    if len(cuts) > 0:
        drawn = steps_of(key, extent, cuts, -0.22, 0.18) * drawn
    return jnp.clip(drawn, min=-bound, max=bound).astype(kind)


def bell_draw_with(rng, shape, deviation, limit, cuts, heavy, kind=jnp.bfloat16):
    result = deviation * jax.random.normal(rng, shape, jnp.float32)
    if cuts:
        result = result * steps_of(rng, shape, cuts, -0.22, 0.18)
    return jnp.clip(raised(result, jax.random.fold_in(rng, 3), *heavy), -limit, limit).astype(kind)


def setup_inputs(seed: int = 0) -> dict:
    seeds = jax.random.split(jax.random.key(seed), 22)
    return {
        "inputs": noise(seeds[0], (IMAGES, SEQ, D), 1.0, 6.0, ((0, 32),)),
        "cotangent": bell_draw_with(seeds[1], (IMAGES, SEQ, D), 1.0, 6.0, ((0, 32),), (0, 2, 32, 2.75)),
        "group_sizes": draw_group_sizes(jax.random.fold_in(seeds[21], 71), 0),
        "mask_patterns": place_ends((jax.random.randint(seeds[3], (GROUPS, PATCHES), 0, 5) < 2).astype(jnp.int32), jax.random.fold_in(seeds[3], 1), 0, 1),
        "mask_token": noise(seeds[4], (D,), 1.0, 6.0, (), jnp.float32),
        "norm1_gain": jnp.clip(1.0 + 0.15 * jax.random.normal(seeds[5], (D,), jnp.float32), 0.25, 1.75),
        "norm1_bias": noise(seeds[6], (D,), 0.3, 4.0, (), jnp.float32),
        "qkv_weight": noise(seeds[7], (D, 3 * D), D ** -0.5, 0.21875, ((0, 8), (1, 4))),
        "query_bias": noise(seeds[8], (D,), 0.3, 4.0, (), jnp.float32),
        "value_bias": noise(seeds[9], (D,), 0.1, 1.5, (), jnp.float32),
        "bias_table": noise(seeds[10], (TABLE, HEADS), 0.5, 6.0, (), jnp.float32),
        "proj_weight": noise(seeds[11], (D, D), (D // 24) ** -0.5, 1.0, ((0, 8), (1, 4))),
        "proj_bias": noise(seeds[12], (D,), 0.1, 1.5, (), jnp.float32),
        "gamma_attn": jnp.clip(jnp.exp(jax.random.uniform(seeds[13], (D,), jnp.float32, math.log(0.5), math.log(1.5))), 0.5, 1.5),
        "norm2_gain": jnp.clip(1.0 + 0.15 * jax.random.normal(seeds[14], (D,), jnp.float32), 0.25, 1.75),
        "norm2_bias": noise(seeds[15], (D,), 0.3, 4.0, (), jnp.float32),
        "fc1_weight": noise(seeds[16], (D, FF), D ** -0.5, 0.21875, ((0, 8), (1, 4))),
        "fc1_bias": noise(seeds[17], (FF,), 0.3, 4.0, (), jnp.float32),
        "fc2_weight": noise(seeds[18], (FF, D), FF ** -0.5, 0.109375, ((0, 8), (1, 4))),
        "fc2_bias": noise(seeds[19], (D,), 0.1, 1.5, (), jnp.float32),
        "gamma_mlp": jnp.clip(jnp.exp(jax.random.uniform(seeds[20], (D,), jnp.float32, math.log(0.5), math.log(1.5))), 0.5, 1.5),
    }


EPSILON = 1e-06

@jax.custom_vjp
def low(v):
    return lax.optimization_barrier(v.astype(jnp.bfloat16)).astype(jnp.float32)

@jax.custom_vjp
def low_back(v):
    return v

def low_keep(v):
    return (low(v), None)

def low_pass(kept, grad):
    return (grad,)

def back_keep(v):
    return (v, None)

def back_low(kept, grad):
    return (low(grad),)
low.defvjp(low_keep, low_pass)
low_back.defvjp(back_keep, back_low)

def position_index(grid_side, table_rows):
    side = 2 * grid_side - 1
    cells = jnp.arange(grid_side * grid_side, dtype=jnp.int32)
    cell_row = cells // grid_side
    cell_col = cells % grid_side
    inner = (cell_row[:, None] - cell_row[None, :] + grid_side - 1) * side + (cell_col[:, None] - cell_col[None, :] + grid_side - 1)
    count = grid_side * grid_side
    top_row = jnp.full((1, count), table_rows - 3, jnp.int32)
    left_col = jnp.full((count, 1), table_rows - 2, jnp.int32)
    corner = jnp.full((1, 1), table_rows - 1, jnp.int32)
    upper = jnp.concatenate([corner, top_row], axis=1)
    lower = jnp.concatenate([left_col, inner.astype(jnp.int32)], axis=1)
    return jnp.concatenate([upper, lower], axis=0).astype(jnp.int32)

def layer_norm(values, norm_gain, norm_shift):
    centre = lax.optimization_barrier(jnp.mean(values, axis=-1, keepdims=True))
    centred = values - centre
    spread = lax.optimization_barrier(jnp.mean(centred * centred, axis=-1, keepdims=True))
    return centred * lax.rsqrt(spread + EPSILON) * norm_gain + norm_shift

def product(subscripts, left_side, right_side):
    return jnp.einsum(subscripts, left_side, right_side, precision=lax.Precision.HIGHEST)

def reference(inputs, cotangent, group_sizes, mask_patterns, mask_token, norm1_gain, norm1_bias, qkv_weight, query_bias, value_bias, bias_table, proj_weight, proj_bias, gamma_attn, norm2_gain, norm2_bias, fc1_weight, fc1_bias, fc2_weight, fc2_bias, gamma_mlp):
    image_ids = jnp.arange(IMAGES, dtype=jnp.int32)
    bounds = jnp.cumsum(group_sizes).astype(jnp.int32)[:GROUPS - 1]
    member = lax.optimization_barrier(jnp.sum((image_ids[:, None] >= bounds[None, :]).astype(jnp.int32), axis=1)).astype(jnp.int32)
    patterns = jnp.take(mask_patterns, member, axis=0).astype(jnp.int32)
    mask_rows = jnp.concatenate([jnp.zeros((IMAGES, 1), jnp.int32), patterns], axis=1)
    rel_index = position_index(GRID, TABLE)
    params = tuple((param.astype(jnp.float32) for param in (mask_token, norm1_gain, norm1_bias, qkv_weight, query_bias, value_bias, bias_table, proj_weight, proj_bias, gamma_attn, norm2_gain, norm2_bias, fc1_weight, fc1_bias, fc2_weight, fc2_bias, gamma_mlp)))
    score_scale = HEAD_DIM ** (-0.5)

    def forward(weights, embedded):
        token_row, gain_one, shift_one, qkv_mat, bias_query, bias_value, bias_rel, proj_mat, bias_proj, gamma_one, gain_two, shift_two, fc1_mat, bias_fc1, fc2_mat, bias_fc2, gamma_two = weights
        rel_bias = jnp.transpose(bias_rel[rel_index], (2, 0, 1))

        def one_block(block_data):
            rows_in, flags = block_data
            start_rows = jnp.where((flags == 1)[..., None], token_row, rows_in)
            first_normed = low(layer_norm(start_rows, gain_one, shift_one))
            projected = low_back(product('bsd,de->bse', first_normed, qkv_mat))
            shape_four = (IMG_DEV, SEQ, HEADS, HEAD_DIM)
            queries = low((projected[..., :D] + bias_query) * score_scale).reshape(shape_four)
            key_rows = low(projected[..., D:2 * D]).reshape(shape_four)
            values = low(projected[..., 2 * D:] + bias_value).reshape(shape_four)
            scores = low_back(product('bshe,bche->bhsc', queries, key_rows) + rel_bias[None])
            probs = low(jax.nn.softmax(scores, axis=-1))
            attended = low(low_back(product('bhsc,bche->bshe', probs, values).reshape(IMG_DEV, SEQ, D)))
            attn_out = low_back(product('bsd,de->bse', attended, proj_mat)) + bias_proj
            middle = start_rows + gamma_one * attn_out
            second_normed = low(layer_norm(middle, gain_two, shift_two))
            hidden = low_back(product('bsd,df->bsf', second_normed, fc1_mat)) + bias_fc1
            activated = low(jax.nn.gelu(hidden, approximate=False))
            branch = low_back(product('bsf,fd->bsd', activated, fc2_mat)) + bias_fc2
            return middle + gamma_two * branch
        blocks = (embedded.reshape(IMAGES // IMG_DEV, IMG_DEV, SEQ, D), mask_rows.reshape(IMAGES // IMG_DEV, IMG_DEV, SEQ))
        outputs = lax.map(jax.checkpoint(one_block), blocks)
        return outputs.reshape(IMAGES, SEQ, D)
    layer_out, pullback = jax.vjp(forward, params, inputs.astype(jnp.float32))
    grads, input_grad = pullback(cotangent.astype(jnp.float32))
    grad_mask_token, grad_norm1_gain, grad_norm1_bias, grad_qkv, grad_query_bias, grad_value_bias, grad_bias_table, grad_proj, grad_proj_bias, grad_gamma_attn, grad_norm2_gain, grad_norm2_bias, grad_fc1, grad_fc1_bias, grad_fc2, grad_fc2_bias, grad_gamma_mlp = grads
    return (layer_out.astype(jnp.bfloat16), input_grad, grad_mask_token, grad_norm1_gain, grad_norm1_bias, grad_qkv, grad_query_bias, grad_value_bias, grad_bias_table, grad_proj, grad_proj_bias, grad_gamma_attn, grad_norm2_gain, grad_norm2_bias, grad_fc1, grad_fc1_bias, grad_fc2, grad_fc2_bias, grad_gamma_mlp)
```

```python
import functools
import math

import jax
import jax.numpy as jnp
from jax import lax
from jax.experimental import pallas as pl
from jax.experimental.pallas import tpu as pltpu
from jax.sharding import PartitionSpec as P

EPSILON = 1e-06
ROOT_HALF = 0.7071067811865476
DENSITY = 0.3989422804014327


def offset_table(grid_side):
    side = 2 * grid_side - 1
    cells = jnp.arange(grid_side, dtype=jnp.int32)
    offsets = cells[:, None] - cells[None, :] + grid_side - 1
    return (offsets[:, :, None] == jnp.arange(side, dtype=jnp.int32)[None, None, :]).astype(
        jnp.float32
    )


def relative_bias(bias_table, grid_side):
    table_rows, head_count = bias_table.shape
    side = 2 * grid_side - 1
    count = grid_side * grid_side
    onehot = offset_table(grid_side)
    inner_table = bias_table[: side * side].reshape(side, side, head_count)
    half = jnp.einsum("bcq,pqh->pbch", onehot, inner_table, precision=lax.Precision.HIGHEST)
    inner = jnp.einsum("adp,pbch->habdc", onehot, half, precision=lax.Precision.HIGHEST).reshape(
        head_count, count, count
    )
    top_row = jnp.broadcast_to(bias_table[table_rows - 3][:, None, None], (head_count, 1, count))
    left_col = jnp.broadcast_to(bias_table[table_rows - 2][:, None, None], (head_count, count, 1))
    corner = bias_table[table_rows - 1][:, None, None]
    upper = jnp.concatenate([corner, top_row], axis=2)
    lower = jnp.concatenate([left_col, inner], axis=2)
    return jnp.concatenate([upper, lower], axis=1)


def relative_bias_back(table_terms, grid_side):
    head_count = table_terms.shape[0]
    side = 2 * grid_side - 1
    onehot = offset_table(grid_side)
    inner = table_terms[:, 1:, 1:].reshape(head_count, grid_side, grid_side, grid_side, grid_side)
    half = jnp.einsum("adp,habdc->pbch", onehot, inner, precision=lax.Precision.HIGHEST)
    grad_inner = jnp.einsum("bcq,pbch->pqh", onehot, half, precision=lax.Precision.HIGHEST).reshape(
        side * side, head_count
    )
    top_sum = jnp.sum(table_terms[:, 0, 1:], axis=1)
    left_sum = jnp.sum(table_terms[:, 1:, 0], axis=1)
    corner_sum = table_terms[:, 0, 0]
    return jnp.concatenate([grad_inner, jnp.stack([top_sum, left_sum, corner_sum], axis=0)], axis=0)


def normalize(values, norm_gain, norm_shift):
    centre = jnp.mean(values, axis=-1, keepdims=True)
    centred = values - centre
    spread = jnp.mean(centred * centred, axis=-1, keepdims=True)
    scaling = lax.rsqrt(spread + EPSILON)
    normed = centred * scaling
    return (normed * norm_gain + norm_shift, normed, scaling)


def normalize_back(grad_out, normed, scaling, norm_gain):
    scaled = grad_out * norm_gain
    first_mean = jnp.mean(scaled, axis=-1, keepdims=True)
    second_mean = jnp.mean(scaled * normed, axis=-1, keepdims=True)
    return (scaled - first_mean - normed * second_mean) * scaling


def contract_rows(left_side, right_side):
    return lax.dot_general(
        left_side, right_side, (((0,), (0,)), ((), ())), preferred_element_type=jnp.float32
    )


def contract_cols(left_side, right_side):
    return lax.dot_general(
        left_side, right_side, (((1,), (1,)), ((), ())), preferred_element_type=jnp.float32
    )


AXES = ("wide", "narrow")


class Links:
    def __init__(self, wide, narrow):
        self.wide, self.narrow = wide, narrow
        self.y = 1 << ((wide.bit_length() - 1) // 2)
        self.z = wide // self.y
        self.core = 2
        self.x = narrow // 2
        self.size = {"z": self.z, "y": self.y, "x": self.x, "core": 2}
        self.unit = {"core": 1, "x": 2, "y": narrow, "z": narrow * self.y}

    def fits(self, model_width):
        return model_width % (32 * self.wide) == 0 and model_width % (128 * self.x) == 0

    def place(self):
        w, n = lax.axis_index("wide"), lax.axis_index("narrow")
        return {"z": w // self.y, "y": w % self.y, "x": n // 2, "core": n % 2}

    def swap(self, value, **offsets):
        mask = sum(self.unit[axis] * offset for axis, offset in offsets.items())
        count = self.wide * self.narrow
        return lax.ppermute(value, AXES, [(k, k ^ mask) for k in range(count)])

    def others(self, value, axis):
        return [self.swap(value, **{axis: d}) for d in range(1, self.size[axis])]


def pick(value, axis, index, count):
    size = value.shape[axis] // count
    return lax.dynamic_slice_in_dim(value, index * size, size, axis)


def halves_to_rows(links, here, shard):
    c = here["core"]
    mine = pick(shard, 0, c, 2)
    theirs = links.swap(pick(shard, 0, 1 - c, 2), core=1)
    return jnp.where(
        c == 0,
        jnp.concatenate([mine, theirs], axis=1),
        jnp.concatenate([theirs, mine], axis=1),
    )


def gather(links, piece, order):
    held = jnp.concatenate([piece[None]] + [p[None] for p in links.others(piece, "z")], axis=0)
    for axis in order:
        held = jnp.concatenate([held] + links.others(held, axis), axis=0)
    return held, links.swap(held, core=1)


def native_gather(shard):
    return lax.all_gather(
        lax.all_gather(shard, "narrow", axis=1, tiled=True), "wide", axis=0, tiled=True
    )


def place_pieces(links, rows, cols, parts):
    wide, narrow = links.wide, links.narrow
    block_rows = rows // wide
    half = block_rows // 2
    block_cols = cols // links.x

    def kernel(*refs):
        out, sem = refs[-2], refs[-1]
        w, n = lax.axis_index("wide"), lax.axis_index("narrow")
        me = {"z": w // links.y, "y": w % links.y, "x": n // 2, "core": n % 2}
        for number, (held, _, order, row_at) in enumerate(parts):
            count, tall = held.shape[0], held.shape[1]
            for core in range(2):
                source = refs[2 * number + core]
                for k in range(count):
                    rest, off = k, {}
                    for axis in ("z",) + order:
                        off[axis] = rest % links.size[axis]
                        rest //= links.size[axis]
                    at = {axis: me[axis] ^ off[axis] for axis in ("z", "y", "x")}
                    row = (at["z"] * links.y + at["y"]) * block_rows + (me["core"] ^ core) * half + row_at
                    col = at["x"] * block_cols
                    pltpu.make_async_copy(
                        source.at[k],
                        out.at[
                            pl.ds(pl.multiple_of(row, 8), tall),
                            pl.ds(pl.multiple_of(col, 128), block_cols),
                        ],
                        sem,
                    ).start()
        pltpu.make_async_copy(out, out, sem).wait()

    operands = [array for held, other, _, _ in parts for array in (held, other)]
    return pl.pallas_call(
        kernel,
        out_shape=jax.ShapeDtypeStruct((rows, cols), operands[0].dtype),
        in_specs=[pl.BlockSpec(memory_space=pl.ANY)] * len(operands),
        out_specs=pl.BlockSpec(memory_space=pltpu.VMEM),
        scratch_shapes=[pltpu.SemaphoreType.DMA],
    )(*operands)


def scatter_sum(links, here, partial, orders):
    rows, cols = partial.shape
    if not links.fits(min(rows, cols)):
        low = lax.psum_scatter(
            partial.astype(jnp.bfloat16), "wide", scatter_dimension=0, tiled=True
        )
        return lax.psum_scatter(low, "narrow", scatter_dimension=1, tiled=True).astype(jnp.float32)
    block_rows = rows // links.wide
    half = block_rows // 2
    c = here["core"]
    low = partial.astype(jnp.bfloat16).reshape(links.z, links.y, 2, half, cols)
    kept = pick(low, 2, c, 2)[:, :, 0].astype(jnp.float32)
    came = links.swap(pick(low, 2, 1 - c, 2)[:, :, 0], core=1)
    tall = half // len(orders)
    sums = []
    for number, order in enumerate(orders):
        keep = kept[:, :, number * tall : (number + 1) * tall] + came[
            :, :, number * tall : (number + 1) * tall
        ].astype(jnp.float32)
        for axis in order + ("z",):
            dim = {"x": 3, "y": 1, "z": 0}[axis]
            size = links.size[axis]
            arrived = [
                links.swap(
                    pick(keep, dim, here[axis] ^ d, size).astype(jnp.bfloat16), **{axis: d}
                )
                for d in range(1, size)
            ]
            keep = pick(keep, dim, here[axis], size)
            for term in arrived:
                keep = keep + term.astype(jnp.float32)
        sums.append(keep.reshape(tall, cols // links.x))
    mine = jnp.concatenate(sums, axis=0) if len(sums) > 1 else sums[0]
    theirs = links.swap(pick(mine, 1, 1 - c, 2), core=1)
    mine = pick(mine, 1, c, 2)
    return jnp.where(
        c == 0,
        jnp.concatenate([mine, theirs], axis=0),
        jnp.concatenate([theirs, mine], axis=0),
    )


def tree_sum(terms):
    while len(terms) > 1:
        terms = [terms[k] + terms[k + 1] for k in range(0, len(terms), 2)]
    return terms[0]


def sum_everywhere(links, value):
    value = value + links.swap(value, core=1)
    value = tree_sum(
        [value]
        + [
            links.swap(value, x=k % links.x, y=k // links.x)
            for k in range(1, links.x * links.y)
        ]
    )
    return tree_sum([value] + links.others(value, "z"))


def sum_small(links, values):
    flat = jnp.concatenate([v.reshape(-1) for v in values])
    padded = jnp.pad(flat, (0, -flat.shape[0] % 1024)).reshape(-1, 128)
    total = sum_everywhere(links, padded).reshape(-1)
    out, at = [], 0
    for v in values:
        out.append(total[at : at + v.size].reshape(v.shape))
        at += v.size
    return out


def local(
    links,
    inputs,
    cotangent,
    group_sizes,
    mask_patterns,
    mask_token,
    norm1_gain,
    norm1_bias,
    qkv_weight,
    query_bias,
    value_bias,
    bias_table,
    proj_weight,
    proj_bias,
    gamma_attn,
    norm2_gain,
    norm2_bias,
    fc1_weight,
    fc1_bias,
    fc2_weight,
    fc2_bias,
    gamma_mlp,
):
    image_count, length, model_width = inputs.shape
    table_rows, head_count = bias_table.shape
    head_dim = model_width // head_count
    grid_side = math.isqrt(length - 1)
    group_count = mask_patterns.shape[0]
    row_count = image_count * length
    score_scale = head_dim ** (-0.5)
    shape_four = (image_count, length, head_count, head_dim)
    image_ids = lax.axis_index(("wide", "narrow")) * image_count + jnp.arange(
        image_count, dtype=jnp.int32
    )
    bounds = jnp.cumsum(group_sizes)[: group_count - 1]
    member = jnp.sum((image_ids[:, None] >= bounds[None, :]).astype(jnp.int32), axis=1)
    chosen = (member[:, None] == jnp.arange(group_count, dtype=jnp.int32)[None, :]).astype(
        jnp.int32
    )
    patterns = jnp.sum(chosen[:, :, None] * mask_patterns[None, :, :], axis=1)
    mask_rows = (
        jnp.concatenate([jnp.zeros((image_count, 1), jnp.int32), patterns], axis=1).reshape(
            row_count, 1
        )
        == 1
    )
    embedded = jnp.where(
        mask_rows, mask_token[None, :], inputs.reshape(row_count, model_width).astype(jnp.float32)
    )
    rel_bias = relative_bias(bias_table, grid_side)
    here = links.place()

    def both_orders(shard):
        piece = halves_to_rows(links, here, shard)
        tall = piece.shape[0] // 2
        return [
            gather(links, piece[:tall], ("x", "y")) + (("x", "y"), 0),
            gather(links, piece[tall:], ("y", "x")) + (("y", "x"), tall),
        ]

    if links.fits(model_width):
        qkv_full = place_pieces(links, model_width, 3 * model_width, both_orders(qkv_weight))
        proj_full = place_pieces(links, model_width, model_width, both_orders(proj_weight))
        fc1_full = place_pieces(
            links,
            model_width,
            4 * model_width,
            [gather(links, halves_to_rows(links, here, fc1_weight), ("x", "y")) + (("x", "y"), 0)],
        )
        fc2_full = place_pieces(
            links,
            4 * model_width,
            model_width,
            [gather(links, halves_to_rows(links, here, fc2_weight), ("y", "x")) + (("y", "x"), 0)],
        )
    else:
        qkv_full, proj_full, fc1_full, fc2_full = (
            native_gather(shard) for shard in (qkv_weight, proj_weight, fc1_weight, fc2_weight)
        )
    normed1_out, normed1, scaling1 = normalize(embedded, norm1_gain, norm1_bias)
    first_low = normed1_out.astype(jnp.bfloat16)
    projected = jnp.dot(first_low, qkv_full, preferred_element_type=jnp.float32)
    queries = (
        ((projected[:, :model_width] + query_bias) * score_scale)
        .astype(jnp.bfloat16)
        .reshape(shape_four)
    )
    key_rows = projected[:, model_width : 2 * model_width].astype(jnp.bfloat16).reshape(shape_four)
    values = (projected[:, 2 * model_width :] + value_bias).astype(jnp.bfloat16).reshape(shape_four)
    scores = (
        jnp.einsum("ishe,iche->ihsc", queries, key_rows, preferred_element_type=jnp.float32)
        + rel_bias[None]
    )
    row_peak = jnp.max(scores, axis=-1, keepdims=True)
    row_total = jnp.sum(jnp.exp(scores - row_peak), axis=-1, keepdims=True)
    log_total = row_peak + jnp.log(row_total)
    probs_low = jnp.exp(scores - log_total).astype(jnp.bfloat16)
    attended = (
        jnp.einsum("ihsc,iche->ishe", probs_low, values, preferred_element_type=jnp.float32)
        .reshape(row_count, model_width)
        .astype(jnp.bfloat16)
    )
    attn_out = jnp.dot(attended, proj_full, preferred_element_type=jnp.float32) + proj_bias
    middle = embedded + gamma_attn * attn_out
    normed2_out, normed2, scaling2 = normalize(middle, norm2_gain, norm2_bias)
    second_low = normed2_out.astype(jnp.bfloat16)
    hidden = jnp.dot(second_low, fc1_full, preferred_element_type=jnp.float32) + fc1_bias
    gelu_low = jax.nn.gelu(hidden, approximate=False).astype(jnp.bfloat16)
    branch = jnp.dot(gelu_low, fc2_full, preferred_element_type=jnp.float32) + fc2_bias
    layer_out = (
        (middle + gamma_mlp * branch).astype(jnp.bfloat16).reshape(image_count, length, model_width)
    )
    upstream = cotangent.reshape(row_count, model_width).astype(jnp.float32)
    grad_gamma_mlp = jnp.sum(upstream * branch, axis=0)
    grad_branch = gamma_mlp * upstream
    grad_fc2_bias = jnp.sum(grad_branch, axis=0)
    branch_low = grad_branch.astype(jnp.bfloat16)
    grad_fc2 = contract_rows(gelu_low, branch_low)
    grad_gelu = contract_cols(branch_low, fc2_full)
    cumulative = 0.5 * (1.0 + lax.erf(hidden * ROOT_HALF))
    grad_hidden = grad_gelu * (cumulative + hidden * DENSITY * jnp.exp(-0.5 * hidden * hidden))
    grad_fc1_bias = jnp.sum(grad_hidden, axis=0)
    hidden_low = grad_hidden.astype(jnp.bfloat16)
    grad_fc1 = contract_rows(second_low, hidden_low)
    grad_normed2 = contract_cols(hidden_low, fc1_full)
    grad_norm2_gain = jnp.sum(grad_normed2 * normed2, axis=0)
    grad_norm2_bias = jnp.sum(grad_normed2, axis=0)
    grad_middle = upstream + normalize_back(grad_normed2, normed2, scaling2, norm2_gain)
    grad_fc1_part = scatter_sum(links, here, grad_fc1, [("x", "y")])
    grad_fc2_part = scatter_sum(links, here, grad_fc2, [("y", "x")])
    grad_gamma_attn = jnp.sum(grad_middle * attn_out, axis=0)
    grad_attn = gamma_attn * grad_middle
    grad_proj_bias = jnp.sum(grad_attn, axis=0)
    attn_low = grad_attn.astype(jnp.bfloat16)
    grad_proj = contract_rows(attended, attn_low)
    grad_attended = contract_cols(attn_low, proj_full).astype(jnp.bfloat16).reshape(shape_four)
    scores_again = (
        jnp.einsum("ishe,iche->ihsc", queries, key_rows, preferred_element_type=jnp.float32)
        + rel_bias[None]
    )
    probs = jnp.exp(scores_again - log_total)
    probs_again = probs.astype(jnp.bfloat16)
    grad_probs = jnp.einsum(
        "ishe,iche->ihsc", grad_attended, values, preferred_element_type=jnp.float32
    )
    grad_values = jnp.einsum(
        "ihsc,ishe->iche", probs_again, grad_attended, preferred_element_type=jnp.float32
    ).reshape(row_count, model_width)
    grad_scores = probs * (grad_probs - jnp.sum(probs * grad_probs, axis=-1, keepdims=True))
    scores_low = grad_scores.astype(jnp.bfloat16)
    table_terms = jnp.sum(scores_low, axis=0, dtype=jnp.float32)
    grad_bias_table = relative_bias_back(table_terms, grid_side)
    grad_queries = (
        jnp.einsum(
            "ihsc,iche->ishe", scores_low, key_rows, preferred_element_type=jnp.float32
        ).reshape(row_count, model_width)
        * score_scale
    )
    grad_keys = jnp.einsum(
        "ihsc,ishe->iche", scores_low, queries, preferred_element_type=jnp.float32
    ).reshape(row_count, model_width)
    grad_query_bias = jnp.sum(grad_queries, axis=0)
    grad_value_bias = jnp.sum(grad_values, axis=0)
    mixed_low = jnp.concatenate([grad_queries, grad_keys, grad_values], axis=1).astype(jnp.bfloat16)
    grad_qkv = contract_rows(first_low, mixed_low)
    grad_normed1 = contract_cols(mixed_low, qkv_full)
    grad_norm1_gain = jnp.sum(grad_normed1 * normed1, axis=0)
    grad_norm1_bias = jnp.sum(grad_normed1, axis=0)
    grad_start = grad_middle + normalize_back(grad_normed1, normed1, scaling1, norm1_gain)
    input_grad = jnp.where(mask_rows, 0.0, grad_start).reshape(image_count, length, model_width)
    grad_mask_token = jnp.sum(jnp.where(mask_rows, grad_start, 0.0), axis=0)
    grad_qkv_part = scatter_sum(links, here, grad_qkv, [("x", "y"), ("y", "x")])
    grad_proj_part = scatter_sum(links, here, grad_proj, [("x", "y"), ("y", "x")])
    small_sums = sum_small(
        links,
        (
            grad_mask_token,
            grad_norm1_gain,
            grad_norm1_bias,
            grad_query_bias,
            grad_value_bias,
            grad_bias_table,
            grad_proj_bias,
            grad_gamma_attn,
            grad_norm2_gain,
            grad_norm2_bias,
            grad_fc1_bias,
            grad_fc2_bias,
            grad_gamma_mlp,
        ),
    )
    (
        sum_mask_token,
        sum_norm1_gain,
        sum_norm1_bias,
        sum_query_bias,
        sum_value_bias,
        sum_bias_table,
        sum_proj_bias,
        sum_gamma_attn,
        sum_norm2_gain,
        sum_norm2_bias,
        sum_fc1_bias,
        sum_fc2_bias,
        sum_gamma_mlp,
    ) = small_sums
    return (
        layer_out,
        input_grad,
        sum_mask_token,
        sum_norm1_gain,
        sum_norm1_bias,
        grad_qkv_part,
        sum_query_bias,
        sum_value_bias,
        sum_bias_table,
        grad_proj_part,
        sum_proj_bias,
        sum_gamma_attn,
        sum_norm2_gain,
        sum_norm2_bias,
        grad_fc1_part,
        sum_fc1_bias,
        grad_fc2_part,
        sum_fc2_bias,
        sum_gamma_mlp,
    )


def solution(mesh):
    placed = (
        P(("wide", "narrow"), None, None),
        P(("wide", "narrow"), None, None),
        P(),
        P(),
        P(),
        P(),
        P(),
        P("wide", "narrow"),
        P(),
        P(),
        P(),
        P("wide", "narrow"),
        P(),
        P(),
        P(),
        P(),
        P("wide", "narrow"),
        P(),
        P("wide", "narrow"),
        P(),
        P(),
    )
    links = Links(mesh.shape["wide"], mesh.shape["narrow"])
    return jax.shard_map(
        functools.partial(local, links),
        mesh=mesh,
        in_specs=placed,
        out_specs=(
            P(("wide", "narrow"), None, None),
            P(("wide", "narrow"), None, None),
            P(),
            P(),
            P(),
            P("wide", "narrow"),
            P(),
            P(),
            P(),
            P("wide", "narrow"),
            P(),
            P(),
            P(),
            P(),
            P("wide", "narrow"),
            P(),
            P("wide", "narrow"),
            P(),
            P(),
        ),
        check_vma=False,
    )
```

```python
import functools
import math

import jax
import jax.numpy as jnp
import numpy as np
from jax import lax
from jax.experimental import pallas as pl
from jax.experimental.pallas import tpu as pltpu
from jax.sharding import PartitionSpec as P

EPSILON = 1e-06
ROOT_HALF = 0.7071067811865476
DENSITY = 0.3989422804014327
BF16 = jnp.bfloat16
F32 = jnp.float32
AXES = ("wide", "narrow")
TILE = 256
CHUNK = 1024
NEVER = -1e30
MIB = 1 << 20


class Links:
    def __init__(self, wide, narrow):
        self.wide, self.narrow = wide, narrow
        self.y = 1 << ((wide.bit_length() - 1) // 2)
        self.z = wide // self.y
        self.x = narrow // 2
        self.size = {"z": self.z, "y": self.y, "x": self.x, "core": 2}
        self.unit = {"core": 1, "x": 2, "y": narrow, "z": narrow * self.y}
        self.boxed = (self.z, self.y, self.x) == (4, 2, 2)

    def place(self):
        w, n = lax.axis_index("wide"), lax.axis_index("narrow")
        return {"z": w // self.y, "y": w % self.y, "x": n // 2, "core": n % 2, "w": w, "n": n}

    def swap(self, value, **offsets):
        mask = sum(self.unit[axis] * offset for axis, offset in offsets.items())
        count = self.wide * self.narrow
        return lax.ppermute(value, AXES, [(k, k ^ mask) for k in range(count)])

    def others(self, value, axis):
        return [self.swap(value, **{axis: d}) for d in range(1, self.size[axis])]


def pick(value, axis, index, count):
    size = value.shape[axis] // count
    return lax.dynamic_slice_in_dim(value, index * size, size, axis)


def after(value, *others):
    return lax.optimization_barrier((value,) + others)[0]


def native_gather(shard):
    return lax.all_gather(
        lax.all_gather(shard, "narrow", axis=1, tiled=True), "wide", axis=0, tiled=True
    )


class Gather:
    orders = (("x", "y"), ("y", "x"))

    def __init__(self, links, block, split):
        self.links, self.block, self.split = links, block, split

    def first(self, *wait):
        block = after(self.block, *wait) if wait else self.block
        self.steps = [block] + self.links.others(block, "z")
        return self.steps[-1]

    def second(self):
        parts = []
        for number, order in enumerate(self.orders):
            cols = slice(0, self.split) if number == 0 else slice(self.split, None)
            held = jnp.concatenate([p[None, :, cols] for p in self.steps], axis=0)
            parts.append([held] + self.links.others(held, order[0]))
        self.steps = parts
        return [p[-1] for p in parts]

    def third(self):
        parts = []
        for part, order in zip(self.steps, self.orders, strict=True):
            held = jnp.concatenate(part, axis=0)
            parts.append([held] + self.links.others(held, order[1]))
        self.steps = parts
        return [p[-1] for p in parts]

    def fourth(self):
        self.operands = []
        for part in self.steps:
            self.operands += part + [self.links.swap(held, core=1) for held in part]
        return self.operands

    def blocks(self, refs, number, me):
        links = self.links
        order = self.orders[number]
        out = []
        for core in range(2):
            for last in range(links.size[order[1]]):
                source = refs[4 * number + 2 * core + last]
                for k in range(source.shape[0]):
                    at = {
                        "z": me["z"] ^ (k % links.z),
                        order[0]: me[order[0]] ^ (k // links.z),
                        order[1]: me[order[1]] ^ last,
                    }
                    out.append((source.at[k], at["z"] * links.y + at["y"], at["x"] * 2 + (me["core"] ^ core)))
        return out


def at_least(n, values):
    out = values[3]
    for k in (2, 1, 0):
        out = jnp.where(n == k, values[k], out)
    return out


def window(ref, row, col, tall, broad):
    if not isinstance(row, int):
        row = pl.multiple_of(row, 8)
    if not isinstance(col, int):
        col = pl.multiple_of(col, 128)
    return ref.at[pl.ds(row, tall), pl.ds(col, broad)]


def columns(ref, col, broad):
    return ref.at[:, pl.ds(col, broad)]


class Weight:
    def __init__(self, operands, copies, joints=(), extra=0):
        self.operands, self.copies, self.joints, self.extra = operands, copies, joints, extra

    def fill(self, refs, target, sem):
        for source, to in self.copies(refs, target):
            pltpu.make_async_copy(source, to, sem).start()

    def wait(self, target, sem):
        pltpu.make_async_copy(target, target, sem).wait()
        for here, there in self.joints:
            target[:, here : here + 128] += target[:, there : there + 128]


def align_side(here, side):
    zero = jnp.zeros((side.shape[0], 64), side.dtype)
    return jnp.where(
        here["n"] % 2 == 0,
        jnp.concatenate([side, zero], axis=1),
        jnp.concatenate([zero, side], axis=1),
    )


def qkv_block(here, shard):
    even = here["n"] % 2 == 0
    main = jnp.where(even, shard[:, :384], shard[:, 192:])
    return jnp.concatenate([main, align_side(here, jnp.where(even, shard[:, 384:], shard[:, :192]))], axis=1)


def qkv_operands(links, gathered, shard):
    if not links.boxed:
        return Weight([native_gather(shard)], lambda refs, target: [(refs[0], target.at[:, pl.ds(0, 2304)])] + [
            (refs[0].at[:, pl.ds(0, 256)], target.at[:, pl.ds(2304, 256)])], extra=256)

    def copies(refs, target):
        me = links.place()
        out = []
        for source, w, n in gathered.blocks(refs, 0, me):
            out.append((source, window(target, w * 96, at_least(n, (0, 768, 1152, 1920)), 96, 384)))
        for source, w, n in gathered.blocks(refs, 1, me):
            for part, places in enumerate(((384, 2304, 1536, 2432), (512, 640, 1664, 1792))):
                out.append((columns(source, 128 * part, 128), window(target, w * 96, at_least(n, places), 96, 128)))
        return out

    return Weight(gathered.operands, copies, ((512, 2304), (1664, 2432)), 256)


def proj_operands(links, gathered, shard):
    if not links.boxed:
        return Weight([native_gather(shard)], lambda refs, target: [(refs[0], target.at[:, pl.ds(0, 768)])] + [
            (refs[0].at[:, pl.ds(0, 256)], target.at[:, pl.ds(768, 256)])], extra=256)

    def copies(refs, target):
        me = links.place()
        out = []
        for source, w, n in gathered.blocks(refs, 0, me):
            for part, places in enumerate(((0, 768, 384, 896), (128, 256, 512, 640))):
                out.append((columns(source, 128 * part, 128), window(target, w * 96, at_least(n, places), 96, 128)))
        return out

    return Weight(gathered.operands[:4], copies, ((128, 768), (512, 896)), 256)


def up_block(shard, chunk):
    return jnp.concatenate(
        [shard[:, 384 * half + 128 * chunk : 384 * half + 128 * chunk + 128] for half in range(2)], axis=1
    )


def down_block(shard_t, chunk):
    piece = shard_t[:, 128 * chunk : 128 * chunk + 128]
    half = piece.shape[0] // 2
    return jnp.concatenate([piece[:half], piece[half:]], axis=1)


def chunk_copies(full, chunk):
    def slices(refs, target):
        return [
            (columns(refs[0], 384 * g + 128 * chunk, 128), columns(target, 128 * g, 128)) for g in range(8)
        ]

    return Weight([full], slices)


def up_operands(links, gathered, col, full, chunk):
    if not links.boxed:
        return chunk_copies(full, chunk)

    def copies(refs, target):
        me = links.place()
        return [
            (columns(source, col, 256), window(target, w * 96, n * 256, 96, 256))
            for source, w, n in gathered.blocks(refs, 0, me)
        ]

    return Weight(gathered.operands[:4], copies)


def down_operands(links, gathered, col, full, chunk):
    if not links.boxed:
        return chunk_copies(full, chunk)

    def copies(refs, target):
        me = links.place()
        return [
            (columns(source, col + 128 * half, 128), window(target, n * 192 + half * 96, w * 128, 96, 128))
            for source, w, n in gathered.blocks([None] * 4 + list(refs), 1, me)
            for half in range(2)
        ]

    return Weight(gathered.operands[4:], copies)


class Scatter:
    orders = (("x", "y"), ("y", "x"))

    def __init__(self, links, here, partials, split):
        self.links, self.here, self.split = links, here, split
        self.partials = [
            p.reshape(links.x, 2, links.z, links.y, p.shape[2], p.shape[3]) for p in partials
        ]

    def first(self):
        c = self.here["core"]
        away = [pick(p, 1, 1 - c, 2)[:, 0] for p in self.partials]
        stay = [pick(p, 1, c, 2)[:, 0] for p in self.partials]
        away = jnp.concatenate(away, axis=-1) if len(away) > 1 else away[0]
        stay = jnp.concatenate(stay, axis=-1) if len(stay) > 1 else stay[0]
        self.terms = (stay, [self.links.swap(away, core=1)])
        return self.terms[1][-1]

    def step(self, stay, came, axis, index_of=None):
        dim = {"x": 0, "z": 1, "y": 2}[axis]
        links, size = self.links, self.links.size[axis]

        def part(at):
            total = pick(stay, dim, at, size).astype(F32)
            for term in came:
                total = total + pick(term, dim, at, size).astype(F32)
            return total

        arrived = [links.swap(part(self.here[axis] ^ d).astype(BF16), **{axis: d}) for d in range(1, size)]
        return part(self.here[axis]), arrived

    def second(self):
        stay, came = self.terms
        parts = []
        for number, order in enumerate(self.orders):
            cols = slice(0, self.split) if number == 0 else slice(self.split, None)
            parts.append(self.step(stay[..., cols], [t[..., cols] for t in came], order[0]))
        self.terms = parts
        return [p[1][-1] for p in parts]

    def third(self):
        self.terms = [
            self.step(stay, came, order[1]) for (stay, came), order in zip(self.terms, self.orders, strict=True)
        ]
        return [p[1][-1] for p in self.terms]

    def fourth(self):
        stay = jnp.concatenate([p[0] for p in self.terms], axis=-1)
        came = [jnp.concatenate([p[1][k] for p in self.terms], axis=-1) for k in range(len(self.terms[0][1]))]
        self.terms = self.step(stay, came, "z")
        return self.terms[1][-1]

    def done(self):
        stay, came = self.terms
        total = stay
        for term in came:
            total = total + term.astype(F32)
        return total.reshape(total.shape[-2:])


def native_scatter(partial):
    low = lax.psum_scatter(partial.astype(BF16), "wide", scatter_dimension=0, tiled=True)
    return lax.psum_scatter(low, "narrow", scatter_dimension=1, tiled=True).astype(F32)


def qkv_home(here, block):
    even = here["n"] % 2 == 0
    main, side = block[:, :384], block[:, 384:]
    return jnp.where(
        even,
        jnp.concatenate([main, side[:, :192]], axis=1),
        jnp.concatenate([side[:, 64:], main], axis=1),
    )


def proj_home(here, block):
    return jnp.where(here["n"] % 2 == 0, block[:, :192], block[:, 64:])


def natural_qkv(tiles):
    tiles = tiles.reshape(4, 768, 640)
    out = []
    for n in range(4):
        main, side = tiles[n, :, :384], tiles[n, :, 384:]
        out += [main, side[:, :192]] if n % 2 == 0 else [side[:, 64:], main]
    return jnp.concatenate(out, axis=1)


def natural_proj(tiles):
    tiles = tiles.reshape(4, 768, 256)
    return jnp.concatenate([tiles[n, :, :192] if n % 2 == 0 else tiles[n, :, 64:] for n in range(4)], axis=1)


def natural_up(chunks):
    tiles = [t.reshape(4, 768, 2, 128) for t in chunks]
    return jnp.stack(tiles, axis=0).transpose(2, 1, 3, 0, 4).reshape(768, -1)


def natural_down(chunks):
    tiles = [t.reshape(4, 8, 96, 2, 128) for t in chunks]
    return jnp.stack(tiles, axis=0).transpose(2, 0, 5, 1, 4, 3).reshape(-1, 768)


def tree_sum(terms):
    while len(terms) > 1:
        terms = [terms[k] + terms[k + 1] for k in range(0, len(terms), 2)]
    return terms[0]


def sum_everywhere(links, value):
    if not links.boxed:
        return lax.psum(value, AXES)
    value = value + links.swap(value, core=1)
    value = tree_sum(
        [value]
        + [links.swap(value, x=k % links.x, y=k // links.x) for k in range(1, links.x * links.y)]
    )
    return tree_sum([value] + links.others(value, "z"))


def whole(shape):
    return pl.BlockSpec(tuple(shape), lambda *_: (0,) * len(shape))


ANY = pl.BlockSpec(memory_space=pl.ANY)


def call(kernel, name, grid, ins, outs, scratch=(), flops=0, limit=56):
    moved = sum(a.size * a.dtype.itemsize for a, _ in ins)
    moved += sum(math.prod(s) * jnp.dtype(d).itemsize for s, d, _ in outs)
    return pl.pallas_call(
        kernel,
        name=name,
        grid=grid,
        in_specs=[spec for _, spec in ins],
        out_specs=[spec for _, _, spec in outs],
        out_shape=[jax.ShapeDtypeStruct(s, d) for s, d, _ in outs],
        scratch_shapes=list(scratch),
        compiler_params=pltpu.CompilerParams(vmem_limit_bytes=limit * MIB),
        cost_estimate=pl.CostEstimate(flops=int(flops), bytes_accessed=int(moved), transcendentals=0),
    )(*[a for a, _ in ins])


def nn(a, b):
    return lax.dot_general(a, b, (((1,), (0,)), ((), ())), preferred_element_type=F32)


def nt(a, b):
    return lax.dot_general(a, b, (((1,), (1,)), ((), ())), preferred_element_type=F32)


def tn(a, b):
    return lax.dot_general(a, b, (((0,), (0,)), ((), ())), preferred_element_type=F32)


def norm(values):
    centre = jnp.mean(values, axis=-1, keepdims=True)
    centred = values - centre
    spread = jnp.mean(centred * centred, axis=-1, keepdims=True)
    scaling = lax.rsqrt(spread + EPSILON)
    return centred * scaling, scaling


def norm_back(grad, normed, scaling, gain):
    scaled = grad * gain
    first = jnp.mean(scaled, axis=-1, keepdims=True)
    second = jnp.mean(scaled * normed, axis=-1, keepdims=True)
    return (scaled - first - normed * second) * scaling


def column_sum(values):
    return jnp.sum(values, axis=0, keepdims=True)


def prepare(sizes, inputs, cotangent, flags, mask_token, gain, shift, gamma_mlp):
    images, length, tall, width = sizes
    rows = images * tall

    def kernel(x_ref, g_ref, flag_ref, token_ref, gain_ref, shift_ref, gamma_ref,
               h0_ref, n1_ref, n1t_ref, g_out, df_ref, dft_ref, sum_ref, x_s, g_s):
        x_s[...] = jnp.zeros_like(x_s)
        g_s[...] = jnp.zeros_like(g_s)
        sum_ref[...] = jnp.zeros_like(sum_ref)

        def body(i, carry):
            at = pl.ds(pl.multiple_of(i * tall, 16), tall)
            x_s[0:length, :] = x_ref[i].astype(F32)
            g_s[0:length, :] = g_ref[i].astype(F32)
            start = jnp.where(flag_ref[at, :] == 1, token_ref[...], x_s[...])
            h0_ref[at, :] = start
            normed, _ = norm(start)
            n1_ref[at, :] = (normed * gain_ref[...] + shift_ref[...]).astype(BF16)
            g = g_s[...]
            g_out[at, :] = g.astype(BF16)
            df = gamma_ref[...] * g
            df_ref[at, :] = df.astype(BF16)
            sum_ref[...] += column_sum(df)
            return carry

        lax.fori_loop(0, images, body, 0)
        n1t_ref[...] = n1_ref[...].T
        dft_ref[...] = df_ref[...].T

    row = whole((1, width))
    return call(
        kernel, "prepare", (),
        [(inputs, whole(inputs.shape)), (cotangent, whole(cotangent.shape)), (flags, whole((rows, 1))),
         (mask_token, row), (gain, row), (shift, row), (gamma_mlp, row)],
        [((rows, width), F32, whole((rows, width))), ((rows, width), BF16, whole((rows, width))),
         ((width, rows), BF16, whole((width, rows))), ((rows, width), BF16, whole((rows, width))),
         ((rows, width), BF16, whole((rows, width))), ((width, rows), BF16, whole((width, rows))),
         ((1, width), F32, row)],
        [pltpu.VMEM((tall, width), F32), pltpu.VMEM((tall, width), F32)],
        flops=rows * width * 40,
    )


def table_columns(grid_side, broad):
    side = 2 * grid_side - 1
    q = np.arange(broad)
    entry = (q // grid_side) * side + q % grid_side + grid_side - 1
    return jnp.asarray(np.where(q < side * grid_side, entry, -(1 << 20)).astype(np.int32)[None])


def three_parts(values):
    high = values.astype(BF16)
    rest = values - high.astype(F32)
    middle = rest.astype(BF16)
    return high, middle, (rest - middle.astype(F32)).astype(BF16)


def bias_kernel(table_t, entry, grid_side, tall, broad):
    heads = table_t.shape[0]
    length = grid_side * grid_side + 1
    wide = entry.shape[1]
    inner = (2 * grid_side - 1) ** 2

    def kernel(table_ref, entry_ref, out_ref, *halves):
        def put(at, count, values):
            for half, ref in enumerate(halves):
                ref[pl.ds(at, count), :] = values[:, 128 * half : 128 * half + 128]

        parts = three_parts(table_ref[...])
        left, top, corner = (table_ref[:, inner + 1 : inner + 2], table_ref[:, inner : inner + 1],
                             table_ref[:, inner + 2 : inner + 3])
        lane = lax.broadcasted_iota(jnp.int32, (heads, broad), 1)

        def column(b, carry):
            which = lax.broadcasted_iota(jnp.int32, (table_ref.shape[1], wide), 0) + b
            select = jnp.where(which == entry_ref[...], 1.0, 0.0).astype(BF16)
            spread = nn(parts[0], select) + nn(parts[1], select) + nn(parts[2], select)
            for a in range(grid_side):
                shift = (grid_side - 1 - a) * grid_side - 1
                moved = pltpu.roll(spread, (wide - shift) % wide, 1)[:, :broad]
                moved = jnp.where(lane == 0, top, moved)
                put(pl.multiple_of((1 + grid_side * a + b) * heads, 16), heads, moved)
            return carry

        lax.fori_loop(0, grid_side, column, 0)
        put(0, heads, jnp.where(lane == 0, corner, left))
        rest = (tall - length) * heads
        put(length * heads, rest, jnp.full((rest, broad), NEVER, F32))
        for h in range(out_ref.shape[0]):
            for half, ref in enumerate(halves):
                out_ref[h, :, 128 * half : 128 * half + 128] = ref[pl.ds(h, tall, stride=heads), :]

    return call(
        kernel, "bias", (),
        [(table_t, whole(table_t.shape)), (entry, whole(entry.shape))],
        [((12, tall, broad), F32, whole((12, tall, broad)))],
        [pltpu.VMEM((tall * heads, 128), F32)] * (broad // 128),
        flops=2 * 48 * 768 * wide * grid_side,
    )[0]


def bias_back_kernel(terms, entry, grid_side, width):
    count, tall, broad = terms.shape
    heads = 16
    wide = entry.shape[1]
    inner = (2 * grid_side - 1) ** 2
    length = grid_side * grid_side + 1

    def kernel(terms_ref, entry_ref, out_ref, *halves):
        def get(at, count):
            return jnp.concatenate([ref[pl.ds(at, count), :] for ref in halves], axis=1)

        lane = lax.broadcasted_iota(jnp.int32, (heads, broad), 1)
        inside = (lane >= 1) & (lane < length)
        for h in range(heads):
            values = terms_ref[h] if h < count else jnp.zeros((tall, broad), F32)
            for half, ref in enumerate(halves):
                ref[pl.ds(h, tall, stride=heads), :] = values[:, 128 * half : 128 * half + 128]

        def column(b, carry):
            total, edge = carry
            which = lax.broadcasted_iota(jnp.int32, (width, wide), 0) + b
            select = jnp.where(which == entry_ref[...], 1.0, 0.0).astype(BF16)
            spread = jnp.zeros((heads, wide), F32)
            for a in range(grid_side):
                shift = (grid_side - 1 - a) * grid_side - 1
                found = get(pl.multiple_of((1 + grid_side * a + b) * heads, 16), heads)
                edge = edge + jnp.where(lane == 0, found, 0.0)
                found = jnp.where(inside, found, 0.0)
                found = jnp.concatenate([found, jnp.zeros((heads, wide - broad), F32)], axis=1)
                spread = spread + pltpu.roll(found, shift % wide, 1)
            parts = three_parts(spread)
            total = total + nt(parts[0], select) + nt(parts[1], select) + nt(parts[2], select)
            return total, edge

        total, edge = lax.fori_loop(
            0, grid_side, column, (jnp.zeros((heads, width), F32), jnp.zeros((heads, broad), F32))
        )
        first = get(0, heads)
        top = jnp.sum(edge, axis=1, keepdims=True)
        left = jnp.sum(jnp.where(inside, first, 0.0), axis=1, keepdims=True)
        corner = first[:, 0:1]
        place = lax.broadcasted_iota(jnp.int32, (heads, width), 1)
        total = jnp.where(place == inner, top, total)
        total = jnp.where(place == inner + 1, left, total)
        out_ref[...] = jnp.where(place == inner + 2, corner, total)

    return call(
        kernel, "bias_back", (),
        [(terms, whole(terms.shape)), (entry, whole(entry.shape))],
        [((heads, width), F32, whole((heads, width)))],
        [pltpu.VMEM((tall * heads, 128), F32)] * (broad // 128),
        flops=2 * 48 * 768 * wide * grid_side,
    )[0]


def project(sizes, first_low, weight, scale, shift):
    images, length, tall, width = sizes
    rows = images * tall
    cols = scale.shape[1]
    count = len(weight.operands)

    def kernel(*refs):
        n1_ref, scale_ref, shift_ref = refs[:3]
        out_ref, w_s, sem = refs[3 + count :]
        step = pl.program_id(0)

        @pl.when(step == 0)
        def _():
            weight.fill(refs[3 : 3 + count], w_s, sem)
            weight.wait(w_s, sem)

        w = w_s[:, pl.ds(pl.multiple_of(step * TILE, TILE), TILE)]
        out_ref[...] = ((nn(n1_ref[...], w) + shift_ref[...]) * scale_ref[...]).astype(BF16)

    tile = pl.BlockSpec((1, TILE), lambda t: (0, t))
    return call(
        kernel, "project", (cols // TILE,),
        [(first_low, whole((rows, width))), (scale, tile), (shift, tile)] + [(a, ANY) for a in weight.operands],
        [((rows, cols), BF16, pl.BlockSpec((rows, TILE), lambda t: (0, t)))],
        [pltpu.VMEM((width, cols + weight.extra), BF16), pltpu.SemaphoreType.DMA],
        flops=2 * rows * width * cols,
    )[0]


def head_masks(tall):
    lane = lax.broadcasted_iota(jnp.int32, (tall, 128), 1)
    return [lane < 64, lane >= 64]


def attend(sizes, mixed, bias, first, pairs):
    images, length, tall, width = sizes
    rows = images * tall
    every = width // 128
    broad = bias.shape[2]

    def kernel(q_ref, k_ref, v_ref, bias_ref, out_ref, p_ref):
        masks = head_masks(tall)

        def body(i, carry):
            at = pl.ds(pl.multiple_of(i * tall, 16), tall)
            q, k, v = q_ref[at, :], k_ref[at, :], v_ref[at, :]
            vt = v.T
            outs = []
            for h in range(2):
                s = nt(k, jnp.where(masks[h], q, jnp.zeros_like(q))) + bias_ref[h, :, 0:tall]
                e = jnp.exp(s - jnp.max(s, axis=0, keepdims=True))
                p = (e / jnp.sum(e, axis=0, keepdims=True)).astype(BF16)
                p_ref[h, i, :, 0:tall] = p
                outs.append(nn(vt[64 * h : 64 * h + 64, :], p))
            out_ref[at, :] = jnp.concatenate(outs, axis=0).T.astype(BF16)
            return carry

        lax.fori_loop(0, images, body, 0)

    def column(at):
        return pl.BlockSpec((rows, 128), lambda t: (0, at + t))

    return call(
        kernel, "attend", (pairs,),
        [(mixed, column(first)), (mixed, column(every + first)), (mixed, column(2 * every + first)),
         (bias, pl.BlockSpec((2, tall, broad), lambda t: (first + t, 0, 0)))],
        [((rows, 128 * pairs), BF16, column(0)),
         ((2 * pairs, images, tall, broad), BF16,
          pl.BlockSpec((2, images, tall, broad), lambda t: (t, 0, 0, 0)))],
        flops=4 * rows * tall * 128 * pairs,
    )


def attend_back(sizes, mixed, probs, grad_out, score_scale, first, pairs):
    images, length, tall, width = sizes
    rows = images * tall
    every = width // 128
    broad = probs.shape[3]

    def kernel(q_ref, k_ref, v_ref, do_ref, p_ref, dq_ref, dk_ref, dv_ref, terms_ref, qb_ref, vb_ref):
        masks = head_masks(tall)
        terms_ref[...] = jnp.zeros_like(terms_ref)
        qb_ref[...] = jnp.zeros_like(qb_ref)
        vb_ref[...] = jnp.zeros_like(vb_ref)

        def body(i, carry):
            at = pl.ds(pl.multiple_of(i * tall, 16), tall)
            q, k, v, do = q_ref[at, :], k_ref[at, :], v_ref[at, :], do_ref[at, :]
            kt = k.T
            dv = jnp.zeros((tall, 128), F32)
            dk = jnp.zeros((tall, 128), F32)
            dqs = []
            for h in range(2):
                do_h = jnp.where(masks[h], do, jnp.zeros_like(do))
                q_h = jnp.where(masks[h], q, jnp.zeros_like(q))
                p_low = p_ref[h, i, :, 0:tall]
                p = p_low.astype(F32)
                t = p * nt(v, do_h)
                ds = t - p * jnp.sum(t, axis=0, keepdims=True)
                ds_low = ds.astype(BF16)
                terms_ref[h, :, 0:tall] += ds_low.astype(F32)
                dv = dv + nn(p_low, do_h)
                dk = dk + nn(ds_low, q_h)
                dqs.append(nn(kt[64 * h : 64 * h + 64, :], ds_low))
            dq = jnp.concatenate(dqs, axis=0).T * score_scale
            dq_ref[at, :] = dq.astype(BF16)
            dk_ref[at, :] = dk.astype(BF16)
            dv_ref[at, :] = dv.astype(BF16)
            qb_ref[...] += column_sum(dq)
            vb_ref[...] += column_sum(dv)
            return carry

        lax.fori_loop(0, images, body, 0)

    def column(at):
        return pl.BlockSpec((rows, 128), lambda t: (0, at + t))

    one = pl.BlockSpec((1, 128), lambda t: (0, t))
    return call(
        kernel, "attend_back", (pairs,),
        [(mixed, column(first)), (mixed, column(every + first)), (mixed, column(2 * every + first)),
         (grad_out, column(first)),
         (probs, pl.BlockSpec((2, images, tall, broad), lambda t: (t, 0, 0, 0)))],
        [((rows, 128 * pairs), BF16, column(0))] * 3
        + [((2 * pairs, tall, broad), F32, pl.BlockSpec((2, tall, broad), lambda t: (t, 0, 0))),
           ((1, 128 * pairs), F32, one), ((1, 128 * pairs), F32, one)],
        flops=8 * rows * tall * 128 * pairs,
    )


def merge(sizes, attended, start, weight, proj_bias, gamma, gain, shift):
    images, length, tall, width = sizes
    rows = images * tall
    count = len(weight.operands)

    def kernel(*refs):
        att_refs, refs = refs[: len(attended)], refs[len(attended) :]
        h0_ref, bias_ref, gamma_ref, gain_ref, shift_ref = refs[:5]
        h1_ref, n2_ref, n2t_ref, w_s, sem = refs[5 + count :]
        weight.fill(refs[5 : 5 + count], w_s, sem)
        weight.wait(w_s, sem)
        part = width // len(attended)
        h1_ref[...] = sum(nn(r[...], w_s[part * k : part * k + part, 0:width]) for k, r in enumerate(att_refs))

        def body(i, carry):
            at = pl.ds(pl.multiple_of(i * 80, 16), 80)
            middle = h0_ref[at, :] + gamma_ref[...] * (h1_ref[at, :] + bias_ref[...])
            h1_ref[at, :] = middle
            normed, _ = norm(middle)
            n2_ref[at, :] = (normed * gain_ref[...] + shift_ref[...]).astype(BF16)
            return carry

        lax.fori_loop(0, rows // 80, body, 0)
        n2t_ref[...] = n2_ref[...].T

    row = whole((1, width))
    return call(
        kernel, "merge", (),
        [(a, whole(a.shape)) for a in attended]
        + [(start, whole((rows, width))), (proj_bias, row), (gamma, row), (gain, row), (shift, row)] + [(a, ANY) for a in weight.operands],
        [((rows, width), F32, whole((rows, width))), ((rows, width), BF16, whole((rows, width))),
         ((width, rows), BF16, whole((width, rows)))],
        [pltpu.VMEM((width, width + weight.extra), BF16), pltpu.SemaphoreType.DMA],
        flops=2 * rows * width * width,
    )


def feed(sizes, second_low, second_t, down_low, down_t, up, down, bias, sums):
    images, length, tall, width = sizes
    rows = images * tall
    ups, downs = len(up.operands), len(down.operands)
    carried = [] if sums is None else list(sums)

    def kernel(*refs):
        n2_ref, n2t_ref, df_ref, dft_ref, bias_ref = refs[:5]
        rest = refs[5:]
        up_refs, rest = rest[:ups], rest[ups:]
        down_refs, rest = rest[:downs], rest[downs:]
        sum_refs, rest = rest[: len(carried)], rest[len(carried) :]
        f_ref, dn_ref, gup_ref, gdown_ref, gbias_ref, up_s, down_s, sems = rest
        step = pl.program_id(0)

        @pl.when(step == 0)
        def _():
            up.fill(up_refs, up_s, sems.at[0])
            down.fill(down_refs, down_s, sems.at[1])
            if carried:
                pltpu.make_async_copy(sum_refs[0], f_ref, sems.at[2]).start()
                pltpu.make_async_copy(sum_refs[1], dn_ref, sems.at[3]).start()
            up.wait(up_s, sems.at[0])
            down.wait(down_s, sems.at[1])
            if not carried:
                f_ref[...] = jnp.zeros_like(f_ref)
                dn_ref[...] = jnp.zeros_like(dn_ref)

        at = pl.ds(pl.multiple_of(step * TILE, TILE), TILE)
        up_w, down_w = up_s[:, at], down_s[:, at]
        u = nn(n2_ref[...], up_w) + bias_ref[...]
        dz = nn(df_ref[...], down_w)
        bell = jnp.exp(-0.5 * u * u)
        below = 0.5 * (1.0 + lax.erf(u * ROOT_HALF))
        z = (u * below).astype(BF16)
        du = dz * (below + u * (DENSITY * bell))
        gbias_ref[...] = column_sum(du)
        du = du.astype(BF16)
        gup_ref[0] = nn(n2t_ref[...], du).astype(BF16).reshape(8, 96, TILE)
        grad = nn(dft_ref[...], z).astype(BF16)
        for n in range(4):
            for w in range(2):
                for half in range(2):
                    gdown_ref[n, w, :, 128 * half : 128 * half + 128] = grad[
                        192 * n + 96 * half : 192 * n + 96 * half + 96, 128 * w : 128 * w + 128
                    ]
        if carried:
            @pl.when(step == 0)
            def _():
                pltpu.make_async_copy(sum_refs[0], f_ref, sems.at[2]).wait()
                pltpu.make_async_copy(sum_refs[1], dn_ref, sems.at[3]).wait()

        f_ref[...] += nt(z, down_w)
        dn_ref[...] += nt(du, up_w)

    tile = pl.BlockSpec((1, TILE), lambda t: (0, t))
    full = whole((rows, width))
    flipped = whole((width, rows))
    steps = CHUNK // TILE
    shape = (4, 8, 96, TILE)
    return call(
        kernel, "feed", (steps,),
        [(second_low, full), (second_t, flipped), (down_low, full), (down_t, flipped), (bias, tile)]
        + [(a, ANY) for a in up.operands + down.operands + carried],
        [((rows, width), F32, full), ((rows, width), F32, full),
         (shape, BF16, pl.BlockSpec((1, 8, 96, TILE), lambda t: (t, 0, 0, 0))),
         (shape, BF16, pl.BlockSpec((4, 2, 96, TILE), lambda t: (0, t, 0, 0))), ((1, CHUNK), F32, tile)],
        [pltpu.VMEM((width, CHUNK), BF16), pltpu.VMEM((width, CHUNK), BF16), pltpu.SemaphoreType.DMA((4,))],
        flops=12 * rows * width * CHUNK,
    )


def middle_back(sizes, attended, branch, grad_n2, middle, start, upstream, weight, rows_in):
    images, length, tall, width = sizes
    rows = images * tall
    count = len(weight.operands)

    def kernel(*refs):
        att_refs, refs = refs[: len(attended)], refs[len(attended) :]
        f_ref, dn_ref, h1_ref, h0_ref, g_ref, b2_ref, gm_ref, gain_ref, ga_ref = refs[:9]
        out_ref, dh_ref, do_ref, gproj_ref, sum_ref, w_s, acc_s, sem = refs[9 + count :]
        step = pl.program_id(0)

        @pl.when(step == 0)
        def _():
            weight.fill(refs[9 : 9 + count], w_s, sem)
            acc_s[...] = jnp.zeros_like(acc_s)
            sum_ref[...] = jnp.zeros_like(sum_ref)
            weight.wait(w_s, sem)

        f = f_ref[...] + b2_ref[...]
        h1 = h1_ref[...]
        g = g_ref[...].astype(F32)
        layer = h1 + gm_ref[...] * f
        out_ref[0] = layer[0:length].astype(BF16)
        normed, scaling = norm(h1)
        dn = dn_ref[...]
        dh = g + norm_back(dn, normed, scaling, gain_ref[...])
        dh_ref[...] = dh
        da = ga_ref[...] * dh
        sum_ref[0:1, :] += column_sum(g * f)
        sum_ref[1:2, :] += column_sum(dn * normed)
        sum_ref[2:3, :] += column_sum(dn)
        sum_ref[3:4, :] += column_sum(dh * (h1 - h0_ref[...])) / ga_ref[...]
        sum_ref[4:5, :] += column_sum(da)
        da = da.astype(BF16)
        do_ref[...] = nt(da, w_s[:, 0:width]).astype(BF16)
        part = width // len(attended)
        for k, r in enumerate(att_refs):
            acc_s[part * k : part * k + part, :] += tn(r[...], da)

        @pl.when(step == images - 1)
        def _():
            for n, at in enumerate((0, 128, 384, 512)):
                gproj_ref[n] = acc_s[:, at : at + 256].astype(BF16).reshape(8, 96, 256)

    row = whole((1, width))
    band = pl.BlockSpec((tall, width), lambda i: (i, 0))
    return call(
        kernel, "middle_back", (images,),
        [(a, pl.BlockSpec((tall, a.shape[1]), lambda i: (i, 0))) for a in attended]
        + [(a, band) for a in (branch, grad_n2, middle, start, upstream)] + [(a, row) for a in rows_in]
        + [(a, ANY) for a in weight.operands],
        [((images, length, width), BF16, pl.BlockSpec((1, length, width), lambda i: (i, 0, 0))),
         ((rows, width), F32, band), ((rows, width), BF16, band),
         ((4, 8, 96, 256), BF16, whole((4, 8, 96, 256))), ((8, width), F32, whole((8, width)))],
        [pltpu.VMEM((width, width + weight.extra), BF16), pltpu.VMEM((width, width), F32),
         pltpu.SemaphoreType.DMA],
        flops=4 * rows * width * width,
    )


def mixed_grad(sizes, first_t, grads):
    images, length, tall, width = sizes
    rows = images * tall
    plan = ((0, 1, 0), (2, 1, 128), (3, 4, 0), (5, 4, 128))

    def kernel(n1t_ref, *refs):
        out_ref = refs[-1]
        step = pl.program_id(0)
        for n, (main, side, at) in enumerate(plan):
            @pl.when(step == n)
            def _(main=main, side=side, at=at):
                out_ref[0, :, :, 0:384] = nn(n1t_ref[...], refs[main][...]).astype(BF16).reshape(8, 96, 384)
                out_ref[0, :, :, 384:640] = (
                    nn(n1t_ref[...], refs[side][:, at : at + 256]).astype(BF16).reshape(8, 96, 256)
                )

    return call(
        kernel, "mixed_grad", (4,),
        [(first_t, whole((width, rows)))] + [(g, whole(g.shape)) for g in grads],
        [((4, 8, 96, 640), BF16, pl.BlockSpec((1, 8, 96, 640), lambda t: (t, 0, 0, 0)))],
        flops=6 * rows * width * width,
    )[0]


def start_back(sizes, grads, weight, start, grad_middle, flags, gain):
    images, length, tall, width = sizes
    rows = images * tall
    count = len(weight.operands)

    def kernel(*refs):
        grad_refs, refs = refs[: len(grads)], refs[len(grads) :]
        h0_ref, dh_ref, flag_ref, gain_ref = refs[:4]
        out_ref, sum_ref, w_s, sem = refs[4 + count :]
        step = pl.program_id(0)

        @pl.when(step == 0)
        def _():
            weight.fill(refs[4 : 4 + count], w_s, sem)
            sum_ref[...] = jnp.zeros_like(sum_ref)
            weight.wait(w_s, sem)

        part = 3 * width // len(grads)
        dn = sum(nt(r[...], w_s[:, part * k : part * k + part]) for k, r in enumerate(grad_refs))
        normed, scaling = norm(h0_ref[...])
        dh = dh_ref[...] + norm_back(dn, normed, scaling, gain_ref[...])
        masked = flag_ref[...] == 1
        out_ref[0] = jnp.where(masked, 0.0, dh)[0:length]
        sum_ref[0:1, :] += column_sum(dn * normed)
        sum_ref[1:2, :] += column_sum(dn)
        sum_ref[2:3, :] += column_sum(jnp.where(masked, dh, 0.0))

    band = pl.BlockSpec((tall, width), lambda i: (i, 0))
    return call(
        kernel, "start_back", (images,),
        [(g, pl.BlockSpec((tall, g.shape[1]), lambda i: (i, 0))) for g in grads] + [(start, band), (grad_middle, band),
         (flags, pl.BlockSpec((tall, 1), lambda i: (i, 0))), (gain, whole((1, width)))]
        + [(a, ANY) for a in weight.operands],
        [((images, length, width), F32, pl.BlockSpec((1, length, width), lambda i: (i, 0, 0))),
         ((8, width), F32, whole((8, width)))],
        [pltpu.VMEM((width, 3 * width + weight.extra), BF16), pltpu.SemaphoreType.DMA],
        flops=6 * rows * width * width,
    )


def local(
    links,
    inputs,
    cotangent,
    group_sizes,
    mask_patterns,
    mask_token,
    norm1_gain,
    norm1_bias,
    qkv_weight,
    query_bias,
    value_bias,
    bias_table,
    proj_weight,
    proj_bias,
    gamma_attn,
    norm2_gain,
    norm2_bias,
    fc1_weight,
    fc1_bias,
    fc2_weight,
    fc2_bias,
    gamma_mlp,
):
    images, length, width = inputs.shape
    table_rows, heads = bias_table.shape
    grid_side = math.isqrt(length - 1)
    group_count = mask_patterns.shape[0]
    tall = -(-length // 16) * 16
    rows = images * tall
    hidden = fc1_bias.shape[0]
    chunks = hidden // CHUNK
    sizes = (images, length, tall, width)
    score_scale = (width // heads) ** (-0.5)
    here = links.place()

    image_ids = lax.axis_index(AXES) * images + jnp.arange(images, dtype=jnp.int32)
    bounds = jnp.cumsum(group_sizes)[: group_count - 1]
    member = jnp.sum((image_ids[:, None] >= bounds[None, :]).astype(jnp.int32), axis=1)
    chosen = (member[:, None] == jnp.arange(group_count, dtype=jnp.int32)[None, :]).astype(jnp.int32)
    patterns = jnp.sum(chosen[:, :, None] * mask_patterns[None, :, :], axis=1)
    flags = jnp.pad(patterns, ((0, 0), (1, tall - length))).reshape(rows, 1)

    def row(v):
        return v.reshape(1, -1)

    boxed = links.boxed
    fc2_t = fc2_weight.T
    if boxed:
        mix = Gather(links, qkv_block(here, qkv_weight), 384)
        near = Gather(
            links,
            jnp.concatenate(
                [align_side(here, proj_weight), up_block(fc1_weight, 0), down_block(fc2_t, 0)], axis=1
            ),
            512,
        )
        far = Gather(
            links,
            jnp.concatenate(
                [up_block(fc1_weight, 1), up_block(fc1_weight, 2), down_block(fc2_t, 1), down_block(fc2_t, 2)],
                axis=1,
            ),
            512,
        )
        full_up = full_down = None
    else:
        mix = near = far = None
        full_up, full_down = native_gather(fc1_weight), native_gather(fc2_weight).T

    entry = table_columns(grid_side, 384)
    table_t = jnp.pad(bias_table.T, ((0, 16 - heads), (0, width - table_rows)))
    if boxed:
        mark = mix.first()
    bias = bias_kernel(table_t, entry, grid_side, tall, 256)
    if boxed:
        mark = mix.second()
        cotangent = after(cotangent, bias, *mix.steps[0][:1])
    start, first_low, first_t, upstream, down_low, down_t, sum_fc2 = prepare(
        sizes, inputs, cotangent, flags, row(mask_token), row(norm1_gain), row(norm1_bias), row(gamma_mlp)
    )
    if boxed:
        mark = mix.third()
        ahead = near.first(mix.steps[0][0])
        mix.fourth()
        first_low = after(first_low, ahead)
        mark = near.second()
    qkv = qkv_operands(links, mix, qkv_weight)
    nothing = jnp.zeros((width,), F32)
    scale = row(jnp.concatenate([nothing + score_scale, nothing + 1.0, nothing + 1.0]))
    mixed = project(sizes, first_low, qkv, scale, row(jnp.concatenate([query_bias, nothing, value_bias])))
    groups = ((0, 3), (3, 3))
    attended, probs = [], []
    for number, (first, pairs) in enumerate(groups):
        if boxed and number == 0:
            mark = near.third()
            ahead = far.first(mixed)
            mixed_here = after(mixed, *[p[0] for p in near.steps])
        elif boxed:
            near.fourth()
            far.second()
            mixed_here = after(mixed, ahead, attended[-1], *[p[0] for p in far.steps])
        else:
            mixed_here = mixed
        out, kept = attend(sizes, mixed_here, bias, first, pairs)
        attended.append(out)
        probs.append(kept)
    proj = proj_operands(links, near, proj_weight)
    if boxed:
        far.third()
        start_here = after(start, *[p[0] for p in far.steps])
    else:
        start_here = start
    middle, second_low, second_t = merge(
        sizes, attended, start_here, proj, row(proj_bias), row(gamma_attn), row(norm2_gain), row(norm2_bias)
    )
    if boxed:
        far.fourth()
        ups = [up_operands(links, near, 256, None, 0), up_operands(links, far, 0, None, 1),
               up_operands(links, far, 256, None, 2)]
        downs = [down_operands(links, near, 0, None, 0), down_operands(links, far, 0, None, 1),
                 down_operands(links, far, 256, None, 2)]
    else:
        ups = [up_operands(links, None, 0, full_up, k) for k in range(chunks)]
        downs = [down_operands(links, None, 0, full_down, k) for k in range(chunks)]

    fc1_groups = fc1_bias.reshape(8, chunks, 128)
    sums, up_grads, down_grads, hidden_sums = None, [], [], []
    early = None
    for k in range(chunks):
        if boxed and k == 2:
            early = Scatter(links, here, up_grads + down_grads, 512)
            mark = early.first()
        chunk_bias = fc1_groups[:, k].reshape(1, -1)
        branch, grad_n2, up_grad, down_grad, hidden_sum = feed(
            sizes, second_low, second_t, down_low, down_t, ups[k], downs[k], chunk_bias, sums
        )
        sums = (branch, grad_n2)
        up_grads.append(up_grad)
        down_grads.append(down_grad)
        hidden_sums.append(hidden_sum.reshape(8, 128))
    sum_fc1 = jnp.stack(hidden_sums, axis=1)

    if boxed:
        early.second()
        branch = after(branch, mark)
    layer_out, grad_middle, grad_att, grad_proj, middle_sums = middle_back(
        sizes, attended, branch, grad_n2, middle, start, upstream, proj,
        [row(fc2_bias), row(gamma_mlp), row(norm2_gain), row(gamma_attn)],
    )
    if boxed:
        late = Scatter(links, here, [grad_proj, up_grads[2], down_grads[2]], 512)

    back = []
    for number, (first, pairs) in enumerate(groups):
        grad_here = grad_att
        if boxed and number == 0:
            mark = early.third()
            ahead = late.first()
            grad_here = after(grad_att, *[p[0] for p in early.terms])
        elif boxed:
            early.fourth()
            late.second()
            grad_here = after(grad_att, back[-1][0], early.terms[0], *[p[0] for p in late.terms])
        back.append(attend_back(sizes, mixed, probs[number], grad_here, score_scale, first, pairs))
    grads = [b[k] for k in range(3) for b in back]
    if boxed:
        late.third()
        first_t = after(first_t, *[p[0] for p in late.terms])
    grad_mix = mixed_grad(sizes, first_t, grads)
    if boxed:
        late.fourth()
        last = Scatter(links, here, [grad_mix], 384)
        last.first()
        flags = after(flags, grad_mix)
    input_grad, start_sums = start_back(sizes, grads, qkv, start, grad_middle, flags, row(norm1_gain))
    terms = jnp.concatenate([b[3] for b in back], axis=0)
    if boxed:
        last.second()
    grad_table = bias_back_kernel(terms, entry, grid_side, width)
    sum_query, sum_value = (jnp.concatenate([b[k] for b in back], axis=1) for k in (4, 5))
    small = jnp.concatenate(
        [grad_table, start_sums, middle_sums, sum_query, sum_value, sum_fc2, sum_fc1.reshape(-1, width)], axis=0
    )
    small = sum_everywhere(links, jnp.pad(small, ((0, -small.shape[0] % 8), (0, 0))))
    if boxed:
        last.third()
        last.fourth()
        grad_qkv = qkv_home(here, last.done())
        near_block, far_block = early.done(), late.done()
        grad_proj = proj_home(here, far_block[:, 0:256])
        up_parts = [near_block[:, 0:256], near_block[:, 256:512], far_block[:, 256:512]]
        down_parts = [near_block[:, 512:768], near_block[:, 768:1024], far_block[:, 512:768]]
        grad_fc1 = jnp.concatenate(
            [up_parts[k][:, 128 * half : 128 * half + 128] for half in range(2) for k in range(chunks)], axis=1
        )
        grad_fc2 = jnp.concatenate(
            [jnp.concatenate([p[:, :128], p[:, 128:]], axis=0) for p in down_parts], axis=1
        ).T
    else:
        grad_qkv = native_scatter(natural_qkv(grad_mix))
        grad_proj = native_scatter(natural_proj(grad_proj))
        grad_fc1 = native_scatter(natural_up(up_grads))
        grad_fc2 = native_scatter(natural_down(down_grads))
    base = 16
    return (
        layer_out,
        input_grad,
        small[base + 2],
        small[base],
        small[base + 1],
        grad_qkv,
        small[base + 16],
        small[base + 17],
        small[:heads, :table_rows].T,
        grad_proj,
        small[base + 12],
        small[base + 11],
        small[base + 9],
        small[base + 10],
        grad_fc1,
        small[base + 19 : base + 19 + hidden // width].reshape(-1),
        grad_fc2,
        small[base + 18],
        small[base + 8],
    )


def solution(mesh):
    images = P(AXES, None, None)
    both = P("wide", "narrow")
    same = P()
    links = Links(mesh.shape["wide"], mesh.shape["narrow"])
    return jax.shard_map(
        functools.partial(local, links),
        mesh=mesh,
        in_specs=(
            images, images, same, same, same, same, same, both, same, same, same, both, same, same,
            same, same, both, same, both, same, same,
        ),
        out_specs=(
            images, images, same, same, same, both, same, same, same, both, same, same, same, same,
            both, same, both, same, same,
        ),
        check_vma=False,
    )
```

```python
import functools
import math

import jax
import jax.numpy as jnp
import numpy as np
from jax import lax
from jax.experimental import pallas as pl
from jax.experimental.pallas import tpu as pltpu
from jax.sharding import PartitionSpec as P

EPSILON = 1e-06
ROOT_HALF = 0.7071067811865476
DENSITY = 0.3989422804014327
BF16 = jnp.bfloat16
F32 = jnp.float32
AXES = ("wide", "narrow")
TILE = 512
BAND = 200
CHUNK = 1024
NEVER = -1e30
MIB = 1 << 20


class Links:
    def __init__(self, wide, narrow):
        self.wide, self.narrow = wide, narrow
        self.y = 1 << ((wide.bit_length() - 1) // 2)
        self.z = wide // self.y
        self.x = narrow // 2
        self.size = {"z": self.z, "y": self.y, "x": self.x, "core": 2}
        self.unit = {"core": 1, "x": 2, "y": narrow, "z": narrow * self.y}
        self.boxed = (self.z, self.y, self.x) == (4, 2, 2)

    def place(self):
        w, n = lax.axis_index("wide"), lax.axis_index("narrow")
        return {"z": w // self.y, "y": w % self.y, "x": n // 2, "core": n % 2, "w": w, "n": n}

    def swap(self, value, **offsets):
        mask = sum(self.unit[axis] * offset for axis, offset in offsets.items())
        count = self.wide * self.narrow
        return lax.ppermute(value, AXES, [(k, k ^ mask) for k in range(count)])

    def others(self, value, axis):
        return [self.swap(value, **{axis: d}) for d in range(1, self.size[axis])]


def pick(value, axis, index, count):
    size = value.shape[axis] // count
    return lax.dynamic_slice_in_dim(value, index * size, size, axis)


def after(value, *others):
    return lax.optimization_barrier((value,) + others)[0]


def tied(values, wait):
    if not wait:
        return list(values)
    return list(lax.optimization_barrier(tuple(values) + tuple(wait)))[: len(values)]


def native_gather(shard):
    return lax.all_gather(
        lax.all_gather(shard, "narrow", axis=1, tiled=True), "wide", axis=0, tiled=True
    )


class Gather:
    orders = (("x", "y"), ("y", "x"))

    def __init__(self, links, block, split):
        self.links, self.block, self.split = links, block, split

    def first(self, *wait):
        block = after(self.block, *wait) if wait else self.block
        self.sent = [block]
        self.steps = [block] + self.links.others(block, "z")

    def second(self, *wait):
        steps = tied(self.steps, wait)
        self.steps, self.sent = [], []
        for number, order in enumerate(self.orders):
            cols = slice(0, self.split) if number == 0 else slice(self.split, None)
            held = jnp.concatenate([p[None, :, cols] for p in steps], axis=0)
            self.sent.append(held)
            self.steps.append([held] + self.links.others(held, order[0]))

    def third(self, *wait):
        steps = tied([v for p in self.steps for v in p], wait)
        half = len(self.steps[0])
        self.steps, self.sent = [], []
        for part, order in zip((steps[:half], steps[half:]), self.orders, strict=True):
            held = jnp.concatenate(part, axis=0)
            self.sent.append(held)
            self.steps.append([held] + self.links.others(held, order[1]))

    def fourth(self, *wait):
        steps = tied([v for p in self.steps for v in p], wait)
        half = len(self.steps[0])
        self.operands = []
        for part in (steps[:half], steps[half:]):
            self.operands += part + [self.links.swap(held, core=1) for held in part]
        self.sent = steps

    def blocks(self, refs, number, me):
        links = self.links
        order = self.orders[number]
        out = []
        for core in range(2):
            for last in range(links.size[order[1]]):
                source = refs[4 * number + 2 * core + last]
                for k in range(source.shape[0]):
                    at = {
                        "z": me["z"] ^ (k % links.z),
                        order[0]: me[order[0]] ^ (k // links.z),
                        order[1]: me[order[1]] ^ last,
                    }
                    out.append((source.at[k], at["z"] * links.y + at["y"], at["x"] * 2 + (me["core"] ^ core)))
        return out


def at_least(n, values):
    out = values[3]
    for k in (2, 1, 0):
        out = jnp.where(n == k, values[k], out)
    return out


def window(ref, row, col, tall, broad):
    if not isinstance(row, int):
        row = pl.multiple_of(row, 8)
    if not isinstance(col, int):
        col = pl.multiple_of(col, 128)
    return ref.at[pl.ds(row, tall), pl.ds(col, broad)]


def columns(ref, col, broad):
    return ref.at[:, pl.ds(col, broad)]


class Weight:
    def __init__(self, operands, copies, joints=(), extra=0):
        self.operands, self.copies, self.joints, self.extra = operands, copies, joints, extra

    def fill(self, refs, target, sem):
        for source, to in self.copies(refs, target):
            pltpu.make_async_copy(source, to, sem).start()

    def wait(self, target, sem):
        pltpu.make_async_copy(target, target, sem).wait()
        for here, there in self.joints:
            target[:, here : here + 128] += target[:, there : there + 128]


def align_side(here, side):
    zero = jnp.zeros((side.shape[0], 64), side.dtype)
    return jnp.where(
        here["n"] % 2 == 0,
        jnp.concatenate([side, zero], axis=1),
        jnp.concatenate([zero, side], axis=1),
    )


def qkv_block(here, shard):
    even = here["n"] % 2 == 0
    main = jnp.where(even, shard[:, :384], shard[:, 192:])
    return jnp.concatenate([main, align_side(here, jnp.where(even, shard[:, 384:], shard[:, :192]))], axis=1)


def qkv_operands(links, gathered, shard):
    if not links.boxed:
        return Weight([native_gather(shard)], lambda refs, target: [(refs[0], target.at[:, pl.ds(0, 2304)])] + [
            (refs[0].at[:, pl.ds(0, 256)], target.at[:, pl.ds(2304, 256)])], extra=256)

    def copies(refs, target):
        me = links.place()
        out = []
        for source, w, n in gathered.blocks(refs, 0, me):
            out.append((source, window(target, w * 96, at_least(n, (0, 768, 1152, 1920)), 96, 384)))
        for source, w, n in gathered.blocks(refs, 1, me):
            for part, places in enumerate(((384, 2304, 1536, 2432), (512, 640, 1664, 1792))):
                out.append((columns(source, 128 * part, 128), window(target, w * 96, at_least(n, places), 96, 128)))
        return out

    return Weight(gathered.operands, copies, ((512, 2304), (1664, 2432)), 256)


def proj_operands(links, gathered, shard):
    if not links.boxed:
        return Weight([native_gather(shard)], lambda refs, target: [(refs[0], target.at[:, pl.ds(0, 768)])] + [
            (refs[0].at[:, pl.ds(0, 256)], target.at[:, pl.ds(768, 256)])], extra=256)

    def copies(refs, target):
        me = links.place()
        out = []
        for source, w, n in gathered.blocks(refs, 0, me):
            for part, places in enumerate(((0, 768, 384, 896), (128, 256, 512, 640))):
                out.append((columns(source, 128 * part, 128), window(target, w * 96, at_least(n, places), 96, 128)))
        return out

    return Weight(gathered.operands[:4], copies, ((128, 768), (512, 896)), 256)


def up_block(shard, chunk):
    return jnp.concatenate(
        [shard[:, 384 * half + 128 * chunk : 384 * half + 128 * chunk + 128] for half in range(2)], axis=1
    )


def down_block(shard_t, chunk):
    piece = shard_t[:, 128 * chunk : 128 * chunk + 128]
    half = piece.shape[0] // 2
    return jnp.concatenate([piece[:half], piece[half:]], axis=1)


def chunk_copies(full, chunk):
    def slices(refs, target):
        return [
            (columns(refs[0], 384 * g + 128 * chunk, 128), columns(target, 128 * g, 128)) for g in range(8)
        ]

    return Weight([full], slices)


def up_operands(links, gathered, col, full, chunk):
    if not links.boxed:
        return chunk_copies(full, chunk)

    def copies(refs, target):
        me = links.place()
        return [
            (columns(source, col, 256), window(target, w * 96, n * 256, 96, 256))
            for source, w, n in gathered.blocks(refs, 0, me)
        ]

    return Weight(gathered.operands[:4], copies)


def down_operands(links, gathered, col, full, chunk):
    if not links.boxed:
        return chunk_copies(full, chunk)

    def copies(refs, target):
        me = links.place()
        return [
            (columns(source, col + 128 * half, 128), window(target, n * 192 + half * 96, w * 128, 96, 128))
            for source, w, n in gathered.blocks([None] * 4 + list(refs), 1, me)
            for half in range(2)
        ]

    return Weight(gathered.operands[4:], copies)


class Scatter:
    orders = (("x", "y"), ("y", "x"))

    def __init__(self, links, here, split):
        self.links, self.here, self.split = links, here, split
        self.pairs = []

    def first(self, away, stay):
        shape = (self.links.x, self.links.z, self.links.y) + away.shape[2:]
        self.pairs.append((stay.reshape(shape), self.links.swap(away.reshape(shape), core=1)))

    def step(self, sources, axis):
        dim = {"x": 0, "z": 1, "y": 2}[axis]
        links, size = self.links, self.links.size[axis]

        def part(at):
            out = []
            for stay, *came in sources:
                total = pick(stay, dim, at, size).astype(F32)
                for term in came:
                    total = total + pick(term, dim, at, size).astype(F32)
                out.append(total)
            return jnp.concatenate(out, axis=-1) if len(out) > 1 else out[0]

        sent = [part(self.here[axis] ^ d).astype(BF16) for d in range(1, size)]
        self.sent += sent
        arrived = [links.swap(value, **{axis: d}) for d, value in enumerate(sent, 1)]
        return [part(self.here[axis])] + arrived

    def second(self, picks, *wait):
        flat = tied([v for pair in self.pairs for v in pair], wait)
        self.sent = []
        self.terms = [
            self.step([(flat[2 * k][..., cols], flat[2 * k + 1][..., cols]) for k, cols in part], order[0])
            for part, order in zip(picks, self.orders, strict=True)
        ]

    def third(self, *wait):
        flat = tied([v for t in self.terms for v in t], wait)
        half = len(self.terms[0])
        self.sent = []
        self.terms = [
            self.step([t], order[1]) for t, order in zip((flat[:half], flat[half:]), self.orders, strict=True)
        ]

    def fourth(self, *wait):
        flat = tied([v for t in self.terms for v in t], wait)
        half = len(self.terms[0])
        self.sent = []
        self.terms = self.step([flat[:half], flat[half:]], "z")

    def done(self, *wait):
        terms = tied(self.terms, wait)
        total = terms[0]
        for term in terms[1:]:
            total = total + term.astype(F32)
        return total.reshape(total.shape[-2:])


def all_tiles(here, away, stay):
    return jnp.where(
        here["core"] == 0, jnp.stack([stay, away], axis=1), jnp.stack([away, stay], axis=1)
    ).reshape((4,) + away.shape[1:])


def native_scatter(partial):
    low = lax.psum_scatter(partial.astype(BF16), "wide", scatter_dimension=0, tiled=True)
    return lax.psum_scatter(low, "narrow", scatter_dimension=1, tiled=True).astype(F32)


def qkv_home(here, block):
    even = here["n"] % 2 == 0
    main, side = block[:, :384], block[:, 384:]
    return jnp.where(
        even,
        jnp.concatenate([main, side[:, :192]], axis=1),
        jnp.concatenate([side[:, 64:], main], axis=1),
    )


def proj_home(here, block):
    return jnp.where(here["n"] % 2 == 0, block[:, :192], block[:, 64:])


def natural_qkv(tiles):
    tiles = tiles.reshape(4, 768, 640)
    out = []
    for n in range(4):
        main, side = tiles[n, :, :384], tiles[n, :, 384:]
        out += [main, side[:, :192]] if n % 2 == 0 else [side[:, 64:], main]
    return jnp.concatenate(out, axis=1)


def natural_proj(tiles):
    tiles = tiles.reshape(4, 768, 256)
    return jnp.concatenate([tiles[n, :, :192] if n % 2 == 0 else tiles[n, :, 64:] for n in range(4)], axis=1)


def natural_up(chunks):
    tiles = [t.reshape(4, 768, 2, 128) for t in chunks]
    return jnp.stack(tiles, axis=0).transpose(2, 1, 3, 0, 4).reshape(768, -1)


def natural_down(chunks):
    tiles = [t.reshape(4, 8, 96, 2, 128) for t in chunks]
    return jnp.stack(tiles, axis=0).transpose(2, 0, 5, 1, 4, 3).reshape(-1, 768)


def tree_sum(terms):
    while len(terms) > 1:
        terms = [terms[k] + terms[k + 1] for k in range(0, len(terms), 2)]
    return terms[0]


def sum_everywhere(links, value):
    if not links.boxed:
        return lax.psum(value, AXES)
    value = value + links.swap(value, core=1)
    value = tree_sum(
        [value]
        + [links.swap(value, x=k % links.x, y=k // links.x) for k in range(1, links.x * links.y)]
    )
    return tree_sum([value] + links.others(value, "z"))


def whole(shape):
    return pl.BlockSpec(tuple(shape), lambda *_: (0,) * len(shape))


ANY = pl.BlockSpec(memory_space=pl.ANY)


def call(kernel, name, grid, ins, outs, scratch=(), flops=0, limit=56, aliases=None):
    moved = sum(a.size * a.dtype.itemsize for a, _ in ins)
    moved += sum(math.prod(s) * jnp.dtype(d).itemsize for s, d, _ in outs)
    return pl.pallas_call(
        kernel,
        name=name,
        grid=grid,
        in_specs=[spec for _, spec in ins],
        out_specs=[spec for _, _, spec in outs],
        out_shape=[jax.ShapeDtypeStruct(s, d) for s, d, _ in outs],
        scratch_shapes=list(scratch),
        input_output_aliases=aliases or {},
        compiler_params=pltpu.CompilerParams(vmem_limit_bytes=limit * MIB),
        cost_estimate=pl.CostEstimate(flops=int(flops), bytes_accessed=int(moved), transcendentals=0),
    )(*[a for a, _ in ins])


def nn(a, b):
    return lax.dot_general(a, b, (((1,), (0,)), ((), ())), preferred_element_type=F32)


def nt(a, b):
    return lax.dot_general(a, b, (((1,), (1,)), ((), ())), preferred_element_type=F32)


def tn(a, b):
    return lax.dot_general(a, b, (((0,), (0,)), ((), ())), preferred_element_type=F32)


def norm(values):
    centre = jnp.mean(values, axis=-1, keepdims=True)
    centred = values - centre
    spread = jnp.mean(centred * centred, axis=-1, keepdims=True)
    scaling = lax.rsqrt(spread + EPSILON)
    return centred * scaling, scaling


def norm_back(grad, normed, scaling, gain):
    scaled = grad * gain
    first = jnp.mean(scaled, axis=-1, keepdims=True)
    second = jnp.mean(scaled * normed, axis=-1, keepdims=True)
    return (scaled - first - normed * second) * scaling


def banded(tall, body):
    if BAND >= tall:
        body(slice(0, tall), 0)
        return

    def step(k, carry):
        at = pl.multiple_of(k * BAND, 8)
        body(pl.ds(at, BAND), at)
        return carry

    lax.fori_loop(0, tall // BAND, step, 0)


def column_sum(values):
    return jnp.sum(values, axis=0, keepdims=True)


def prepare(sizes, inputs, cotangent, flags, mask_token, gain, shift, gamma_mlp):
    images, length, tall, width = sizes
    rows = images * tall

    def kernel(x_ref, g_ref, flag_ref, token_ref, gain_ref, shift_ref, gamma_ref,
               h0_ref, n1_ref, g_out, df_ref, sum_ref, x_s, g_s):
        @pl.when(pl.program_id(0) == 0)
        def _():
            x_s[...] = jnp.zeros_like(x_s)
            g_s[...] = jnp.zeros_like(g_s)
            sum_ref[...] = jnp.zeros_like(sum_ref)

        x_s[0:length, :] = x_ref[0].astype(F32)
        g_s[0:length, :] = g_ref[0].astype(F32)

        def body(at, first):
            start = jnp.where(flag_ref[at, :] == 1, token_ref[...], x_s[at, :])
            h0_ref[at, :] = start
            normed, _ = norm(start)
            n1_ref[at, :] = (normed * gain_ref[...] + shift_ref[...]).astype(BF16)
            g = g_s[at, :]
            g_out[at, :] = g.astype(BF16)
            df = gamma_ref[...] * g
            df_ref[at, :] = df.astype(BF16)
            sum_ref[...] += column_sum(df)

        banded(tall, body)

    row = whole((1, width))
    image = pl.BlockSpec((1, length, width), lambda i: (i, 0, 0))
    band = pl.BlockSpec((tall, width), lambda i: (i, 0))
    return call(
        kernel, "prepare", (images,),
        [(inputs, image), (cotangent, image), (flags, pl.BlockSpec((tall, 1), lambda i: (i, 0))),
         (mask_token, row), (gain, row), (shift, row), (gamma_mlp, row)],
        [((rows, width), F32, band), ((rows, width), BF16, band), ((rows, width), BF16, band),
         ((rows, width), BF16, band), ((1, width), F32, row)],
        [pltpu.VMEM((tall, width), F32), pltpu.VMEM((tall, width), F32)],
        flops=rows * width * 40,
    )


def table_columns(grid_side, broad):
    side = 2 * grid_side - 1
    q = np.arange(broad)
    entry = (q // grid_side) * side + q % grid_side + grid_side - 1
    return jnp.asarray(np.where(q < side * grid_side, entry, -(1 << 20)).astype(np.int32)[None])


def three_parts(values):
    high = values.astype(BF16)
    rest = values - high.astype(F32)
    middle = rest.astype(BF16)
    return high, middle, (rest - middle.astype(F32)).astype(BF16)


def bias_kernel(table_t, entry, grid_side, tall, broad):
    heads = table_t.shape[0]
    length = grid_side * grid_side + 1
    wide = entry.shape[1]
    inner = (2 * grid_side - 1) ** 2

    def kernel(table_ref, entry_ref, out_ref, *halves):
        def put(at, count, values):
            for half, ref in enumerate(halves):
                ref[pl.ds(at, count), :] = values[:, 128 * half : 128 * half + 128]

        parts = jnp.concatenate(three_parts(table_ref[...]), axis=0)
        left, top, corner = (table_ref[:, inner + 1 : inner + 2], table_ref[:, inner : inner + 1],
                             table_ref[:, inner + 2 : inner + 3])
        lane = lax.broadcasted_iota(jnp.int32, (heads, broad), 1)

        def column(b, carry):
            which = lax.broadcasted_iota(jnp.int32, (table_ref.shape[1], wide), 0) + b
            select = jnp.where(which == entry_ref[...], 1.0, 0.0).astype(BF16)
            spread = nn(parts, select)
            spread = spread[:heads] + spread[heads : 2 * heads] + spread[2 * heads :]
            for a in range(grid_side):
                shift = (grid_side - 1 - a) * grid_side - 1
                moved = pltpu.roll(spread, (wide - shift) % wide, 1)[:, :broad]
                moved = jnp.where(lane == 0, top, moved)
                put(pl.multiple_of((1 + grid_side * a + b) * heads, 16), heads, moved)
            return carry

        lax.fori_loop(0, grid_side, column, 0)
        put(0, heads, jnp.where(lane == 0, corner, left))
        rest = (tall - length) * heads
        put(length * heads, rest, jnp.full((rest, broad), NEVER, F32))
        for h in range(out_ref.shape[0]):
            for half, ref in enumerate(halves):
                out_ref[h, :, 128 * half : 128 * half + 128] = ref[pl.ds(h, tall, stride=heads), :]

    return call(
        kernel, "bias", (),
        [(table_t, whole(table_t.shape)), (entry, whole(entry.shape))],
        [((12, tall, broad), F32, whole((12, tall, broad)))],
        [pltpu.VMEM((tall * heads, 128), F32)] * (broad // 128),
        flops=2 * 48 * 768 * wide * grid_side,
    )[0]


def bias_back_kernel(terms, entry, grid_side, width):
    count, tall, broad = terms.shape
    heads = 16
    wide = entry.shape[1]
    inner = (2 * grid_side - 1) ** 2
    length = grid_side * grid_side + 1

    def kernel(terms_ref, entry_ref, out_ref, *halves):
        def get(at, count):
            return jnp.concatenate([ref[pl.ds(at, count), :] for ref in halves], axis=1)

        lane = lax.broadcasted_iota(jnp.int32, (heads, broad), 1)
        inside = (lane >= 1) & (lane < length)
        for h in range(heads):
            values = terms_ref[h] if h < count else jnp.zeros((tall, broad), F32)
            for half, ref in enumerate(halves):
                ref[pl.ds(h, tall, stride=heads), :] = values[:, 128 * half : 128 * half + 128]

        def column(b, carry):
            total, edge = carry
            which = lax.broadcasted_iota(jnp.int32, (width, wide), 0) + b
            select = jnp.where(which == entry_ref[...], 1.0, 0.0).astype(BF16)
            spread = jnp.zeros((heads, wide), F32)
            for a in range(grid_side):
                shift = (grid_side - 1 - a) * grid_side - 1
                found = get(pl.multiple_of((1 + grid_side * a + b) * heads, 16), heads)
                edge = edge + jnp.where(lane == 0, found, 0.0)
                found = jnp.where(inside, found, 0.0)
                found = jnp.concatenate([found, jnp.zeros((heads, wide - broad), F32)], axis=1)
                spread = spread + pltpu.roll(found, shift % wide, 1)
            found = nt(jnp.concatenate(three_parts(spread), axis=0), select)
            total = total + found[:heads] + found[heads : 2 * heads] + found[2 * heads :]
            return total, edge

        total, edge = lax.fori_loop(
            0, grid_side, column, (jnp.zeros((heads, width), F32), jnp.zeros((heads, broad), F32))
        )
        first = get(0, heads)
        top = jnp.sum(edge, axis=1, keepdims=True)
        left = jnp.sum(jnp.where(inside, first, 0.0), axis=1, keepdims=True)
        corner = first[:, 0:1]
        place = lax.broadcasted_iota(jnp.int32, (heads, width), 1)
        total = jnp.where(place == inner, top, total)
        total = jnp.where(place == inner + 1, left, total)
        out_ref[...] = jnp.where(place == inner + 2, corner, total)

    return call(
        kernel, "bias_back", (),
        [(terms, whole(terms.shape)), (entry, whole(entry.shape))],
        [((heads, width), F32, whole((heads, width)))],
        [pltpu.VMEM((tall * heads, 128), F32)] * (broad // 128),
        flops=2 * 48 * 768 * wide * grid_side,
    )[0]


def project(sizes, first_low, weight, scale, shift):
    images, length, tall, width = sizes
    rows = images * tall
    cols = scale.shape[1]
    count = len(weight.operands)

    def kernel(*refs):
        n1_ref, scale_ref, shift_ref = refs[:3]
        out_ref, w_s, sem = refs[3 + count :]
        step = pl.program_id(0)

        @pl.when(step == 0)
        def _():
            weight.fill(refs[3 : 3 + count], w_s, sem)
            weight.wait(w_s, sem)

        w = w_s[:, pl.ds(pl.multiple_of(step * width, 128), width)]
        out_ref[...] = ((nn(n1_ref[...], w) + shift_ref[...]) * scale_ref[...]).astype(BF16)

    tile = pl.BlockSpec((1, width), lambda t: (0, t))
    return call(
        kernel, "project", (cols // width,),
        [(first_low, whole((rows, width))), (scale, tile), (shift, tile)] + [(a, ANY) for a in weight.operands],
        [((rows, cols), BF16, pl.BlockSpec((rows, width), lambda t: (0, t)))],
        [pltpu.VMEM((width, cols + weight.extra), BF16), pltpu.SemaphoreType.DMA],
        flops=2 * rows * width * cols,
    )[0]


def head_masks(tall):
    lane = lax.broadcasted_iota(jnp.int32, (tall, 128), 1)
    return [lane < 64, lane >= 64]


def attend(sizes, mixed, bias, first, pairs):
    images, length, tall, width = sizes
    rows = images * tall
    every = width // 128
    broad = bias.shape[2]

    def kernel(q_ref, k_ref, v_ref, bias_ref, out_ref, p_ref):
        masks = head_masks(tall)
        units = [(i, h) for i in range(images) for h in range(2)]
        scores, probs = [], []
        for i, h in units:
            q, k = q_ref[tall * i : tall * i + tall, :], k_ref[tall * i : tall * i + tall, :]
            scores.append(nt(k, jnp.where(masks[h], q, jnp.zeros_like(q))) + bias_ref[h, :, 0:tall])
        for (i, h), s in zip(units, scores, strict=True):
            e = jnp.exp(s - jnp.max(s, axis=0, keepdims=True))
            p = (e * (1.0 / jnp.sum(e, axis=0, keepdims=True))).astype(BF16)
            p_ref[h, i, :, 0:tall] = p
            probs.append(p)
        for i in range(images):
            vt = v_ref[tall * i : tall * i + tall, :].T
            out = [nn(vt[64 * h : 64 * h + 64, :], probs[2 * i + h]) for h in range(2)]
            out_ref[tall * i : tall * i + tall, :] = jnp.concatenate(out, axis=0).T.astype(BF16)

    def column(at):
        return pl.BlockSpec((rows, 128), lambda t: (0, at + t))

    return call(
        kernel, "attend", (pairs,),
        [(mixed, column(first)), (mixed, column(every + first)), (mixed, column(2 * every + first)),
         (bias, pl.BlockSpec((2, tall, broad), lambda t: (first + t, 0, 0)))],
        [((rows, 128 * pairs), BF16, column(0)),
         ((2 * pairs, images, tall, broad), BF16,
          pl.BlockSpec((2, images, tall, broad), lambda t: (t, 0, 0, 0)))],
        flops=4 * rows * tall * 128 * pairs,
    )


def attend_back(sizes, mixed, probs, grad_out, score_scale, first, pairs, so_far):
    images, length, tall, width = sizes
    rows = images * tall
    every = width // 128
    broad = probs.shape[3]

    def kernel(q_ref, k_ref, v_ref, do_ref, p_ref, *refs):
        grad_ref, terms_ref, qb_ref, vb_ref = refs[-4:]
        masks = head_masks(tall)
        units = [(i, h) for i in range(images) for h in range(2)]

        def part(ref, i):
            return ref[tall * i : tall * i + tall, :]

        def own(value, h):
            return jnp.where(masks[h], value, jnp.zeros_like(value))

        grads = [nt(part(v_ref, i), own(part(do_ref, i), h)) for i, h in units]
        lows = []
        for (i, h), grad in zip(units, grads, strict=True):
            p = p_ref[h, i, :, 0:tall].astype(F32)
            t = p * grad
            lows.append((t - p * jnp.sum(t, axis=0, keepdims=True)).astype(BF16))
        for h in range(2):
            terms_ref[h, :, 0:tall] = sum(lows[2 * i + h].astype(F32) for i in range(images))
            terms_ref[h, :, tall:] = jnp.zeros((tall, broad - tall), F32)
        query_sum, value_sum = 0.0, 0.0
        for i in range(images):
            kt = part(k_ref, i).T
            dv = sum(nn(p_ref[h, i, :, 0:tall], own(part(do_ref, i), h)) for h in range(2))
            dk = sum(nn(lows[2 * i + h], own(part(q_ref, i), h)) for h in range(2))
            dq = jnp.concatenate(
                [nn(kt[64 * h : 64 * h + 64, :], lows[2 * i + h]) for h in range(2)], axis=0
            ).T * score_scale
            for number, grad in enumerate((dq, dk, dv)):
                grad_ref[number, tall * i : tall * i + tall, :] = grad.astype(BF16)
            query_sum += column_sum(dq)
            value_sum += column_sum(dv)
        qb_ref[...] = query_sum
        vb_ref[...] = value_sum

    def column(at):
        return pl.BlockSpec((rows, 128), lambda t: (0, at + t))

    one = pl.BlockSpec((1, 128), lambda t: (0, t))
    return call(
        kernel, "attend_back", (pairs,),
        [(mixed, column(first)), (mixed, column(every + first)), (mixed, column(2 * every + first)),
         (grad_out, column(first)),
         (probs, pl.BlockSpec((2, images, tall, broad), lambda t: (t, 0, 0, 0)))]
        + ([] if so_far is None else [(so_far, ANY)]),
        [((3, rows, width), BF16, pl.BlockSpec((3, rows, 128), lambda t: (0, 0, first + t)))]
        + [((2 * pairs, tall, broad), F32, pl.BlockSpec((2, tall, broad), lambda t: (t, 0, 0))),
           ((1, 128 * pairs), F32, one), ((1, 128 * pairs), F32, one)],
        flops=8 * rows * tall * 128 * pairs,
        aliases={} if so_far is None else {5: 0},
    )


def merge(sizes, attended, start, weight, proj_bias, gamma, gain, shift):
    images, length, tall, width = sizes
    rows = images * tall
    count = len(weight.operands)

    def kernel(*refs):
        att_refs, refs = refs[: len(attended)], refs[len(attended) :]
        h0_ref, bias_ref, gamma_ref, gain_ref, shift_ref = refs[:5]
        h1_ref, n2_ref, w_s, out_s, sem = refs[5 + count :]
        step = pl.program_id(0)

        @pl.when(step == 0)
        def _():
            weight.fill(refs[5 : 5 + count], w_s, sem)
            weight.wait(w_s, sem)
            part = width // len(attended)
            out_s[...] = sum(nn(r[...], w_s[part * k : part * k + part, 0:width]) for k, r in enumerate(att_refs))

        @pl.when(step > 0)
        def _():
            def body(at, first):
                out = out_s[pl.ds(pl.multiple_of((step - 1) * tall + first, 8), min(BAND, tall)), :]
                middle = h0_ref[at, :] + gamma_ref[...] * (out + bias_ref[...])
                h1_ref[at, :] = middle
                normed, _ = norm(middle)
                n2_ref[at, :] = (normed * gain_ref[...] + shift_ref[...]).astype(BF16)

            banded(tall, body)

    row = whole((1, width))
    band = pl.BlockSpec((tall, width), lambda i: (jnp.maximum(i - 1, 0), 0))
    return call(
        kernel, "merge", (images + 1,),
        [(a, whole(a.shape)) for a in attended]
        + [(start, band), (proj_bias, row), (gamma, row), (gain, row), (shift, row)]
        + [(a, ANY) for a in weight.operands],
        [((rows, width), F32, band), ((rows, width), BF16, band)],
        [pltpu.VMEM((width, width + weight.extra), BF16), pltpu.VMEM((rows, width), F32),
         pltpu.SemaphoreType.DMA],
        flops=2 * rows * width * width,
    )


def part_by_core(store, away_ref, stay_ref):
    c = lax.axis_index("narrow") % 2
    for x in range(2):
        away_ref[x] = store[2 * x + 1 - c]
        stay_ref[x] = store[2 * x + c]


def feed(sizes, second_low, down_low, up, down, bias, sums):
    images, length, tall, width = sizes
    rows = images * tall
    ups, downs = len(up.operands), len(down.operands)
    carried = [] if sums is None else list(sums)

    def kernel(*refs):
        n2_ref, df_ref, bias_ref = refs[:3]
        rest = refs[3:]
        up_refs, rest = rest[:ups], rest[ups:]
        down_refs, rest = rest[:downs], rest[downs:]
        sum_refs, rest = rest[: len(carried)], rest[len(carried) :]
        f_ref, dn_ref, away_ref, stay_ref, gbias_ref, up_s, down_s, grad_s, sems = rest
        step = pl.program_id(0)

        @pl.when(step == 0)
        def _():
            up.fill(up_refs, up_s, sems.at[0])
            down.fill(down_refs, down_s, sems.at[1])
            if carried:
                pltpu.make_async_copy(sum_refs[0], f_ref, sems.at[2]).start()
                pltpu.make_async_copy(sum_refs[1], dn_ref, sems.at[3]).start()
            up.wait(up_s, sems.at[0])
            down.wait(down_s, sems.at[1])
            if carried:
                pltpu.make_async_copy(sum_refs[0], f_ref, sems.at[2]).wait()
                pltpu.make_async_copy(sum_refs[1], dn_ref, sems.at[3]).wait()
            else:
                f_ref[...] = jnp.zeros_like(f_ref)
                dn_ref[...] = jnp.zeros_like(dn_ref)

        at = pl.ds(pl.multiple_of(step * TILE, TILE), TILE)
        up_w, down_w = up_s[:, at], down_s[:, at]
        u = nn(n2_ref[...], up_w) + bias_ref[...]
        dz = nn(df_ref[...], down_w)
        bell = jnp.exp(-0.5 * u * u)
        below = 0.5 * (1.0 + lax.erf(u * ROOT_HALF))
        z = (u * below).astype(BF16)
        du = dz * (below + u * (DENSITY * bell))
        gbias_ref[...] = column_sum(du)
        du = du.astype(BF16)
        grad = tn(n2_ref[...], du).astype(BF16)
        for k in range(TILE // 256):
            grad_s[step * (TILE // 256) + k, :, :, 0:256] = grad[:, 256 * k : 256 * k + 256].reshape(8, 96, 256)
        grad = tn(df_ref[...], z).astype(BF16)
        for n in range(4):
            for w in range(TILE // 128):
                for half in range(2):
                    grad_s[n, step * (TILE // 128) + w, :, 256 + 128 * half : 384 + 128 * half] = grad[
                        192 * n + 96 * half : 192 * n + 96 * half + 96, 128 * w : 128 * w + 128
                    ]
        f_ref[...] += nt(z, down_w)
        dn_ref[...] += nt(du, up_w)

        @pl.when(step == CHUNK // TILE - 1)
        def _():
            part_by_core(grad_s, away_ref, stay_ref)

    tile = pl.BlockSpec((1, TILE), lambda t: (0, t))
    full = whole((rows, width))
    shape = (2, 8, 96, 512)
    return call(
        kernel, "feed", (CHUNK // TILE,),
        [(second_low, full), (down_low, full), (bias, tile)]
        + [(a, ANY) for a in up.operands + down.operands + carried],
        [((rows, width), F32, full), ((rows, width), F32, full),
         (shape, BF16, whole(shape)), (shape, BF16, whole(shape)), ((1, CHUNK), F32, tile)],
        [pltpu.VMEM((width, CHUNK), BF16), pltpu.VMEM((width, CHUNK), BF16), pltpu.VMEM((4, 8, 96, 512), BF16),
         pltpu.SemaphoreType.DMA((4,))],
        flops=12 * rows * width * CHUNK,
    )


def middle_back(sizes, attended, branch, grad_n2, middle, start, upstream, weight, rows_in):
    images, length, tall, width = sizes
    rows = images * tall
    count = len(weight.operands)

    def kernel(*refs):
        att_refs, refs = refs[: len(attended)], refs[len(attended) :]
        f_ref, dn_ref, h1_ref, h0_ref, g_ref, b2_ref, gm_ref, gain_ref, ga_ref = refs[:9]
        out_ref, dh_ref, do_ref, away_ref, stay_ref, sum_ref, w_s, da_s, grad_s, layer_s, sem = refs[9 + count :]
        step = pl.program_id(0)

        @pl.when(step == 0)
        def _():
            weight.fill(refs[9 : 9 + count], w_s, sem)
            sum_ref[...] = jnp.zeros_like(sum_ref)

        @pl.when(step < images)
        def _():
            def body(at, first):
                f = f_ref[at, :] + b2_ref[...]
                h1 = h1_ref[at, :]
                g = g_ref[at, :].astype(F32)
                layer_s[at, :] = h1 + gm_ref[...] * f
                normed, scaling = norm(h1)
                dn = dn_ref[at, :]
                dh = g + norm_back(dn, normed, scaling, gain_ref[...])
                dh_ref[at, :] = dh
                da = ga_ref[...] * dh
                sum_ref[0:1, :] += column_sum(g * f)
                sum_ref[1:2, :] += column_sum(dn * normed)
                sum_ref[2:3, :] += column_sum(dn)
                sum_ref[3:4, :] += column_sum(dh * (h1 - h0_ref[at, :]))
                sum_ref[4:5, :] += column_sum(da)
                da_s[pl.ds(pl.multiple_of(step * tall + first, 8), min(BAND, tall)), :] = da.astype(BF16)

            banded(tall, body)
            out_ref[0] = layer_s[0:length, :].astype(BF16)

        @pl.when(step == images)
        def _():
            sum_ref[3:4, :] = sum_ref[3:4, :] / ga_ref[...]
            weight.wait(w_s, sem)
            do_ref[...] = nt(da_s[...], w_s[:, 0:width]).astype(BF16)
            grad = jnp.concatenate([tn(r[...], da_s[...]) for r in att_refs], axis=0).astype(BF16)
            for n, at in enumerate((0, 128, 384, 512)):
                grad_s[n] = grad[:, at : at + 256].reshape(8, 96, 256)
            part_by_core(grad_s, away_ref, stay_ref)

    row = whole((1, width))

    def at(i):
        return jnp.minimum(i, images - 1)

    band = pl.BlockSpec((tall, width), lambda i: (at(i), 0))
    shape = (2, 8, 96, 256)
    return call(
        kernel, "middle_back", (images + 1,),
        [(a, whole(a.shape)) for a in attended]
        + [(a, band) for a in (branch, grad_n2, middle, start, upstream)] + [(a, row) for a in rows_in]
        + [(a, ANY) for a in weight.operands],
        [((images, length, width), BF16, pl.BlockSpec((1, length, width), lambda i: (at(i), 0, 0))),
         ((rows, width), F32, band), ((rows, width), BF16, whole((rows, width))),
         (shape, BF16, whole(shape)), (shape, BF16, whole(shape)), ((8, width), F32, whole((8, width)))],
        [pltpu.VMEM((width, width + weight.extra), BF16), pltpu.VMEM((rows, width), BF16),
         pltpu.VMEM((4, 8, 96, 256), BF16), pltpu.VMEM((tall, width), F32), pltpu.SemaphoreType.DMA],
        flops=4 * rows * width * width,
    )


def mixed_grad(sizes, first_low, grads):
    images, length, tall, width = sizes
    rows = images * tall

    def kernel(n1_ref, grad_ref, away_ref, stay_ref):
        step = pl.program_id(0)
        c = lax.axis_index("narrow") % 2
        n = 2 * (step % 2) + jnp.where(step < 2, 1 - c, c)
        main = grad_ref[at_least(n, (0, 1, 1, 2)), :, pl.ds(pl.multiple_of(at_least(n, (0, 0, 384, 384)), 128), 384)]
        side = grad_ref[at_least(n, (0, 0, 2, 2)), :, pl.ds(pl.multiple_of(at_least(n, (384, 512, 0, 128)), 128), 256)]
        main = tn(n1_ref[...], main).astype(BF16).reshape(8, 96, 384)
        side = tn(n1_ref[...], side).astype(BF16).reshape(8, 96, 256)
        for role, ref in enumerate((away_ref, stay_ref)):
            @pl.when(step // 2 == role)
            def _(ref=ref):
                ref[0, :, :, 0:384] = main
                ref[0, :, :, 384:640] = side

    shape = (2, 8, 96, 640)
    return call(
        kernel, "mixed_grad", (4,),
        [(first_low, whole((rows, width))), (grads, whole(grads.shape))],
        [(shape, BF16, pl.BlockSpec((1, 8, 96, 640), lambda t: (jnp.minimum(t, 1), 0, 0, 0))),
         (shape, BF16, pl.BlockSpec((1, 8, 96, 640), lambda t: (jnp.maximum(t - 2, 0), 0, 0, 0)))],
        flops=6 * rows * width * width,
    )


def start_back(sizes, grads, weight, start, grad_middle, flags, gain):
    images, length, tall, width = sizes
    rows = images * tall
    count = len(weight.operands)

    def kernel(*refs):
        grad_ref, h0_ref, dh_ref, flag_ref, gain_ref = refs[:5]
        out_ref, sum_ref, w_s, dn_s, out_s, sem = refs[5 + count :]
        step = pl.program_id(0)

        @pl.when(step == 0)
        def _():
            weight.fill(refs[5 : 5 + count], w_s, sem)
            sum_ref[...] = jnp.zeros_like(sum_ref)
            dn_s[...] = jnp.zeros_like(dn_s)
            weight.wait(w_s, sem)

        @pl.when(step < 3)
        def _():
            dn_s[...] += nt(grad_ref[0], w_s[:, pl.ds(pl.multiple_of(step * width, 128), width)])

        @pl.when(step > 2)
        def _():
            def body(at, first):
                dn = dn_s[pl.ds(pl.multiple_of((step - 3) * tall + first, 8), min(BAND, tall)), :]
                normed, scaling = norm(h0_ref[at, :])
                dh = dh_ref[at, :] + norm_back(dn, normed, scaling, gain_ref[...])
                masked = flag_ref[at, :] == 1
                out_s[at, :] = jnp.where(masked, 0.0, dh)
                sum_ref[0:1, :] += column_sum(dn * normed)
                sum_ref[1:2, :] += column_sum(dn)
                sum_ref[2:3, :] += column_sum(jnp.where(masked, dh, 0.0))

            banded(tall, body)
            out_ref[0] = out_s[0:length, :]

    def at(i):
        return jnp.maximum(i - 3, 0)

    band = pl.BlockSpec((tall, width), lambda i: (at(i), 0))
    return call(
        kernel, "start_back", (images + 3,),
        [(grads, pl.BlockSpec((1, rows, width), lambda i: (jnp.minimum(i, 2), 0, 0)))]
        + [(start, band), (grad_middle, band), (flags, pl.BlockSpec((tall, 1), lambda i: (at(i), 0))),
           (gain, whole((1, width)))]
        + [(a, ANY) for a in weight.operands],
        [((images, length, width), F32, pl.BlockSpec((1, length, width), lambda i: (at(i), 0, 0))),
         ((8, width), F32, whole((8, width)))],
        [pltpu.VMEM((width, 3 * width + weight.extra), BF16), pltpu.VMEM((rows, width), F32),
         pltpu.VMEM((tall, width), F32), pltpu.SemaphoreType.DMA],
        flops=6 * rows * width * width,
    )


def local(
    links,
    inputs,
    cotangent,
    group_sizes,
    mask_patterns,
    mask_token,
    norm1_gain,
    norm1_bias,
    qkv_weight,
    query_bias,
    value_bias,
    bias_table,
    proj_weight,
    proj_bias,
    gamma_attn,
    norm2_gain,
    norm2_bias,
    fc1_weight,
    fc1_bias,
    fc2_weight,
    fc2_bias,
    gamma_mlp,
):
    images, length, width = inputs.shape
    table_rows, heads = bias_table.shape
    grid_side = math.isqrt(length - 1)
    group_count = mask_patterns.shape[0]
    tall = -(-length // 8) * 8
    rows = images * tall
    hidden = fc1_bias.shape[0]
    chunks = hidden // CHUNK
    sizes = (images, length, tall, width)
    score_scale = (width // heads) ** (-0.5)
    here = links.place()

    image_ids = lax.axis_index(AXES) * images + jnp.arange(images, dtype=jnp.int32)
    bounds = jnp.cumsum(group_sizes)[: group_count - 1]
    member = jnp.sum((image_ids[:, None] >= bounds[None, :]).astype(jnp.int32), axis=1)
    chosen = (member[:, None] == jnp.arange(group_count, dtype=jnp.int32)[None, :]).astype(jnp.int32)
    patterns = jnp.sum(chosen[:, :, None] * mask_patterns[None, :, :], axis=1)
    flags = jnp.pad(patterns, ((0, 0), (1, tall - length))).reshape(rows, 1)

    def row(v):
        return v.reshape(1, -1)

    boxed = links.boxed
    fc2_t = fc2_weight.T
    if boxed:
        mix = Gather(links, qkv_block(here, qkv_weight), 384)
        near = Gather(
            links,
            jnp.concatenate(
                [align_side(here, proj_weight), up_block(fc1_weight, 0), down_block(fc2_t, 0)], axis=1
            ),
            512,
        )
        far = Gather(
            links,
            jnp.concatenate(
                [up_block(fc1_weight, 1), up_block(fc1_weight, 2), down_block(fc2_t, 1), down_block(fc2_t, 2)],
                axis=1,
            ),
            512,
        )
        full_up = full_down = None
    else:
        mix = near = far = None
        full_up, full_down = native_gather(fc1_weight), native_gather(fc2_weight).T

    entry = table_columns(grid_side, 384)
    table_t = jnp.pad(bias_table.T, ((0, 16 - heads), (0, width - table_rows)))

    def behind(value, *exchanges):
        return after(value, *[v for e in exchanges for v in e.sent]) if boxed else value

    if boxed:
        mix.first()
    start, first_low, upstream, down_low, sum_fc2 = prepare(
        sizes, inputs, cotangent, flags, row(mask_token), row(norm1_gain), row(norm1_bias), row(gamma_mlp)
    )
    if boxed:
        mix.second(first_low)
    bias = bias_kernel(behind(table_t, mix), entry, grid_side, tall, 256)
    if boxed:
        mix.third(bias)
        near.first(*mix.sent)
        mix.fourth()
    qkv = qkv_operands(links, mix, qkv_weight)
    nothing = jnp.zeros((width,), F32)
    scale = row(jnp.concatenate([nothing + score_scale, nothing + 1.0, nothing + 1.0]))
    mixed = project(
        sizes, behind(first_low, near), qkv, scale, row(jnp.concatenate([query_bias, nothing, value_bias]))
    )
    groups = ((0, 3), (3, 3))
    attended, probs = [], []
    if boxed:
        near.second(mixed)
        far.first(mixed)
    for number, (first, pairs) in enumerate(groups):
        out, kept = attend(sizes, behind(mixed, near, far), bias, first, pairs)
        attended.append(out)
        probs.append(kept)
        if boxed and number == 0:
            near.third(out)
    if boxed:
        near.fourth(attended[1])
        far.second(attended[1])
    proj = proj_operands(links, near, proj_weight)
    middle, second_low = merge(
        sizes, attended, behind(start, far), proj, row(proj_bias), row(gamma_attn), row(norm2_gain), row(norm2_bias)
    )
    if boxed:
        far.third(second_low)

    fc1_groups = fc1_bias.reshape(8, chunks, 128)
    ups = [up_operands(links, near, 256, full_up, 0), None, None]
    downs = [down_operands(links, near, 0, full_down, 0), None, None]
    halves = [[(0, slice(0, 256))], [(0, slice(256, 512))]]
    sums, pairs_out, hidden_sums = None, [], []
    waves = [Scatter(links, here, 256), Scatter(links, here, 256), Scatter(links, here, 512)]
    second_here = behind(second_low, far)
    for k in range(chunks):
        branch, grad_n2, away, stay, hidden_sum = feed(
            sizes, second_here, down_low, ups[k], downs[k], fc1_groups[:, k].reshape(1, -1), sums
        )
        if k == 0:
            if boxed:
                far.fourth(away)
                waves[0].first(away, stay)
            ups[1:] = [up_operands(links, far, 0, full_up, 1), up_operands(links, far, 256, full_up, 2)]
            downs[1:] = [down_operands(links, far, 0, full_down, 1), down_operands(links, far, 256, full_down, 2)]
            second_here = second_low
        elif k == 1 and boxed:
            waves[0].second(halves, away)
            waves[1].first(away, stay)
            second_here = behind(second_low, waves[0])
        elif boxed:
            waves[0].third(away)
            waves[1].second(halves, away)
            waves[2].first(away, stay)
        sums = (branch, grad_n2)
        pairs_out.append((away, stay))
        hidden_sums.append(hidden_sum.reshape(8, 128))
    sum_fc1 = jnp.stack(hidden_sums, axis=1)

    layer_out, grad_middle, grad_att, proj_away, proj_stay, middle_sums = middle_back(
        sizes, attended, behind(branch, waves[0], waves[1]), grad_n2, middle, start, upstream, proj,
        [row(fc2_bias), row(gamma_mlp), row(norm2_gain), row(gamma_attn)],
    )
    if boxed:
        waves[0].fourth(grad_att)
        waves[1].third(grad_att)
        waves[2].first(proj_away, proj_stay)

    back, grads = [], None
    for number, (first, pairs) in enumerate(groups):
        grad_here = behind(grad_att, *(waves[:2] if number == 0 else waves[1:]))
        grads, *rest = attend_back(sizes, mixed, probs[number], grad_here, score_scale, first, pairs, grads)
        back.append(rest)
        if boxed and number == 0:
            waves[1].fourth(grads)
            waves[2].second([[(1, slice(0, 256)), (0, slice(0, 256))], [(0, slice(256, 512))]], grads)
    if boxed:
        waves[2].third(grads)
    mix_away, mix_stay = mixed_grad(sizes, behind(first_low, waves[2]), grads)
    last = Scatter(links, here, 384)
    if boxed:
        last.first(mix_away, mix_stay)
        waves[2].fourth(mix_away)
        last.second([[(0, slice(0, 384))], [(0, slice(384, 640))]])
    input_grad, start_sums = start_back(
        sizes, grads, qkv, start, grad_middle, behind(flags, waves[2], last), row(norm1_gain)
    )
    terms = jnp.concatenate([b[0] for b in back], axis=0)
    grad_table = bias_back_kernel(after(terms, start_sums), entry, grid_side, width)
    sum_query, sum_value = (jnp.concatenate([b[k] for b in back], axis=1) for k in (1, 2))
    small = jnp.concatenate(
        [grad_table, start_sums, middle_sums, sum_query, sum_value, sum_fc2, sum_fc1.reshape(-1, width)], axis=0
    )
    if boxed:
        last.third(grad_table)
        small = after(small, *last.sent)
    small = sum_everywhere(links, jnp.pad(small, ((0, -small.shape[0] % 8), (0, 0))))
    if boxed:
        last.fourth()
        grad_qkv = qkv_home(here, last.done())
        blocks = [waves[0].done(grads), waves[1].done(mix_away), waves[2].done(start_sums)]
        grad_proj = proj_home(here, blocks[2][:, 0:256])
        up_parts = [blocks[0][:, 0:256], blocks[1][:, 0:256], blocks[2][:, 256:512]]
        down_parts = [blocks[0][:, 256:512], blocks[1][:, 256:512], blocks[2][:, 512:768]]
        grad_fc1 = jnp.concatenate(
            [up_parts[k][:, 128 * half : 128 * half + 128] for half in range(2) for k in range(chunks)], axis=1
        )
        grad_fc2 = jnp.concatenate(
            [jnp.concatenate([p[:, :128], p[:, 128:]], axis=0) for p in down_parts], axis=1
        ).T
    else:
        tiles = [all_tiles(here, *pair) for pair in pairs_out]
        grad_qkv = native_scatter(natural_qkv(all_tiles(here, mix_away, mix_stay)))
        grad_proj = native_scatter(natural_proj(all_tiles(here, proj_away, proj_stay)))
        grad_fc1 = native_scatter(natural_up([t[..., :256] for t in tiles]))
        grad_fc2 = native_scatter(natural_down([t[..., 256:] for t in tiles]))
    base = 16
    return (
        layer_out,
        input_grad,
        small[base + 2],
        small[base],
        small[base + 1],
        grad_qkv,
        small[base + 16],
        small[base + 17],
        small[:heads, :table_rows].T,
        grad_proj,
        small[base + 12],
        small[base + 11],
        small[base + 9],
        small[base + 10],
        grad_fc1,
        small[base + 19 : base + 19 + hidden // width].reshape(-1),
        grad_fc2,
        small[base + 18],
        small[base + 8],
    )


def solution(mesh):
    images = P(AXES, None, None)
    both = P("wide", "narrow")
    same = P()
    links = Links(mesh.shape["wide"], mesh.shape["narrow"])
    return jax.shard_map(
        functools.partial(local, links),
        mesh=mesh,
        in_specs=(
            images, images, same, same, same, same, same, both, same, same, same, both, same, same,
            same, same, both, same, both, same, same,
        ),
        out_specs=(
            images, images, same, same, same, both, same, same, same, both, same, same, same, same,
            both, same, both, same, same,
        ),
        check_vma=False,
    )
```

```python
import functools
import math

import jax
import jax.numpy as jnp
import numpy as np
from jax import lax
from jax.experimental import pallas as pl
from jax.experimental.pallas import tpu as pltpu
from jax.sharding import PartitionSpec as P

EPSILON = 1e-06
ROOT_HALF = 0.7071067811865476
DENSITY = 0.3989422804014327
BF16 = jnp.bfloat16
F32 = jnp.float32
AXES = ("wide", "narrow")
TILE = 512
BAND = 200
CHUNK = 1024
NEVER = -1e30
MIB = 1 << 20


class Links:
    def __init__(self, wide, narrow):
        self.wide, self.narrow = wide, narrow
        self.y = 1 << ((wide.bit_length() - 1) // 2)
        self.z = wide // self.y
        self.x = narrow // 2
        self.size = {"z": self.z, "y": self.y, "x": self.x, "core": 2}
        self.unit = {"core": 1, "x": 2, "y": narrow, "z": narrow * self.y}
        self.boxed = (self.z, self.y, self.x) == (4, 2, 2)

    def place(self):
        w, n = lax.axis_index("wide"), lax.axis_index("narrow")
        return {"z": w // self.y, "y": w % self.y, "x": n // 2, "core": n % 2, "w": w, "n": n}

    def swap(self, value, **offsets):
        mask = sum(self.unit[axis] * offset for axis, offset in offsets.items())
        count = self.wide * self.narrow
        return lax.ppermute(value, AXES, [(k, k ^ mask) for k in range(count)])

    def others(self, value, axis):
        return [self.swap(value, **{axis: d}) for d in range(1, self.size[axis])]


def pick(value, axis, index, count):
    size = value.shape[axis] // count
    return lax.dynamic_slice_in_dim(value, index * size, size, axis)


def after(value, *others):
    return lax.optimization_barrier((value,) + others)[0]


def tied(values, wait):
    if not wait:
        return list(values)
    return list(lax.optimization_barrier(tuple(values) + tuple(wait)))[: len(values)]


def native_gather(shard):
    return lax.all_gather(
        lax.all_gather(shard, "narrow", axis=1, tiled=True), "wide", axis=0, tiled=True
    )


class Gather:
    orders = (("x", "y"), ("y", "x"))

    def __init__(self, links, block, split):
        self.links, self.block, self.split = links, block, split

    def first(self, *wait):
        block = after(self.block, *wait) if wait else self.block
        self.sent = [block]
        self.steps = [block] + self.links.others(block, "z")
        self.flying = self.steps[1:]

    def second(self, *wait):
        parts = arrange([after(self.steps[0], *wait) if wait else self.steps[0]] + self.steps[1:], self.split)
        self.steps, self.sent = [], []
        for held, order in zip(parts, self.orders, strict=True):
            self.sent.append(held)
            self.steps.append([held] + self.links.others(held, order[0]))
        self.flying = [v for p in self.steps for v in p[1:]]

    def third(self, *wait):
        parts = stack([[after(self.steps[0][0], *wait)] + self.steps[0][1:], self.steps[1]], apart=True)
        self.steps, self.sent = [], []
        for held, order in zip(parts, self.orders, strict=True):
            self.sent.append(held)
            self.steps.append([held] + self.links.others(held, order[1]))
        self.flying = [v for p in self.steps for v in p[1:]]

    def fourth(self, *wait):
        held = stack([[after(self.steps[0][0], *wait)] + self.steps[0][1:], self.steps[1]], apart=False)[0]
        self.sent = [held]
        self.operands = [held, self.links.swap(held, core=1)]
        self.flying = self.operands[1:]

    def blocks(self, refs, number, me):
        links = self.links
        order = self.orders[number]
        first = 0 if number == 0 else self.split
        out = []
        for core in range(2):
            for k in range(refs[core].shape[0]):
                at, rest = {}, k
                for axis in ("z",) + order:
                    at[axis] = me[axis] ^ (rest % links.size[axis])
                    rest //= links.size[axis]
                source = functools.partial(block_columns, refs[core], k, first)
                out.append((source, at["z"] * links.y + at["y"], at["x"] * 2 + (me["core"] ^ core)))
        return out


def block_columns(ref, k, first, col, broad):
    return ref.at[k, :, pl.ds(first + col, broad)]


def at_least(n, values):
    out = values[3]
    for k in (2, 1, 0):
        out = jnp.where(n == k, values[k], out)
    return out


def window(ref, row, col, tall, broad):
    if not isinstance(row, int):
        row = pl.multiple_of(row, 8)
    if not isinstance(col, int):
        col = pl.multiple_of(col, 128)
    return ref.at[pl.ds(row, tall), pl.ds(col, broad)]


def columns(ref, col, broad):
    return ref.at[:, pl.ds(col, broad)]


class Weight:
    def __init__(self, operands, copies, joints=(), extra=0):
        self.operands, self.copies, self.joints, self.extra = operands, copies, joints, extra

    def fill(self, refs, target, sem):
        for source, to in self.copies(refs, target):
            pltpu.make_async_copy(source, to, sem).start()

    def wait(self, target, sem):
        pltpu.make_async_copy(target, target, sem).wait()
        for here, there in self.joints:
            target[:, here : here + 128] += target[:, there : there + 128]


def align_side(here, side):
    zero = jnp.zeros((side.shape[0], 64), side.dtype)
    return jnp.where(
        here["n"] % 2 == 0,
        jnp.concatenate([side, zero], axis=1),
        jnp.concatenate([zero, side], axis=1),
    )


def qkv_block(here, shard):
    even = here["n"] % 2 == 0
    main = jnp.where(even, shard[:, :384], shard[:, 192:])
    return jnp.concatenate([main, align_side(here, jnp.where(even, shard[:, 384:], shard[:, :192]))], axis=1)


def qkv_operands(links, gathered, shard):
    if not links.boxed:
        return Weight([native_gather(shard)], lambda refs, target: [(refs[0], target.at[:, pl.ds(0, 2304)])] + [
            (refs[0].at[:, pl.ds(0, 256)], target.at[:, pl.ds(2304, 256)])], extra=256)

    def copies(refs, target):
        me = links.place()
        out = []
        for source, w, n in gathered.blocks(refs, 0, me):
            out.append((source(0, 384), window(target, w * 96, at_least(n, (0, 768, 1152, 1920)), 96, 384)))
        for source, w, n in gathered.blocks(refs, 1, me):
            for part, places in enumerate(((384, 2304, 1536, 2432), (512, 640, 1664, 1792))):
                out.append((source(128 * part, 128), window(target, w * 96, at_least(n, places), 96, 128)))
        return out

    return Weight(gathered.operands, copies, ((512, 2304), (1664, 2432)), 256)


def proj_operands(links, gathered, shard):
    if not links.boxed:
        return Weight([native_gather(shard)], lambda refs, target: [(refs[0], target.at[:, pl.ds(0, 768)])] + [
            (refs[0].at[:, pl.ds(0, 256)], target.at[:, pl.ds(768, 256)])], extra=256)

    def copies(refs, target):
        me = links.place()
        out = []
        for part, (col, places) in enumerate(((0, (0, 768, 384, 896)), (256, (128, 256, 512, 640)))):
            for source, w, n in gathered.blocks(refs, part, me):
                out.append((source(col, 128), window(target, w * 96, at_least(n, places), 96, 128)))
        return out

    return Weight(gathered.operands, copies, ((128, 768), (512, 896)), 256)


def up_block(shard, chunk):
    return jnp.concatenate(
        [shard[:, 384 * half + 128 * chunk : 384 * half + 128 * chunk + 128] for half in range(2)], axis=1
    )


def down_block(shard_t, chunk):
    piece = shard_t[:, 128 * chunk : 128 * chunk + 128]
    half = piece.shape[0] // 2
    return jnp.concatenate([piece[:half], piece[half:]], axis=1)


def chunk_copies(full, chunk):
    def slices(refs, target):
        return [
            (columns(refs[0], 384 * g + 128 * chunk, 128), columns(target, 128 * g, 128)) for g in range(8)
        ]

    return Weight([full], slices)


def up_operands(links, gathered, col, full, chunk):
    if not links.boxed:
        return chunk_copies(full, chunk)

    def copies(refs, target):
        me = links.place()
        return [
            (source(col, 256), window(target, w * 96, n * 256, 96, 256))
            for source, w, n in gathered.blocks(refs, 0, me)
        ]

    return Weight(gathered.operands, copies)


def down_operands(links, gathered, col, full, chunk):
    if not links.boxed:
        return chunk_copies(full, chunk)

    def copies(refs, target):
        me = links.place()
        return [
            (source(col + 128 * half, 128), window(target, n * 192 + half * 96, w * 128, 96, 128))
            for source, w, n in gathered.blocks(refs, 1, me)
            for half in range(2)
        ]

    return Weight(gathered.operands, copies)


class Scatter:
    orders = (("x", "y"), ("y", "x"))

    def __init__(self, links, here, split):
        self.links, self.here, self.split = links, here, split
        self.pairs, self.flying, self.stage = [], [], 0

    def first(self, away, stay):
        shape = (self.links.x, self.links.z, self.links.y) + away.shape[2:]
        self.pairs.append((stay.reshape(shape), self.links.swap(away.reshape(shape), core=1)))
        self.flying.append(self.pairs[-1][1])

    def jobs(self, step, picks):
        if step == "second":
            return [
                ([(self.pairs[k], cols) for k, cols in part], order[0])
                for part, order in zip(picks, self.orders, strict=True)
            ]
        whole_of = [(t, (0, t[0].shape[-1])) for t in self.terms]
        if step == "third":
            return [([t], order[1]) for t, order in zip(whole_of, self.orders, strict=True)]
        return [(whole_of, "z")]

    def take(self, results):
        self.sent = [v for r in results for v in r[1:]]
        self.terms = []
        axes = [order[self.stage] for order in self.orders] if self.stage < 2 else ["z"]
        for (keep, *sent), axis in zip(results, axes, strict=True):
            self.terms.append([keep] + [self.links.swap(v, **{axis: d}) for d, v in enumerate(sent, 1)])
        self.stage += 1
        self.flying = [v for t in self.terms for v in t[1:]]

    def done(self, *wait):
        terms = tied(self.terms[0], wait)
        total = terms[0]
        for term in terms[1:]:
            total = total + term.astype(F32)
        return total.reshape(total.shape[-2:])


def exchange(links, wait, *items):
    jobs = [job for scatter, step, picks in items for job in scatter.jobs(step, picks)]
    group, cols = jobs[0][0][0]
    jobs[0][0][0] = ((after(group[0], *wait),) + tuple(group[1:]), cols)
    results = fold(links, jobs)
    for scatter, step, _ in items:
        count = 1 if step == "fourth" else 2
        scatter.take(results[:count])
        results = results[count:]


def all_tiles(here, away, stay):
    return jnp.where(
        here["core"] == 0, jnp.stack([stay, away], axis=1), jnp.stack([away, stay], axis=1)
    ).reshape((4,) + away.shape[1:])


def native_scatter(partial):
    low = lax.psum_scatter(partial.astype(BF16), "wide", scatter_dimension=0, tiled=True)
    return lax.psum_scatter(low, "narrow", scatter_dimension=1, tiled=True).astype(F32)


def qkv_home(here, block):
    even = here["n"] % 2 == 0
    main, side = block[:, :384], block[:, 384:]
    return jnp.where(
        even,
        jnp.concatenate([main, side[:, :192]], axis=1),
        jnp.concatenate([side[:, 64:], main], axis=1),
    )


def proj_home(here, block):
    return jnp.where(here["n"] % 2 == 0, block[:, :192], block[:, 64:])


def natural_qkv(tiles):
    tiles = tiles.reshape(4, 768, 640)
    out = []
    for n in range(4):
        main, side = tiles[n, :, :384], tiles[n, :, 384:]
        out += [main, side[:, :192]] if n % 2 == 0 else [side[:, 64:], main]
    return jnp.concatenate(out, axis=1)


def natural_proj(tiles):
    tiles = tiles.reshape(4, 768, 256)
    return jnp.concatenate([tiles[n, :, :192] if n % 2 == 0 else tiles[n, :, 64:] for n in range(4)], axis=1)


def natural_up(chunks):
    tiles = [t.reshape(4, 768, 2, 128) for t in chunks]
    return jnp.stack(tiles, axis=0).transpose(2, 1, 3, 0, 4).reshape(768, -1)


def natural_down(chunks):
    tiles = [t.reshape(4, 8, 96, 2, 128) for t in chunks]
    return jnp.stack(tiles, axis=0).transpose(2, 0, 5, 1, 4, 3).reshape(-1, 768)


def tree_sum(terms):
    while len(terms) > 1:
        terms = [terms[k] + terms[k + 1] for k in range(0, len(terms), 2)]
    return terms[0]


def sum_everywhere(links, here, away, stay, wait):
    if links.boxed:
        half = after(stay + links.swap(away, core=1), *wait)
        half = tree_sum(
            [half] + [links.swap(half, x=k % links.x, y=k // links.x) for k in range(1, links.x * links.y)]
        )
        half = tree_sum([half] + links.others(half, "z"))
        other = links.swap(half, core=1)
    else:
        first = jnp.where(here["core"] == 0, stay, away)
        second = jnp.where(here["core"] == 0, away, stay)
        return lax.psum(jnp.concatenate([first, second], axis=0), AXES)
    return jnp.where(
        here["core"] == 0, jnp.concatenate([half, other], axis=0), jnp.concatenate([other, half], axis=0)
    )


def whole(shape):
    return pl.BlockSpec(tuple(shape), lambda *_: (0,) * len(shape))


def kept(shape):
    return pl.BlockSpec(tuple(shape), lambda *_: (0,) * len(shape), pipeline_mode=pl.Buffered(1))


ANY = pl.BlockSpec(memory_space=pl.ANY)
FAR = pl.BlockSpec(memory_space=pltpu.HBM)
SCALARS = pl.BlockSpec(memory_space=pltpu.SMEM)


LIMITS = {"stack": 16, "arrange": 8, "fold": 24, "pack": 8, "prepare": 16, "bias": 16, "bias_back": 20, "project": 24, "attend": 18, "merge": 20, "feed": 42, "middle_back": 28, "attend_back": 22, "mixed_grad": 24, "start_back": 28}


def call(kernel, name, grid, ins, outs, scratch=(), flops=0, aliases=None):
    moved = sum(a.size * a.dtype.itemsize for a, _ in ins)
    moved += sum(math.prod(s) * jnp.dtype(d).itemsize for s, d, _ in outs)
    return pl.pallas_call(
        kernel,
        name=name,
        grid=grid,
        in_specs=[spec for _, spec in ins],
        out_specs=[spec for _, _, spec in outs],
        out_shape=[jax.ShapeDtypeStruct(s, d) for s, d, _ in outs],
        scratch_shapes=list(scratch),
        input_output_aliases=aliases or {},
        compiler_params=pltpu.CompilerParams(vmem_limit_bytes=LIMITS[name] * MIB),
        cost_estimate=pl.CostEstimate(flops=int(flops), bytes_accessed=int(moved), transcendentals=0),
    )(*[a for a, _ in ins])


def nn(a, b):
    return lax.dot_general(a, b, (((1,), (0,)), ((), ())), preferred_element_type=F32)


def nt(a, b):
    return lax.dot_general(a, b, (((1,), (1,)), ((), ())), preferred_element_type=F32)


def tn(a, b):
    return lax.dot_general(a, b, (((0,), (0,)), ((), ())), preferred_element_type=F32)


def arrange(blocks, split):
    rows, cols = blocks[0].shape
    count = len(blocks)

    def kernel(*refs):
        for k in range(count):
            refs[count][k] = refs[k][:, :split]
            refs[count + 1][k] = refs[k][:, split:]

    return call(
        kernel, "arrange", (),
        [(b, whole(b.shape)) for b in blocks],
        [((count, rows, part), BF16, whole((count, rows, part))) for part in (split, cols - split)],
    )


def stack(parts, apart):
    flat = [v for part in parts for v in part]
    outs = [(sum(v.shape[0] for v in part), part[0].shape[1], part[0].shape[2]) for part in parts]
    if not apart:
        outs = [(outs[0][0], outs[0][1], sum(o[2] for o in outs))]

    def kernel(*refs):
        number, col = 0, 0
        for k, part in enumerate(parts):
            out = refs[len(flat) + (k if apart else 0)]
            at, cols = 0, part[0].shape[2]
            for v in part:
                out[at : at + v.shape[0], :, col : col + cols] = refs[number][...]
                at += v.shape[0]
                number += 1
            col += 0 if apart else cols

    return call(
        kernel, "stack", (), [(v, whole(v.shape)) for v in flat], [(shape, BF16, whole(shape)) for shape in outs]
    )


def fold(links, jobs):
    arrays, index = [], {}
    for sources, _ in jobs:
        for group, _ in sources:
            for array in group:
                if id(array) not in index:
                    index[id(array)] = len(arrays)
                    arrays.append(array)
    dims = {"x": 0, "z": 1, "y": 2}
    outs = []
    for sources, axis in jobs:
        first = sources[0][0][0]
        cols = sum(part[1] - part[0] for _, part in sources)
        shape = tuple(1 if k == dims[axis] else first.shape[k] for k in range(4)) + (cols,)
        outs += [(shape, F32 if d == 0 else BF16, whole(shape)) for d in range(links.size[axis])]

    def kernel(*refs):
        me = links.place()
        at_out = len(arrays)
        for sources, axis in jobs:
            for d in range(links.size[axis]):
                where = [slice(None)] * 4
                where[dims[axis]] = pl.ds(me[axis] ^ d, 1)
                col = 0
                for group, (begin, end) in sources:
                    picked = tuple(where) + (slice(begin, end),)
                    total = refs[index[id(group[0])]][picked].astype(F32)
                    for array in group[1:]:
                        total = total + refs[index[id(array)]][picked].astype(F32)
                    out = refs[at_out]
                    out[..., col : col + end - begin] = total.astype(out.dtype)
                    col += end - begin
                at_out += 1

    results = call(kernel, "fold", (), [(a, whole(a.shape)) for a in arrays], outs)
    out = []
    for _, axis in jobs:
        out.append(results[: links.size[axis]])
        results = results[links.size[axis] :]
    return out


def pack(links, table, heads, start_sums, middle_sums, halves, sum_fc2, hidden_sums):
    width = table.shape[1]

    def kernel(table_ref, start_ref, middle_ref, q0, v0, q1, v1, fc2_ref, a_ref, b_ref, c_ref, away_ref, stay_ref, all_s):
        all_s[...] = jnp.zeros_like(all_s)
        rows = [(table_ref, heads), (start_ref, 3), (middle_ref, 5)]
        at = 0
        for ref, count in rows:
            for k in range(count):
                all_s[(at + k) // 16, (at + k) % 16 : (at + k) % 16 + 1, :] = ref[k : k + 1, :]
            at += count
        for pair in ((q0, q1), (v0, v1)):
            for k, ref in enumerate(pair):
                all_s[at // 16, at % 16 : at % 16 + 1, k * 384 : k * 384 + 384] = ref[...]
            at += 1
        all_s[at // 16, at % 16 : at % 16 + 1, :] = fc2_ref[...]
        at += 1
        for k, ref in enumerate((a_ref, b_ref, c_ref)):
            all_s[(at + k) // 16, (at + k) % 16 : (at + k) % 16 + 1, :] = ref[:, 0:width]
            all_s[(at + 3) // 16, (at + 3) % 16 : (at + 3) % 16 + 1, k * 256 : k * 256 + 256] = ref[:, width : width + 256]
        c = lax.axis_index("narrow") % 2
        away_ref[...] = all_s[1 - c]
        stay_ref[...] = all_s[c]

    operands = [table, start_sums, middle_sums, *halves[0], *halves[1], sum_fc2, *hidden_sums]
    return call(
        kernel, "pack", (), [(a, whole(a.shape)) for a in operands],
        [((16, width), F32, whole((16, width)))] * 2, [pltpu.VMEM((2, 16, width), F32)],
    )


def norm(values):
    centre = jnp.mean(values, axis=-1, keepdims=True)
    centred = values - centre
    spread = jnp.mean(centred * centred, axis=-1, keepdims=True)
    scaling = lax.rsqrt(spread + EPSILON)
    return centred * scaling, scaling


def norm_back(grad, normed, scaling, gain):
    scaled = grad * gain
    first = jnp.mean(scaled, axis=-1, keepdims=True)
    second = jnp.mean(scaled * normed, axis=-1, keepdims=True)
    return (scaled - first - normed * second) * scaling


def banded(tall, body):
    if BAND >= tall:
        body(slice(0, tall), 0)
        return

    def step(k, carry):
        at = pl.multiple_of(k * BAND, 8)
        body(pl.ds(at, BAND), at)
        return carry

    lax.fori_loop(0, tall // BAND, step, 0)


def column_sum(values):
    return jnp.sum(values, axis=0, keepdims=True)


TOKEN, GAIN1, SHIFT1, GAMMA2, BIAS1, GAMMA1, GAIN2, SHIFT2, BIAS2 = range(9)


def row_of(ref, k):
    return ref[k : k + 1, :]


def masked_rows(image, sizes_ref, patterns_ref, tall):
    bound, group = 0, 0
    for k in range(sizes_ref.shape[0] - 1):
        bound = bound + sizes_ref[k]
        group = group + (image >= bound).astype(jnp.int32)
    columns_of = patterns_ref[...].T
    which = lax.broadcasted_iota(jnp.int32, columns_of.shape, 1) == group
    return jnp.sum(jnp.where(which, columns_of, 0.0), axis=1, keepdims=True)[0:tall] > 0.5


def first_image(images):
    return lax.axis_index(AXES) * images


def prepare(sizes, inputs, cotangent, group_sizes, mask_patterns, vectors):
    images, length, tall, width = sizes
    rows = images * tall
    groups, patches = mask_patterns.shape

    def kernel(x_ref, g_ref, sizes_ref, mask_ref, *refs):
        vector_refs, refs = refs[: len(vectors)], refs[len(vectors) :]
        h0_ref, n1_ref, g_out, df_ref, sum_ref, params_ref, patterns_ref, x_s, g_s, mask_s, sems, *vector_s = refs
        step = pl.program_id(0)

        @pl.when(step == 0)
        def _():
            x_s[...] = jnp.zeros_like(x_s)
            g_s[...] = jnp.zeros_like(g_s)
            sum_ref[...] = jnp.zeros_like(sum_ref)
            params_ref[...] = jnp.zeros_like(params_ref)
            patterns_ref[...] = jnp.zeros_like(patterns_ref)
            moves = [pltpu.make_async_copy(mask_ref, mask_s, sems.at[len(vectors)])]
            moves += [
                pltpu.make_async_copy(a, b, sems.at[k]) for k, (a, b) in enumerate(zip(vector_refs, vector_s, strict=True))
            ]
            for move in moves:
                move.start()
            for move in moves:
                move.wait()
            patterns_ref[0:groups, 1 : patches + 1] = mask_s[...].astype(F32)
            for k, ref in zip(vectors, vector_s, strict=True):
                params_ref[k : k + 1, :] = ref[...].reshape(1, width)

        x_s[0:length, :] = x_ref[0].astype(F32)
        g_s[0:length, :] = g_ref[0].astype(F32)
        masked = masked_rows(first_image(images) + step, sizes_ref, patterns_ref, tall)
        start = jnp.where(masked, row_of(params_ref, TOKEN), x_s[...])
        h0_ref[...] = start
        normed, _ = norm(start)
        n1_ref[...] = (normed * row_of(params_ref, GAIN1) + row_of(params_ref, SHIFT1)).astype(BF16)
        g = g_s[...]
        g_out[...] = g.astype(BF16)
        df = row_of(params_ref, GAMMA2) * g
        df_ref[...] = df.astype(BF16)
        sum_ref[...] += column_sum(df)

    image = pl.BlockSpec((1, length, width), lambda i: (i, 0, 0))
    band = pl.BlockSpec((tall, width), lambda i: (i, 0))
    return call(
        kernel, "prepare", (images,),
        [(inputs, image), (cotangent, image), (group_sizes, SCALARS), (mask_patterns, FAR)]
        + [(v, FAR) for v in vectors.values()],
        [((rows, width), F32, band), ((rows, width), BF16, band), ((rows, width), BF16, band),
         ((rows, width), BF16, band), ((1, width), F32, whole((1, width))), ((16, width), F32, whole((16, width))),
         ((8, 256), F32, whole((8, 256)))],
        [pltpu.VMEM((tall, width), F32), pltpu.VMEM((tall, width), F32), pltpu.VMEM(mask_patterns.shape, jnp.int32),
         pltpu.SemaphoreType.DMA((len(vectors) + 1,))] + [pltpu.VMEM((width,), F32) for _ in vectors],
        flops=rows * width * 40,
    )


def table_columns(grid_side, broad):
    side = 2 * grid_side - 1
    q = np.arange(broad)
    entry = (q // grid_side) * side + q % grid_side + grid_side - 1
    return jnp.asarray(np.where(q < side * grid_side, entry, -(1 << 20)).astype(np.int32)[None])


def three_parts(values):
    high = values.astype(BF16)
    rest = values - high.astype(F32)
    middle = rest.astype(BF16)
    return high, middle, (rest - middle.astype(F32)).astype(BF16)


def bias_kernel(table_t, entry, grid_side, tall, broad):
    heads = table_t.shape[0]
    length = grid_side * grid_side + 1
    wide = entry.shape[1]
    inner = (2 * grid_side - 1) ** 2

    def kernel(table_ref, entry_ref, out_ref, *halves):
        def put(at, count, values):
            for half, ref in enumerate(halves):
                ref[pl.ds(at, count), :] = values[:, 128 * half : 128 * half + 128]

        parts = jnp.concatenate(three_parts(table_ref[...]), axis=0)
        left, top, corner = (table_ref[:, inner + 1 : inner + 2], table_ref[:, inner : inner + 1],
                             table_ref[:, inner + 2 : inner + 3])
        lane = lax.broadcasted_iota(jnp.int32, (heads, broad), 1)

        def column(b, carry):
            which = lax.broadcasted_iota(jnp.int32, (table_ref.shape[1], wide), 0) + b
            select = jnp.where(which == entry_ref[...], 1.0, 0.0).astype(BF16)
            spread = nn(parts, select)
            spread = spread[:heads] + spread[heads : 2 * heads] + spread[2 * heads :]
            for a in range(grid_side):
                shift = (grid_side - 1 - a) * grid_side - 1
                moved = pltpu.roll(spread, (wide - shift) % wide, 1)[:, :broad]
                moved = jnp.where(lane == 0, top, moved)
                put(pl.multiple_of((1 + grid_side * a + b) * heads, 16), heads, moved)
            return carry

        lax.fori_loop(0, grid_side, column, 0)
        put(0, heads, jnp.where(lane == 0, corner, left))
        rest = (tall - length) * heads
        put(length * heads, rest, jnp.full((rest, broad), NEVER, F32))
        for h in range(out_ref.shape[0]):
            for half, ref in enumerate(halves):
                out_ref[h, :, 128 * half : 128 * half + 128] = ref[pl.ds(h, tall, stride=heads), :]

    return call(
        kernel, "bias", (),
        [(table_t, whole(table_t.shape)), (entry, whole(entry.shape))],
        [((12, tall, broad), F32, whole((12, tall, broad)))],
        [pltpu.VMEM((tall * heads, 128), F32)] * (broad // 128),
        flops=2 * 48 * 768 * wide * grid_side,
    )[0]


def bias_back_kernel(terms, entry, grid_side, width):
    count, tall, broad = terms.shape
    heads = 16
    wide = entry.shape[1]
    inner = (2 * grid_side - 1) ** 2
    length = grid_side * grid_side + 1

    def kernel(terms_ref, entry_ref, out_ref, *halves):
        def get(at, count):
            return jnp.concatenate([ref[pl.ds(at, count), :] for ref in halves], axis=1)

        lane = lax.broadcasted_iota(jnp.int32, (heads, broad), 1)
        inside = (lane >= 1) & (lane < length)
        for h in range(heads):
            values = terms_ref[h] if h < count else jnp.zeros((tall, broad), F32)
            for half, ref in enumerate(halves):
                ref[pl.ds(h, tall, stride=heads), :] = values[:, 128 * half : 128 * half + 128]

        def column(b, carry):
            total, edge = carry
            which = lax.broadcasted_iota(jnp.int32, (width, wide), 0) + b
            select = jnp.where(which == entry_ref[...], 1.0, 0.0).astype(BF16)
            spread = jnp.zeros((heads, wide), F32)
            for a in range(grid_side):
                shift = (grid_side - 1 - a) * grid_side - 1
                found = get(pl.multiple_of((1 + grid_side * a + b) * heads, 16), heads)
                edge = edge + jnp.where(lane == 0, found, 0.0)
                found = jnp.where(inside, found, 0.0)
                found = jnp.concatenate([found, jnp.zeros((heads, wide - broad), F32)], axis=1)
                spread = spread + pltpu.roll(found, shift % wide, 1)
            found = nt(jnp.concatenate(three_parts(spread), axis=0), select)
            total = total + found[:heads] + found[heads : 2 * heads] + found[2 * heads :]
            return total, edge

        total, edge = lax.fori_loop(
            0, grid_side, column, (jnp.zeros((heads, width), F32), jnp.zeros((heads, broad), F32))
        )
        first = get(0, heads)
        top = jnp.sum(edge, axis=1, keepdims=True)
        left = jnp.sum(jnp.where(inside, first, 0.0), axis=1, keepdims=True)
        corner = first[:, 0:1]
        place = lax.broadcasted_iota(jnp.int32, (heads, width), 1)
        total = jnp.where(place == inner, top, total)
        total = jnp.where(place == inner + 1, left, total)
        out_ref[...] = jnp.where(place == inner + 2, corner, total)

    return call(
        kernel, "bias_back", (),
        [(terms, whole(terms.shape)), (entry, whole(entry.shape))],
        [((heads, width), F32, whole((heads, width)))],
        [pltpu.VMEM((tall * heads, 128), F32)] * (broad // 128),
        flops=2 * 48 * 768 * wide * grid_side,
    )[0]


def project(sizes, first_low, weight, params, score_scale):
    images, length, tall, width = sizes
    rows = images * tall
    cols = 3 * width
    count = len(weight.operands)

    def kernel(*refs):
        n1_ref, params_ref = refs[:2]
        out_ref, w_s, sem = refs[2 + count :]
        step = pl.program_id(0)

        @pl.when(step == 0)
        def _():
            weight.fill(refs[2 : 2 + count], w_s, sem)
            weight.wait(w_s, sem)

        w = w_s[:, pl.ds(pl.multiple_of(step * width, 128), width)]
        scale = jnp.where(step == 0, score_scale, 1.0)
        out_ref[...] = ((nn(n1_ref[...], w) + params_ref[pl.ds(9 + step, 1), :]) * scale).astype(BF16)

    return call(
        kernel, "project", (cols // width,),
        [(first_low, kept((rows, width))), (params, kept(params.shape))] + [(a, ANY) for a in weight.operands],
        [((rows, cols), BF16, pl.BlockSpec((rows, width), lambda t: (0, t)))],
        [pltpu.VMEM((width, cols + weight.extra), BF16), pltpu.SemaphoreType.DMA],
        flops=2 * rows * width * cols,
    )[0]


def head_masks(tall):
    lane = lax.broadcasted_iota(jnp.int32, (tall, 128), 1)
    return [lane < 64, lane >= 64]


def attend(sizes, mixed, bias, first, pairs):
    images, length, tall, width = sizes
    rows = images * tall
    every = width // 128
    broad = bias.shape[2]

    def kernel(q_ref, k_ref, v_ref, bias_ref, out_ref, p_ref):
        masks = head_masks(tall)
        units = [(i, h) for i in range(images) for h in range(2)]
        scores, probs = [], []
        for i, h in units:
            q, k = q_ref[tall * i : tall * i + tall, :], k_ref[tall * i : tall * i + tall, :]
            scores.append(nt(k, jnp.where(masks[h], q, jnp.zeros_like(q))) + bias_ref[h, :, 0:tall])
        for (i, h), s in zip(units, scores, strict=True):
            e = jnp.exp(s - jnp.max(s, axis=0, keepdims=True))
            p = (e * (1.0 / jnp.sum(e, axis=0, keepdims=True))).astype(BF16)
            p_ref[h, i, :, 0:tall] = p
            probs.append(p)
        for i in range(images):
            vt = v_ref[tall * i : tall * i + tall, :].T
            out = [nn(vt[64 * h : 64 * h + 64, :], probs[2 * i + h]) for h in range(2)]
            out_ref[tall * i : tall * i + tall, :] = jnp.concatenate(out, axis=0).T.astype(BF16)

    def column(at):
        return pl.BlockSpec((rows, 128), lambda t: (0, at + t))

    return call(
        kernel, "attend", (pairs,),
        [(mixed, column(first)), (mixed, column(every + first)), (mixed, column(2 * every + first)),
         (bias, pl.BlockSpec((2, tall, broad), lambda t: (first + t, 0, 0)))],
        [((rows, 128 * pairs), BF16, column(0)),
         ((2 * pairs, images, tall, broad), BF16,
          pl.BlockSpec((2, images, tall, broad), lambda t: (t, 0, 0, 0)))],
        flops=4 * rows * tall * 128 * pairs,
    )


def attend_back(sizes, mixed, probs, grad_out, score_scale, first, pairs, so_far):
    images, length, tall, width = sizes
    rows = images * tall
    every = width // 128
    broad = probs.shape[3]

    def kernel(q_ref, k_ref, v_ref, do_ref, p_ref, *refs):
        grad_ref, terms_ref, qb_ref, vb_ref = refs[-4:]
        masks = head_masks(tall)
        units = [(i, h) for i in range(images) for h in range(2)]

        def part(ref, i):
            return ref[tall * i : tall * i + tall, :]

        def own(value, h):
            return jnp.where(masks[h], value, jnp.zeros_like(value))

        grads = [nt(part(v_ref, i), own(part(do_ref, i), h)) for i, h in units]
        lows = []
        for (i, h), grad in zip(units, grads, strict=True):
            p = p_ref[h, i, :, 0:tall].astype(F32)
            t = p * grad
            lows.append((t - p * jnp.sum(t, axis=0, keepdims=True)).astype(BF16))
        for h in range(2):
            terms_ref[h, :, 0:tall] = sum(lows[2 * i + h].astype(F32) for i in range(images))
            terms_ref[h, :, tall:] = jnp.zeros((tall, broad - tall), F32)
        query_sum, value_sum = 0.0, 0.0
        for i in range(images):
            kt = part(k_ref, i).T
            dv = sum(nn(p_ref[h, i, :, 0:tall], own(part(do_ref, i), h)) for h in range(2))
            dk = sum(nn(lows[2 * i + h], own(part(q_ref, i), h)) for h in range(2))
            dq = jnp.concatenate(
                [nn(kt[64 * h : 64 * h + 64, :], lows[2 * i + h]) for h in range(2)], axis=0
            ).T * score_scale
            for number, grad in enumerate((dq, dk, dv)):
                grad_ref[number, tall * i : tall * i + tall, :] = grad.astype(BF16)
            query_sum += column_sum(dq)
            value_sum += column_sum(dv)
        qb_ref[...] = query_sum
        vb_ref[...] = value_sum

    def column(at):
        return pl.BlockSpec((rows, 128), lambda t: (0, at + t))

    one = pl.BlockSpec((1, 128), lambda t: (0, t))
    return call(
        kernel, "attend_back", (pairs,),
        [(mixed, column(first)), (mixed, column(every + first)), (mixed, column(2 * every + first)),
         (grad_out, column(first)),
         (probs, pl.BlockSpec((2, images, tall, broad), lambda t: (first + t, 0, 0, 0)))]
        + ([] if so_far is None else [(so_far, ANY)]),
        [((3, rows, width), BF16, pl.BlockSpec((3, rows, 128), lambda t: (0, 0, first + t)))]
        + [((2 * pairs, tall, broad), F32, pl.BlockSpec((2, tall, broad), lambda t: (t, 0, 0))),
           ((1, 128 * pairs), F32, one), ((1, 128 * pairs), F32, one)],
        flops=8 * rows * tall * 128 * pairs,
        aliases={} if so_far is None else {5: 0},
    )


def merge(sizes, attended, start, weight, params):
    images, length, tall, width = sizes
    rows = images * tall
    count = len(weight.operands)

    def kernel(*refs):
        att_refs, refs = refs[: len(attended)], refs[len(attended) :]
        h0_ref, params_ref = refs[:2]
        h1_ref, n2_ref, w_s, out_s, sem = refs[2 + count :]
        step = pl.program_id(0)

        @pl.when(step == 0)
        def _():
            weight.fill(refs[2 : 2 + count], w_s, sem)
            weight.wait(w_s, sem)
            part = width // len(attended)
            out_s[...] = sum(nn(r[...], w_s[part * k : part * k + part, 0:width]) for k, r in enumerate(att_refs))

        @pl.when(step > 0)
        def _():
            def body(at, first):
                out = out_s[pl.ds(pl.multiple_of((step - 1) * tall + first, 8), min(BAND, tall)), :]
                middle = h0_ref[at, :] + row_of(params_ref, GAMMA1) * (out + row_of(params_ref, BIAS1))
                h1_ref[at, :] = middle
                normed, _ = norm(middle)
                n2_ref[at, :] = (normed * row_of(params_ref, GAIN2) + row_of(params_ref, SHIFT2)).astype(BF16)

            banded(tall, body)

    band = pl.BlockSpec((tall, width), lambda i: (jnp.maximum(i - 1, 0), 0))
    return call(
        kernel, "merge", (images + 1,),
        [(a, kept(a.shape)) for a in attended]
        + [(start, band), (params, kept(params.shape))]
        + [(a, ANY) for a in weight.operands],
        [((rows, width), F32, band), ((rows, width), BF16, band)],
        [pltpu.VMEM((width, width + weight.extra), BF16), pltpu.VMEM((rows, width), F32),
         pltpu.SemaphoreType.DMA],
        flops=2 * rows * width * width,
    )


def part_by_core(store, away_ref, stay_ref):
    c = lax.axis_index("narrow") % 2
    for x in range(2):
        away_ref[x] = store[2 * x + 1 - c]
        stay_ref[x] = store[2 * x + c]


def feed(sizes, second_low, down_low, up, down, bias, sums):
    images, length, tall, width = sizes
    rows = images * tall
    shared = up.operands[0] is down.operands[0]
    ups, downs = len(up.operands), 0 if shared else len(down.operands)
    carried = [] if sums is None else list(sums)

    def kernel(*refs):
        n2_ref, df_ref, bias_ref = refs[:3]
        rest = refs[3:]
        up_refs, rest = rest[:ups], rest[ups:]
        down_refs, rest = (up_refs if shared else rest[:downs]), rest[downs:]
        sum_refs, rest = rest[: len(carried)], rest[len(carried) :]
        f_ref, dn_ref, away_ref, stay_ref, gbias_ref, up_s, down_s, grad_s, sems = rest
        step = pl.program_id(0)

        @pl.when(step == 0)
        def _():
            up.fill(up_refs, up_s, sems.at[0])
            down.fill(down_refs, down_s, sems.at[1])
            if carried:
                pltpu.make_async_copy(sum_refs[0], f_ref, sems.at[2]).start()
                pltpu.make_async_copy(sum_refs[1], dn_ref, sems.at[3]).start()
            up.wait(up_s, sems.at[0])
            down.wait(down_s, sems.at[1])
            if carried:
                pltpu.make_async_copy(sum_refs[0], f_ref, sems.at[2]).wait()
                pltpu.make_async_copy(sum_refs[1], dn_ref, sems.at[3]).wait()
            else:
                f_ref[...] = jnp.zeros_like(f_ref)
                dn_ref[...] = jnp.zeros_like(dn_ref)

        at = pl.ds(pl.multiple_of(step * TILE, TILE), TILE)
        up_w, down_w = up_s[:, at], down_s[:, at]
        u = nn(n2_ref[...], up_w) + bias_ref[...]
        dz = nn(df_ref[...], down_w)
        bell = jnp.exp(-0.5 * u * u)
        below = 0.5 * (1.0 + lax.erf(u * ROOT_HALF))
        z = (u * below).astype(BF16)
        du = dz * (below + u * (DENSITY * bell))
        gbias_ref[...] = column_sum(du)
        du = du.astype(BF16)
        grad = tn(n2_ref[...], du).astype(BF16)
        for k in range(TILE // 256):
            grad_s[step * (TILE // 256) + k, :, :, 0:256] = grad[:, 256 * k : 256 * k + 256].reshape(8, 96, 256)
        grad = tn(df_ref[...], z).astype(BF16)
        for n in range(4):
            for w in range(TILE // 128):
                for half in range(2):
                    grad_s[n, step * (TILE // 128) + w, :, 256 + 128 * half : 384 + 128 * half] = grad[
                        192 * n + 96 * half : 192 * n + 96 * half + 96, 128 * w : 128 * w + 128
                    ]
        f_ref[...] += nt(z, down_w)
        dn_ref[...] += nt(du, up_w)

        @pl.when(step == CHUNK // TILE - 1)
        def _():
            part_by_core(grad_s, away_ref, stay_ref)

    tile = pl.BlockSpec((1, TILE), lambda t: (0, t))
    full = whole((rows, width))
    shape = (2, 8, 96, 512)
    return call(
        kernel, "feed", (CHUNK // TILE,),
        [(second_low, kept((rows, width))), (down_low, kept((rows, width))), (bias, tile)]
        + [(a, ANY) for a in up.operands + ([] if shared else down.operands) + carried],
        [((rows, width), F32, full), ((rows, width), F32, full),
         (shape, BF16, whole(shape)), (shape, BF16, whole(shape)), ((1, CHUNK), F32, tile)],
        [pltpu.VMEM((width, CHUNK), BF16), pltpu.VMEM((width, CHUNK), BF16), pltpu.VMEM((4, 8, 96, 512), BF16),
         pltpu.SemaphoreType.DMA((4,))],
        flops=12 * rows * width * CHUNK,
    )


def middle_back(sizes, attended, branch, grad_n2, middle, start, upstream, weight, params):
    images, length, tall, width = sizes
    rows = images * tall
    count = len(weight.operands)

    def kernel(*refs):
        att_refs, refs = refs[: len(attended)], refs[len(attended) :]
        f_ref, dn_ref, h1_ref, h0_ref, g_ref, params_ref = refs[:6]
        out_ref, dh_ref, do_ref, away_ref, stay_ref, sum_ref, w_s, da_s, grad_s, layer_s, sem = refs[6 + count :]
        step = pl.program_id(0)

        @pl.when(step == 0)
        def _():
            weight.fill(refs[6 : 6 + count], w_s, sem)
            sum_ref[...] = jnp.zeros_like(sum_ref)

        @pl.when(step < images)
        def _():
            def body(at, first):
                f = f_ref[at, :] + row_of(params_ref, BIAS2)
                h1 = h1_ref[at, :]
                g = g_ref[at, :].astype(F32)
                layer_s[at, :] = h1 + row_of(params_ref, GAMMA2) * f
                normed, scaling = norm(h1)
                dn = dn_ref[at, :]
                dh = g + norm_back(dn, normed, scaling, row_of(params_ref, GAIN2))
                dh_ref[at, :] = dh
                da = row_of(params_ref, GAMMA1) * dh
                sum_ref[0:1, :] += column_sum(g * f)
                sum_ref[1:2, :] += column_sum(dn * normed)
                sum_ref[2:3, :] += column_sum(dn)
                sum_ref[3:4, :] += column_sum(dh * (h1 - h0_ref[at, :]))
                sum_ref[4:5, :] += column_sum(da)
                da_s[pl.ds(pl.multiple_of(step * tall + first, 8), min(BAND, tall)), :] = da.astype(BF16)

            banded(tall, body)
            out_ref[0] = layer_s[0:length, :].astype(BF16)

        @pl.when(step == images)
        def _():
            sum_ref[3:4, :] = sum_ref[3:4, :] / row_of(params_ref, GAMMA1)
            weight.wait(w_s, sem)
            do_ref[...] = nt(da_s[...], w_s[:, 0:width]).astype(BF16)
            grad = jnp.concatenate([tn(r[...], da_s[...]) for r in att_refs], axis=0).astype(BF16)
            for n, at in enumerate((0, 128, 384, 512)):
                grad_s[n] = grad[:, at : at + 256].reshape(8, 96, 256)
            part_by_core(grad_s, away_ref, stay_ref)

    def at(i):
        return jnp.minimum(i, images - 1)

    band = pl.BlockSpec((tall, width), lambda i: (at(i), 0))
    shape = (2, 8, 96, 256)
    return call(
        kernel, "middle_back", (images + 1,),
        [(a, kept(a.shape)) for a in attended]
        + [(a, band) for a in (branch, grad_n2, middle, start, upstream)] + [(params, kept(params.shape))]
        + [(a, ANY) for a in weight.operands],
        [((images, length, width), BF16, pl.BlockSpec((1, length, width), lambda i: (at(i), 0, 0))),
         ((rows, width), F32, band), ((rows, width), BF16, whole((rows, width))),
         (shape, BF16, whole(shape)), (shape, BF16, whole(shape)), ((8, width), F32, whole((8, width)))],
        [pltpu.VMEM((width, width + weight.extra), BF16), pltpu.VMEM((rows, width), BF16),
         pltpu.VMEM((4, 8, 96, 256), BF16), pltpu.VMEM((tall, width), F32), pltpu.SemaphoreType.DMA],
        flops=4 * rows * width * width,
    )


def mixed_grad(sizes, first_low, grads):
    images, length, tall, width = sizes
    rows = images * tall

    def kernel(n1_ref, grad_ref, away_ref, stay_ref):
        step = pl.program_id(0)
        c = lax.axis_index("narrow") % 2
        n = 2 * (step % 2) + jnp.where(step < 2, 1 - c, c)
        main = grad_ref[at_least(n, (0, 1, 1, 2)), :, pl.ds(pl.multiple_of(at_least(n, (0, 0, 384, 384)), 128), 384)]
        side = grad_ref[at_least(n, (0, 0, 2, 2)), :, pl.ds(pl.multiple_of(at_least(n, (384, 512, 0, 128)), 128), 256)]
        main = tn(n1_ref[...], main).astype(BF16).reshape(8, 96, 384)
        side = tn(n1_ref[...], side).astype(BF16).reshape(8, 96, 256)
        for role, ref in enumerate((away_ref, stay_ref)):
            @pl.when(step // 2 == role)
            def _(ref=ref):
                ref[0, :, :, 0:384] = main
                ref[0, :, :, 384:640] = side

    shape = (2, 8, 96, 640)
    return call(
        kernel, "mixed_grad", (4,),
        [(first_low, kept((rows, width))), (grads, kept(grads.shape))],
        [(shape, BF16, pl.BlockSpec((1, 8, 96, 640), lambda t: (jnp.minimum(t, 1), 0, 0, 0))),
         (shape, BF16, pl.BlockSpec((1, 8, 96, 640), lambda t: (jnp.maximum(t - 2, 0), 0, 0, 0)))],
        flops=6 * rows * width * width,
    )


def start_back(sizes, grads, weight, start, grad_middle, group_sizes, patterns, params):
    images, length, tall, width = sizes
    rows = images * tall
    count = len(weight.operands)

    def kernel(*refs):
        grad_ref, h0_ref, dh_ref, sizes_ref, patterns_ref, params_ref = refs[:6]
        out_ref, sum_ref, w_s, dn_s, out_s, sem = refs[6 + count :]
        step = pl.program_id(0)

        @pl.when(step == 0)
        def _():
            weight.fill(refs[6 : 6 + count], w_s, sem)
            sum_ref[...] = jnp.zeros_like(sum_ref)
            dn_s[...] = jnp.zeros_like(dn_s)
            weight.wait(w_s, sem)

        @pl.when(step < 3)
        def _():
            dn_s[...] += nt(grad_ref[0], w_s[:, pl.ds(pl.multiple_of(step * width, 128), width)])

        @pl.when(step > 2)
        def _():
            masked = masked_rows(first_image(images) + step - 3, sizes_ref, patterns_ref, tall)

            def body(at, first):
                dn = dn_s[pl.ds(pl.multiple_of((step - 3) * tall + first, 8), min(BAND, tall)), :]
                normed, scaling = norm(h0_ref[at, :])
                dh = dh_ref[at, :] + norm_back(dn, normed, scaling, row_of(params_ref, GAIN1))
                out_s[at, :] = jnp.where(masked, 0.0, dh)
                sum_ref[0:1, :] += column_sum(dn * normed)
                sum_ref[1:2, :] += column_sum(dn)
                sum_ref[2:3, :] += column_sum(jnp.where(masked, dh, 0.0))

            banded(tall, body)
            out_ref[0] = out_s[0:length, :]

    def at(i):
        return jnp.maximum(i - 3, 0)

    band = pl.BlockSpec((tall, width), lambda i: (at(i), 0))
    return call(
        kernel, "start_back", (images + 3,),
        [(grads, pl.BlockSpec((1, rows, width), lambda i: (jnp.minimum(i, 2), 0, 0)))]
        + [(start, band), (grad_middle, band), (group_sizes, SCALARS), (patterns, kept(patterns.shape)),
           (params, kept(params.shape))]
        + [(a, ANY) for a in weight.operands],
        [((images, length, width), F32, pl.BlockSpec((1, length, width), lambda i: (at(i), 0, 0))),
         ((8, width), F32, whole((8, width)))],
        [pltpu.VMEM((width, 3 * width + weight.extra), BF16), pltpu.VMEM((rows, width), F32),
         pltpu.VMEM((tall, width), F32), pltpu.SemaphoreType.DMA],
        flops=6 * rows * width * width,
    )


def local(
    links,
    inputs,
    cotangent,
    group_sizes,
    mask_patterns,
    mask_token,
    norm1_gain,
    norm1_bias,
    qkv_weight,
    query_bias,
    value_bias,
    bias_table,
    proj_weight,
    proj_bias,
    gamma_attn,
    norm2_gain,
    norm2_bias,
    fc1_weight,
    fc1_bias,
    fc2_weight,
    fc2_bias,
    gamma_mlp,
):
    images, length, width = inputs.shape
    table_rows, heads = bias_table.shape
    grid_side = math.isqrt(length - 1)
    group_count = mask_patterns.shape[0]
    tall = -(-length // 8) * 8
    rows = images * tall
    hidden = fc1_bias.shape[0]
    chunks = hidden // CHUNK
    sizes = (images, length, tall, width)
    score_scale = (width // heads) ** (-0.5)
    here = links.place()

    vectors = {
        TOKEN: mask_token, GAIN1: norm1_gain, SHIFT1: norm1_bias, GAMMA2: gamma_mlp, BIAS1: proj_bias,
        GAMMA1: gamma_attn, GAIN2: norm2_gain, SHIFT2: norm2_bias, BIAS2: fc2_bias, 9: query_bias, 11: value_bias,
    }

    boxed = links.boxed
    fc2_t = fc2_weight.T
    if boxed:
        mix = Gather(links, qkv_block(here, qkv_weight), 384)
        side = align_side(here, proj_weight)
        near = Gather(
            links,
            jnp.concatenate(
                [side[:, :128], up_block(fc1_weight, 0), down_block(fc2_t, 0), side[:, 128:]], axis=1
            ),
            384,
        )
        far = Gather(
            links,
            jnp.concatenate(
                [up_block(fc1_weight, 1), up_block(fc1_weight, 2), down_block(fc2_t, 1), down_block(fc2_t, 2)],
                axis=1,
            ),
            512,
        )
        full_up = full_down = None
    else:
        mix = near = far = None
        full_up, full_down = native_gather(fc1_weight), native_gather(fc2_weight).T

    entry = table_columns(grid_side, 384)

    def behind(value, *exchanges):
        return after(value, *[v for e in exchanges for v in e.sent]) if boxed else value

    def met(value, *exchanges):
        return [value] + [v for e in exchanges for v in e.flying]

    if boxed:
        mix.first()
    start, first_low, upstream, down_low, sum_fc2, params, patterns = prepare(
        sizes, inputs, cotangent, group_sizes, mask_patterns, vectors
    )
    if boxed:
        gap = met(first_low, mix)
        mix.second(*gap)
        near.first(*gap)
    table_t = jnp.pad(after(bias_table, first_low).T, ((0, 16 - heads), (0, width - table_rows)))
    bias = bias_kernel(behind(table_t, mix), entry, grid_side, tall, 256)
    if boxed:
        mix.third(*met(bias, mix))
        mix.fourth(*met(bias, near))
        near.second(*mix.sent)
    qkv = qkv_operands(links, mix, qkv_weight)
    mixed = project(sizes, behind(first_low, near), qkv, params, score_scale)
    if boxed:
        gap = met(mixed, near)
        near.third(*gap)
        far.first(*gap)
    attended, probs = attend(sizes, behind(mixed, near), bias, 0, width // 128)
    if boxed:
        near.fourth(*met(attended, far))
        far.second(*near.sent)
    proj = proj_operands(links, near, proj_weight)
    middle, second_low = merge(sizes, [attended], behind(start, far), proj, params)
    if boxed:
        far.third(*met(second_low, far))

    fc1_groups = fc1_bias.reshape(8, chunks, 128)
    ups = [up_operands(links, near, 128, full_up, 0), None, None]
    downs = [down_operands(links, near, 0, full_down, 0), None, None]
    halves = [[(0, (0, 256))], [(0, (256, 512))]]
    sums, pairs_out, hidden_sums = None, [], []
    waves = [Scatter(links, here, 256), Scatter(links, here, 256), Scatter(links, here, 512)]
    second_here = behind(second_low, far)
    for k in range(chunks):
        branch, grad_n2, away, stay, hidden_sum = feed(
            sizes, second_here, down_low, ups[k], downs[k], fc1_groups[:, k].reshape(1, -1), sums
        )
        if k == 0:
            if boxed:
                far.fourth(*met(away, far))
                waves[0].first(away, stay)
            ups[1:] = [up_operands(links, far, 0, full_up, 1), up_operands(links, far, 256, full_up, 2)]
            downs[1:] = [down_operands(links, far, 0, full_down, 1), down_operands(links, far, 256, full_down, 2)]
            second_here = second_low
        elif k == 1 and boxed:
            exchange(links, [away], (waves[0], "second", halves))
            waves[1].first(after(away, *waves[0].sent), stay)
            second_here = behind(second_low, waves[0])
        elif boxed:
            exchange(links, [away], (waves[0], "third", None), (waves[1], "second", halves))
            waves[2].first(after(away, *waves[1].sent), stay)
        sums = (branch, grad_n2)
        pairs_out.append((away, stay))
        hidden_sums.append(hidden_sum)

    layer_out, grad_middle, grad_att, proj_away, proj_stay, middle_sums = middle_back(
        sizes, [attended], behind(branch, waves[0], waves[1]), grad_n2, middle, start, upstream, proj, params
    )
    if boxed:
        exchange(links, [grad_att], (waves[0], "fourth", None), (waves[1], "third", None))
        waves[2].first(after(proj_away, *waves[1].sent), proj_stay)

    back, grads = [], None
    for number, (first, pairs) in enumerate(((0, 3), (3, 3))):
        grad_here = behind(grad_att, *(waves[:2] if number == 0 else waves[1:]))
        grads, *rest = attend_back(sizes, mixed, probs, grad_here, score_scale, first, pairs, grads)
        back.append(rest)
        if boxed and number == 0:
            gap = met(grads, waves[0])
            exchange(
                links, gap, (waves[1], "fourth", None),
                (waves[2], "second", [[(1, (0, 256)), (0, (0, 256))], [(0, (256, 512))]]),
            )
    if boxed:
        gap_grads = met(grads, waves[1])
        exchange(links, gap_grads, (waves[2], "third", None))
    mix_away, mix_stay = mixed_grad(sizes, behind(first_low, waves[2]), grads)
    last = Scatter(links, here, 384)
    terms = jnp.concatenate([b[0] for b in back], axis=0)
    if boxed:
        exchange(links, [mix_away], (waves[2], "fourth", None))
        last.first(after(mix_away, *waves[2].sent), mix_stay)
    grad_table = bias_back_kernel(after(behind(terms, waves[2]), mix_away), entry, grid_side, width)
    if boxed:
        gap_table = met(grad_table, waves[2])
        exchange(links, gap_table, (last, "second", [[(0, (0, 384))], [(0, (384, 640))]]))
    input_grad, start_sums = start_back(
        sizes, grads, qkv, start, behind(grad_middle, last), group_sizes, patterns, params
    )
    small_away, small_stay = pack(
        links, grad_table, heads, start_sums, middle_sums, [b[1:] for b in back], sum_fc2, hidden_sums
    )
    if boxed:
        exchange(links, [start_sums], (last, "third", None))
        small_away = after(small_away, *last.sent)
    small = sum_everywhere(links, here, small_away, small_stay, last.flying)
    if boxed:
        exchange(links, [], (last, "fourth", None))
        grad_qkv = qkv_home(here, last.done())
        blocks = [waves[0].done(*gap), waves[1].done(*gap_grads), waves[2].done(*gap_table)]
        grad_proj = proj_home(here, blocks[2][:, 0:256])
        up_parts = [blocks[0][:, 0:256], blocks[1][:, 0:256], blocks[2][:, 256:512]]
        down_parts = [blocks[0][:, 256:512], blocks[1][:, 256:512], blocks[2][:, 512:768]]
        grad_fc1 = jnp.concatenate(
            [up_parts[k][:, 128 * half : 128 * half + 128] for half in range(2) for k in range(chunks)], axis=1
        )
        grad_fc2 = jnp.concatenate(
            [jnp.concatenate([p[:, :128], p[:, 128:]], axis=0) for p in down_parts], axis=1
        ).T
    else:
        tiles = [all_tiles(here, *pair) for pair in pairs_out]
        grad_qkv = native_scatter(natural_qkv(all_tiles(here, mix_away, mix_stay)))
        grad_proj = native_scatter(natural_proj(all_tiles(here, proj_away, proj_stay)))
        grad_fc1 = native_scatter(natural_up([t[..., :256] for t in tiles]))
        grad_fc2 = native_scatter(natural_down([t[..., 256:] for t in tiles]))
    at = heads
    hidden_rows = [
        jnp.concatenate([small[at + 11 + k], small[at + 14, 256 * k : 256 * k + 256]]).reshape(8, 128) for k in range(chunks)
    ]
    sum_fc1 = jnp.stack(hidden_rows, axis=1).reshape(-1)
    return (
        layer_out,
        input_grad,
        small[at + 2],
        small[at],
        small[at + 1],
        grad_qkv,
        small[at + 8],
        small[at + 9],
        small[:heads, :table_rows].T,
        grad_proj,
        small[at + 7],
        small[at + 6],
        small[at + 4],
        small[at + 5],
        grad_fc1,
        sum_fc1,
        grad_fc2,
        small[at + 10],
        small[at + 3],
    )


def solution(mesh):
    images = P(AXES, None, None)
    both = P("wide", "narrow")
    same = P()
    links = Links(mesh.shape["wide"], mesh.shape["narrow"])
    return jax.shard_map(
        functools.partial(local, links),
        mesh=mesh,
        in_specs=(
            images, images, same, same, same, same, same, both, same, same, same, both, same, same,
            same, same, both, same, both, same, same,
        ),
        out_specs=(
            images, images, same, same, same, both, same, same, same, both, same, same, same, same,
            both, same, both, same, same,
        ),
        check_vma=False,
    )
```

```python
import functools
import math

import jax
import jax.numpy as jnp
import numpy as np
from jax import lax
from jax.experimental import pallas as pl
from jax.experimental.pallas import tpu as pltpu
from jax.sharding import PartitionSpec as P

EPSILON = 1e-06
ROOT_HALF = 0.7071067811865476
DENSITY = 0.3989422804014327
BF16 = jnp.bfloat16
F32 = jnp.float32
AXES = ("wide", "narrow")
TILE = 512
BAND = 200
CHUNK = 1024
NEVER = -1e30
MIB = 1 << 20


class Links:
    def __init__(self, wide, narrow):
        self.wide, self.narrow = wide, narrow
        self.y = 1 << ((wide.bit_length() - 1) // 2)
        self.z = wide // self.y
        self.x = narrow // 2
        self.size = {"z": self.z, "y": self.y, "x": self.x, "core": 2}
        self.unit = {"core": 1, "x": 2, "y": narrow, "z": narrow * self.y}
        self.boxed = (self.z, self.y, self.x) == (4, 2, 2)

    def place(self):
        w, n = lax.axis_index("wide"), lax.axis_index("narrow")
        return {"z": w // self.y, "y": w % self.y, "x": n // 2, "core": n % 2, "w": w, "n": n}

    def swap(self, value, **offsets):
        mask = sum(self.unit[axis] * offset for axis, offset in offsets.items())
        count = self.wide * self.narrow
        return lax.ppermute(value, AXES, [(k, k ^ mask) for k in range(count)])

    def others(self, value, axis):
        return [self.swap(value, **{axis: d}) for d in range(1, self.size[axis])]


def pick(value, axis, index, count):
    size = value.shape[axis] // count
    return lax.dynamic_slice_in_dim(value, index * size, size, axis)


def after(value, *others):
    return lax.optimization_barrier((value,) + others)[0]


def tied(values, wait):
    if not wait:
        return list(values)
    return list(lax.optimization_barrier(tuple(values) + tuple(wait)))[: len(values)]


def native_gather(shard):
    return lax.all_gather(
        lax.all_gather(shard, "narrow", axis=1, tiled=True), "wide", axis=0, tiled=True
    )


class Gather:
    orders = (("x", "y"), ("y", "x"))

    def __init__(self, links, block, split, groups):
        self.links, self.block, self.split, self.groups = links, block, split, groups

    def first(self, *wait):
        block = after(self.block, *wait) if wait else self.block
        self.sent = [block]
        self.steps = [block] + self.links.others(block, "z")
        self.flying = self.steps[1:]

    def second(self, *wait):
        parts = arrange([after(self.steps[0], *wait) if wait else self.steps[0]] + self.steps[1:], self.split)
        self.steps, self.sent = [], []
        for held, order in zip(parts, self.orders, strict=True):
            self.sent.append(held)
            self.steps.append([held] + self.links.others(held, order[0]))
        self.flying = [v for p in self.steps for v in p[1:]]

    def third(self, *wait):
        parts = stack([[after(self.steps[0][0], *wait)] + self.steps[0][1:], self.steps[1]])
        self.steps, self.sent = [], []
        for held, order in zip(parts, self.orders, strict=True):
            self.sent.append(held)
            self.steps.append([held] + self.links.others(held, order[1]))
        self.flying = [v for p in self.steps for v in p[1:]]

    def fourth(self, far, *wait):
        first = after(self.steps[0][0], *wait)
        self.operands = []
        held = regroup([[first] + self.steps[0][1:], self.steps[1]], self.groups, far)
        for number, array in enumerate(held):
            self.operands.append([array, self.links.swap(array, core=1)])
        self.sent = held
        self.flying = [pair[1] for pair in self.operands]

    def blocks(self, refs, number, me):
        links = self.links
        order = self.orders[number]
        out = []
        for core in range(2):
            for k in range(refs[core].shape[0]):
                at, rest = {}, k
                for axis in ("z",) + order:
                    at[axis] = me[axis] ^ (rest % links.size[axis])
                    rest //= links.size[axis]
                source = functools.partial(block_columns, refs[core], k)
                out.append((source, at["z"] * links.y + at["y"], at["x"] * 2 + (me["core"] ^ core)))
        return out


def block_columns(ref, k, col, broad):
    return ref.at[k, :, pl.ds(col, broad)]


def at_least(n, values):
    out = values[3]
    for k in (2, 1, 0):
        out = jnp.where(n == k, values[k], out)
    return out


def window(ref, row, col, tall, broad):
    if not isinstance(row, int):
        row = pl.multiple_of(row, 8)
    if not isinstance(col, int):
        col = pl.multiple_of(col, 128)
    return ref.at[pl.ds(row, tall), pl.ds(col, broad)]


def columns(ref, col, broad):
    return ref.at[:, pl.ds(col, broad)]


class Weight:
    def __init__(self, operands, copies, joints=(), extra=0):
        self.operands, self.copies, self.joints, self.extra = operands, copies, joints, extra

    def fill(self, refs, target, sem):
        for source, to in self.copies(refs, target):
            pltpu.make_async_copy(source, to, sem).start()

    def wait(self, target, sem):
        pltpu.make_async_copy(target, target, sem).wait()
        for here, there in self.joints:
            target[:, here : here + 128] += target[:, there : there + 128]


def align_side(here, side):
    zero = jnp.zeros((side.shape[0], 64), side.dtype)
    return jnp.where(
        here["n"] % 2 == 0,
        jnp.concatenate([side, zero], axis=1),
        jnp.concatenate([zero, side], axis=1),
    )


def qkv_block(here, shard):
    even = here["n"] % 2 == 0
    main = jnp.where(even, shard[:, :384], shard[:, 192:])
    return jnp.concatenate([main, align_side(here, jnp.where(even, shard[:, 384:], shard[:, :192]))], axis=1)


def qkv_operands(links, gathered, shard):
    if not links.boxed:
        return Weight([native_gather(shard)], lambda refs, target: [(refs[0], target.at[:, pl.ds(0, 2304)])] + [
            (refs[0].at[:, pl.ds(0, 256)], target.at[:, pl.ds(2304, 256)])], extra=256)

    def copies(refs, target):
        me = links.place()
        out = []
        for source, w, n in gathered.blocks(refs, 0, me):
            out.append((source(0, 384), window(target, w * 96, at_least(n, (0, 768, 1152, 1920)), 96, 384)))
        for source, w, n in gathered.blocks(refs, 1, me):
            for part, places in enumerate(((384, 2304, 1536, 2432), (512, 640, 1664, 1792))):
                out.append((source(384 + 128 * part, 128), window(target, w * 96, at_least(n, places), 96, 128)))
        return out

    return Weight(gathered.operands[0], copies, ((512, 2304), (1664, 2432)), 256)


def proj_operands(links, gathered, shard):
    if not links.boxed:
        return Weight([native_gather(shard)], lambda refs, target: [(refs[0], target.at[:, pl.ds(0, 768)])] + [
            (refs[0].at[:, pl.ds(0, 256)], target.at[:, pl.ds(768, 256)])], extra=256)

    def copies(refs, target):
        me = links.place()
        out = []
        for part, (col, places) in enumerate(((0, (0, 768, 384, 896)), (128, (128, 256, 512, 640)))):
            for source, w, n in gathered.blocks(refs, part, me):
                out.append((source(col, 128), window(target, w * 96, at_least(n, places), 96, 128)))
        return out

    return Weight(gathered.operands[0], copies, ((128, 768), (512, 896)), 256)


def up_block(shard, chunk):
    return jnp.concatenate(
        [shard[:, 384 * half + 128 * chunk : 384 * half + 128 * chunk + 128] for half in range(2)], axis=1
    )


def down_block(shard_t, chunk):
    piece = shard_t[:, 128 * chunk : 128 * chunk + 128]
    half = piece.shape[0] // 2
    return jnp.concatenate([piece[:half], piece[half:]], axis=1)


def chunk_copies(full, chunk):
    def slices(refs, target):
        return [
            (columns(refs[0], 384 * g + 128 * chunk, 128), columns(target, 128 * g, 128)) for g in range(8)
        ]

    return Weight([full], slices)


def up_operands(links, gathered, group, full, chunk):
    if not links.boxed:
        return chunk_copies(full, chunk)

    def copies(refs, target):
        me = links.place()
        return [
            (source(0, 256), window(target, w * 96, n * 256, 96, 256))
            for source, w, n in gathered.blocks(refs, 0, me)
        ]

    return Weight(gathered.operands[group], copies)


def down_operands(links, gathered, group, full, chunk):
    if not links.boxed:
        return chunk_copies(full, chunk)

    def copies(refs, target):
        me = links.place()
        return [
            (source(256 + 128 * half, 128), window(target, n * 192 + half * 96, w * 128, 96, 128))
            for source, w, n in gathered.blocks(refs, 1, me)
            for half in range(2)
        ]

    return Weight(gathered.operands[group], copies)


class Scatter:
    orders = (("x", "y"), ("y", "x"))

    def __init__(self, links, here, split):
        self.links, self.here, self.split = links, here, split
        self.pairs, self.flying, self.stage = [], [], 0

    def first(self, away, stay):
        shape = (self.links.x, self.links.z, self.links.y) + away.shape[2:]
        self.pairs.append((stay.reshape(shape), self.links.swap(away.reshape(shape), core=1)))
        self.flying.append(self.pairs[-1][1])

    def jobs(self, step, picks):
        if step == "second":
            return [
                ([(self.pairs[k], cols) for k, cols in part], order[0])
                for part, order in zip(picks, self.orders, strict=True)
            ]
        whole_of = [(t, (0, t[0].shape[-1])) for t in self.terms]
        if step == "third":
            return [([t], order[1]) for t, order in zip(whole_of, self.orders, strict=True)]
        return [(whole_of, "z")]

    def take(self, results):
        self.sent = [v for r in results for v in r[1:]]
        self.terms = []
        axes = [order[self.stage] for order in self.orders] if self.stage < 2 else ["z"]
        for (keep, *sent), axis in zip(results, axes, strict=True):
            self.terms.append([keep] + [self.links.swap(v, **{axis: d}) for d, v in enumerate(sent, 1)])
        self.stage += 1
        self.flying = [v for t in self.terms for v in t[1:]]

    def done(self, *wait):
        terms = tied(self.terms[0], wait)
        total = terms[0]
        for term in terms[1:]:
            total = total + term.astype(F32)
        return total.reshape(total.shape[-2:])


def exchange(links, wait, *items):
    jobs = [job for scatter, step, picks in items for job in scatter.jobs(step, picks)]
    group, cols = jobs[0][0][0]
    jobs[0][0][0] = ((after(group[0], *wait),) + tuple(group[1:]), cols)
    results = fold(links, jobs)
    for scatter, step, _ in items:
        count = 1 if step == "fourth" else 2
        scatter.take(results[:count])
        results = results[count:]


def all_tiles(here, away, stay):
    return jnp.where(
        here["core"] == 0, jnp.stack([stay, away], axis=1), jnp.stack([away, stay], axis=1)
    ).reshape((4,) + away.shape[1:])


def native_scatter(partial):
    low = lax.psum_scatter(partial.astype(BF16), "wide", scatter_dimension=0, tiled=True)
    return lax.psum_scatter(low, "narrow", scatter_dimension=1, tiled=True).astype(F32)


def qkv_home(here, block):
    even = here["n"] % 2 == 0
    main, side = block[:, :384], block[:, 384:]
    return jnp.where(
        even,
        jnp.concatenate([main, side[:, :192]], axis=1),
        jnp.concatenate([side[:, 64:], main], axis=1),
    )


def proj_home(here, block):
    return jnp.where(here["n"] % 2 == 0, block[:, :192], block[:, 64:])


def natural_qkv(tiles):
    tiles = tiles.reshape(4, 768, 640)
    out = []
    for n in range(4):
        main, side = tiles[n, :, :384], tiles[n, :, 384:]
        out += [main, side[:, :192]] if n % 2 == 0 else [side[:, 64:], main]
    return jnp.concatenate(out, axis=1)


def natural_proj(tiles):
    tiles = tiles.reshape(4, 768, 256)
    return jnp.concatenate([tiles[n, :, :192] if n % 2 == 0 else tiles[n, :, 64:] for n in range(4)], axis=1)


def natural_up(chunks):
    tiles = [t.reshape(4, 768, 2, 128) for t in chunks]
    return jnp.stack(tiles, axis=0).transpose(2, 1, 3, 0, 4).reshape(768, -1)


def natural_down(chunks):
    tiles = [t.reshape(4, 8, 96, 2, 128) for t in chunks]
    return jnp.stack(tiles, axis=0).transpose(2, 0, 5, 1, 4, 3).reshape(-1, 768)


def tree_sum(terms):
    while len(terms) > 1:
        terms = [terms[k] + terms[k + 1] for k in range(0, len(terms), 2)]
    return terms[0]


def sum_everywhere(links, here, away, stay, wait):
    if links.boxed:
        half = after(stay + links.swap(away, core=1), *wait)
        for axis in ("x", "y", "z"):
            step = 1
            while step < links.size[axis]:
                half = half + links.swap(half, **{axis: step})
                step *= 2
        other = links.swap(half, core=1)
    else:
        first = jnp.where(here["core"] == 0, stay, away)
        second = jnp.where(here["core"] == 0, away, stay)
        return lax.psum(jnp.concatenate([first, second], axis=0), AXES)
    return jnp.where(
        here["core"] == 0, jnp.concatenate([half, other], axis=0), jnp.concatenate([other, half], axis=0)
    )


def whole(shape):
    return pl.BlockSpec(tuple(shape), lambda *_: (0,) * len(shape))


def kept(shape):
    return pl.BlockSpec(tuple(shape), lambda *_: (0,) * len(shape), pipeline_mode=pl.Buffered(1))


ANY = pl.BlockSpec(memory_space=pl.ANY)
FAR = pl.BlockSpec(memory_space=pltpu.HBM)
SCALARS = pl.BlockSpec(memory_space=pltpu.SMEM)


LIMITS = {"stack": 16, "arrange": 8, "fold": 24, "pack": 8, "prepare": 16, "bias": 16, "bias_back": 20, "project": 24, "attend": 18, "merge": 20, "feed": 36, "middle_back": 28, "attend_back": 22, "mixed_grad": 24, "start_back": 28}


def call(kernel, name, grid, ins, outs, scratch=(), flops=0, aliases=None):
    moved = sum(a.size * a.dtype.itemsize for a, *_ in ins)
    moved += sum(math.prod(s) * jnp.dtype(d).itemsize for s, d, *_ in outs)
    return pl.pallas_call(
        kernel,
        name=name,
        grid=grid,
        in_specs=[spec for _, spec, *_ in ins],
        out_specs=[spec for _, _, spec, *_ in outs],
        out_shape=[pltpu.HBM(s, d) if far else jax.ShapeDtypeStruct(s, d) for s, d, _, *far in outs],
        scratch_shapes=list(scratch),
        input_output_aliases=aliases or {},
        compiler_params=pltpu.CompilerParams(vmem_limit_bytes=LIMITS[name] * MIB),
        cost_estimate=pl.CostEstimate(flops=int(flops), bytes_accessed=int(moved), transcendentals=0),
    )(*[pltpu.with_memory_space_constraint(a, pltpu.HBM) if far else a for a, _, *far in ins])


def nn(a, b):
    return lax.dot_general(a, b, (((1,), (0,)), ((), ())), preferred_element_type=F32)


def nt(a, b):
    return lax.dot_general(a, b, (((1,), (1,)), ((), ())), preferred_element_type=F32)


def tn(a, b):
    return lax.dot_general(a, b, (((0,), (0,)), ((), ())), preferred_element_type=F32)


def arrange(blocks, split):
    rows, cols = blocks[0].shape
    count = len(blocks)

    def kernel(*refs):
        for k in range(count):
            refs[count][k] = refs[k][:, :split]
            refs[count + 1][k] = refs[k][:, split:]

    return call(
        kernel, "arrange", (),
        [(b, whole(b.shape)) for b in blocks],
        [((count, rows, part), BF16, whole((count, rows, part))) for part in (split, cols - split)],
    )


def stack(parts):
    flat = [v for part in parts for v in part]
    outs = [(sum(v.shape[0] for v in part), part[0].shape[1], part[0].shape[2]) for part in parts]

    def kernel(*refs):
        number = 0
        for k, part in enumerate(parts):
            at = 0
            for v in part:
                refs[len(flat) + k][at : at + v.shape[0]] = refs[number][...]
                at += v.shape[0]
                number += 1

    return call(
        kernel, "stack", (), [(v, whole(v.shape)) for v in flat], [(shape, BF16, whole(shape)) for shape in outs]
    )


def regroup(parts, groups, far):
    flat = [v for part in parts for v in part]
    count, rows = sum(v.shape[0] for v in parts[0]), parts[0][0].shape[1]
    outs = [(count, rows, sum(end - begin for begin, end in group)) for group in groups]

    def kernel(*refs):
        for out, group in zip(refs[len(flat) :], groups, strict=True):
            number, col = 0, 0
            for part, (begin, end) in zip(parts, group, strict=True):
                at = 0
                for v in part:
                    if end > begin:
                        out[at : at + v.shape[0], :, col : col + end - begin] = refs[number][:, :, begin:end]
                    at += v.shape[0]
                    number += 1
                col += end - begin

    return call(
        kernel, "stack", (), [(v, whole(v.shape)) for v in flat],
        [(shape, BF16, whole(shape), FAR) if far else (shape, BF16, whole(shape)) for shape in outs],
    )


def fold(links, jobs):
    arrays, index = [], {}
    for sources, _ in jobs:
        for group, _ in sources:
            for array in group:
                if id(array) not in index:
                    index[id(array)] = len(arrays)
                    arrays.append(array)
    dims = {"x": 0, "z": 1, "y": 2}
    outs = []
    for sources, axis in jobs:
        first = sources[0][0][0]
        cols = sum(part[1] - part[0] for _, part in sources)
        shape = tuple(1 if k == dims[axis] else first.shape[k] for k in range(4)) + (cols,)
        outs += [(shape, F32 if d == 0 else BF16, whole(shape)) for d in range(links.size[axis])]

    def kernel(*refs):
        me = links.place()
        at_out = len(arrays)
        for sources, axis in jobs:
            for d in range(links.size[axis]):
                where = [slice(None)] * 4
                where[dims[axis]] = pl.ds(me[axis] ^ d, 1)
                col = 0
                for group, (begin, end) in sources:
                    picked = tuple(where) + (slice(begin, end),)
                    total = refs[index[id(group[0])]][picked].astype(F32)
                    for array in group[1:]:
                        total = total + refs[index[id(array)]][picked].astype(F32)
                    out = refs[at_out]
                    out[..., col : col + end - begin] = total.astype(out.dtype)
                    col += end - begin
                at_out += 1

    results = call(kernel, "fold", (), [(a, whole(a.shape)) for a in arrays], outs)
    out = []
    for _, axis in jobs:
        out.append(results[: links.size[axis]])
        results = results[links.size[axis] :]
    return out


def pack(links, table, heads, start_sums, middle_sums, halves, sum_fc2, hidden_sums):
    width = table.shape[1]

    def kernel(table_ref, start_ref, middle_ref, q0, v0, q1, v1, fc2_ref, a_ref, b_ref, c_ref, away_ref, stay_ref, all_s):
        all_s[...] = jnp.zeros_like(all_s)
        rows = [(table_ref, heads), (start_ref, 3), (middle_ref, 5)]
        at = 0
        for ref, count in rows:
            for k in range(count):
                all_s[(at + k) // 16, (at + k) % 16 : (at + k) % 16 + 1, :] = ref[k : k + 1, :]
            at += count
        for pair in ((q0, q1), (v0, v1)):
            for k, ref in enumerate(pair):
                all_s[at // 16, at % 16 : at % 16 + 1, k * 384 : k * 384 + 384] = ref[...]
            at += 1
        all_s[at // 16, at % 16 : at % 16 + 1, :] = fc2_ref[...]
        at += 1
        for k, ref in enumerate((a_ref, b_ref, c_ref)):
            all_s[(at + k) // 16, (at + k) % 16 : (at + k) % 16 + 1, :] = ref[:, 0:width]
            all_s[(at + 3) // 16, (at + 3) % 16 : (at + 3) % 16 + 1, k * 256 : k * 256 + 256] = ref[:, width : width + 256]
        c = lax.axis_index("narrow") % 2
        away_ref[...] = all_s[1 - c]
        stay_ref[...] = all_s[c]

    operands = [table, start_sums, middle_sums, *halves[0], *halves[1], sum_fc2, *hidden_sums]
    return call(
        kernel, "pack", (), [(a, whole(a.shape)) for a in operands],
        [((16, width), F32, whole((16, width)))] * 2, [pltpu.VMEM((2, 16, width), F32)],
    )


def norm(values):
    centre = jnp.mean(values, axis=-1, keepdims=True)
    centred = values - centre
    spread = jnp.mean(centred * centred, axis=-1, keepdims=True)
    scaling = lax.rsqrt(spread + EPSILON)
    return centred * scaling, scaling


def norm_back(grad, normed, scaling, gain):
    scaled = grad * gain
    first = jnp.mean(scaled, axis=-1, keepdims=True)
    second = jnp.mean(scaled * normed, axis=-1, keepdims=True)
    return (scaled - first - normed * second) * scaling


def banded(tall, body):
    if BAND >= tall:
        body(slice(0, tall), 0)
        return

    def step(k, carry):
        at = pl.multiple_of(k * BAND, 8)
        body(pl.ds(at, BAND), at)
        return carry

    lax.fori_loop(0, tall // BAND, step, 0)


def column_sum(values):
    return jnp.sum(values, axis=0, keepdims=True)


TOKEN, GAIN1, SHIFT1, GAMMA2, BIAS1, GAMMA1, GAIN2, SHIFT2, BIAS2 = range(9)


def row_of(ref, k):
    return ref[k : k + 1, :]


def masked_rows(image, sizes_ref, patterns_ref, tall):
    bound, group = 0, 0
    for k in range(sizes_ref.shape[0] - 1):
        bound = bound + sizes_ref[k]
        group = group + (image >= bound).astype(jnp.int32)
    columns_of = patterns_ref[...].T
    which = lax.broadcasted_iota(jnp.int32, columns_of.shape, 1) == group
    return jnp.sum(jnp.where(which, columns_of, 0.0), axis=1, keepdims=True)[0:tall] > 0.5


def first_image(images):
    return lax.axis_index(AXES) * images


def prepare(sizes, inputs, cotangent, group_sizes, mask_patterns, vectors):
    images, length, tall, width = sizes
    rows = images * tall
    groups, patches = mask_patterns.shape

    def kernel(x_ref, g_ref, sizes_ref, mask_ref, *refs):
        vector_refs, refs = refs[: len(vectors)], refs[len(vectors) :]
        h0_ref, n1_ref, g_out, df_ref, sum_ref, params_ref, patterns_ref, x_s, g_s, mask_s, sems, *vector_s = refs
        step = pl.program_id(0)

        @pl.when(step == 0)
        def _():
            x_s[...] = jnp.zeros_like(x_s)
            g_s[...] = jnp.zeros_like(g_s)
            sum_ref[...] = jnp.zeros_like(sum_ref)
            params_ref[...] = jnp.zeros_like(params_ref)
            patterns_ref[...] = jnp.zeros_like(patterns_ref)
            moves = [pltpu.make_async_copy(mask_ref, mask_s, sems.at[len(vectors)])]
            moves += [
                pltpu.make_async_copy(a, b, sems.at[k]) for k, (a, b) in enumerate(zip(vector_refs, vector_s, strict=True))
            ]
            for move in moves:
                move.start()
            for move in moves:
                move.wait()
            patterns_ref[0:groups, 1 : patches + 1] = mask_s[...].astype(F32)
            for k, ref in zip(vectors, vector_s, strict=True):
                params_ref[k : k + 1, :] = ref[...].reshape(1, width)

        x_s[0:length, :] = x_ref[0].astype(F32)
        g_s[0:length, :] = g_ref[0].astype(F32)
        masked = masked_rows(first_image(images) + step, sizes_ref, patterns_ref, tall)
        start = jnp.where(masked, row_of(params_ref, TOKEN), x_s[...])
        h0_ref[...] = start
        normed, _ = norm(start)
        n1_ref[...] = (normed * row_of(params_ref, GAIN1) + row_of(params_ref, SHIFT1)).astype(BF16)
        g = g_s[...]
        g_out[...] = g.astype(BF16)
        df = row_of(params_ref, GAMMA2) * g
        df_ref[...] = df.astype(BF16)
        sum_ref[...] += column_sum(df)

    image = pl.BlockSpec((1, length, width), lambda i: (i, 0, 0))
    band = pl.BlockSpec((tall, width), lambda i: (i, 0))
    return call(
        kernel, "prepare", (images,),
        [(inputs, image), (cotangent, image), (group_sizes, SCALARS), (mask_patterns, ANY, FAR)]
        + [(v, ANY, FAR) for v in vectors.values()],
        [((rows, width), F32, band, FAR), ((rows, width), BF16, band), ((rows, width), BF16, band, FAR),
         ((rows, width), BF16, band, FAR), ((1, width), F32, whole((1, width))), ((16, width), F32, whole((16, width))),
         ((8, 256), F32, whole((8, 256)))],
        [pltpu.VMEM((tall, width), F32), pltpu.VMEM((tall, width), F32), pltpu.VMEM(mask_patterns.shape, jnp.int32),
         pltpu.SemaphoreType.DMA((len(vectors) + 1,))] + [pltpu.VMEM((width,), F32) for _ in vectors],
        flops=rows * width * 40,
    )


def table_columns(grid_side, broad):
    side = 2 * grid_side - 1
    q = np.arange(broad)
    entry = (q // grid_side) * side + q % grid_side + grid_side - 1
    return jnp.asarray(np.where(q < side * grid_side, entry, -(1 << 20)).astype(np.int32)[None])


def three_parts(values):
    high = values.astype(BF16)
    rest = values - high.astype(F32)
    middle = rest.astype(BF16)
    return high, middle, (rest - middle.astype(F32)).astype(BF16)


def bias_kernel(table_t, entry, grid_side, tall, broad):
    heads = table_t.shape[0]
    length = grid_side * grid_side + 1
    wide = entry.shape[1]
    inner = (2 * grid_side - 1) ** 2

    def kernel(table_ref, entry_ref, out_ref, *halves):
        def put(at, count, values):
            for half, ref in enumerate(halves):
                ref[pl.ds(at, count), :] = values[:, 128 * half : 128 * half + 128]

        parts = jnp.concatenate(three_parts(table_ref[...]), axis=0)
        left, top, corner = (table_ref[:, inner + 1 : inner + 2], table_ref[:, inner : inner + 1],
                             table_ref[:, inner + 2 : inner + 3])
        lane = lax.broadcasted_iota(jnp.int32, (heads, broad), 1)

        def column(b, carry):
            which = lax.broadcasted_iota(jnp.int32, (table_ref.shape[1], wide), 0) + b
            select = jnp.where(which == entry_ref[...], 1.0, 0.0).astype(BF16)
            spread = nn(parts, select)
            spread = spread[:heads] + spread[heads : 2 * heads] + spread[2 * heads :]
            for a in range(grid_side):
                shift = (grid_side - 1 - a) * grid_side - 1
                moved = pltpu.roll(spread, (wide - shift) % wide, 1)[:, :broad]
                moved = jnp.where(lane == 0, top, moved)
                put(pl.multiple_of((1 + grid_side * a + b) * heads, 16), heads, moved)
            return carry

        lax.fori_loop(0, grid_side, column, 0)
        put(0, heads, jnp.where(lane == 0, corner, left))
        rest = (tall - length) * heads
        put(length * heads, rest, jnp.full((rest, broad), NEVER, F32))
        for h in range(out_ref.shape[0]):
            for half, ref in enumerate(halves):
                out_ref[h, :, 128 * half : 128 * half + 128] = ref[pl.ds(h, tall, stride=heads), :]

    return call(
        kernel, "bias", (),
        [(table_t, whole(table_t.shape)), (entry, whole(entry.shape))],
        [((12, tall, broad), F32, whole((12, tall, broad)))],
        [pltpu.VMEM((tall * heads, 128), F32)] * (broad // 128),
        flops=2 * 48 * 768 * wide * grid_side,
    )[0]


def bias_back_kernel(terms, entry, grid_side, width):
    count, tall, broad = terms.shape
    heads = 16
    wide = entry.shape[1]
    inner = (2 * grid_side - 1) ** 2
    length = grid_side * grid_side + 1

    def kernel(terms_ref, entry_ref, out_ref, *halves):
        def get(at, count):
            return jnp.concatenate([ref[pl.ds(at, count), :] for ref in halves], axis=1)

        lane = lax.broadcasted_iota(jnp.int32, (heads, broad), 1)
        inside = (lane >= 1) & (lane < length)
        for h in range(heads):
            values = terms_ref[h] if h < count else jnp.zeros((tall, broad), F32)
            for half, ref in enumerate(halves):
                ref[pl.ds(h, tall, stride=heads), :] = values[:, 128 * half : 128 * half + 128]

        def column(b, carry):
            total, edge = carry
            which = lax.broadcasted_iota(jnp.int32, (width, wide), 0) + b
            select = jnp.where(which == entry_ref[...], 1.0, 0.0).astype(BF16)
            spread = jnp.zeros((heads, wide), F32)
            for a in range(grid_side):
                shift = (grid_side - 1 - a) * grid_side - 1
                found = get(pl.multiple_of((1 + grid_side * a + b) * heads, 16), heads)
                edge = edge + jnp.where(lane == 0, found, 0.0)
                found = jnp.where(inside, found, 0.0)
                found = jnp.concatenate([found, jnp.zeros((heads, wide - broad), F32)], axis=1)
                spread = spread + pltpu.roll(found, shift % wide, 1)
            found = nt(jnp.concatenate(three_parts(spread), axis=0), select)
            total = total + found[:heads] + found[heads : 2 * heads] + found[2 * heads :]
            return total, edge

        total, edge = lax.fori_loop(
            0, grid_side, column, (jnp.zeros((heads, width), F32), jnp.zeros((heads, broad), F32))
        )
        first = get(0, heads)
        top = jnp.sum(edge, axis=1, keepdims=True)
        left = jnp.sum(jnp.where(inside, first, 0.0), axis=1, keepdims=True)
        corner = first[:, 0:1]
        place = lax.broadcasted_iota(jnp.int32, (heads, width), 1)
        total = jnp.where(place == inner, top, total)
        total = jnp.where(place == inner + 1, left, total)
        out_ref[...] = jnp.where(place == inner + 2, corner, total)

    return call(
        kernel, "bias_back", (),
        [(terms, whole(terms.shape)), (entry, whole(entry.shape))],
        [((heads, width), F32, whole((heads, width)))],
        [pltpu.VMEM((tall * heads, 128), F32)] * (broad // 128),
        flops=2 * 48 * 768 * wide * grid_side,
    )[0]


def project(sizes, first_low, weight, params, score_scale):
    images, length, tall, width = sizes
    rows = images * tall
    cols = 3 * width
    count = len(weight.operands)

    def kernel(*refs):
        n1_ref, params_ref = refs[:2]
        out_ref, w_s, sem = refs[2 + count :]
        step = pl.program_id(0)

        @pl.when(step == 0)
        def _():
            weight.fill(refs[2 : 2 + count], w_s, sem)
            weight.wait(w_s, sem)

        w = w_s[:, pl.ds(pl.multiple_of(step * width, 128), width)]
        scale = jnp.where(step == 0, score_scale, 1.0)
        out_ref[...] = ((nn(n1_ref[...], w) + params_ref[pl.ds(9 + step, 1), :]) * scale).astype(BF16)

    return call(
        kernel, "project", (cols // width,),
        [(first_low, kept((rows, width))), (params, kept(params.shape))] + [(a, ANY) for a in weight.operands],
        [((rows, cols), BF16, pl.BlockSpec((rows, width), lambda t: (0, t)))],
        [pltpu.VMEM((width, cols + weight.extra), BF16), pltpu.SemaphoreType.DMA],
        flops=2 * rows * width * cols,
    )[0]


def head_masks(tall):
    lane = lax.broadcasted_iota(jnp.int32, (tall, 128), 1)
    return [lane < 64, lane >= 64]


def attend(sizes, mixed, bias, first, pairs):
    images, length, tall, width = sizes
    rows = images * tall
    every = width // 128
    broad = bias.shape[2]

    def kernel(q_ref, k_ref, v_ref, bias_ref, out_ref, p_ref):
        masks = head_masks(tall)
        units = [(i, h) for i in range(images) for h in range(2)]
        scores, probs = [], []
        for i, h in units:
            q, k = q_ref[tall * i : tall * i + tall, :], k_ref[tall * i : tall * i + tall, :]
            scores.append(nt(k, jnp.where(masks[h], q, jnp.zeros_like(q))) + bias_ref[h, :, 0:tall])
        for (i, h), s in zip(units, scores, strict=True):
            e = jnp.exp(s - jnp.max(s, axis=0, keepdims=True))
            p = (e * (1.0 / jnp.sum(e, axis=0, keepdims=True))).astype(BF16)
            p_ref[h, i, :, 0:tall] = p
            probs.append(p)
        for i in range(images):
            vt = v_ref[tall * i : tall * i + tall, :].T
            out = [nn(vt[64 * h : 64 * h + 64, :], probs[2 * i + h]) for h in range(2)]
            out_ref[tall * i : tall * i + tall, :] = jnp.concatenate(out, axis=0).T.astype(BF16)

    def column(at):
        return pl.BlockSpec((rows, 128), lambda t: (0, at + t))

    return call(
        kernel, "attend", (pairs,),
        [(mixed, column(first)), (mixed, column(every + first)), (mixed, column(2 * every + first)),
         (bias, pl.BlockSpec((2, tall, broad), lambda t: (first + t, 0, 0)))],
        [((rows, 128 * pairs), BF16, column(0), FAR),
         ((2 * pairs, images, tall, broad), BF16,
          pl.BlockSpec((2, images, tall, broad), lambda t: (t, 0, 0, 0)), FAR)],
        flops=4 * rows * tall * 128 * pairs,
    )


def attend_back(sizes, mixed, probs, grad_out, score_scale, first, pairs, so_far):
    images, length, tall, width = sizes
    rows = images * tall
    every = width // 128
    broad = probs.shape[3]

    def kernel(q_ref, k_ref, v_ref, do_ref, p_ref, *refs):
        grad_ref, terms_ref, qb_ref, vb_ref = refs[-4:]
        masks = head_masks(tall)
        units = [(i, h) for i in range(images) for h in range(2)]

        def part(ref, i):
            return ref[tall * i : tall * i + tall, :]

        def own(value, h):
            return jnp.where(masks[h], value, jnp.zeros_like(value))

        grads = [nt(part(v_ref, i), own(part(do_ref, i), h)) for i, h in units]
        lows = []
        for (i, h), grad in zip(units, grads, strict=True):
            p = p_ref[h, i, :, 0:tall].astype(F32)
            t = p * grad
            lows.append((t - p * jnp.sum(t, axis=0, keepdims=True)).astype(BF16))
        for h in range(2):
            terms_ref[h, :, 0:tall] = sum(lows[2 * i + h].astype(F32) for i in range(images))
            terms_ref[h, :, tall:] = jnp.zeros((tall, broad - tall), F32)
        query_sum, value_sum = 0.0, 0.0
        for i in range(images):
            kt = part(k_ref, i).T
            dv = sum(nn(p_ref[h, i, :, 0:tall], own(part(do_ref, i), h)) for h in range(2))
            dk = sum(nn(lows[2 * i + h], own(part(q_ref, i), h)) for h in range(2))
            dq = jnp.concatenate(
                [nn(kt[64 * h : 64 * h + 64, :], lows[2 * i + h]) for h in range(2)], axis=0
            ).T * score_scale
            for number, grad in enumerate((dq, dk, dv)):
                grad_ref[number, tall * i : tall * i + tall, :] = grad.astype(BF16)
            query_sum += column_sum(dq)
            value_sum += column_sum(dv)
        qb_ref[...] = query_sum
        vb_ref[...] = value_sum

    def column(at):
        return pl.BlockSpec((rows, 128), lambda t: (0, at + t))

    one = pl.BlockSpec((1, 128), lambda t: (0, t))
    return call(
        kernel, "attend_back", (pairs,),
        [(mixed, column(first)), (mixed, column(every + first)), (mixed, column(2 * every + first)),
         (grad_out, column(first)),
         (probs, pl.BlockSpec((2, images, tall, broad), lambda t: (first + t, 0, 0, 0)), FAR)]
        + ([] if so_far is None else [(so_far, ANY)]),
        [((3, rows, width), BF16, pl.BlockSpec((3, rows, 128), lambda t: (0, 0, first + t)))]
        + [((2 * pairs, tall, broad), F32, pl.BlockSpec((2, tall, broad), lambda t: (t, 0, 0))),
           ((1, 128 * pairs), F32, one), ((1, 128 * pairs), F32, one)],
        flops=8 * rows * tall * 128 * pairs,
        aliases={} if so_far is None else {5: 0},
    )


def merge(sizes, attended, start, weight, params):
    images, length, tall, width = sizes
    rows = images * tall
    count = len(weight.operands)

    def kernel(*refs):
        att_refs, refs = refs[: len(attended)], refs[len(attended) :]
        h0_ref, params_ref = refs[:2]
        h1_ref, n2_ref, w_s, out_s, sem = refs[2 + count :]
        step = pl.program_id(0)

        @pl.when(step == 0)
        def _():
            weight.fill(refs[2 : 2 + count], w_s, sem)
            weight.wait(w_s, sem)
            part = width // len(attended)
            out_s[...] = sum(nn(r[...], w_s[part * k : part * k + part, 0:width]) for k, r in enumerate(att_refs))

        @pl.when(step > 0)
        def _():
            def body(at, first):
                out = out_s[pl.ds(pl.multiple_of((step - 1) * tall + first, 8), min(BAND, tall)), :]
                middle = h0_ref[at, :] + row_of(params_ref, GAMMA1) * (out + row_of(params_ref, BIAS1))
                h1_ref[at, :] = middle
                normed, _ = norm(middle)
                n2_ref[at, :] = (normed * row_of(params_ref, GAIN2) + row_of(params_ref, SHIFT2)).astype(BF16)

            banded(tall, body)

    band = pl.BlockSpec((tall, width), lambda i: (jnp.maximum(i - 1, 0), 0))
    return call(
        kernel, "merge", (images + 1,),
        [(a, kept(a.shape), FAR) for a in attended]
        + [(start, band, FAR), (params, kept(params.shape))]
        + [(a, ANY, FAR) for a in weight.operands],
        [((rows, width), F32, band, FAR), ((rows, width), BF16, band)],
        [pltpu.VMEM((width, width + weight.extra), BF16), pltpu.VMEM((rows, width), F32),
         pltpu.SemaphoreType.DMA],
        flops=2 * rows * width * width,
    )


def part_by_core(store, away_ref, stay_ref):
    c = lax.axis_index("narrow") % 2
    for x in range(2):
        away_ref[x] = store[2 * x + 1 - c]
        stay_ref[x] = store[2 * x + c]


def feed(sizes, second_low, down_low, up, down, bias, sums, last):
    images, length, tall, width = sizes
    rows = images * tall
    shared = up.operands[0] is down.operands[0]
    far = () if last else (FAR,)
    ups, downs = len(up.operands), 0 if shared else len(down.operands)
    carried = [] if sums is None else list(sums)

    def kernel(*refs):
        n2_ref, df_ref, bias_ref = refs[:3]
        rest = refs[3:]
        up_refs, rest = rest[:ups], rest[ups:]
        down_refs, rest = (up_refs if shared else rest[:downs]), rest[downs:]
        sum_refs, rest = rest[: len(carried)], rest[len(carried) :]
        f_ref, dn_ref, away_ref, stay_ref, gbias_ref, up_s, down_s, grad_s, sems = rest
        step = pl.program_id(0)

        @pl.when(step == 0)
        def _():
            up.fill(up_refs, up_s, sems.at[0])
            down.fill(down_refs, down_s, sems.at[1])
            if carried:
                pltpu.make_async_copy(sum_refs[0], f_ref, sems.at[2]).start()
                pltpu.make_async_copy(sum_refs[1], dn_ref, sems.at[3]).start()
            up.wait(up_s, sems.at[0])
            down.wait(down_s, sems.at[1])
            if not carried:
                f_ref[...] = jnp.zeros_like(f_ref)
                dn_ref[...] = jnp.zeros_like(dn_ref)

        at = pl.ds(pl.multiple_of(step * TILE, TILE), TILE)
        up_w, down_w = up_s[:, at], down_s[:, at]
        u = nn(n2_ref[...], up_w) + bias_ref[...]
        dz = nn(df_ref[...], down_w)
        bell = jnp.exp(-0.5 * u * u)
        below = 0.5 * (1.0 + lax.erf(u * ROOT_HALF))
        z = (u * below).astype(BF16)
        du = dz * (below + u * (DENSITY * bell))
        gbias_ref[...] = column_sum(du)
        du = du.astype(BF16)
        grad = tn(n2_ref[...], du).astype(BF16)
        for k in range(TILE // 256):
            grad_s[step * (TILE // 256) + k, :, :, 0:256] = grad[:, 256 * k : 256 * k + 256].reshape(8, 96, 256)
        grad = tn(df_ref[...], z).astype(BF16)
        for n in range(4):
            for w in range(TILE // 128):
                for half in range(2):
                    grad_s[n, step * (TILE // 128) + w, :, 256 + 128 * half : 384 + 128 * half] = grad[
                        192 * n + 96 * half : 192 * n + 96 * half + 96, 128 * w : 128 * w + 128
                    ]
        if carried:
            @pl.when(step == 0)
            def _():
                pltpu.make_async_copy(sum_refs[0], f_ref, sems.at[2]).wait()
                pltpu.make_async_copy(sum_refs[1], dn_ref, sems.at[3]).wait()

        f_ref[...] += nt(z, down_w)
        dn_ref[...] += nt(du, up_w)

        @pl.when(step == CHUNK // TILE - 1)
        def _():
            part_by_core(grad_s, away_ref, stay_ref)

    tile = pl.BlockSpec((1, TILE), lambda t: (0, t))
    full = whole((rows, width))
    shape = (2, 8, 96, 512)
    return call(
        kernel, "feed", (CHUNK // TILE,),
        [(second_low, kept((rows, width))), (down_low, kept((rows, width))), (bias, tile)]
        + [(a, ANY, FAR) for a in up.operands + ([] if shared else down.operands) + carried],
        [((rows, width), F32, kept((rows, width)), *far), ((rows, width), F32, kept((rows, width)), *far),
         (shape, BF16, kept(shape)), (shape, BF16, kept(shape)), ((1, CHUNK), F32, tile)],
        [pltpu.VMEM((width, CHUNK), BF16), pltpu.VMEM((width, CHUNK), BF16), pltpu.VMEM((4, 8, 96, 512), BF16),
         pltpu.SemaphoreType.DMA((4,))],
        flops=12 * rows * width * CHUNK,
    )


def middle_back(sizes, attended, branch, grad_n2, middle, start, upstream, weight, params):
    images, length, tall, width = sizes
    rows = images * tall
    count = len(weight.operands)

    def kernel(*refs):
        att_refs, refs = refs[: len(attended)], refs[len(attended) :]
        f_ref, dn_ref, h1_ref, h0_ref, g_ref, params_ref = refs[:6]
        out_ref, dh_ref, do_ref, away_ref, stay_ref, sum_ref, w_s, da_s, grad_s, layer_s, sem = refs[6 + count :]
        step = pl.program_id(0)

        @pl.when(step == 0)
        def _():
            weight.fill(refs[6 : 6 + count], w_s, sem)
            sum_ref[...] = jnp.zeros_like(sum_ref)

        @pl.when(step < images)
        def _():
            def body(at, first):
                f = f_ref[at, :] + row_of(params_ref, BIAS2)
                h1 = h1_ref[at, :]
                g = g_ref[at, :].astype(F32)
                layer_s[at, :] = h1 + row_of(params_ref, GAMMA2) * f
                normed, scaling = norm(h1)
                dn = dn_ref[at, :]
                dh = g + norm_back(dn, normed, scaling, row_of(params_ref, GAIN2))
                dh_ref[at, :] = dh
                da = row_of(params_ref, GAMMA1) * dh
                sum_ref[0:1, :] += column_sum(g * f)
                sum_ref[1:2, :] += column_sum(dn * normed)
                sum_ref[2:3, :] += column_sum(dn)
                sum_ref[3:4, :] += column_sum(dh * (h1 - h0_ref[at, :]))
                sum_ref[4:5, :] += column_sum(da)
                da_s[pl.ds(pl.multiple_of(step * tall + first, 8), min(BAND, tall)), :] = da.astype(BF16)

            banded(tall, body)
            out_ref[0] = layer_s[0:length, :].astype(BF16)

        @pl.when(step == images)
        def _():
            sum_ref[3:4, :] = sum_ref[3:4, :] / row_of(params_ref, GAMMA1)
            weight.wait(w_s, sem)
            do_ref[...] = nt(da_s[...], w_s[:, 0:width]).astype(BF16)
            grad = jnp.concatenate([tn(r[...], da_s[...]) for r in att_refs], axis=0).astype(BF16)
            for n, at in enumerate((0, 128, 384, 512)):
                grad_s[n] = grad[:, at : at + 256].reshape(8, 96, 256)
            part_by_core(grad_s, away_ref, stay_ref)

    def at(i):
        return jnp.minimum(i, images - 1)

    band = pl.BlockSpec((tall, width), lambda i: (at(i), 0))
    shape = (2, 8, 96, 256)
    return call(
        kernel, "middle_back", (images + 1,),
        [(a, kept(a.shape), FAR) for a in attended]
        + [(a, band) for a in (branch, grad_n2)] + [(a, band, FAR) for a in (middle, start, upstream)] + [(params, kept(params.shape))]
        + [(a, ANY, FAR) for a in weight.operands],
        [((images, length, width), BF16, pl.BlockSpec((1, length, width), lambda i: (at(i), 0, 0))),
         ((rows, width), F32, band), ((rows, width), BF16, whole((rows, width))),
         (shape, BF16, whole(shape)), (shape, BF16, whole(shape)), ((8, width), F32, whole((8, width)))],
        [pltpu.VMEM((width, width + weight.extra), BF16), pltpu.VMEM((rows, width), BF16),
         pltpu.VMEM((4, 8, 96, 256), BF16), pltpu.VMEM((tall, width), F32), pltpu.SemaphoreType.DMA],
        flops=4 * rows * width * width,
    )


def mixed_grad(sizes, first_low, grads):
    images, length, tall, width = sizes
    rows = images * tall

    def kernel(n1_ref, grad_ref, away_ref, stay_ref):
        step = pl.program_id(0)
        c = lax.axis_index("narrow") % 2
        n = 2 * (step % 2) + jnp.where(step < 2, 1 - c, c)
        main = grad_ref[at_least(n, (0, 1, 1, 2)), :, pl.ds(pl.multiple_of(at_least(n, (0, 0, 384, 384)), 128), 384)]
        side = grad_ref[at_least(n, (0, 0, 2, 2)), :, pl.ds(pl.multiple_of(at_least(n, (384, 512, 0, 128)), 128), 256)]
        main = tn(n1_ref[...], main).astype(BF16).reshape(8, 96, 384)
        side = tn(n1_ref[...], side).astype(BF16).reshape(8, 96, 256)
        for role, ref in enumerate((away_ref, stay_ref)):
            @pl.when(step // 2 == role)
            def _(ref=ref):
                ref[0, :, :, 0:384] = main
                ref[0, :, :, 384:640] = side

    shape = (2, 8, 96, 640)
    return call(
        kernel, "mixed_grad", (4,),
        [(first_low, kept((rows, width))), (grads, kept(grads.shape))],
        [(shape, BF16, pl.BlockSpec((1, 8, 96, 640), lambda t: (jnp.minimum(t, 1), 0, 0, 0))),
         (shape, BF16, pl.BlockSpec((1, 8, 96, 640), lambda t: (jnp.maximum(t - 2, 0), 0, 0, 0)))],
        flops=6 * rows * width * width,
    )


def start_back(sizes, grads, weight, start, grad_middle, group_sizes, patterns, params):
    images, length, tall, width = sizes
    rows = images * tall
    count = len(weight.operands)

    def kernel(*refs):
        grad_ref, h0_ref, dh_ref, sizes_ref, patterns_ref, params_ref = refs[:6]
        out_ref, sum_ref, w_s, dn_s, out_s, sem = refs[6 + count :]
        step = pl.program_id(0)

        @pl.when(step == 0)
        def _():
            weight.fill(refs[6 : 6 + count], w_s, sem)
            sum_ref[...] = jnp.zeros_like(sum_ref)
            dn_s[...] = jnp.zeros_like(dn_s)
            weight.wait(w_s, sem)

        @pl.when(step < 3)
        def _():
            dn_s[...] += nt(grad_ref[0], w_s[:, pl.ds(pl.multiple_of(step * width, 128), width)])

        @pl.when(step > 2)
        def _():
            masked = masked_rows(first_image(images) + step - 3, sizes_ref, patterns_ref, tall)

            def body(at, first):
                dn = dn_s[pl.ds(pl.multiple_of((step - 3) * tall + first, 8), min(BAND, tall)), :]
                normed, scaling = norm(h0_ref[at, :])
                dh = dh_ref[at, :] + norm_back(dn, normed, scaling, row_of(params_ref, GAIN1))
                out_s[at, :] = jnp.where(masked, 0.0, dh)
                sum_ref[0:1, :] += column_sum(dn * normed)
                sum_ref[1:2, :] += column_sum(dn)
                sum_ref[2:3, :] += column_sum(jnp.where(masked, dh, 0.0))

            banded(tall, body)
            out_ref[0] = out_s[0:length, :]

    def at(i):
        return jnp.maximum(i - 3, 0)

    band = pl.BlockSpec((tall, width), lambda i: (at(i), 0))
    return call(
        kernel, "start_back", (images + 3,),
        [(grads, pl.BlockSpec((1, rows, width), lambda i: (jnp.minimum(i, 2), 0, 0)))]
        + [(start, band), (grad_middle, band), (group_sizes, SCALARS), (patterns, kept(patterns.shape)),
           (params, kept(params.shape))]
        + [(a, ANY) for a in weight.operands],
        [((images, length, width), F32, pl.BlockSpec((1, length, width), lambda i: (at(i), 0, 0))),
         ((8, width), F32, whole((8, width)))],
        [pltpu.VMEM((width, 3 * width + weight.extra), BF16), pltpu.VMEM((rows, width), F32),
         pltpu.VMEM((tall, width), F32), pltpu.SemaphoreType.DMA],
        flops=6 * rows * width * width,
    )


def local(
    links,
    inputs,
    cotangent,
    group_sizes,
    mask_patterns,
    mask_token,
    norm1_gain,
    norm1_bias,
    qkv_weight,
    query_bias,
    value_bias,
    bias_table,
    proj_weight,
    proj_bias,
    gamma_attn,
    norm2_gain,
    norm2_bias,
    fc1_weight,
    fc1_bias,
    fc2_weight,
    fc2_bias,
    gamma_mlp,
):
    images, length, width = inputs.shape
    table_rows, heads = bias_table.shape
    grid_side = math.isqrt(length - 1)
    group_count = mask_patterns.shape[0]
    tall = -(-length // 8) * 8
    rows = images * tall
    hidden = fc1_bias.shape[0]
    chunks = hidden // CHUNK
    sizes = (images, length, tall, width)
    score_scale = (width // heads) ** (-0.5)
    here = links.place()

    vectors = {
        TOKEN: mask_token, GAIN1: norm1_gain, SHIFT1: norm1_bias, GAMMA2: gamma_mlp, BIAS1: proj_bias,
        GAMMA1: gamma_attn, GAIN2: norm2_gain, SHIFT2: norm2_bias, BIAS2: fc2_bias, 9: query_bias, 11: value_bias,
    }

    boxed = links.boxed
    fc2_t = fc2_weight.T
    if boxed:
        mix = Gather(links, qkv_block(here, qkv_weight), 384, [((0, 384), (0, 256))])
        side = align_side(here, proj_weight)
        near = Gather(
            links,
            jnp.concatenate(
                [side[:, :128], up_block(fc1_weight, 0), down_block(fc2_t, 0), side[:, 128:]], axis=1
            ),
            384,
            [((0, 128), (256, 384)), ((128, 384), (0, 256))],
        )
        far = Gather(
            links,
            jnp.concatenate(
                [up_block(fc1_weight, 1), up_block(fc1_weight, 2), down_block(fc2_t, 1), down_block(fc2_t, 2)],
                axis=1,
            ),
            512,
            [((0, 256), (0, 256)), ((256, 512), (256, 512))],
        )
        full_up = full_down = None
    else:
        mix = near = far = None
        full_up, full_down = native_gather(fc1_weight), native_gather(fc2_weight).T

    entry = table_columns(grid_side, 384)

    def behind(value, *exchanges):
        return after(value, *[v for e in exchanges for v in e.sent]) if boxed else value

    def met(value, *exchanges):
        return [value] + [v for e in exchanges for v in e.flying]

    if boxed:
        mix.first()
    start, first_low, upstream, down_low, sum_fc2, params, patterns = prepare(
        sizes, inputs, cotangent, group_sizes, mask_patterns, vectors
    )
    if boxed:
        gap = met(first_low, mix)
        mix.second(*gap)
        near.first(*gap)
    table_t = jnp.pad(after(bias_table, first_low).T, ((0, 16 - heads), (0, width - table_rows)))
    bias = bias_kernel(behind(table_t, mix), entry, grid_side, tall, 256)
    if boxed:
        mix.third(*met(bias, mix))
        mix.fourth(False, *met(bias, near))
        near.second(*mix.sent)
    qkv = qkv_operands(links, mix, qkv_weight)
    mixed = project(sizes, behind(first_low, near), qkv, params, score_scale)
    if boxed:
        gap = met(mixed, near)
        near.third(*gap)
        far.first(*gap)
    attended, probs = attend(sizes, behind(mixed, near), bias, 0, width // 128)
    if boxed:
        near.fourth(False, *met(attended, far))
        far.second(*near.sent)
    proj = proj_operands(links, near, proj_weight)
    middle, second_low = merge(sizes, [attended], behind(start, far), proj, params)
    if boxed:
        far.third(*met(second_low, far))

    fc1_groups = fc1_bias.reshape(8, chunks, 128)
    ups = [up_operands(links, near, 1, full_up, 0), None, None]
    downs = [down_operands(links, near, 1, full_down, 0), None, None]
    halves = [[(0, (0, 256))], [(0, (256, 512))]]
    sums, pairs_out, hidden_sums = None, [], []
    waves = [Scatter(links, here, 256), Scatter(links, here, 256), Scatter(links, here, 512)]
    second_here = behind(second_low, far)
    for k in range(chunks):
        branch, grad_n2, away, stay, hidden_sum = feed(
            sizes, second_here, down_low, ups[k], downs[k], fc1_groups[:, k].reshape(1, -1), sums, k == chunks - 1
        )
        if k == 0:
            if boxed:
                far.fourth(True, *met(away, far))
                waves[0].first(after(away, *far.sent), stay)
            ups[1:] = [up_operands(links, far, 0, full_up, 1), up_operands(links, far, 1, full_up, 2)]
            downs[1:] = [down_operands(links, far, 0, full_down, 1), down_operands(links, far, 1, full_down, 2)]
            second_here = second_low
        elif k == 1 and boxed:
            exchange(links, [away], (waves[0], "second", halves))
            waves[1].first(after(away, *waves[0].sent), stay)
            second_here = behind(second_low, waves[0])
        elif boxed:
            exchange(links, [away], (waves[0], "third", None), (waves[1], "second", halves))
            waves[2].first(after(away, *waves[1].sent), stay)
        sums = (branch, grad_n2)
        pairs_out.append((away, stay))
        hidden_sums.append(hidden_sum)

    layer_out, grad_middle, grad_att, proj_away, proj_stay, middle_sums = middle_back(
        sizes, [attended], behind(branch, waves[0], waves[1]), grad_n2, middle, start, upstream, proj, params
    )
    if boxed:
        exchange(links, [grad_att], (waves[0], "fourth", None), (waves[1], "third", None))
        waves[2].first(after(proj_away, *waves[1].sent), proj_stay)

    back, grads = [], None
    for number, (first, pairs) in enumerate(((0, 3), (3, 3))):
        grad_here = behind(grad_att, *(waves[:2] if number == 0 else waves[1:]))
        grads, *rest = attend_back(sizes, mixed, probs, grad_here, score_scale, first, pairs, grads)
        back.append(rest)
        if boxed and number == 0:
            gap = met(grads, waves[0])
            exchange(
                links, gap, (waves[1], "fourth", None),
                (waves[2], "second", [[(1, (0, 256)), (0, (0, 256))], [(0, (256, 512))]]),
            )
    if boxed:
        gap_grads = met(grads, waves[1])
        exchange(links, gap_grads, (waves[2], "third", None))
    mix_away, mix_stay = mixed_grad(sizes, behind(first_low, waves[2]), grads)
    last = Scatter(links, here, 384)
    terms = jnp.concatenate([b[0] for b in back], axis=0)
    if boxed:
        exchange(links, [mix_away], (waves[2], "fourth", None))
        last.first(after(mix_away, *waves[2].sent), mix_stay)
    grad_table = bias_back_kernel(after(behind(terms, waves[2]), mix_away), entry, grid_side, width)
    if boxed:
        gap_table = met(grad_table, waves[2])
        exchange(links, gap_table, (last, "second", [[(0, (0, 384))], [(0, (384, 640))]]))
    input_grad, start_sums = start_back(
        sizes, grads, qkv, start, behind(grad_middle, last), group_sizes, patterns, params
    )
    small_away, small_stay = pack(
        links, grad_table, heads, start_sums, middle_sums, [b[1:] for b in back], sum_fc2, hidden_sums
    )
    if boxed:
        exchange(links, [start_sums], (last, "third", None))
        small_away = after(small_away, *last.sent)
    small = sum_everywhere(links, here, small_away, small_stay, last.flying)
    if boxed:
        exchange(links, [], (last, "fourth", None))
        grad_qkv = qkv_home(here, last.done())
        blocks = [waves[0].done(*gap), waves[1].done(*gap_grads), waves[2].done(*gap_table)]
        grad_proj = proj_home(here, blocks[2][:, 0:256])
        up_parts = [blocks[0][:, 0:256], blocks[1][:, 0:256], blocks[2][:, 256:512]]
        down_parts = [blocks[0][:, 256:512], blocks[1][:, 256:512], blocks[2][:, 512:768]]
        grad_fc1 = jnp.concatenate(
            [up_parts[k][:, 128 * half : 128 * half + 128] for half in range(2) for k in range(chunks)], axis=1
        )
        grad_fc2 = jnp.concatenate(
            [jnp.concatenate([p[:, :128], p[:, 128:]], axis=0) for p in down_parts], axis=1
        ).T
    else:
        tiles = [all_tiles(here, *pair) for pair in pairs_out]
        grad_qkv = native_scatter(natural_qkv(all_tiles(here, mix_away, mix_stay)))
        grad_proj = native_scatter(natural_proj(all_tiles(here, proj_away, proj_stay)))
        grad_fc1 = native_scatter(natural_up([t[..., :256] for t in tiles]))
        grad_fc2 = native_scatter(natural_down([t[..., 256:] for t in tiles]))
    at = heads
    hidden_rows = [
        jnp.concatenate([small[at + 11 + k], small[at + 14, 256 * k : 256 * k + 256]]).reshape(8, 128) for k in range(chunks)
    ]
    sum_fc1 = jnp.stack(hidden_rows, axis=1).reshape(-1)
    return (
        layer_out,
        input_grad,
        small[at + 2],
        small[at],
        small[at + 1],
        grad_qkv,
        small[at + 8],
        small[at + 9],
        small[:heads, :table_rows].T,
        grad_proj,
        small[at + 7],
        small[at + 6],
        small[at + 4],
        small[at + 5],
        grad_fc1,
        sum_fc1,
        grad_fc2,
        small[at + 10],
        small[at + 3],
    )


def solution(mesh):
    images = P(AXES, None, None)
    both = P("wide", "narrow")
    same = P()
    links = Links(mesh.shape["wide"], mesh.shape["narrow"])
    return jax.shard_map(
        functools.partial(local, links),
        mesh=mesh,
        in_specs=(
            images, images, same, same, same, same, same, both, same, same, same, both, same, same,
            same, same, both, same, both, same, same,
        ),
        out_specs=(
            images, images, same, same, same, both, same, same, same, both, same, same, same, same,
            both, same, both, same, same,
        ),
        check_vma=False,
    )
```

```python
import functools
import math

import jax
import jax.numpy as jnp
import numpy as np
from jax import lax
from jax.experimental import pallas as pl
from jax.experimental.pallas import tpu as pltpu
from jax.sharding import PartitionSpec as P

EPSILON = 1e-06
ROOT_HALF = 0.7071067811865476
DENSITY = 0.3989422804014327
BF16 = jnp.bfloat16
F32 = jnp.float32
AXES = ("wide", "narrow")
TILE = 512
BAND = 200
CHUNK = 1024
NEVER = -1e30
MIB = 1 << 20


class Links:
    def __init__(self, wide, narrow):
        self.wide, self.narrow = wide, narrow
        self.y = 1 << ((wide.bit_length() - 1) // 2)
        self.z = wide // self.y
        self.x = narrow // 2
        self.size = {"z": self.z, "y": self.y, "x": self.x, "core": 2}
        self.unit = {"core": 1, "x": 2, "y": narrow, "z": narrow * self.y}
        self.boxed = (self.z, self.y, self.x) == (4, 2, 2)

    def place(self):
        w, n = lax.axis_index("wide"), lax.axis_index("narrow")
        return {"z": w // self.y, "y": w % self.y, "x": n // 2, "core": n % 2, "w": w, "n": n}

    def swap(self, value, **offsets):
        mask = sum(self.unit[axis] * offset for axis, offset in offsets.items())
        count = self.wide * self.narrow
        return lax.ppermute(value, AXES, [(k, k ^ mask) for k in range(count)])

    def others(self, value, axis):
        return [self.swap(value, **{axis: d}) for d in range(1, self.size[axis])]


def pick(value, axis, index, count):
    size = value.shape[axis] // count
    return lax.dynamic_slice_in_dim(value, index * size, size, axis)


def after(value, *others):
    return lax.optimization_barrier((value,) + others)[0]


def tied(values, wait):
    if not wait:
        return list(values)
    return list(lax.optimization_barrier(tuple(values) + tuple(wait)))[: len(values)]


def native_gather(shard):
    return lax.all_gather(
        lax.all_gather(shard, "narrow", axis=1, tiled=True), "wide", axis=0, tiled=True
    )


class Gather:
    orders = (("x", "y"), ("y", "x"))

    def __init__(self, links, block, split, groups):
        self.links, self.block, self.split, self.groups = links, block, split, groups

    def first(self, *wait):
        block = after(self.block, *wait) if wait else self.block
        self.sent = [block]
        self.steps = [block] + self.links.others(block, "z")
        self.flying = self.steps[1:]

    def second(self, *wait):
        parts = arrange([after(self.steps[0], *wait) if wait else self.steps[0]] + self.steps[1:], self.split)
        self.steps, self.sent = [], []
        for held, order in zip(parts, self.orders, strict=True):
            self.sent.append(held)
            self.steps.append([held] + self.links.others(held, order[0]))
        self.flying = [v for p in self.steps for v in p[1:]]

    def third(self, *wait):
        parts = stack([[after(self.steps[0][0], *wait)] + self.steps[0][1:], self.steps[1]])
        self.steps, self.sent = [], []
        for held, order in zip(parts, self.orders, strict=True):
            self.sent.append(held)
            self.steps.append([held] + self.links.others(held, order[1]))
        self.flying = [v for p in self.steps for v in p[1:]]

    def fourth(self, far, *wait):
        first = after(self.steps[0][0], *wait)
        self.operands = []
        held = regroup([[first] + self.steps[0][1:], self.steps[1]], self.groups, far)
        for number, array in enumerate(held):
            self.operands.append([array, self.links.swap(array, core=1)])
        self.sent = held
        self.flying = [pair[1] for pair in self.operands]

    def blocks(self, refs, number, me):
        links = self.links
        order = self.orders[number]
        out = []
        for core in range(2):
            for k in range(refs[core].shape[0]):
                at, rest = {}, k
                for axis in ("z",) + order:
                    at[axis] = me[axis] ^ (rest % links.size[axis])
                    rest //= links.size[axis]
                source = functools.partial(block_columns, refs[core], k)
                out.append((source, at["z"] * links.y + at["y"], at["x"] * 2 + (me["core"] ^ core)))
        return out


def block_columns(ref, k, col, broad):
    return ref.at[k, :, pl.ds(col, broad)]


def at_least(n, values):
    out = values[3]
    for k in (2, 1, 0):
        out = jnp.where(n == k, values[k], out)
    return out


def window(ref, row, col, tall, broad):
    if not isinstance(row, int):
        row = pl.multiple_of(row, 8)
    if not isinstance(col, int):
        col = pl.multiple_of(col, 128)
    return ref.at[pl.ds(row, tall), pl.ds(col, broad)]


def columns(ref, col, broad):
    return ref.at[:, pl.ds(col, broad)]


class Weight:
    def __init__(self, operands, copies, joints=(), extra=0):
        self.operands, self.copies, self.joints, self.extra = operands, copies, joints, extra

    def fill(self, refs, target, sem):
        for source, to in self.copies(refs, target):
            pltpu.make_async_copy(source, to, sem).start()

    def wait(self, target, sem):
        pltpu.make_async_copy(target, target, sem).wait()
        for here, there in self.joints:
            target[:, here : here + 128] += target[:, there : there + 128]


def align_side(here, side):
    zero = jnp.zeros((side.shape[0], 64), side.dtype)
    return jnp.where(
        here["n"] % 2 == 0,
        jnp.concatenate([side, zero], axis=1),
        jnp.concatenate([zero, side], axis=1),
    )


def qkv_block(here, shard):
    even = here["n"] % 2 == 0
    main = jnp.where(even, shard[:, :384], shard[:, 192:])
    return jnp.concatenate([main, align_side(here, jnp.where(even, shard[:, 384:], shard[:, :192]))], axis=1)


def qkv_operands(links, gathered, shard):
    if not links.boxed:
        return Weight([native_gather(shard)], lambda refs, target: [(refs[0], target.at[:, pl.ds(0, 2304)])] + [
            (refs[0].at[:, pl.ds(0, 256)], target.at[:, pl.ds(2304, 256)])], extra=256)

    def copies(refs, target):
        me = links.place()
        out = []
        for source, w, n in gathered.blocks(refs, 0, me):
            out.append((source(0, 384), window(target, w * 96, at_least(n, (0, 768, 1152, 1920)), 96, 384)))
        for source, w, n in gathered.blocks(refs, 1, me):
            for part, places in enumerate(((384, 2304, 1536, 2432), (512, 640, 1664, 1792))):
                out.append((source(384 + 128 * part, 128), window(target, w * 96, at_least(n, places), 96, 128)))
        return out

    return Weight(gathered.operands[0], copies, ((512, 2304), (1664, 2432)), 256)


def proj_operands(links, gathered, shard):
    if not links.boxed:
        return Weight([native_gather(shard)], lambda refs, target: [(refs[0], target.at[:, pl.ds(0, 768)])] + [
            (refs[0].at[:, pl.ds(0, 256)], target.at[:, pl.ds(768, 256)])], extra=256)

    def copies(refs, target):
        me = links.place()
        out = []
        for part, (col, places) in enumerate(((0, (0, 768, 384, 896)), (128, (128, 256, 512, 640)))):
            for source, w, n in gathered.blocks(refs, part, me):
                out.append((source(col, 128), window(target, w * 96, at_least(n, places), 96, 128)))
        return out

    return Weight(gathered.operands[0], copies, ((128, 768), (512, 896)), 256)


def up_block(shard, chunk):
    return jnp.concatenate(
        [shard[:, 384 * half + 128 * chunk : 384 * half + 128 * chunk + 128] for half in range(2)], axis=1
    )


def down_block(shard_t, chunk):
    piece = shard_t[:, 128 * chunk : 128 * chunk + 128]
    half = piece.shape[0] // 2
    return jnp.concatenate([piece[:half], piece[half:]], axis=1)


def chunk_copies(full, chunk):
    def slices(refs, target):
        return [
            (columns(refs[0], 384 * g + 128 * chunk, 128), columns(target, 128 * g, 128)) for g in range(8)
        ]

    return Weight([full], slices)


def up_operands(links, gathered, group, full, chunk):
    if not links.boxed:
        return chunk_copies(full, chunk)

    def copies(refs, target):
        me = links.place()
        return [
            (source(0, 256), window(target, w * 96, n * 256, 96, 256))
            for source, w, n in gathered.blocks(refs, 0, me)
        ]

    return Weight(gathered.operands[group], copies)


def down_operands(links, gathered, group, full, chunk):
    if not links.boxed:
        return chunk_copies(full, chunk)

    def copies(refs, target):
        me = links.place()
        return [
            (source(256 + 128 * half, 128), window(target, n * 192 + half * 96, w * 128, 96, 128))
            for source, w, n in gathered.blocks(refs, 1, me)
            for half in range(2)
        ]

    return Weight(gathered.operands[group], copies)


class Scatter:
    orders = (("x", "y"), ("y", "x"))

    def __init__(self, links, here, split):
        self.links, self.here, self.split = links, here, split
        self.pairs, self.flying, self.stage = [], [], 0

    def first(self, away, stay):
        shape = (self.links.x, self.links.z, self.links.y) + away.shape[2:]
        self.pairs.append((stay.reshape(shape), self.links.swap(away.reshape(shape), core=1)))
        self.flying.append(self.pairs[-1][1])

    def jobs(self, step, picks):
        if step == "second":
            return [
                ([(self.pairs[k], cols) for k, cols in part], order[0])
                for part, order in zip(picks, self.orders, strict=True)
            ]
        whole_of = [(t, (0, t[0].shape[-1])) for t in self.terms]
        if step == "third":
            return [([t], order[1]) for t, order in zip(whole_of, self.orders, strict=True)]
        if step == "fifth":
            return [([(self.terms[0], (0, self.terms[0][0].shape[-1]))], "z_low")]
        return [(whole_of, "z_high" if step == "halves" else "z")]

    def take(self, results, unit):
        self.sent = [v for r in results for v in r[1:]]
        self.terms = []
        axes = [(order[self.stage], 1) for order in self.orders] if self.stage < 2 else [("z", unit)]
        for (keep, *sent), (axis, step) in zip(results, axes, strict=True):
            self.terms.append([keep] + [self.links.swap(v, **{axis: d * step}) for d, v in enumerate(sent, 1)])
        self.stage += 1
        self.flying = [v for t in self.terms for v in t[1:]]

    def done(self, *wait):
        terms = tied(self.terms[0], wait)
        total = terms[0]
        for term in terms[1:]:
            total = total + term.astype(F32)
        return total.reshape(total.shape[-2:])


def exchange(links, wait, *items):
    jobs = [job for scatter, step, picks in items for job in scatter.jobs(step, picks)]
    group, cols = jobs[0][0][0]
    jobs[0][0][0] = ((after(group[0], *wait),) + tuple(group[1:]), cols)
    results = fold(links, jobs)
    for scatter, step, _ in items:
        count = 2 if step in ("second", "third") else 1
        scatter.take(results[:count], 2 if step == "halves" else 1)
        results = results[count:]


def all_tiles(here, away, stay):
    return jnp.where(
        here["core"] == 0, jnp.stack([stay, away], axis=1), jnp.stack([away, stay], axis=1)
    ).reshape((4,) + away.shape[1:])


def native_scatter(partial):
    low = lax.psum_scatter(partial.astype(BF16), "wide", scatter_dimension=0, tiled=True)
    return lax.psum_scatter(low, "narrow", scatter_dimension=1, tiled=True).astype(F32)


def qkv_home(here, block):
    even = here["n"] % 2 == 0
    main, side = block[:, :384], block[:, 384:]
    return jnp.where(
        even,
        jnp.concatenate([main, side[:, :192]], axis=1),
        jnp.concatenate([side[:, 64:], main], axis=1),
    )


def proj_home(here, block):
    return jnp.where(here["n"] % 2 == 0, block[:, :192], block[:, 64:])


def natural_qkv(tiles):
    tiles = tiles.reshape(4, 768, 640)
    out = []
    for n in range(4):
        main, side = tiles[n, :, :384], tiles[n, :, 384:]
        out += [main, side[:, :192]] if n % 2 == 0 else [side[:, 64:], main]
    return jnp.concatenate(out, axis=1)


def natural_proj(tiles):
    tiles = tiles.reshape(4, 768, 256)
    return jnp.concatenate([tiles[n, :, :192] if n % 2 == 0 else tiles[n, :, 64:] for n in range(4)], axis=1)


def natural_up(chunks):
    tiles = [t.reshape(4, 768, 2, 128) for t in chunks]
    return jnp.stack(tiles, axis=0).transpose(2, 1, 3, 0, 4).reshape(768, -1)


def natural_down(chunks):
    tiles = [t.reshape(4, 8, 96, 2, 128) for t in chunks]
    return jnp.stack(tiles, axis=0).transpose(2, 0, 5, 1, 4, 3).reshape(-1, 768)


def tree_sum(terms):
    while len(terms) > 1:
        terms = [terms[k] + terms[k + 1] for k in range(0, len(terms), 2)]
    return terms[0]


def sum_everywhere(links, here, away, stay, wait):
    if links.boxed:
        half = stay + links.swap(away, core=1)
        for axis in ("x", "y", "z"):
            step = 1
            while step < links.size[axis]:
                half = half + links.swap(half, **{axis: step})
                step *= 2
            if axis == "x":
                half = after(half, *wait)
        other = links.swap(half, core=1)
    else:
        first = jnp.where(here["core"] == 0, stay, away)
        second = jnp.where(here["core"] == 0, away, stay)
        return lax.psum(jnp.concatenate([first, second], axis=0), AXES)
    return jnp.where(
        here["core"] == 0, jnp.concatenate([half, other], axis=0), jnp.concatenate([other, half], axis=0)
    )


def whole(shape):
    return pl.BlockSpec(tuple(shape), lambda *_: (0,) * len(shape))


def kept(shape):
    return pl.BlockSpec(tuple(shape), lambda *_: (0,) * len(shape), pipeline_mode=pl.Buffered(1))


ANY = pl.BlockSpec(memory_space=pl.ANY)
FAR = pl.BlockSpec(memory_space=pltpu.HBM)
SCALARS = pl.BlockSpec(memory_space=pltpu.SMEM)


LIMITS = {"stack": 16, "arrange": 8, "fold": 24, "pack": 8, "prepare": 16, "bias": 16, "bias_back": 20, "project": 24, "attend": 18, "merge": 20, "feed": 28, "middle_back": 28, "attend_back": 22, "mixed_grad": 24, "start_back": 28}


def call(kernel, name, grid, ins, outs, scratch=(), flops=0, aliases=None):
    moved = sum(a.size * a.dtype.itemsize for a, *_ in ins)
    moved += sum(math.prod(s) * jnp.dtype(d).itemsize for s, d, *_ in outs)
    return pl.pallas_call(
        kernel,
        name=name,
        grid=grid,
        in_specs=[spec for _, spec, *_ in ins],
        out_specs=[spec for _, _, spec, *_ in outs],
        out_shape=[pltpu.HBM(s, d) if far else jax.ShapeDtypeStruct(s, d) for s, d, _, *far in outs],
        scratch_shapes=list(scratch),
        input_output_aliases=aliases or {},
        compiler_params=pltpu.CompilerParams(vmem_limit_bytes=LIMITS[name] * MIB),
        cost_estimate=pl.CostEstimate(flops=int(flops), bytes_accessed=int(moved), transcendentals=0),
    )(*[pltpu.with_memory_space_constraint(a, pltpu.HBM) if far else a for a, _, *far in ins])


def nn(a, b):
    return lax.dot_general(a, b, (((1,), (0,)), ((), ())), preferred_element_type=F32)


def nt(a, b):
    return lax.dot_general(a, b, (((1,), (1,)), ((), ())), preferred_element_type=F32)


def tn(a, b):
    return lax.dot_general(a, b, (((0,), (0,)), ((), ())), preferred_element_type=F32)


def arrange(blocks, split):
    rows, cols = blocks[0].shape
    count = len(blocks)

    def kernel(*refs):
        for k in range(count):
            refs[count][k] = refs[k][:, :split]
            refs[count + 1][k] = refs[k][:, split:]

    return call(
        kernel, "arrange", (),
        [(b, whole(b.shape)) for b in blocks],
        [((count, rows, part), BF16, whole((count, rows, part))) for part in (split, cols - split)],
    )


def stack(parts):
    flat = [v for part in parts for v in part]
    outs = [(sum(v.shape[0] for v in part), part[0].shape[1], part[0].shape[2]) for part in parts]

    def kernel(*refs):
        number = 0
        for k, part in enumerate(parts):
            at = 0
            for v in part:
                refs[len(flat) + k][at : at + v.shape[0]] = refs[number][...]
                at += v.shape[0]
                number += 1

    return call(
        kernel, "stack", (), [(v, whole(v.shape)) for v in flat], [(shape, BF16, whole(shape)) for shape in outs]
    )


def regroup(parts, groups, far):
    flat = [v for part in parts for v in part]
    count, rows = sum(v.shape[0] for v in parts[0]), parts[0][0].shape[1]
    outs = [(count, rows, sum(end - begin for begin, end in group)) for group in groups]

    def kernel(*refs):
        for out, group in zip(refs[len(flat) :], groups, strict=True):
            number, col = 0, 0
            for part, (begin, end) in zip(parts, group, strict=True):
                at = 0
                for v in part:
                    if end > begin:
                        out[at : at + v.shape[0], :, col : col + end - begin] = refs[number][:, :, begin:end]
                    at += v.shape[0]
                    number += 1
                col += end - begin

    return call(
        kernel, "stack", (), [(v, whole(v.shape)) for v in flat],
        [(shape, BF16, whole(shape), FAR) if far else (shape, BF16, whole(shape)) for shape in outs],
    )


def fold(links, jobs):
    arrays, index = [], {}
    for sources, _ in jobs:
        for group, _ in sources:
            for array in group:
                if id(array) not in index:
                    index[id(array)] = len(arrays)
                    arrays.append(array)
    dims = {"x": 0, "z": 1, "z_high": 1, "z_low": 1, "y": 2}
    size = dict(links.size, z_high=2, z_low=2)
    held = {"x": 1, "y": 1, "z": 1, "z_high": links.z // 2, "z_low": 1}
    outs = []
    for sources, axis in jobs:
        first = sources[0][0][0]
        cols = sum(part[1] - part[0] for _, part in sources)
        shape = tuple(held[axis] if k == dims[axis] else first.shape[k] for k in range(4)) + (cols,)
        outs += [(shape, F32 if d == 0 else BF16, whole(shape)) for d in range(size[axis])]

    def kernel(*refs):
        me = links.place()
        me["z_high"], me["z_low"] = me["z"] // 2, me["z"] % 2
        at_out = len(arrays)
        for sources, axis in jobs:
            for d in range(size[axis]):
                where = [slice(None)] * 4
                where[dims[axis]] = pl.ds((me[axis] ^ d) * held[axis], held[axis])
                col = 0
                for group, (begin, end) in sources:
                    picked = tuple(where) + (slice(begin, end),)
                    total = refs[index[id(group[0])]][picked].astype(F32)
                    for array in group[1:]:
                        total = total + refs[index[id(array)]][picked].astype(F32)
                    out = refs[at_out]
                    out[..., col : col + end - begin] = total.astype(out.dtype)
                    col += end - begin
                at_out += 1

    results = call(kernel, "fold", (), [(a, whole(a.shape)) for a in arrays], outs)
    out = []
    for _, axis in jobs:
        out.append(results[: size[axis]])
        results = results[size[axis] :]
    return out


def pack(links, table, heads, start_sums, middle_sums, halves, sum_fc2, hidden_sums):
    width = table.shape[1]

    def kernel(table_ref, start_ref, middle_ref, q0, v0, q1, v1, fc2_ref, a_ref, b_ref, c_ref, away_ref, stay_ref, all_s):
        all_s[...] = jnp.zeros_like(all_s)
        rows = [(table_ref, heads), (start_ref, 3), (middle_ref, 5)]
        at = 0
        for ref, count in rows:
            for k in range(count):
                all_s[(at + k) // 16, (at + k) % 16 : (at + k) % 16 + 1, :] = ref[k : k + 1, :]
            at += count
        for pair in ((q0, q1), (v0, v1)):
            for k, ref in enumerate(pair):
                all_s[at // 16, at % 16 : at % 16 + 1, k * 384 : k * 384 + 384] = ref[...]
            at += 1
        all_s[at // 16, at % 16 : at % 16 + 1, :] = fc2_ref[...]
        at += 1
        for k, ref in enumerate((a_ref, b_ref, c_ref)):
            all_s[(at + k) // 16, (at + k) % 16 : (at + k) % 16 + 1, :] = ref[:, 0:width]
            all_s[(at + 3) // 16, (at + 3) % 16 : (at + 3) % 16 + 1, k * 256 : k * 256 + 256] = ref[:, width : width + 256]
        c = lax.axis_index("narrow") % 2
        away_ref[...] = all_s[1 - c]
        stay_ref[...] = all_s[c]

    operands = [table, start_sums, middle_sums, *halves[0], *halves[1], sum_fc2, *hidden_sums]
    return call(
        kernel, "pack", (), [(a, whole(a.shape)) for a in operands],
        [((16, width), F32, whole((16, width)))] * 2, [pltpu.VMEM((2, 16, width), F32)],
    )


def norm(values):
    centre = jnp.mean(values, axis=-1, keepdims=True)
    centred = values - centre
    spread = jnp.mean(centred * centred, axis=-1, keepdims=True)
    scaling = lax.rsqrt(spread + EPSILON)
    return centred * scaling, scaling


def norm_back(grad, normed, scaling, gain):
    scaled = grad * gain
    first = jnp.mean(scaled, axis=-1, keepdims=True)
    second = jnp.mean(scaled * normed, axis=-1, keepdims=True)
    return (scaled - first - normed * second) * scaling


def banded(tall, body):
    if BAND >= tall:
        body(slice(0, tall), 0)
        return

    def step(k, carry):
        at = pl.multiple_of(k * BAND, 8)
        body(pl.ds(at, BAND), at)
        return carry

    lax.fori_loop(0, tall // BAND, step, 0)


def column_sum(values):
    return jnp.sum(values, axis=0, keepdims=True)


TOKEN, GAIN1, SHIFT1, GAMMA2, BIAS1, GAMMA1, GAIN2, SHIFT2, BIAS2 = range(9)


def row_of(ref, k):
    return ref[k : k + 1, :]


def masked_rows(image, sizes_ref, patterns_ref, tall):
    bound, group = 0, 0
    for k in range(sizes_ref.shape[0] - 1):
        bound = bound + sizes_ref[k]
        group = group + (image >= bound).astype(jnp.int32)
    columns_of = patterns_ref[...].T
    which = lax.broadcasted_iota(jnp.int32, columns_of.shape, 1) == group
    return jnp.sum(jnp.where(which, columns_of, 0.0), axis=1, keepdims=True)[0:tall] > 0.5


def first_image(images):
    return lax.axis_index(AXES) * images


def prepare(sizes, inputs, cotangent, group_sizes, mask_patterns, vectors):
    images, length, tall, width = sizes
    rows = images * tall
    groups, patches = mask_patterns.shape

    def kernel(x_ref, g_ref, sizes_ref, mask_ref, *refs):
        vector_refs, refs = refs[: len(vectors)], refs[len(vectors) :]
        h0_ref, n1_ref, g_out, df_ref, sum_ref, params_ref, patterns_ref, x_s, g_s, mask_s, sems, *vector_s = refs
        step = pl.program_id(0)

        @pl.when(step == 0)
        def _():
            x_s[...] = jnp.zeros_like(x_s)
            g_s[...] = jnp.zeros_like(g_s)
            sum_ref[...] = jnp.zeros_like(sum_ref)
            params_ref[...] = jnp.zeros_like(params_ref)
            patterns_ref[...] = jnp.zeros_like(patterns_ref)
            moves = [pltpu.make_async_copy(mask_ref, mask_s, sems.at[len(vectors)])]
            moves += [
                pltpu.make_async_copy(a, b, sems.at[k]) for k, (a, b) in enumerate(zip(vector_refs, vector_s, strict=True))
            ]
            for move in moves:
                move.start()
            for move in moves:
                move.wait()
            patterns_ref[0:groups, 1 : patches + 1] = mask_s[...].astype(F32)
            for k, ref in zip(vectors, vector_s, strict=True):
                params_ref[k : k + 1, :] = ref[...].reshape(1, width)

        x_s[0:length, :] = x_ref[0].astype(F32)
        g_s[0:length, :] = g_ref[0].astype(F32)
        masked = masked_rows(first_image(images) + step, sizes_ref, patterns_ref, tall)
        start = jnp.where(masked, row_of(params_ref, TOKEN), x_s[...])
        h0_ref[...] = start
        normed, _ = norm(start)
        n1_ref[...] = (normed * row_of(params_ref, GAIN1) + row_of(params_ref, SHIFT1)).astype(BF16)
        g = g_s[...]
        g_out[...] = g.astype(BF16)
        df = row_of(params_ref, GAMMA2) * g
        df_ref[...] = df.astype(BF16)
        sum_ref[...] += column_sum(df)

    image = pl.BlockSpec((1, length, width), lambda i: (i, 0, 0))
    band = pl.BlockSpec((tall, width), lambda i: (i, 0))
    return call(
        kernel, "prepare", (images,),
        [(inputs, image), (cotangent, image), (group_sizes, SCALARS), (mask_patterns, ANY, FAR)]
        + [(v, ANY, FAR) for v in vectors.values()],
        [((rows, width), F32, band), ((rows, width), BF16, band), ((rows, width), BF16, band, FAR),
         ((rows, width), BF16, band, FAR), ((1, width), F32, whole((1, width))), ((16, width), F32, whole((16, width))),
         ((8, 256), F32, whole((8, 256)))],
        [pltpu.VMEM((tall, width), F32), pltpu.VMEM((tall, width), F32), pltpu.VMEM(mask_patterns.shape, jnp.int32),
         pltpu.SemaphoreType.DMA((len(vectors) + 1,))] + [pltpu.VMEM((width,), F32) for _ in vectors],
        flops=rows * width * 40,
    )


def table_columns(grid_side, broad):
    side = 2 * grid_side - 1
    q = np.arange(broad)
    entry = (q // grid_side) * side + q % grid_side + grid_side - 1
    return jnp.asarray(np.where(q < side * grid_side, entry, -(1 << 20)).astype(np.int32)[None])


def three_parts(values):
    high = values.astype(BF16)
    rest = values - high.astype(F32)
    middle = rest.astype(BF16)
    return high, middle, (rest - middle.astype(F32)).astype(BF16)


def bias_kernel(table_t, entry, grid_side, tall, broad):
    heads = table_t.shape[0]
    length = grid_side * grid_side + 1
    wide = entry.shape[1]
    inner = (2 * grid_side - 1) ** 2

    def kernel(table_ref, entry_ref, out_ref, *halves):
        def put(at, count, values):
            for half, ref in enumerate(halves):
                ref[pl.ds(at, count), :] = values[:, 128 * half : 128 * half + 128]

        parts = jnp.concatenate(three_parts(table_ref[...]), axis=0)
        left, top, corner = (table_ref[:, inner + 1 : inner + 2], table_ref[:, inner : inner + 1],
                             table_ref[:, inner + 2 : inner + 3])
        lane = lax.broadcasted_iota(jnp.int32, (heads, broad), 1)

        def column(b, carry):
            which = lax.broadcasted_iota(jnp.int32, (table_ref.shape[1], wide), 0) + b
            select = jnp.where(which == entry_ref[...], 1.0, 0.0).astype(BF16)
            spread = nn(parts, select)
            spread = spread[:heads] + spread[heads : 2 * heads] + spread[2 * heads :]
            for a in range(grid_side):
                shift = (grid_side - 1 - a) * grid_side - 1
                moved = pltpu.roll(spread, (wide - shift) % wide, 1)[:, :broad]
                moved = jnp.where(lane == 0, top, moved)
                put(pl.multiple_of((1 + grid_side * a + b) * heads, 16), heads, moved)
            return carry

        lax.fori_loop(0, grid_side, column, 0)
        put(0, heads, jnp.where(lane == 0, corner, left))
        rest = (tall - length) * heads
        put(length * heads, rest, jnp.full((rest, broad), NEVER, F32))
        for h in range(out_ref.shape[0]):
            for half, ref in enumerate(halves):
                out_ref[h, :, 128 * half : 128 * half + 128] = ref[pl.ds(h, tall, stride=heads), :]

    return call(
        kernel, "bias", (),
        [(table_t, whole(table_t.shape)), (entry, whole(entry.shape))],
        [((12, tall, broad), F32, whole((12, tall, broad)))],
        [pltpu.VMEM((tall * heads, 128), F32)] * (broad // 128),
        flops=2 * 48 * 768 * wide * grid_side,
    )[0]


def bias_back_kernel(terms, entry, grid_side, width):
    count, tall, broad = terms.shape
    heads = 16
    wide = entry.shape[1]
    inner = (2 * grid_side - 1) ** 2
    length = grid_side * grid_side + 1

    def kernel(terms_ref, entry_ref, out_ref, *halves):
        def get(at, count):
            return jnp.concatenate([ref[pl.ds(at, count), :] for ref in halves], axis=1)

        lane = lax.broadcasted_iota(jnp.int32, (heads, broad), 1)
        inside = (lane >= 1) & (lane < length)
        for h in range(heads):
            values = terms_ref[h] if h < count else jnp.zeros((tall, broad), F32)
            for half, ref in enumerate(halves):
                ref[pl.ds(h, tall, stride=heads), :] = values[:, 128 * half : 128 * half + 128]

        def column(b, carry):
            total, edge = carry
            which = lax.broadcasted_iota(jnp.int32, (width, wide), 0) + b
            select = jnp.where(which == entry_ref[...], 1.0, 0.0).astype(BF16)
            spread = jnp.zeros((heads, wide), F32)
            for a in range(grid_side):
                shift = (grid_side - 1 - a) * grid_side - 1
                found = get(pl.multiple_of((1 + grid_side * a + b) * heads, 16), heads)
                edge = edge + jnp.where(lane == 0, found, 0.0)
                found = jnp.where(inside, found, 0.0)
                found = jnp.concatenate([found, jnp.zeros((heads, wide - broad), F32)], axis=1)
                spread = spread + pltpu.roll(found, shift % wide, 1)
            found = nt(jnp.concatenate(three_parts(spread), axis=0), select)
            total = total + found[:heads] + found[heads : 2 * heads] + found[2 * heads :]
            return total, edge

        total, edge = lax.fori_loop(
            0, grid_side, column, (jnp.zeros((heads, width), F32), jnp.zeros((heads, broad), F32))
        )
        first = get(0, heads)
        top = jnp.sum(edge, axis=1, keepdims=True)
        left = jnp.sum(jnp.where(inside, first, 0.0), axis=1, keepdims=True)
        corner = first[:, 0:1]
        place = lax.broadcasted_iota(jnp.int32, (heads, width), 1)
        total = jnp.where(place == inner, top, total)
        total = jnp.where(place == inner + 1, left, total)
        out_ref[...] = jnp.where(place == inner + 2, corner, total)

    return call(
        kernel, "bias_back", (),
        [(terms, whole(terms.shape)), (entry, whole(entry.shape))],
        [((heads, width), F32, whole((heads, width)))],
        [pltpu.VMEM((tall * heads, 128), F32)] * (broad // 128),
        flops=2 * 48 * 768 * wide * grid_side,
    )[0]


def project(sizes, first_low, weight, params, score_scale):
    images, length, tall, width = sizes
    rows = images * tall
    cols = 3 * width
    count = len(weight.operands)

    def kernel(*refs):
        n1_ref, params_ref = refs[:2]
        out_ref, w_s, sem = refs[2 + count :]
        step = pl.program_id(0)

        @pl.when(step == 0)
        def _():
            weight.fill(refs[2 : 2 + count], w_s, sem)
            weight.wait(w_s, sem)

        w = w_s[:, pl.ds(pl.multiple_of(step * width, 128), width)]
        scale = jnp.where(step == 0, score_scale, 1.0)
        out_ref[...] = ((nn(n1_ref[...], w) + params_ref[pl.ds(9 + step, 1), :]) * scale).astype(BF16)

    return call(
        kernel, "project", (cols // width,),
        [(first_low, kept((rows, width))), (params, kept(params.shape))] + [(a, ANY) for a in weight.operands],
        [((rows, cols), BF16, pl.BlockSpec((rows, width), lambda t: (0, t)))],
        [pltpu.VMEM((width, cols + weight.extra), BF16), pltpu.SemaphoreType.DMA],
        flops=2 * rows * width * cols,
    )[0]


def head_masks(tall):
    lane = lax.broadcasted_iota(jnp.int32, (tall, 128), 1)
    return [lane < 64, lane >= 64]


def attend(sizes, mixed, bias, first, pairs):
    images, length, tall, width = sizes
    rows = images * tall
    every = width // 128
    broad = bias.shape[2]

    def kernel(q_ref, k_ref, v_ref, bias_ref, out_ref, p_ref):
        masks = head_masks(tall)
        units = [(i, h) for i in range(images) for h in range(2)]
        scores, probs = [], []
        for i, h in units:
            q, k = q_ref[tall * i : tall * i + tall, :], k_ref[tall * i : tall * i + tall, :]
            scores.append(nt(k, jnp.where(masks[h], q, jnp.zeros_like(q))) + bias_ref[h, :, 0:tall])
        for (i, h), s in zip(units, scores, strict=True):
            e = jnp.exp(s - jnp.max(s, axis=0, keepdims=True))
            p = (e * (1.0 / jnp.sum(e, axis=0, keepdims=True))).astype(BF16)
            p_ref[h, i, :, 0:tall] = p
            probs.append(p)
        for i in range(images):
            vt = v_ref[tall * i : tall * i + tall, :].T
            out = [nn(vt[64 * h : 64 * h + 64, :], probs[2 * i + h]) for h in range(2)]
            out_ref[tall * i : tall * i + tall, :] = jnp.concatenate(out, axis=0).T.astype(BF16)

    def column(at):
        return pl.BlockSpec((rows, 128), lambda t: (0, at + t))

    return call(
        kernel, "attend", (pairs,),
        [(mixed, column(first)), (mixed, column(every + first)), (mixed, column(2 * every + first)),
         (bias, pl.BlockSpec((2, tall, broad), lambda t: (first + t, 0, 0)))],
        [((rows, 128 * pairs), BF16, column(0), FAR),
         ((2 * pairs, images, tall, broad), BF16,
          pl.BlockSpec((2, images, tall, broad), lambda t: (t, 0, 0, 0)), FAR)],
        flops=4 * rows * tall * 128 * pairs,
    )


def attend_back(sizes, mixed, probs, grad_out, score_scale, first, pairs, so_far):
    images, length, tall, width = sizes
    rows = images * tall
    every = width // 128
    broad = probs.shape[3]

    def kernel(q_ref, k_ref, v_ref, do_ref, p_ref, *refs):
        grad_ref, terms_ref, qb_ref, vb_ref = refs[-4:]
        masks = head_masks(tall)
        units = [(i, h) for i in range(images) for h in range(2)]

        def part(ref, i):
            return ref[tall * i : tall * i + tall, :]

        def own(value, h):
            return jnp.where(masks[h], value, jnp.zeros_like(value))

        grads = [nt(part(v_ref, i), own(part(do_ref, i), h)) for i, h in units]
        lows = []
        for (i, h), grad in zip(units, grads, strict=True):
            p = p_ref[h, i, :, 0:tall].astype(F32)
            t = p * grad
            lows.append((t - p * jnp.sum(t, axis=0, keepdims=True)).astype(BF16))
        for h in range(2):
            terms_ref[h, :, 0:tall] = sum(lows[2 * i + h].astype(F32) for i in range(images))
            terms_ref[h, :, tall:] = jnp.zeros((tall, broad - tall), F32)
        query_sum, value_sum = 0.0, 0.0
        for i in range(images):
            kt = part(k_ref, i).T
            dv = sum(nn(p_ref[h, i, :, 0:tall], own(part(do_ref, i), h)) for h in range(2))
            dk = sum(nn(lows[2 * i + h], own(part(q_ref, i), h)) for h in range(2))
            dq = jnp.concatenate(
                [nn(kt[64 * h : 64 * h + 64, :], lows[2 * i + h]) for h in range(2)], axis=0
            ).T * score_scale
            for number, grad in enumerate((dq, dk, dv)):
                grad_ref[number, tall * i : tall * i + tall, :] = grad.astype(BF16)
            query_sum += column_sum(dq)
            value_sum += column_sum(dv)
        qb_ref[...] = query_sum
        vb_ref[...] = value_sum

    def column(at):
        return pl.BlockSpec((rows, 128), lambda t: (0, at + t))

    one = pl.BlockSpec((1, 128), lambda t: (0, t))
    return call(
        kernel, "attend_back", (pairs,),
        [(mixed, column(first)), (mixed, column(every + first)), (mixed, column(2 * every + first)),
         (grad_out, column(first)),
         (probs, pl.BlockSpec((2, images, tall, broad), lambda t: (first + t, 0, 0, 0)), FAR)]
        + ([] if so_far is None else [(so_far, ANY)]),
        [((3, rows, width), BF16, pl.BlockSpec((3, rows, 128), lambda t: (0, 0, first + t)))]
        + [((2 * pairs, tall, broad), F32, pl.BlockSpec((2, tall, broad), lambda t: (t, 0, 0))),
           ((1, 128 * pairs), F32, one), ((1, 128 * pairs), F32, one)],
        flops=8 * rows * tall * 128 * pairs,
        aliases={} if so_far is None else {5: 0},
    )


def merge(sizes, attended, start, weight, params):
    images, length, tall, width = sizes
    rows = images * tall
    count = len(weight.operands)

    def kernel(*refs):
        att_refs, refs = refs[: len(attended)], refs[len(attended) :]
        h0_ref, params_ref = refs[:2]
        h1_ref, n2_ref, w_s, out_s, sem = refs[2 + count :]
        step = pl.program_id(0)

        @pl.when(step == 0)
        def _():
            weight.fill(refs[2 : 2 + count], w_s, sem)
            weight.wait(w_s, sem)
            part = width // len(attended)
            out_s[...] = sum(nn(r[...], w_s[part * k : part * k + part, 0:width]) for k, r in enumerate(att_refs))

        @pl.when(step > 0)
        def _():
            def body(at, first):
                out = out_s[pl.ds(pl.multiple_of((step - 1) * tall + first, 8), min(BAND, tall)), :]
                middle = h0_ref[at, :] + row_of(params_ref, GAMMA1) * (out + row_of(params_ref, BIAS1))
                h1_ref[at, :] = middle
                normed, _ = norm(middle)
                n2_ref[at, :] = (normed * row_of(params_ref, GAIN2) + row_of(params_ref, SHIFT2)).astype(BF16)

            banded(tall, body)

    band = pl.BlockSpec((tall, width), lambda i: (jnp.maximum(i - 1, 0), 0))
    return call(
        kernel, "merge", (images + 1,),
        [(a, kept(a.shape), FAR) for a in attended]
        + [(start, band), (params, kept(params.shape))]
        + [(a, ANY, FAR) for a in weight.operands],
        [((rows, width), F32, band), ((rows, width), BF16, band)],
        [pltpu.VMEM((width, width + weight.extra), BF16), pltpu.VMEM((rows, width), F32),
         pltpu.SemaphoreType.DMA],
        flops=2 * rows * width * width,
    )


def part_by_core(store, away_ref, stay_ref):
    c = lax.axis_index("narrow") % 2
    for x in range(2):
        away_ref[x] = store[2 * x + 1 - c]
        stay_ref[x] = store[2 * x + c]


def feed(sizes, second_low, down_low, up, down, bias, sums, last):
    images, length, tall, width = sizes
    rows = images * tall
    shared = up.operands[0] is down.operands[0]
    far = () if last else (FAR,)
    ups, downs = len(up.operands), 0 if shared else len(down.operands)
    carried = [] if sums is None else list(sums)

    def kernel(*refs):
        n2_ref, df_ref, bias_ref = refs[:3]
        rest = refs[3:]
        up_refs, rest = rest[:ups], rest[ups:]
        down_refs, rest = (up_refs if shared else rest[:downs]), rest[downs:]
        sum_refs, rest = rest[: len(carried)], rest[len(carried) :]
        f_ref, dn_ref, away_ref, stay_ref, gbias_ref, up_s, down_s, grad_s, sems = rest
        step = pl.program_id(0)

        @pl.when(step == 0)
        def _():
            up.fill(up_refs, up_s, sems.at[0])
            down.fill(down_refs, down_s, sems.at[1])
            if carried:
                pltpu.make_async_copy(sum_refs[0], f_ref, sems.at[2]).start()
                pltpu.make_async_copy(sum_refs[1], dn_ref, sems.at[3]).start()
            up.wait(up_s, sems.at[0])
            down.wait(down_s, sems.at[1])
            if not carried:
                f_ref[...] = jnp.zeros_like(f_ref)
                dn_ref[...] = jnp.zeros_like(dn_ref)

        at = pl.ds(pl.multiple_of(step * TILE, TILE), TILE)
        up_w, down_w = up_s[:, at], down_s[:, at]
        u = nn(n2_ref[...], up_w) + bias_ref[...]
        dz = nn(df_ref[...], down_w)
        bell = jnp.exp(-0.5 * u * u)
        below = 0.5 * (1.0 + lax.erf(u * ROOT_HALF))
        z = (u * below).astype(BF16)
        du = dz * (below + u * (DENSITY * bell))
        gbias_ref[...] = column_sum(du)
        du = du.astype(BF16)
        grad = tn(n2_ref[...], du).astype(BF16)
        for k in range(TILE // 256):
            grad_s[step * (TILE // 256) + k, :, :, 0:256] = grad[:, 256 * k : 256 * k + 256].reshape(8, 96, 256)
        grad = tn(df_ref[...], z).astype(BF16)
        for n in range(4):
            for w in range(TILE // 128):
                for half in range(2):
                    grad_s[n, step * (TILE // 128) + w, :, 256 + 128 * half : 384 + 128 * half] = grad[
                        192 * n + 96 * half : 192 * n + 96 * half + 96, 128 * w : 128 * w + 128
                    ]
        if carried:
            @pl.when(step == 0)
            def _():
                pltpu.make_async_copy(sum_refs[0], f_ref, sems.at[2]).wait()
                pltpu.make_async_copy(sum_refs[1], dn_ref, sems.at[3]).wait()

        f_ref[...] += nt(z, down_w)
        dn_ref[...] += nt(du, up_w)

        @pl.when(step == CHUNK // TILE - 1)
        def _():
            part_by_core(grad_s, away_ref, stay_ref)

    tile = pl.BlockSpec((1, TILE), lambda t: (0, t))
    full = whole((rows, width))
    shape = (2, 8, 96, 512)
    return call(
        kernel, "feed", (CHUNK // TILE,),
        [(second_low, kept((rows, width))), (down_low, kept((rows, width))), (bias, tile)]
        + [(a, ANY, FAR) for a in up.operands + ([] if shared else down.operands) + carried],
        [((rows, width), F32, kept((rows, width)), *far), ((rows, width), F32, kept((rows, width)), *far),
         (shape, BF16, kept(shape)), (shape, BF16, kept(shape)), ((1, CHUNK), F32, tile)],
        [pltpu.VMEM((width, CHUNK), BF16), pltpu.VMEM((width, CHUNK), BF16), pltpu.VMEM((4, 8, 96, 512), BF16),
         pltpu.SemaphoreType.DMA((4,))],
        flops=12 * rows * width * CHUNK,
    )


def middle_back(sizes, attended, branch, grad_n2, middle, start, upstream, weight, params):
    images, length, tall, width = sizes
    rows = images * tall
    count = len(weight.operands)

    def kernel(*refs):
        att_refs, refs = refs[: len(attended)], refs[len(attended) :]
        f_ref, dn_ref, h1_ref, h0_ref, g_ref, params_ref = refs[:6]
        out_ref, dh_ref, do_ref, away_ref, stay_ref, sum_ref, w_s, da_s, grad_s, layer_s, sem = refs[6 + count :]
        step = pl.program_id(0)

        @pl.when(step == 0)
        def _():
            weight.fill(refs[6 : 6 + count], w_s, sem)
            sum_ref[...] = jnp.zeros_like(sum_ref)

        @pl.when(step < images)
        def _():
            def body(at, first):
                f = f_ref[at, :] + row_of(params_ref, BIAS2)
                h1 = h1_ref[at, :]
                g = g_ref[at, :].astype(F32)
                layer_s[at, :] = h1 + row_of(params_ref, GAMMA2) * f
                normed, scaling = norm(h1)
                dn = dn_ref[at, :]
                dh = g + norm_back(dn, normed, scaling, row_of(params_ref, GAIN2))
                dh_ref[at, :] = dh
                da = row_of(params_ref, GAMMA1) * dh
                sum_ref[0:1, :] += column_sum(g * f)
                sum_ref[1:2, :] += column_sum(dn * normed)
                sum_ref[2:3, :] += column_sum(dn)
                sum_ref[3:4, :] += column_sum(dh * (h1 - h0_ref[at, :]))
                sum_ref[4:5, :] += column_sum(da)
                da_s[pl.ds(pl.multiple_of(step * tall + first, 8), min(BAND, tall)), :] = da.astype(BF16)

            banded(tall, body)
            out_ref[0] = layer_s[0:length, :].astype(BF16)

        @pl.when(step == images)
        def _():
            sum_ref[3:4, :] = sum_ref[3:4, :] / row_of(params_ref, GAMMA1)
            weight.wait(w_s, sem)
            do_ref[...] = nt(da_s[...], w_s[:, 0:width]).astype(BF16)
            grad = jnp.concatenate([tn(r[...], da_s[...]) for r in att_refs], axis=0).astype(BF16)
            for n, at in enumerate((0, 128, 384, 512)):
                grad_s[n] = grad[:, at : at + 256].reshape(8, 96, 256)
            part_by_core(grad_s, away_ref, stay_ref)

    def at(i):
        return jnp.minimum(i, images - 1)

    band = pl.BlockSpec((tall, width), lambda i: (at(i), 0))
    shape = (2, 8, 96, 256)
    return call(
        kernel, "middle_back", (images + 1,),
        [(a, kept(a.shape), FAR) for a in attended]
        + [(a, band) for a in (branch, grad_n2, middle, start)] + [(a, band, FAR) for a in (upstream,)] + [(params, kept(params.shape))]
        + [(a, ANY, FAR) for a in weight.operands],
        [((images, length, width), BF16, pl.BlockSpec((1, length, width), lambda i: (at(i), 0, 0))),
         ((rows, width), F32, band), ((rows, width), BF16, whole((rows, width))),
         (shape, BF16, whole(shape)), (shape, BF16, whole(shape)), ((8, width), F32, whole((8, width)))],
        [pltpu.VMEM((width, width + weight.extra), BF16), pltpu.VMEM((rows, width), BF16),
         pltpu.VMEM((4, 8, 96, 256), BF16), pltpu.VMEM((tall, width), F32), pltpu.SemaphoreType.DMA],
        flops=4 * rows * width * width,
    )


def mixed_grad(sizes, first_low, grads):
    images, length, tall, width = sizes
    rows = images * tall

    def kernel(n1_ref, grad_ref, away_ref, stay_ref):
        step = pl.program_id(0)
        c = lax.axis_index("narrow") % 2
        n = 2 * (step % 2) + jnp.where(step < 2, 1 - c, c)
        main = grad_ref[at_least(n, (0, 1, 1, 2)), :, pl.ds(pl.multiple_of(at_least(n, (0, 0, 384, 384)), 128), 384)]
        side = grad_ref[at_least(n, (0, 0, 2, 2)), :, pl.ds(pl.multiple_of(at_least(n, (384, 512, 0, 128)), 128), 256)]
        main = tn(n1_ref[...], main).astype(BF16).reshape(8, 96, 384)
        side = tn(n1_ref[...], side).astype(BF16).reshape(8, 96, 256)
        for role, ref in enumerate((away_ref, stay_ref)):
            @pl.when(step // 2 == role)
            def _(ref=ref):
                ref[0, :, :, 0:384] = main
                ref[0, :, :, 384:640] = side

    shape = (2, 8, 96, 640)
    return call(
        kernel, "mixed_grad", (4,),
        [(first_low, kept((rows, width))), (grads, kept(grads.shape))],
        [(shape, BF16, pl.BlockSpec((1, 8, 96, 640), lambda t: (jnp.minimum(t, 1), 0, 0, 0))),
         (shape, BF16, pl.BlockSpec((1, 8, 96, 640), lambda t: (jnp.maximum(t - 2, 0), 0, 0, 0)))],
        flops=6 * rows * width * width,
    )


def start_back(sizes, grads, weight, start, grad_middle, group_sizes, patterns, params):
    images, length, tall, width = sizes
    rows = images * tall
    count = len(weight.operands)

    def kernel(*refs):
        grad_ref, h0_ref, dh_ref, sizes_ref, patterns_ref, params_ref = refs[:6]
        out_ref, sum_ref, w_s, dn_s, out_s, sem = refs[6 + count :]
        step = pl.program_id(0)

        @pl.when(step == 0)
        def _():
            weight.fill(refs[6 : 6 + count], w_s, sem)
            sum_ref[...] = jnp.zeros_like(sum_ref)
            dn_s[...] = jnp.zeros_like(dn_s)
            weight.wait(w_s, sem)

        @pl.when(step < 3)
        def _():
            dn_s[...] += nt(grad_ref[0], w_s[:, pl.ds(pl.multiple_of(step * width, 128), width)])

        @pl.when(step > 2)
        def _():
            masked = masked_rows(first_image(images) + step - 3, sizes_ref, patterns_ref, tall)

            def body(at, first):
                dn = dn_s[pl.ds(pl.multiple_of((step - 3) * tall + first, 8), min(BAND, tall)), :]
                normed, scaling = norm(h0_ref[at, :])
                dh = dh_ref[at, :] + norm_back(dn, normed, scaling, row_of(params_ref, GAIN1))
                out_s[at, :] = jnp.where(masked, 0.0, dh)
                sum_ref[0:1, :] += column_sum(dn * normed)
                sum_ref[1:2, :] += column_sum(dn)
                sum_ref[2:3, :] += column_sum(jnp.where(masked, dh, 0.0))

            banded(tall, body)
            out_ref[0] = out_s[0:length, :]

    def at(i):
        return jnp.maximum(i - 3, 0)

    band = pl.BlockSpec((tall, width), lambda i: (at(i), 0))
    return call(
        kernel, "start_back", (images + 3,),
        [(grads, pl.BlockSpec((1, rows, width), lambda i: (jnp.minimum(i, 2), 0, 0)))]
        + [(start, band), (grad_middle, band), (group_sizes, SCALARS), (patterns, kept(patterns.shape)),
           (params, kept(params.shape))]
        + [(a, ANY) for a in weight.operands],
        [((images, length, width), F32, pl.BlockSpec((1, length, width), lambda i: (at(i), 0, 0))),
         ((8, width), F32, whole((8, width)))],
        [pltpu.VMEM((width, 3 * width + weight.extra), BF16), pltpu.VMEM((rows, width), F32),
         pltpu.VMEM((tall, width), F32), pltpu.SemaphoreType.DMA],
        flops=6 * rows * width * width,
    )


def local(
    links,
    inputs,
    cotangent,
    group_sizes,
    mask_patterns,
    mask_token,
    norm1_gain,
    norm1_bias,
    qkv_weight,
    query_bias,
    value_bias,
    bias_table,
    proj_weight,
    proj_bias,
    gamma_attn,
    norm2_gain,
    norm2_bias,
    fc1_weight,
    fc1_bias,
    fc2_weight,
    fc2_bias,
    gamma_mlp,
):
    images, length, width = inputs.shape
    table_rows, heads = bias_table.shape
    grid_side = math.isqrt(length - 1)
    group_count = mask_patterns.shape[0]
    tall = -(-length // 8) * 8
    rows = images * tall
    hidden = fc1_bias.shape[0]
    chunks = hidden // CHUNK
    sizes = (images, length, tall, width)
    score_scale = (width // heads) ** (-0.5)
    here = links.place()

    vectors = {
        TOKEN: mask_token, GAIN1: norm1_gain, SHIFT1: norm1_bias, GAMMA2: gamma_mlp, BIAS1: proj_bias,
        GAMMA1: gamma_attn, GAIN2: norm2_gain, SHIFT2: norm2_bias, BIAS2: fc2_bias, 9: query_bias, 11: value_bias,
    }

    boxed = links.boxed
    fc2_t = fc2_weight.T
    if boxed:
        mix = Gather(links, qkv_block(here, qkv_weight), 384, [((0, 384), (0, 256))])
        side = align_side(here, proj_weight)
        near = Gather(
            links,
            jnp.concatenate(
                [side[:, :128], up_block(fc1_weight, 0), down_block(fc2_t, 0), side[:, 128:]], axis=1
            ),
            384,
            [((0, 128), (256, 384)), ((128, 384), (0, 256))],
        )
        far = Gather(
            links,
            jnp.concatenate(
                [up_block(fc1_weight, 1), up_block(fc1_weight, 2), down_block(fc2_t, 1), down_block(fc2_t, 2)],
                axis=1,
            ),
            512,
            [((0, 256), (0, 256)), ((256, 512), (256, 512))],
        )
        full_up = full_down = None
    else:
        mix = near = far = None
        full_up, full_down = native_gather(fc1_weight), native_gather(fc2_weight).T

    entry = table_columns(grid_side, 384)

    def behind(value, *exchanges):
        return after(value, *[v for e in exchanges for v in e.sent]) if boxed else value

    def met(value, *exchanges):
        return [value] + [v for e in exchanges for v in e.flying]

    if boxed:
        mix.first()
    start, first_low, upstream, down_low, sum_fc2, params, patterns = prepare(
        sizes, inputs, cotangent, group_sizes, mask_patterns, vectors
    )
    if boxed:
        gap = met(first_low, mix)
        mix.second(*gap)
        near.first(*gap)
    table_t = jnp.pad(after(bias_table, first_low).T, ((0, 16 - heads), (0, width - table_rows)))
    bias = bias_kernel(behind(table_t, mix), entry, grid_side, tall, 256)
    if boxed:
        mix.third(*met(bias, mix))
        mix.fourth(False, *met(bias, near))
        near.second(*mix.sent)
    qkv = qkv_operands(links, mix, qkv_weight)
    mixed = project(sizes, behind(first_low, near), qkv, params, score_scale)
    if boxed:
        gap = met(mixed, near)
        near.third(*gap)
        far.first(*gap)
    attended, probs = attend(sizes, behind(mixed, near), bias, 0, width // 128)
    if boxed:
        near.fourth(False, *met(attended, far))
        far.second(*near.sent)
    proj = proj_operands(links, near, proj_weight)
    middle, second_low = merge(sizes, [attended], behind(start, far), proj, params)
    if boxed:
        far.third(*met(second_low, far))

    fc1_groups = fc1_bias.reshape(8, chunks, 128)
    ups = [up_operands(links, near, 1, full_up, 0), None, None]
    downs = [down_operands(links, near, 1, full_down, 0), None, None]
    halves = [[(0, (0, 256))], [(0, (256, 512))]]
    sums, pairs_out, hidden_sums = None, [], []
    waves = [Scatter(links, here, 256), Scatter(links, here, 256), Scatter(links, here, 512)]
    second_here = behind(second_low, far)
    for k in range(chunks):
        branch, grad_n2, away, stay, hidden_sum = feed(
            sizes, second_here, down_low, ups[k], downs[k], fc1_groups[:, k].reshape(1, -1), sums, k == chunks - 1
        )
        if k == 0:
            if boxed:
                far.fourth(True, *met(away, far))
                waves[0].first(after(away, *far.sent), stay)
            ups[1:] = [up_operands(links, far, 0, full_up, 1), up_operands(links, far, 1, full_up, 2)]
            downs[1:] = [down_operands(links, far, 0, full_down, 1), down_operands(links, far, 1, full_down, 2)]
            second_here = second_low
        elif k == 1 and boxed:
            exchange(links, [away], (waves[0], "second", halves))
            waves[1].first(after(away, *waves[0].sent), stay)
            second_here = behind(second_low, waves[0])
        elif boxed:
            exchange(links, [away], (waves[0], "third", None), (waves[1], "second", halves))
            waves[2].first(after(away, *waves[1].sent), stay)
        sums = (branch, grad_n2)
        pairs_out.append((away, stay))
        hidden_sums.append(hidden_sum)

    layer_out, grad_middle, grad_att, proj_away, proj_stay, middle_sums = middle_back(
        sizes, [attended], behind(branch, waves[0], waves[1]), grad_n2, middle, start, upstream, proj, params
    )
    if boxed:
        exchange(links, [grad_att], (waves[0], "halves", None), (waves[1], "third", None))
        waves[2].first(after(proj_away, *waves[1].sent), proj_stay)

    back, grads = [], None
    for number, (first, pairs) in enumerate(((0, 3), (3, 3))):
        grad_here = behind(grad_att, *(waves[:2] if number == 0 else waves[1:]))
        grads, *rest = attend_back(sizes, mixed, probs, grad_here, score_scale, first, pairs, grads)
        back.append(rest)
        if boxed and number == 0:
            exchange(
                links, [grads], (waves[0], "fifth", None), (waves[1], "halves", None),
                (waves[2], "second", [[(1, (0, 256)), (0, (0, 128))], [(0, (128, 512))]]),
            )
    if boxed:
        gap_grads = met(grads, waves[0])
        exchange(links, gap_grads, (waves[1], "fifth", None), (waves[2], "third", None))
    mix_away, mix_stay = mixed_grad(sizes, behind(first_low, waves[2]), grads)
    last = Scatter(links, here, 384)
    terms = jnp.concatenate([b[0] for b in back], axis=0)
    if boxed:
        gap_mix = met(mix_away, waves[1])
        exchange(links, gap_mix, (waves[2], "halves", None))
        last.first(after(mix_away, *waves[2].sent), mix_stay)
    grad_table = bias_back_kernel(after(behind(terms, waves[2]), mix_away), entry, grid_side, width)
    if boxed:
        exchange(links, [grad_table], (last, "second", [[(0, (0, 384))], [(0, (384, 640))]]))
    input_grad, start_sums = start_back(
        sizes, grads, qkv, start, behind(grad_middle, last), group_sizes, patterns, params
    )
    small_away, small_stay = pack(
        links, grad_table, heads, start_sums, middle_sums, [b[1:] for b in back], sum_fc2, hidden_sums
    )
    if boxed:
        exchange(links, [start_sums], (last, "third", None), (waves[2], "fifth", None))
        small_away = after(small_away, *last.sent)
    small = sum_everywhere(links, here, small_away, small_stay, last.flying)
    if boxed:
        exchange(links, [], (last, "fourth", None))
        grad_qkv = qkv_home(here, last.done())
        blocks = [waves[0].done(*gap_grads), waves[1].done(*gap_mix), waves[2].done(*last.sent)]
        grad_proj = proj_home(here, blocks[2][:, 0:256])
        up_parts = [blocks[0][:, 0:256], blocks[1][:, 0:256], blocks[2][:, 256:512]]
        down_parts = [blocks[0][:, 256:512], blocks[1][:, 256:512], blocks[2][:, 512:768]]
        grad_fc1 = jnp.concatenate(
            [up_parts[k][:, 128 * half : 128 * half + 128] for half in range(2) for k in range(chunks)], axis=1
        )
        grad_fc2 = jnp.concatenate(
            [jnp.concatenate([p[:, :128], p[:, 128:]], axis=0) for p in down_parts], axis=1
        ).T
    else:
        tiles = [all_tiles(here, *pair) for pair in pairs_out]
        grad_qkv = native_scatter(natural_qkv(all_tiles(here, mix_away, mix_stay)))
        grad_proj = native_scatter(natural_proj(all_tiles(here, proj_away, proj_stay)))
        grad_fc1 = native_scatter(natural_up([t[..., :256] for t in tiles]))
        grad_fc2 = native_scatter(natural_down([t[..., 256:] for t in tiles]))
    at = heads
    hidden_rows = [
        jnp.concatenate([small[at + 11 + k], small[at + 14, 256 * k : 256 * k + 256]]).reshape(8, 128) for k in range(chunks)
    ]
    sum_fc1 = jnp.stack(hidden_rows, axis=1).reshape(-1)
    return (
        layer_out,
        input_grad,
        small[at + 2],
        small[at],
        small[at + 1],
        grad_qkv,
        small[at + 8],
        small[at + 9],
        small[:heads, :table_rows].T,
        grad_proj,
        small[at + 7],
        small[at + 6],
        small[at + 4],
        small[at + 5],
        grad_fc1,
        sum_fc1,
        grad_fc2,
        small[at + 10],
        small[at + 3],
    )


def solution(mesh):
    images = P(AXES, None, None)
    both = P("wide", "narrow")
    same = P()
    links = Links(mesh.shape["wide"], mesh.shape["narrow"])
    return jax.shard_map(
        functools.partial(local, links),
        mesh=mesh,
        in_specs=(
            images, images, same, same, same, same, same, both, same, same, same, both, same, same,
            same, same, both, same, both, same, same,
        ),
        out_specs=(
            images, images, same, same, same, both, same, same, same, both, same, same, same, same,
            both, same, both, same, same,
        ),
        check_vma=False,
    )
```

```python
import functools
import math

import jax
import jax.numpy as jnp
import numpy as np
from jax import lax
from jax.experimental import pallas as pl
from jax.experimental.pallas import tpu as pltpu
from jax.sharding import PartitionSpec as P

EPSILON = 1e-06
ROOT_HALF = 0.7071067811865476
DENSITY = 0.3989422804014327
BF16 = jnp.bfloat16
F32 = jnp.float32
AXES = ("wide", "narrow")
TILE = 512
BAND = 200
CHUNK = 1024
NEVER = -1e30
MIB = 1 << 20


class Links:
    def __init__(self, wide, narrow):
        self.wide, self.narrow = wide, narrow
        self.y = 1 << ((wide.bit_length() - 1) // 2)
        self.z = wide // self.y
        self.x = narrow // 2
        self.size = {"z": self.z, "y": self.y, "x": self.x, "core": 2}
        self.unit = {"core": 1, "x": 2, "y": narrow, "z": narrow * self.y}
        self.boxed = (self.z, self.y, self.x) == (4, 2, 2)

    def place(self):
        w, n = lax.axis_index("wide"), lax.axis_index("narrow")
        return {"z": w // self.y, "y": w % self.y, "x": n // 2, "core": n % 2, "w": w, "n": n}

    def swap(self, value, **offsets):
        mask = sum(self.unit[axis] * offset for axis, offset in offsets.items())
        count = self.wide * self.narrow
        return lax.ppermute(value, AXES, [(k, k ^ mask) for k in range(count)])

    def others(self, value, axis):
        return [self.swap(value, **{axis: d}) for d in range(1, self.size[axis])]


def pick(value, axis, index, count):
    size = value.shape[axis] // count
    return lax.dynamic_slice_in_dim(value, index * size, size, axis)


def after(value, *others):
    return lax.optimization_barrier((value,) + others)[0]


def tied(values, wait):
    if not wait:
        return list(values)
    return list(lax.optimization_barrier(tuple(values) + tuple(wait)))[: len(values)]


def native_gather(shard):
    return lax.all_gather(
        lax.all_gather(shard, "narrow", axis=1, tiled=True), "wide", axis=0, tiled=True
    )


class Gather:
    orders = (("x", "y"), ("y", "x"))

    def __init__(self, links, block, split, groups):
        self.links, self.block, self.split, self.groups = links, block, split, groups

    def first(self, *wait):
        block = after(self.block, *wait) if wait else self.block
        self.sent = [block]
        self.steps = [block] + self.links.others(block, "z")
        self.flying = self.steps[1:]

    def second(self, *wait):
        parts = arrange([after(self.steps[0], *wait) if wait else self.steps[0]] + self.steps[1:], self.split)
        self.steps, self.sent = [], []
        for held, order in zip(parts, self.orders, strict=True):
            self.sent.append(held)
            self.steps.append([held] + self.links.others(held, order[0]))
        self.flying = [v for p in self.steps for v in p[1:]]

    def third(self, *wait):
        parts = stack([[after(self.steps[0][0], *wait)] + self.steps[0][1:], self.steps[1]])
        self.steps, self.sent = [], []
        for held, order in zip(parts, self.orders, strict=True):
            self.sent.append(held)
            self.steps.append([held] + self.links.others(held, order[1]))
        self.flying = [v for p in self.steps for v in p[1:]]

    def fourth(self, far, *wait):
        first = after(self.steps[0][0], *wait)
        self.operands = []
        held = regroup([[first] + self.steps[0][1:], self.steps[1]], self.groups, far)
        for number, array in enumerate(held):
            self.operands.append([array, self.links.swap(array, core=1)])
        self.sent = held
        self.flying = [pair[1] for pair in self.operands]

    def blocks(self, refs, number, me):
        links = self.links
        order = self.orders[number]
        out = []
        for core in range(2):
            for k in range(refs[core].shape[0]):
                at, rest = {}, k
                for axis in ("z",) + order:
                    at[axis] = me[axis] ^ (rest % links.size[axis])
                    rest //= links.size[axis]
                source = functools.partial(block_columns, refs[core], k)
                out.append((source, at["z"] * links.y + at["y"], at["x"] * 2 + (me["core"] ^ core)))
        return out


def block_columns(ref, k, col, broad):
    return ref.at[k, :, pl.ds(col, broad)]


def at_least(n, values):
    out = values[3]
    for k in (2, 1, 0):
        out = jnp.where(n == k, values[k], out)
    return out


def window(ref, row, col, tall, broad):
    if not isinstance(row, int):
        row = pl.multiple_of(row, 8)
    if not isinstance(col, int):
        col = pl.multiple_of(col, 128)
    return ref.at[pl.ds(row, tall), pl.ds(col, broad)]


def columns(ref, col, broad):
    return ref.at[:, pl.ds(col, broad)]


class Weight:
    def __init__(self, operands, copies, joints=(), extra=0):
        self.operands, self.copies, self.joints, self.extra = operands, copies, joints, extra

    def fill(self, refs, target, sem):
        for source, to in self.copies(refs, target):
            pltpu.make_async_copy(source, to, sem).start()

    def wait(self, target, sem):
        pltpu.make_async_copy(target, target, sem).wait()
        for here, there in self.joints:
            target[:, here : here + 128] += target[:, there : there + 128]


def align_side(here, side):
    zero = jnp.zeros((side.shape[0], 64), side.dtype)
    return jnp.where(
        here["n"] % 2 == 0,
        jnp.concatenate([side, zero], axis=1),
        jnp.concatenate([zero, side], axis=1),
    )


def qkv_block(here, shard):
    even = here["n"] % 2 == 0
    main = jnp.where(even, shard[:, :384], shard[:, 192:])
    return jnp.concatenate([main, align_side(here, jnp.where(even, shard[:, 384:], shard[:, :192]))], axis=1)


def qkv_operands(links, gathered, shard):
    if not links.boxed:
        return Weight([native_gather(shard)], lambda refs, target: [(refs[0], target.at[:, pl.ds(0, 2304)])] + [
            (refs[0].at[:, pl.ds(0, 256)], target.at[:, pl.ds(2304, 256)])], extra=256)

    def copies(refs, target):
        me = links.place()
        out = []
        for source, w, n in gathered.blocks(refs, 0, me):
            out.append((source(0, 384), window(target, w * 96, at_least(n, (0, 768, 1152, 1920)), 96, 384)))
        for source, w, n in gathered.blocks(refs, 1, me):
            for part, places in enumerate(((384, 2304, 1536, 2432), (512, 640, 1664, 1792))):
                out.append((source(384 + 128 * part, 128), window(target, w * 96, at_least(n, places), 96, 128)))
        return out

    return Weight(gathered.operands[0], copies, ((512, 2304), (1664, 2432)), 256)


def proj_operands(links, gathered, shard):
    if not links.boxed:
        return Weight([native_gather(shard)], lambda refs, target: [(refs[0], target.at[:, pl.ds(0, 768)])] + [
            (refs[0].at[:, pl.ds(0, 256)], target.at[:, pl.ds(768, 256)])], extra=256)

    def copies(refs, target):
        me = links.place()
        out = []
        for part, (col, places) in enumerate(((0, (0, 768, 384, 896)), (128, (128, 256, 512, 640)))):
            for source, w, n in gathered.blocks(refs, part, me):
                out.append((source(col, 128), window(target, w * 96, at_least(n, places), 96, 128)))
        return out

    return Weight(gathered.operands[0], copies, ((128, 768), (512, 896)), 256)


def up_block(shard, chunk):
    return jnp.concatenate(
        [shard[:, 384 * half + 128 * chunk : 384 * half + 128 * chunk + 128] for half in range(2)], axis=1
    )


def down_block(shard_t, chunk):
    piece = shard_t[:, 128 * chunk : 128 * chunk + 128]
    half = piece.shape[0] // 2
    return jnp.concatenate([piece[:half], piece[half:]], axis=1)


def chunk_copies(full, chunk):
    def slices(refs, target):
        return [
            (columns(refs[0], 384 * g + 128 * chunk, 128), columns(target, 128 * g, 128)) for g in range(8)
        ]

    return Weight([full], slices)


def up_operands(links, gathered, group, full, chunk):
    if not links.boxed:
        return chunk_copies(full, chunk)

    def copies(refs, target):
        me = links.place()
        return [
            (source(0, 256), window(target, w * 96, n * 256, 96, 256))
            for source, w, n in gathered.blocks(refs, 0, me)
        ]

    return Weight(gathered.operands[group], copies)


def down_operands(links, gathered, group, full, chunk):
    if not links.boxed:
        return chunk_copies(full, chunk)

    def copies(refs, target):
        me = links.place()
        return [
            (source(256 + 128 * half, 128), window(target, n * 192 + half * 96, w * 128, 96, 128))
            for source, w, n in gathered.blocks(refs, 1, me)
            for half in range(2)
        ]

    return Weight(gathered.operands[group], copies)


class Scatter:
    orders = (("x", "y"), ("y", "x"))

    def __init__(self, links, here, split):
        self.links, self.here, self.split = links, here, split
        self.pairs, self.flying, self.stage = [], [], 0

    def first(self, away, stay):
        shape = (self.links.x, self.links.z, self.links.y) + away.shape[2:]
        self.pairs.append((stay.reshape(shape), self.links.swap(away.reshape(shape), core=1)))
        self.flying.append(self.pairs[-1][1])

    def jobs(self, step, picks):
        if step == "second":
            return [
                ([(self.pairs[k], cols) for k, cols in part], order[0])
                for part, order in zip(picks, self.orders, strict=True)
            ]
        whole_of = [(t, (0, t[0].shape[-1])) for t in self.terms]
        if step == "third":
            return [([t], order[1]) for t, order in zip(whole_of, self.orders, strict=True)]
        if step == "fifth":
            return [([(self.terms[0], (0, self.terms[0][0].shape[-1]))], "z_low")]
        return [(whole_of, "z_high" if step == "halves" else "z")]

    def take(self, results, unit):
        self.sent = [v for r in results for v in r[1:]]
        self.terms = []
        axes = [(order[self.stage], 1) for order in self.orders] if self.stage < 2 else [("z", unit)]
        for (keep, *sent), (axis, step) in zip(results, axes, strict=True):
            self.terms.append([keep] + [self.links.swap(v, **{axis: d * step}) for d, v in enumerate(sent, 1)])
        self.stage += 1
        self.flying = [v for t in self.terms for v in t[1:]]

    def done(self, *wait):
        terms = tied(self.terms[0], wait)
        total = terms[0]
        for term in terms[1:]:
            total = total + term.astype(F32)
        return total.reshape(total.shape[-2:])


def exchange(links, wait, *items):
    jobs = [job for scatter, step, picks in items for job in scatter.jobs(step, picks)]
    group, cols = jobs[0][0][0]
    jobs[0][0][0] = ((after(group[0], *wait),) + tuple(group[1:]), cols)
    results = fold(links, jobs)
    for scatter, step, _ in items:
        count = 2 if step in ("second", "third") else 1
        scatter.take(results[:count], 2 if step == "halves" else 1)
        results = results[count:]


def all_tiles(here, away, stay):
    return jnp.where(
        here["core"] == 0, jnp.stack([stay, away], axis=1), jnp.stack([away, stay], axis=1)
    ).reshape((4,) + away.shape[1:])


def native_scatter(partial):
    low = lax.psum_scatter(partial.astype(BF16), "wide", scatter_dimension=0, tiled=True)
    return lax.psum_scatter(low, "narrow", scatter_dimension=1, tiled=True).astype(F32)


def qkv_home(here, block):
    even = here["n"] % 2 == 0
    main, side = block[:, :384], block[:, 384:]
    return jnp.where(
        even,
        jnp.concatenate([main, side[:, :192]], axis=1),
        jnp.concatenate([side[:, 64:], main], axis=1),
    )


def proj_home(here, block):
    return jnp.where(here["n"] % 2 == 0, block[:, :192], block[:, 64:])


def natural_qkv(tiles):
    tiles = tiles.reshape(4, 768, 640)
    out = []
    for n in range(4):
        main, side = tiles[n, :, :384], tiles[n, :, 384:]
        out += [main, side[:, :192]] if n % 2 == 0 else [side[:, 64:], main]
    return jnp.concatenate(out, axis=1)


def natural_proj(tiles):
    tiles = tiles.reshape(4, 768, 256)
    return jnp.concatenate([tiles[n, :, :192] if n % 2 == 0 else tiles[n, :, 64:] for n in range(4)], axis=1)


def natural_up(chunks):
    tiles = [t.reshape(4, 768, 2, 128) for t in chunks]
    return jnp.stack(tiles, axis=0).transpose(2, 1, 3, 0, 4).reshape(768, -1)


def natural_down(chunks):
    tiles = [t.reshape(4, 8, 96, 2, 128) for t in chunks]
    return jnp.stack(tiles, axis=0).transpose(2, 0, 5, 1, 4, 3).reshape(-1, 768)


def tree_sum(terms):
    while len(terms) > 1:
        terms = [terms[k] + terms[k + 1] for k in range(0, len(terms), 2)]
    return terms[0]


def sum_everywhere(links, here, away, stay, wait):
    if links.boxed:
        half = after(stay + links.swap(away, core=1), *wait)
        first = False
        for axis in ("z", "x", "y"):
            step = 1
            while step < links.size[axis]:
                half = half + links.swap(half, **{axis: step})
                half = after(half, *wait) if first else half
                first = False
                step *= 2
        other = links.swap(half, core=1)
    else:
        first = jnp.where(here["core"] == 0, stay, away)
        second = jnp.where(here["core"] == 0, away, stay)
        return lax.psum(jnp.concatenate([first, second], axis=0), AXES)
    return jnp.where(
        here["core"] == 0, jnp.concatenate([half, other], axis=0), jnp.concatenate([other, half], axis=0)
    )


def whole(shape):
    return pl.BlockSpec(tuple(shape), lambda *_: (0,) * len(shape))


def kept(shape):
    return pl.BlockSpec(tuple(shape), lambda *_: (0,) * len(shape), pipeline_mode=pl.Buffered(1))


ANY = pl.BlockSpec(memory_space=pl.ANY)
FAR = pl.BlockSpec(memory_space=pltpu.HBM)
SCALARS = pl.BlockSpec(memory_space=pltpu.SMEM)


LIMITS = {"stack": 16, "arrange": 8, "fold": 24, "pack": 8, "prepare": 16, "bias": 16, "bias_back": 20, "project": 24, "attend": 18, "merge": 20, "feed": 28, "middle_back": 28, "attend_back": 22, "mixed_grad": 24, "start_back": 28}


def call(kernel, name, grid, ins, outs, scratch=(), flops=0, aliases=None):
    moved = sum(a.size * a.dtype.itemsize for a, *_ in ins)
    moved += sum(math.prod(s) * jnp.dtype(d).itemsize for s, d, *_ in outs)
    return pl.pallas_call(
        kernel,
        name=name,
        grid=grid,
        in_specs=[spec for _, spec, *_ in ins],
        out_specs=[spec for _, _, spec, *_ in outs],
        out_shape=[pltpu.HBM(s, d) if far else jax.ShapeDtypeStruct(s, d) for s, d, _, *far in outs],
        scratch_shapes=list(scratch),
        input_output_aliases=aliases or {},
        compiler_params=pltpu.CompilerParams(vmem_limit_bytes=LIMITS[name] * MIB),
        cost_estimate=pl.CostEstimate(flops=int(flops), bytes_accessed=int(moved), transcendentals=0),
    )(*[pltpu.with_memory_space_constraint(a, pltpu.HBM) if far else a for a, _, *far in ins])


def nn(a, b):
    return lax.dot_general(a, b, (((1,), (0,)), ((), ())), preferred_element_type=F32)


def nt(a, b):
    return lax.dot_general(a, b, (((1,), (1,)), ((), ())), preferred_element_type=F32)


def tn(a, b):
    return lax.dot_general(a, b, (((0,), (0,)), ((), ())), preferred_element_type=F32)


def arrange(blocks, split):
    rows, cols = blocks[0].shape
    count = len(blocks)

    def kernel(*refs):
        for k in range(count):
            refs[count][k] = refs[k][:, :split]
            refs[count + 1][k] = refs[k][:, split:]

    return call(
        kernel, "arrange", (),
        [(b, whole(b.shape)) for b in blocks],
        [((count, rows, part), BF16, whole((count, rows, part))) for part in (split, cols - split)],
    )


def stack(parts):
    flat = [v for part in parts for v in part]
    outs = [(sum(v.shape[0] for v in part), part[0].shape[1], part[0].shape[2]) for part in parts]

    def kernel(*refs):
        number = 0
        for k, part in enumerate(parts):
            at = 0
            for v in part:
                refs[len(flat) + k][at : at + v.shape[0]] = refs[number][...]
                at += v.shape[0]
                number += 1

    return call(
        kernel, "stack", (), [(v, whole(v.shape)) for v in flat], [(shape, BF16, whole(shape)) for shape in outs]
    )


def regroup(parts, groups, far):
    flat = [v for part in parts for v in part]
    count, rows = sum(v.shape[0] for v in parts[0]), parts[0][0].shape[1]
    outs = [(count, rows, sum(end - begin for begin, end in group)) for group in groups]

    def kernel(*refs):
        for out, group in zip(refs[len(flat) :], groups, strict=True):
            number, col = 0, 0
            for part, (begin, end) in zip(parts, group, strict=True):
                at = 0
                for v in part:
                    if end > begin:
                        out[at : at + v.shape[0], :, col : col + end - begin] = refs[number][:, :, begin:end]
                    at += v.shape[0]
                    number += 1
                col += end - begin

    return call(
        kernel, "stack", (), [(v, whole(v.shape)) for v in flat],
        [(shape, BF16, whole(shape), FAR) if far else (shape, BF16, whole(shape)) for shape in outs],
    )


def fold(links, jobs):
    arrays, index = [], {}
    for sources, _ in jobs:
        for group, _ in sources:
            for array in group:
                if id(array) not in index:
                    index[id(array)] = len(arrays)
                    arrays.append(array)
    dims = {"x": 0, "z": 1, "z_high": 1, "z_low": 1, "y": 2}
    size = dict(links.size, z_high=2, z_low=2)
    held = {"x": 1, "y": 1, "z": 1, "z_high": links.z // 2, "z_low": 1}
    outs = []
    for sources, axis in jobs:
        first = sources[0][0][0]
        cols = sum(part[1] - part[0] for _, part in sources)
        shape = tuple(held[axis] if k == dims[axis] else first.shape[k] for k in range(4)) + (cols,)
        outs += [(shape, F32 if d == 0 else BF16, whole(shape)) for d in range(size[axis])]

    def kernel(*refs):
        me = links.place()
        me["z_high"], me["z_low"] = me["z"] // 2, me["z"] % 2
        at_out = len(arrays)
        for sources, axis in jobs:
            for d in range(size[axis]):
                where = [slice(None)] * 4
                where[dims[axis]] = pl.ds((me[axis] ^ d) * held[axis], held[axis])
                col = 0
                for group, (begin, end) in sources:
                    picked = tuple(where) + (slice(begin, end),)
                    total = refs[index[id(group[0])]][picked].astype(F32)
                    for array in group[1:]:
                        total = total + refs[index[id(array)]][picked].astype(F32)
                    out = refs[at_out]
                    out[..., col : col + end - begin] = total.astype(out.dtype)
                    col += end - begin
                at_out += 1

    results = call(kernel, "fold", (), [(a, whole(a.shape)) for a in arrays], outs)
    out = []
    for _, axis in jobs:
        out.append(results[: size[axis]])
        results = results[size[axis] :]
    return out


def pack(links, table, heads, start_sums, middle_sums, halves, sum_fc2, hidden_sums):
    width = table.shape[1]

    def kernel(table_ref, start_ref, middle_ref, q0, v0, q1, v1, fc2_ref, a_ref, b_ref, c_ref, away_ref, stay_ref, all_s):
        all_s[...] = jnp.zeros_like(all_s)
        rows = [(table_ref, heads), (start_ref, 3), (middle_ref, 5)]
        at = 0
        for ref, count in rows:
            for k in range(count):
                all_s[(at + k) // 16, (at + k) % 16 : (at + k) % 16 + 1, :] = ref[k : k + 1, :]
            at += count
        for pair in ((q0, q1), (v0, v1)):
            for k, ref in enumerate(pair):
                all_s[at // 16, at % 16 : at % 16 + 1, k * 384 : k * 384 + 384] = ref[...]
            at += 1
        all_s[at // 16, at % 16 : at % 16 + 1, :] = fc2_ref[...]
        at += 1
        for k, ref in enumerate((a_ref, b_ref, c_ref)):
            all_s[(at + k) // 16, (at + k) % 16 : (at + k) % 16 + 1, :] = ref[:, 0:width]
            all_s[(at + 3) // 16, (at + 3) % 16 : (at + 3) % 16 + 1, k * 256 : k * 256 + 256] = ref[:, width : width + 256]
        c = lax.axis_index("narrow") % 2
        away_ref[...] = all_s[1 - c]
        stay_ref[...] = all_s[c]

    operands = [table, start_sums, middle_sums, *halves[0], *halves[1], sum_fc2, *hidden_sums]
    return call(
        kernel, "pack", (), [(a, whole(a.shape)) for a in operands],
        [((16, width), F32, whole((16, width)))] * 2, [pltpu.VMEM((2, 16, width), F32)],
    )


def norm(values):
    centre = jnp.mean(values, axis=-1, keepdims=True)
    centred = values - centre
    spread = jnp.mean(centred * centred, axis=-1, keepdims=True)
    scaling = lax.rsqrt(spread + EPSILON)
    return centred * scaling, scaling


def norm_back(grad, normed, scaling, gain):
    scaled = grad * gain
    first = jnp.mean(scaled, axis=-1, keepdims=True)
    second = jnp.mean(scaled * normed, axis=-1, keepdims=True)
    return (scaled - first - normed * second) * scaling


def banded(tall, body):
    if BAND >= tall:
        body(slice(0, tall), 0)
        return

    def step(k, carry):
        at = pl.multiple_of(k * BAND, 8)
        body(pl.ds(at, BAND), at)
        return carry

    lax.fori_loop(0, tall // BAND, step, 0)


def column_sum(values):
    return jnp.sum(values, axis=0, keepdims=True)


TOKEN, GAIN1, SHIFT1, GAMMA2, BIAS1, GAMMA1, GAIN2, SHIFT2, BIAS2 = range(9)


def row_of(ref, k):
    return ref[k : k + 1, :]


def masked_rows(image, sizes_ref, patterns_ref, tall):
    bound, group = 0, 0
    for k in range(sizes_ref.shape[0] - 1):
        bound = bound + sizes_ref[k]
        group = group + (image >= bound).astype(jnp.int32)
    columns_of = patterns_ref[...].T
    which = lax.broadcasted_iota(jnp.int32, columns_of.shape, 1) == group
    return jnp.sum(jnp.where(which, columns_of, 0.0), axis=1, keepdims=True)[0:tall] > 0.5


def first_image(images):
    return lax.axis_index(AXES) * images


def prepare(sizes, inputs, cotangent, group_sizes, mask_patterns, vectors):
    images, length, tall, width = sizes
    rows = images * tall
    groups, patches = mask_patterns.shape

    def kernel(x_ref, g_ref, sizes_ref, mask_ref, *refs):
        vector_refs, refs = refs[: len(vectors)], refs[len(vectors) :]
        h0_ref, n1_ref, g_out, df_ref, sum_ref, params_ref, patterns_ref, x_s, g_s, mask_s, sems, *vector_s = refs
        step = pl.program_id(0)

        @pl.when(step == 0)
        def _():
            x_s[...] = jnp.zeros_like(x_s)
            g_s[...] = jnp.zeros_like(g_s)
            sum_ref[...] = jnp.zeros_like(sum_ref)
            params_ref[...] = jnp.zeros_like(params_ref)
            patterns_ref[...] = jnp.zeros_like(patterns_ref)
            moves = [pltpu.make_async_copy(mask_ref, mask_s, sems.at[len(vectors)])]
            moves += [
                pltpu.make_async_copy(a, b, sems.at[k]) for k, (a, b) in enumerate(zip(vector_refs, vector_s, strict=True))
            ]
            for move in moves:
                move.start()
            for move in moves:
                move.wait()
            patterns_ref[0:groups, 1 : patches + 1] = mask_s[...].astype(F32)
            for k, ref in zip(vectors, vector_s, strict=True):
                params_ref[k : k + 1, :] = ref[...].reshape(1, width)

        x_s[0:length, :] = x_ref[0].astype(F32)
        g_s[0:length, :] = g_ref[0].astype(F32)
        masked = masked_rows(first_image(images) + step, sizes_ref, patterns_ref, tall)
        start = jnp.where(masked, row_of(params_ref, TOKEN), x_s[...])
        h0_ref[...] = start
        normed, _ = norm(start)
        n1_ref[...] = (normed * row_of(params_ref, GAIN1) + row_of(params_ref, SHIFT1)).astype(BF16)
        g = g_s[...]
        g_out[...] = g.astype(BF16)
        df = row_of(params_ref, GAMMA2) * g
        df_ref[...] = df.astype(BF16)
        sum_ref[...] += column_sum(df)

    image = pl.BlockSpec((1, length, width), lambda i: (i, 0, 0))
    band = pl.BlockSpec((tall, width), lambda i: (i, 0))
    return call(
        kernel, "prepare", (images,),
        [(inputs, image), (cotangent, image), (group_sizes, SCALARS), (mask_patterns, ANY, FAR)]
        + [(v, ANY, FAR) for v in vectors.values()],
        [((rows, width), F32, band), ((rows, width), BF16, band), ((rows, width), BF16, band, FAR),
         ((rows, width), BF16, band, FAR), ((1, width), F32, whole((1, width))), ((16, width), F32, whole((16, width))),
         ((8, 256), F32, whole((8, 256)))],
        [pltpu.VMEM((tall, width), F32), pltpu.VMEM((tall, width), F32), pltpu.VMEM(mask_patterns.shape, jnp.int32),
         pltpu.SemaphoreType.DMA((len(vectors) + 1,))] + [pltpu.VMEM((width,), F32) for _ in vectors],
        flops=rows * width * 40,
    )


def table_columns(grid_side, broad):
    side = 2 * grid_side - 1
    q = np.arange(broad)
    entry = (q // grid_side) * side + q % grid_side + grid_side - 1
    return jnp.asarray(np.where(q < side * grid_side, entry, -(1 << 20)).astype(np.int32)[None])


def three_parts(values):
    high = values.astype(BF16)
    rest = values - high.astype(F32)
    middle = rest.astype(BF16)
    return high, middle, (rest - middle.astype(F32)).astype(BF16)


def bias_kernel(table_t, entry, grid_side, tall, broad):
    heads = table_t.shape[0]
    length = grid_side * grid_side + 1
    wide = entry.shape[1]
    inner = (2 * grid_side - 1) ** 2

    def kernel(table_ref, entry_ref, out_ref, *halves):
        def put(at, count, values):
            for half, ref in enumerate(halves):
                ref[pl.ds(at, count), :] = values[:, 128 * half : 128 * half + 128]

        parts = jnp.concatenate(three_parts(table_ref[...]), axis=0)
        left, top, corner = (table_ref[:, inner + 1 : inner + 2], table_ref[:, inner : inner + 1],
                             table_ref[:, inner + 2 : inner + 3])
        lane = lax.broadcasted_iota(jnp.int32, (heads, broad), 1)

        def column(b, carry):
            which = lax.broadcasted_iota(jnp.int32, (table_ref.shape[1], wide), 0) + b
            select = jnp.where(which == entry_ref[...], 1.0, 0.0).astype(BF16)
            spread = nn(parts, select)
            spread = spread[:heads] + spread[heads : 2 * heads] + spread[2 * heads :]
            for a in range(grid_side):
                shift = (grid_side - 1 - a) * grid_side - 1
                moved = pltpu.roll(spread, (wide - shift) % wide, 1)[:, :broad]
                moved = jnp.where(lane == 0, top, moved)
                put(pl.multiple_of((1 + grid_side * a + b) * heads, 16), heads, moved)
            return carry

        lax.fori_loop(0, grid_side, column, 0)
        put(0, heads, jnp.where(lane == 0, corner, left))
        rest = (tall - length) * heads
        put(length * heads, rest, jnp.full((rest, broad), NEVER, F32))
        for h in range(out_ref.shape[0]):
            for half, ref in enumerate(halves):
                out_ref[h, :, 128 * half : 128 * half + 128] = ref[pl.ds(h, tall, stride=heads), :]

    return call(
        kernel, "bias", (),
        [(table_t, whole(table_t.shape)), (entry, whole(entry.shape))],
        [((12, tall, broad), F32, whole((12, tall, broad)))],
        [pltpu.VMEM((tall * heads, 128), F32)] * (broad // 128),
        flops=2 * 48 * 768 * wide * grid_side,
    )[0]


def bias_back_kernel(terms, entry, grid_side, width):
    count, tall, broad = terms.shape
    heads = 16
    wide = entry.shape[1]
    inner = (2 * grid_side - 1) ** 2
    length = grid_side * grid_side + 1

    def kernel(terms_ref, entry_ref, out_ref, *halves):
        def get(at, count):
            return jnp.concatenate([ref[pl.ds(at, count), :] for ref in halves], axis=1)

        lane = lax.broadcasted_iota(jnp.int32, (heads, broad), 1)
        inside = (lane >= 1) & (lane < length)
        for h in range(heads):
            values = terms_ref[h] if h < count else jnp.zeros((tall, broad), F32)
            for half, ref in enumerate(halves):
                ref[pl.ds(h, tall, stride=heads), :] = values[:, 128 * half : 128 * half + 128]

        def column(b, carry):
            total, edge = carry
            which = lax.broadcasted_iota(jnp.int32, (width, wide), 0) + b
            select = jnp.where(which == entry_ref[...], 1.0, 0.0).astype(BF16)
            spread = jnp.zeros((heads, wide), F32)
            for a in range(grid_side):
                shift = (grid_side - 1 - a) * grid_side - 1
                found = get(pl.multiple_of((1 + grid_side * a + b) * heads, 16), heads)
                edge = edge + jnp.where(lane == 0, found, 0.0)
                found = jnp.where(inside, found, 0.0)
                found = jnp.concatenate([found, jnp.zeros((heads, wide - broad), F32)], axis=1)
                spread = spread + pltpu.roll(found, shift % wide, 1)
            found = nt(jnp.concatenate(three_parts(spread), axis=0), select)
            total = total + found[:heads] + found[heads : 2 * heads] + found[2 * heads :]
            return total, edge

        total, edge = lax.fori_loop(
            0, grid_side, column, (jnp.zeros((heads, width), F32), jnp.zeros((heads, broad), F32))
        )
        first = get(0, heads)
        top = jnp.sum(edge, axis=1, keepdims=True)
        left = jnp.sum(jnp.where(inside, first, 0.0), axis=1, keepdims=True)
        corner = first[:, 0:1]
        place = lax.broadcasted_iota(jnp.int32, (heads, width), 1)
        total = jnp.where(place == inner, top, total)
        total = jnp.where(place == inner + 1, left, total)
        out_ref[...] = jnp.where(place == inner + 2, corner, total)

    return call(
        kernel, "bias_back", (),
        [(terms, whole(terms.shape)), (entry, whole(entry.shape))],
        [((heads, width), F32, whole((heads, width)))],
        [pltpu.VMEM((tall * heads, 128), F32)] * (broad // 128),
        flops=2 * 48 * 768 * wide * grid_side,
    )[0]


def project(sizes, first_low, weight, params, score_scale):
    images, length, tall, width = sizes
    rows = images * tall
    cols = 3 * width
    count = len(weight.operands)

    def kernel(*refs):
        n1_ref, params_ref = refs[:2]
        out_ref, w_s, sem = refs[2 + count :]
        step = pl.program_id(0)

        @pl.when(step == 0)
        def _():
            weight.fill(refs[2 : 2 + count], w_s, sem)
            weight.wait(w_s, sem)

        w = w_s[:, pl.ds(pl.multiple_of(step * width, 128), width)]
        scale = jnp.where(step == 0, score_scale, 1.0)
        out_ref[...] = ((nn(n1_ref[...], w) + params_ref[pl.ds(9 + step, 1), :]) * scale).astype(BF16)

    return call(
        kernel, "project", (cols // width,),
        [(first_low, kept((rows, width))), (params, kept(params.shape))] + [(a, ANY) for a in weight.operands],
        [((rows, cols), BF16, pl.BlockSpec((rows, width), lambda t: (0, t)))],
        [pltpu.VMEM((width, cols + weight.extra), BF16), pltpu.SemaphoreType.DMA],
        flops=2 * rows * width * cols,
    )[0]


def head_masks(tall):
    lane = lax.broadcasted_iota(jnp.int32, (tall, 128), 1)
    return [lane < 64, lane >= 64]


def attend(sizes, mixed, bias, first, pairs):
    images, length, tall, width = sizes
    rows = images * tall
    every = width // 128
    broad = bias.shape[2]

    def kernel(q_ref, k_ref, v_ref, bias_ref, out_ref, p_ref):
        masks = head_masks(tall)
        units = [(i, h) for i in range(images) for h in range(2)]
        scores, probs = [], []
        for i, h in units:
            q, k = q_ref[tall * i : tall * i + tall, :], k_ref[tall * i : tall * i + tall, :]
            scores.append(nt(k, jnp.where(masks[h], q, jnp.zeros_like(q))) + bias_ref[h, :, 0:tall])
        for (i, h), s in zip(units, scores, strict=True):
            e = jnp.exp(s - jnp.max(s, axis=0, keepdims=True))
            p = (e * (1.0 / jnp.sum(e, axis=0, keepdims=True))).astype(BF16)
            p_ref[h, i, :, 0:tall] = p
            probs.append(p)
        for i in range(images):
            vt = v_ref[tall * i : tall * i + tall, :].T
            out = [nn(vt[64 * h : 64 * h + 64, :], probs[2 * i + h]) for h in range(2)]
            out_ref[tall * i : tall * i + tall, :] = jnp.concatenate(out, axis=0).T.astype(BF16)

    def column(at):
        return pl.BlockSpec((rows, 128), lambda t: (0, at + t))

    return call(
        kernel, "attend", (pairs,),
        [(mixed, column(first)), (mixed, column(every + first)), (mixed, column(2 * every + first)),
         (bias, pl.BlockSpec((2, tall, broad), lambda t: (first + t, 0, 0)))],
        [((rows, 128 * pairs), BF16, column(0), FAR),
         ((2 * pairs, images, tall, broad), BF16,
          pl.BlockSpec((2, images, tall, broad), lambda t: (t, 0, 0, 0)), FAR)],
        flops=4 * rows * tall * 128 * pairs,
    )


def attend_back(sizes, mixed, probs, grad_out, score_scale, first, pairs, so_far):
    images, length, tall, width = sizes
    rows = images * tall
    every = width // 128
    broad = probs.shape[3]

    def kernel(q_ref, k_ref, v_ref, do_ref, p_ref, *refs):
        grad_ref, terms_ref, qb_ref, vb_ref = refs[-4:]
        masks = head_masks(tall)
        units = [(i, h) for i in range(images) for h in range(2)]

        def part(ref, i):
            return ref[tall * i : tall * i + tall, :]

        def own(value, h):
            return jnp.where(masks[h], value, jnp.zeros_like(value))

        grads = [nt(part(v_ref, i), own(part(do_ref, i), h)) for i, h in units]
        lows = []
        for (i, h), grad in zip(units, grads, strict=True):
            p = p_ref[h, i, :, 0:tall].astype(F32)
            t = p * grad
            lows.append((t - p * jnp.sum(t, axis=0, keepdims=True)).astype(BF16))
        for h in range(2):
            terms_ref[h, :, 0:tall] = sum(lows[2 * i + h].astype(F32) for i in range(images))
            terms_ref[h, :, tall:] = jnp.zeros((tall, broad - tall), F32)
        query_sum, value_sum = 0.0, 0.0
        for i in range(images):
            kt = part(k_ref, i).T
            dv = sum(nn(p_ref[h, i, :, 0:tall], own(part(do_ref, i), h)) for h in range(2))
            dk = sum(nn(lows[2 * i + h], own(part(q_ref, i), h)) for h in range(2))
            dq = jnp.concatenate(
                [nn(kt[64 * h : 64 * h + 64, :], lows[2 * i + h]) for h in range(2)], axis=0
            ).T * score_scale
            for number, grad in enumerate((dq, dk, dv)):
                grad_ref[number, tall * i : tall * i + tall, :] = grad.astype(BF16)
            query_sum += column_sum(dq)
            value_sum += column_sum(dv)
        qb_ref[...] = query_sum
        vb_ref[...] = value_sum

    def column(at):
        return pl.BlockSpec((rows, 128), lambda t: (0, at + t))

    one = pl.BlockSpec((1, 128), lambda t: (0, t))
    return call(
        kernel, "attend_back", (pairs,),
        [(mixed, column(first)), (mixed, column(every + first)), (mixed, column(2 * every + first)),
         (grad_out, column(first)),
         (probs, pl.BlockSpec((2, images, tall, broad), lambda t: (first + t, 0, 0, 0)), FAR)]
        + ([] if so_far is None else [(so_far, ANY)]),
        [((3, rows, width), BF16, pl.BlockSpec((3, rows, 128), lambda t: (0, 0, first + t)))]
        + [((2 * pairs, tall, broad), F32, pl.BlockSpec((2, tall, broad), lambda t: (t, 0, 0))),
           ((1, 128 * pairs), F32, one), ((1, 128 * pairs), F32, one)],
        flops=8 * rows * tall * 128 * pairs,
        aliases={} if so_far is None else {5: 0},
    )


def merge(sizes, attended, start, weight, params):
    images, length, tall, width = sizes
    rows = images * tall
    count = len(weight.operands)

    def kernel(*refs):
        att_refs, refs = refs[: len(attended)], refs[len(attended) :]
        h0_ref, params_ref = refs[:2]
        h1_ref, n2_ref, w_s, out_s, sem = refs[2 + count :]
        step = pl.program_id(0)

        @pl.when(step == 0)
        def _():
            weight.fill(refs[2 : 2 + count], w_s, sem)
            weight.wait(w_s, sem)
            part = width // len(attended)
            out_s[...] = sum(nn(r[...], w_s[part * k : part * k + part, 0:width]) for k, r in enumerate(att_refs))

        @pl.when(step > 0)
        def _():
            def body(at, first):
                out = out_s[pl.ds(pl.multiple_of((step - 1) * tall + first, 8), min(BAND, tall)), :]
                middle = h0_ref[at, :] + row_of(params_ref, GAMMA1) * (out + row_of(params_ref, BIAS1))
                h1_ref[at, :] = middle
                normed, _ = norm(middle)
                n2_ref[at, :] = (normed * row_of(params_ref, GAIN2) + row_of(params_ref, SHIFT2)).astype(BF16)

            banded(tall, body)

    band = pl.BlockSpec((tall, width), lambda i: (jnp.maximum(i - 1, 0), 0))
    return call(
        kernel, "merge", (images + 1,),
        [(a, kept(a.shape), FAR) for a in attended]
        + [(start, band), (params, kept(params.shape))]
        + [(a, ANY, FAR) for a in weight.operands],
        [((rows, width), F32, band), ((rows, width), BF16, band)],
        [pltpu.VMEM((width, width + weight.extra), BF16), pltpu.VMEM((rows, width), F32),
         pltpu.SemaphoreType.DMA],
        flops=2 * rows * width * width,
    )


def part_by_core(store, away_ref, stay_ref):
    c = lax.axis_index("narrow") % 2
    for x in range(2):
        away_ref[x] = store[2 * x + 1 - c]
        stay_ref[x] = store[2 * x + c]


def feed(sizes, second_low, down_low, up, down, bias, sums, last):
    images, length, tall, width = sizes
    rows = images * tall
    shared = up.operands[0] is down.operands[0]
    far = () if last else (FAR,)
    ups, downs = len(up.operands), 0 if shared else len(down.operands)
    carried = [] if sums is None else list(sums)

    def kernel(*refs):
        n2_ref, df_ref, bias_ref = refs[:3]
        rest = refs[3:]
        up_refs, rest = rest[:ups], rest[ups:]
        down_refs, rest = (up_refs if shared else rest[:downs]), rest[downs:]
        sum_refs, rest = rest[: len(carried)], rest[len(carried) :]
        f_ref, dn_ref, away_ref, stay_ref, gbias_ref, up_s, down_s, grad_s, sems = rest
        step = pl.program_id(0)

        @pl.when(step == 0)
        def _():
            up.fill(up_refs, up_s, sems.at[0])
            down.fill(down_refs, down_s, sems.at[1])
            if carried:
                pltpu.make_async_copy(sum_refs[0], f_ref, sems.at[2]).start()
                pltpu.make_async_copy(sum_refs[1], dn_ref, sems.at[3]).start()
            up.wait(up_s, sems.at[0])
            down.wait(down_s, sems.at[1])
            if not carried:
                f_ref[...] = jnp.zeros_like(f_ref)
                dn_ref[...] = jnp.zeros_like(dn_ref)

        at = pl.ds(pl.multiple_of(step * TILE, TILE), TILE)
        up_w, down_w = up_s[:, at], down_s[:, at]
        u = nn(n2_ref[...], up_w) + bias_ref[...]
        dz = nn(df_ref[...], down_w)
        bell = jnp.exp(-0.5 * u * u)
        below = 0.5 * (1.0 + lax.erf(u * ROOT_HALF))
        z = (u * below).astype(BF16)
        du = dz * (below + u * (DENSITY * bell))
        gbias_ref[...] = column_sum(du)
        du = du.astype(BF16)
        grad = tn(n2_ref[...], du).astype(BF16)
        for k in range(TILE // 256):
            grad_s[step * (TILE // 256) + k, :, :, 0:256] = grad[:, 256 * k : 256 * k + 256].reshape(8, 96, 256)
        grad = tn(df_ref[...], z).astype(BF16)
        for n in range(4):
            for w in range(TILE // 128):
                for half in range(2):
                    grad_s[n, step * (TILE // 128) + w, :, 256 + 128 * half : 384 + 128 * half] = grad[
                        192 * n + 96 * half : 192 * n + 96 * half + 96, 128 * w : 128 * w + 128
                    ]
        if carried:
            @pl.when(step == 0)
            def _():
                pltpu.make_async_copy(sum_refs[0], f_ref, sems.at[2]).wait()
                pltpu.make_async_copy(sum_refs[1], dn_ref, sems.at[3]).wait()

        f_ref[...] += nt(z, down_w)
        dn_ref[...] += nt(du, up_w)

        @pl.when(step == CHUNK // TILE - 1)
        def _():
            part_by_core(grad_s, away_ref, stay_ref)

    tile = pl.BlockSpec((1, TILE), lambda t: (0, t))
    full = whole((rows, width))
    shape = (2, 8, 96, 512)
    return call(
        kernel, "feed", (CHUNK // TILE,),
        [(second_low, kept((rows, width))), (down_low, kept((rows, width))), (bias, tile)]
        + [(a, ANY, FAR) for a in up.operands[:1]] + [(a, ANY) for a in up.operands[1:]]
        + [(a, ANY, FAR) for a in ([] if shared else down.operands) + carried],
        [((rows, width), F32, kept((rows, width)), *far), ((rows, width), F32, kept((rows, width)), *far),
         (shape, BF16, kept(shape)), (shape, BF16, kept(shape)), ((1, CHUNK), F32, tile)],
        [pltpu.VMEM((width, CHUNK), BF16), pltpu.VMEM((width, CHUNK), BF16), pltpu.VMEM((4, 8, 96, 512), BF16),
         pltpu.SemaphoreType.DMA((4,))],
        flops=12 * rows * width * CHUNK,
    )


def middle_back(sizes, attended, branch, grad_n2, middle, start, upstream, weight, params):
    images, length, tall, width = sizes
    rows = images * tall
    count = len(weight.operands)

    def kernel(*refs):
        att_refs, refs = refs[: len(attended)], refs[len(attended) :]
        f_ref, dn_ref, h1_ref, h0_ref, g_ref, params_ref = refs[:6]
        out_ref, dh_ref, do_ref, away_ref, stay_ref, sum_ref, w_s, da_s, grad_s, layer_s, sem = refs[6 + count :]
        step = pl.program_id(0)

        @pl.when(step == 0)
        def _():
            weight.fill(refs[6 : 6 + count], w_s, sem)
            sum_ref[...] = jnp.zeros_like(sum_ref)

        @pl.when(step < images)
        def _():
            def body(at, first):
                f = f_ref[at, :] + row_of(params_ref, BIAS2)
                h1 = h1_ref[at, :]
                g = g_ref[at, :].astype(F32)
                layer_s[at, :] = h1 + row_of(params_ref, GAMMA2) * f
                normed, scaling = norm(h1)
                dn = dn_ref[at, :]
                dh = g + norm_back(dn, normed, scaling, row_of(params_ref, GAIN2))
                dh_ref[at, :] = dh
                da = row_of(params_ref, GAMMA1) * dh
                sum_ref[0:1, :] += column_sum(g * f)
                sum_ref[1:2, :] += column_sum(dn * normed)
                sum_ref[2:3, :] += column_sum(dn)
                sum_ref[3:4, :] += column_sum(dh * (h1 - h0_ref[at, :]))
                sum_ref[4:5, :] += column_sum(da)
                da_s[pl.ds(pl.multiple_of(step * tall + first, 8), min(BAND, tall)), :] = da.astype(BF16)

            banded(tall, body)
            out_ref[0] = layer_s[0:length, :].astype(BF16)

        @pl.when(step == images)
        def _():
            sum_ref[3:4, :] = sum_ref[3:4, :] / row_of(params_ref, GAMMA1)
            weight.wait(w_s, sem)
            do_ref[...] = nt(da_s[...], w_s[:, 0:width]).astype(BF16)
            grad = jnp.concatenate([tn(r[...], da_s[...]) for r in att_refs], axis=0).astype(BF16)
            for n, at in enumerate((0, 128, 384, 512)):
                grad_s[n] = grad[:, at : at + 256].reshape(8, 96, 256)
            part_by_core(grad_s, away_ref, stay_ref)

    def at(i):
        return jnp.minimum(i, images - 1)

    band = pl.BlockSpec((tall, width), lambda i: (at(i), 0))
    shape = (2, 8, 96, 256)
    return call(
        kernel, "middle_back", (images + 1,),
        [(a, kept(a.shape), FAR) for a in attended]
        + [(a, band) for a in (branch, grad_n2, middle, start)] + [(a, band, FAR) for a in (upstream,)] + [(params, kept(params.shape))]
        + [(a, ANY, FAR) for a in weight.operands],
        [((images, length, width), BF16, pl.BlockSpec((1, length, width), lambda i: (at(i), 0, 0))),
         ((rows, width), F32, band), ((rows, width), BF16, whole((rows, width))),
         (shape, BF16, whole(shape)), (shape, BF16, whole(shape)), ((8, width), F32, whole((8, width)))],
        [pltpu.VMEM((width, width + weight.extra), BF16), pltpu.VMEM((rows, width), BF16),
         pltpu.VMEM((4, 8, 96, 256), BF16), pltpu.VMEM((tall, width), F32), pltpu.SemaphoreType.DMA],
        flops=4 * rows * width * width,
    )


def mixed_grad(sizes, first_low, grads):
    images, length, tall, width = sizes
    rows = images * tall

    def kernel(n1_ref, grad_ref, away_ref, stay_ref):
        step = pl.program_id(0)
        c = lax.axis_index("narrow") % 2
        n = 2 * (step % 2) + jnp.where(step < 2, 1 - c, c)
        main = grad_ref[at_least(n, (0, 1, 1, 2)), :, pl.ds(pl.multiple_of(at_least(n, (0, 0, 384, 384)), 128), 384)]
        side = grad_ref[at_least(n, (0, 0, 2, 2)), :, pl.ds(pl.multiple_of(at_least(n, (384, 512, 0, 128)), 128), 256)]
        main = tn(n1_ref[...], main).astype(BF16).reshape(8, 96, 384)
        side = tn(n1_ref[...], side).astype(BF16).reshape(8, 96, 256)
        for role, ref in enumerate((away_ref, stay_ref)):
            @pl.when(step // 2 == role)
            def _(ref=ref):
                ref[0, :, :, 0:384] = main
                ref[0, :, :, 384:640] = side

    shape = (2, 8, 96, 640)
    return call(
        kernel, "mixed_grad", (4,),
        [(first_low, kept((rows, width))), (grads, kept(grads.shape))],
        [(shape, BF16, pl.BlockSpec((1, 8, 96, 640), lambda t: (jnp.minimum(t, 1), 0, 0, 0))),
         (shape, BF16, pl.BlockSpec((1, 8, 96, 640), lambda t: (jnp.maximum(t - 2, 0), 0, 0, 0)))],
        flops=6 * rows * width * width,
    )


def start_back(sizes, grads, weight, start, grad_middle, group_sizes, patterns, params):
    images, length, tall, width = sizes
    rows = images * tall
    count = len(weight.operands)

    def kernel(*refs):
        grad_ref, h0_ref, dh_ref, sizes_ref, patterns_ref, params_ref = refs[:6]
        out_ref, sum_ref, w_s, dn_s, out_s, sem = refs[6 + count :]
        step = pl.program_id(0)

        @pl.when(step == 0)
        def _():
            weight.fill(refs[6 : 6 + count], w_s, sem)
            sum_ref[...] = jnp.zeros_like(sum_ref)
            dn_s[...] = jnp.zeros_like(dn_s)
            weight.wait(w_s, sem)

        @pl.when(step < 3)
        def _():
            dn_s[...] += nt(grad_ref[0], w_s[:, pl.ds(pl.multiple_of(step * width, 128), width)])

        @pl.when(step > 2)
        def _():
            masked = masked_rows(first_image(images) + step - 3, sizes_ref, patterns_ref, tall)

            def body(at, first):
                dn = dn_s[pl.ds(pl.multiple_of((step - 3) * tall + first, 8), min(BAND, tall)), :]
                normed, scaling = norm(h0_ref[at, :])
                dh = dh_ref[at, :] + norm_back(dn, normed, scaling, row_of(params_ref, GAIN1))
                out_s[at, :] = jnp.where(masked, 0.0, dh)
                sum_ref[0:1, :] += column_sum(dn * normed)
                sum_ref[1:2, :] += column_sum(dn)
                sum_ref[2:3, :] += column_sum(jnp.where(masked, dh, 0.0))

            banded(tall, body)
            out_ref[0] = out_s[0:length, :]

    def at(i):
        return jnp.maximum(i - 3, 0)

    band = pl.BlockSpec((tall, width), lambda i: (at(i), 0))
    return call(
        kernel, "start_back", (images + 3,),
        [(grads, pl.BlockSpec((1, rows, width), lambda i: (jnp.minimum(i, 2), 0, 0)))]
        + [(start, band), (grad_middle, band), (group_sizes, SCALARS), (patterns, kept(patterns.shape)),
           (params, kept(params.shape))]
        + [(a, ANY) for a in weight.operands],
        [((images, length, width), F32, pl.BlockSpec((1, length, width), lambda i: (at(i), 0, 0))),
         ((8, width), F32, whole((8, width)))],
        [pltpu.VMEM((width, 3 * width + weight.extra), BF16), pltpu.VMEM((rows, width), F32),
         pltpu.VMEM((tall, width), F32), pltpu.SemaphoreType.DMA],
        flops=6 * rows * width * width,
    )


def local(
    links,
    inputs,
    cotangent,
    group_sizes,
    mask_patterns,
    mask_token,
    norm1_gain,
    norm1_bias,
    qkv_weight,
    query_bias,
    value_bias,
    bias_table,
    proj_weight,
    proj_bias,
    gamma_attn,
    norm2_gain,
    norm2_bias,
    fc1_weight,
    fc1_bias,
    fc2_weight,
    fc2_bias,
    gamma_mlp,
):
    images, length, width = inputs.shape
    table_rows, heads = bias_table.shape
    grid_side = math.isqrt(length - 1)
    group_count = mask_patterns.shape[0]
    tall = -(-length // 8) * 8
    rows = images * tall
    hidden = fc1_bias.shape[0]
    chunks = hidden // CHUNK
    sizes = (images, length, tall, width)
    score_scale = (width // heads) ** (-0.5)
    here = links.place()

    vectors = {
        TOKEN: mask_token, GAIN1: norm1_gain, SHIFT1: norm1_bias, GAMMA2: gamma_mlp, BIAS1: proj_bias,
        GAMMA1: gamma_attn, GAIN2: norm2_gain, SHIFT2: norm2_bias, BIAS2: fc2_bias, 9: query_bias, 11: value_bias,
    }

    boxed = links.boxed
    fc2_t = fc2_weight.T
    if boxed:
        mix = Gather(links, qkv_block(here, qkv_weight), 384, [((0, 384), (0, 256))])
        side = align_side(here, proj_weight)
        near = Gather(
            links,
            jnp.concatenate(
                [side[:, :128], up_block(fc1_weight, 0), down_block(fc2_t, 0), side[:, 128:]], axis=1
            ),
            384,
            [((0, 128), (256, 384)), ((128, 384), (0, 256))],
        )
        far = Gather(
            links,
            jnp.concatenate(
                [up_block(fc1_weight, 1), up_block(fc1_weight, 2), down_block(fc2_t, 1), down_block(fc2_t, 2)],
                axis=1,
            ),
            512,
            [((0, 256), (0, 256)), ((256, 512), (256, 512))],
        )
        full_up = full_down = None
    else:
        mix = near = far = None
        full_up, full_down = native_gather(fc1_weight), native_gather(fc2_weight).T

    entry = table_columns(grid_side, 384)

    def behind(value, *exchanges):
        return after(value, *[v for e in exchanges for v in e.sent]) if boxed else value

    def met(value, *exchanges):
        return [value] + [v for e in exchanges for v in e.flying]

    if boxed:
        mix.first()
    start, first_low, upstream, down_low, sum_fc2, params, patterns = prepare(
        sizes, inputs, cotangent, group_sizes, mask_patterns, vectors
    )
    if boxed:
        gap = met(first_low, mix)
        mix.second(*gap)
        near.first(*gap)
    table_t = jnp.pad(after(bias_table, first_low).T, ((0, 16 - heads), (0, width - table_rows)))
    bias = bias_kernel(behind(table_t, mix), entry, grid_side, tall, 256)
    if boxed:
        mix.third(*met(bias, mix))
        mix.fourth(False, *met(bias, near))
        near.second(*mix.sent)
    qkv = qkv_operands(links, mix, qkv_weight)
    mixed = project(sizes, behind(first_low, near), qkv, params, score_scale)
    if boxed:
        gap = met(mixed, near)
        near.third(*gap)
        far.first(*gap)
    attended, probs = attend(sizes, behind(mixed, near), bias, 0, width // 128)
    if boxed:
        near.fourth(False, *met(attended, far))
        far.second(*near.sent)
    proj = proj_operands(links, near, proj_weight)
    middle, second_low = merge(sizes, [attended], behind(start, far), proj, params)
    if boxed:
        far.third(*met(second_low, far))

    fc1_groups = fc1_bias.reshape(8, chunks, 128)
    ups = [up_operands(links, near, 1, full_up, 0), None, None]
    downs = [down_operands(links, near, 1, full_down, 0), None, None]
    halves = [[(0, (0, 256))], [(0, (256, 512))]]
    sums, pairs_out, hidden_sums = None, [], []
    waves = [Scatter(links, here, 256), Scatter(links, here, 256), Scatter(links, here, 512)]
    second_here = behind(second_low, far)
    for k in range(chunks):
        branch, grad_n2, away, stay, hidden_sum = feed(
            sizes, second_here, down_low, ups[k], downs[k], fc1_groups[:, k].reshape(1, -1), sums, k == chunks - 1
        )
        if k == 0:
            if boxed:
                far.fourth(True, *met(away, far))
                waves[0].first(after(away, *far.sent), stay)
            ups[1:] = [up_operands(links, far, 0, full_up, 1), up_operands(links, far, 1, full_up, 2)]
            downs[1:] = [down_operands(links, far, 0, full_down, 1), down_operands(links, far, 1, full_down, 2)]
            second_here = second_low
        elif k == 1 and boxed:
            exchange(links, [away], (waves[0], "second", halves))
            waves[1].first(after(away, *waves[0].sent), stay)
            second_here = behind(second_low, waves[0])
        elif boxed:
            exchange(links, [away], (waves[0], "third", None), (waves[1], "second", halves))
            waves[2].first(after(away, *waves[1].sent), stay)
        sums = (branch, grad_n2)
        pairs_out.append((away, stay))
        hidden_sums.append(hidden_sum)

    layer_out, grad_middle, grad_att, proj_away, proj_stay, middle_sums = middle_back(
        sizes, [attended], behind(branch, waves[0], waves[1]), grad_n2, middle, start, upstream, proj, params
    )
    if boxed:
        exchange(links, [grad_att], (waves[0], "halves", None), (waves[1], "third", None))
        waves[2].first(after(proj_away, *waves[1].sent), proj_stay)

    back, grads = [], None
    for number, (first, pairs) in enumerate(((0, 3), (3, 3))):
        grad_here = behind(grad_att, *(waves[:2] if number == 0 else waves[1:]))
        grads, *rest = attend_back(sizes, mixed, probs, grad_here, score_scale, first, pairs, grads)
        back.append(rest)
        if boxed and number == 0:
            exchange(
                links, [grads], (waves[0], "fifth", None), (waves[1], "halves", None),
                (waves[2], "second", [[(1, (0, 256)), (0, (0, 128))], [(0, (128, 512))]]),
            )
    if boxed:
        gap_grads = met(grads, waves[0])
        exchange(links, gap_grads, (waves[1], "fifth", None), (waves[2], "third", None))
    mix_away, mix_stay = mixed_grad(sizes, behind(first_low, waves[2]), grads)
    last = Scatter(links, here, 384)
    terms = jnp.concatenate([b[0] for b in back], axis=0)
    if boxed:
        gap_mix = met(mix_away, waves[1])
        exchange(links, gap_mix, (waves[2], "halves", None))
        last.first(after(mix_away, *waves[2].sent), mix_stay)
    grad_table = bias_back_kernel(after(behind(terms, waves[2]), mix_away), entry, grid_side, width)
    if boxed:
        exchange(links, [grad_table], (last, "second", [[(0, (0, 384))], [(0, (384, 640))]]))
    input_grad, start_sums = start_back(
        sizes, grads, qkv, start, behind(grad_middle, last), group_sizes, patterns, params
    )
    small_away, small_stay = pack(
        links, grad_table, heads, start_sums, middle_sums, [b[1:] for b in back], sum_fc2, hidden_sums
    )
    if boxed:
        exchange(links, [start_sums], (last, "third", None))
        small_away = after(small_away, *last.sent, *waves[2].flying)
    small = sum_everywhere(links, here, small_away, small_stay, last.flying)
    if boxed:
        exchange(links, [], (last, "fourth", None), (waves[2], "fifth", None))
        grad_qkv = qkv_home(here, last.done())
        blocks = [waves[0].done(*gap_grads), waves[1].done(*gap_mix), waves[2].done()]
        grad_proj = proj_home(here, blocks[2][:, 0:256])
        up_parts = [blocks[0][:, 0:256], blocks[1][:, 0:256], blocks[2][:, 256:512]]
        down_parts = [blocks[0][:, 256:512], blocks[1][:, 256:512], blocks[2][:, 512:768]]
        grad_fc1 = jnp.concatenate(
            [up_parts[k][:, 128 * half : 128 * half + 128] for half in range(2) for k in range(chunks)], axis=1
        )
        grad_fc2 = jnp.concatenate(
            [jnp.concatenate([p[:, :128], p[:, 128:]], axis=0) for p in down_parts], axis=1
        ).T
    else:
        tiles = [all_tiles(here, *pair) for pair in pairs_out]
        grad_qkv = native_scatter(natural_qkv(all_tiles(here, mix_away, mix_stay)))
        grad_proj = native_scatter(natural_proj(all_tiles(here, proj_away, proj_stay)))
        grad_fc1 = native_scatter(natural_up([t[..., :256] for t in tiles]))
        grad_fc2 = native_scatter(natural_down([t[..., 256:] for t in tiles]))
    at = heads
    hidden_rows = [
        jnp.concatenate([small[at + 11 + k], small[at + 14, 256 * k : 256 * k + 256]]).reshape(8, 128) for k in range(chunks)
    ]
    sum_fc1 = jnp.stack(hidden_rows, axis=1).reshape(-1)
    return (
        layer_out,
        input_grad,
        small[at + 2],
        small[at],
        small[at + 1],
        grad_qkv,
        small[at + 8],
        small[at + 9],
        small[:heads, :table_rows].T,
        grad_proj,
        small[at + 7],
        small[at + 6],
        small[at + 4],
        small[at + 5],
        grad_fc1,
        sum_fc1,
        grad_fc2,
        small[at + 10],
        small[at + 3],
    )


def solution(mesh):
    images = P(AXES, None, None)
    both = P("wide", "narrow")
    same = P()
    links = Links(mesh.shape["wide"], mesh.shape["narrow"])
    return jax.shard_map(
        functools.partial(local, links),
        mesh=mesh,
        in_specs=(
            images, images, same, same, same, same, same, both, same, same, same, both, same, same,
            same, same, both, same, both, same, same,
        ),
        out_specs=(
            images, images, same, same, same, both, same, same, same, both, same, same, same, same,
            both, same, both, same, same,
        ),
        check_vma=False,
    )
```

```python
import functools
import math

import jax
import jax.numpy as jnp
import numpy as np
from jax import lax
from jax.experimental import pallas as pl
from jax.experimental.pallas import tpu as pltpu
from jax.sharding import PartitionSpec as P

EPSILON = 1e-06
ROOT_HALF = 0.7071067811865476
DENSITY = 0.3989422804014327
BF16 = jnp.bfloat16
F32 = jnp.float32
AXES = ("wide", "narrow")
TILE = 512
BAND = 200
CHUNK = 1024
NEVER = -1e30
MIB = 1 << 20


class Links:
    def __init__(self, wide, narrow):
        self.wide, self.narrow = wide, narrow
        self.y = 1 << ((wide.bit_length() - 1) // 2)
        self.z = wide // self.y
        self.x = narrow // 2
        self.size = {"z": self.z, "y": self.y, "x": self.x, "core": 2}
        self.unit = {"core": 1, "x": 2, "y": narrow, "z": narrow * self.y}
        self.boxed = (self.z, self.y, self.x) == (4, 2, 2)

    def place(self):
        w, n = lax.axis_index("wide"), lax.axis_index("narrow")
        return {"z": w // self.y, "y": w % self.y, "x": n // 2, "core": n % 2, "w": w, "n": n}

    def swap(self, value, **offsets):
        mask = sum(self.unit[axis] * offset for axis, offset in offsets.items())
        count = self.wide * self.narrow
        return lax.ppermute(value, AXES, [(k, k ^ mask) for k in range(count)])

    def others(self, value, axis):
        return [self.swap(value, **{axis: d}) for d in range(1, self.size[axis])]


def pick(value, axis, index, count):
    size = value.shape[axis] // count
    return lax.dynamic_slice_in_dim(value, index * size, size, axis)


def after(value, *others):
    return lax.optimization_barrier((value,) + others)[0]


def tied(values, wait):
    if not wait:
        return list(values)
    return list(lax.optimization_barrier(tuple(values) + tuple(wait)))[: len(values)]


def native_gather(shard):
    return lax.all_gather(
        lax.all_gather(shard, "narrow", axis=1, tiled=True), "wide", axis=0, tiled=True
    )


class Gather:
    orders = (("x", "y"), ("y", "x"))

    def __init__(self, links, block, split, groups):
        self.links, self.block, self.split, self.groups = links, block, split, groups

    def first(self, *wait):
        block = after(self.block, *wait) if wait else self.block
        self.sent = [block]
        self.steps = [block] + self.links.others(block, "z")
        self.flying = self.steps[1:]

    def second(self, *wait):
        parts = arrange([after(self.steps[0], *wait) if wait else self.steps[0]] + self.steps[1:], self.split)
        self.steps, self.sent = [], []
        for held, order in zip(parts, self.orders, strict=True):
            self.sent.append(held)
            self.steps.append([held] + self.links.others(held, order[0]))
        self.flying = [v for p in self.steps for v in p[1:]]

    def third(self, *wait):
        parts = stack([[after(self.steps[0][0], *wait)] + self.steps[0][1:], self.steps[1]])
        self.steps, self.sent = [], []
        for held, order in zip(parts, self.orders, strict=True):
            self.sent.append(held)
            self.steps.append([held] + self.links.others(held, order[1]))
        self.flying = [v for p in self.steps for v in p[1:]]

    def fourth(self, far, *wait):
        first = after(self.steps[0][0], *wait)
        self.operands = []
        held = regroup([[first] + self.steps[0][1:], self.steps[1]], self.groups, far)
        for number, array in enumerate(held):
            self.operands.append([array, self.links.swap(array, core=1)])
        self.sent = held
        self.flying = [pair[1] for pair in self.operands]

    def blocks(self, refs, number, me):
        links = self.links
        order = self.orders[number]
        out = []
        for core in range(2):
            for k in range(refs[core].shape[0]):
                at, rest = {}, k
                for axis in ("z",) + order:
                    at[axis] = me[axis] ^ (rest % links.size[axis])
                    rest //= links.size[axis]
                source = functools.partial(block_columns, refs[core], k)
                out.append((source, at["z"] * links.y + at["y"], at["x"] * 2 + (me["core"] ^ core)))
        return out


def block_columns(ref, k, col, broad):
    return ref.at[k, :, pl.ds(col, broad)]


def at_least(n, values):
    out = values[3]
    for k in (2, 1, 0):
        out = jnp.where(n == k, values[k], out)
    return out


def window(ref, row, col, tall, broad):
    if not isinstance(row, int):
        row = pl.multiple_of(row, 8)
    if not isinstance(col, int):
        col = pl.multiple_of(col, 128)
    return ref.at[pl.ds(row, tall), pl.ds(col, broad)]


def columns(ref, col, broad):
    return ref.at[:, pl.ds(col, broad)]


class Weight:
    def __init__(self, operands, copies, joints=(), extra=0):
        self.operands, self.copies, self.joints, self.extra = operands, copies, joints, extra

    def fill(self, refs, target, sem):
        for source, to in self.copies(refs, target):
            pltpu.make_async_copy(source, to, sem).start()

    def wait(self, target, sem):
        pltpu.make_async_copy(target, target, sem).wait()
        for here, there in self.joints:
            target[:, here : here + 128] += target[:, there : there + 128]


def align_side(here, side):
    zero = jnp.zeros((side.shape[0], 64), side.dtype)
    return jnp.where(
        here["n"] % 2 == 0,
        jnp.concatenate([side, zero], axis=1),
        jnp.concatenate([zero, side], axis=1),
    )


def qkv_block(here, shard):
    even = here["n"] % 2 == 0
    main = jnp.where(even, shard[:, :384], shard[:, 192:])
    return jnp.concatenate([main, align_side(here, jnp.where(even, shard[:, 384:], shard[:, :192]))], axis=1)


def qkv_operands(links, gathered, shard):
    if not links.boxed:
        return Weight([native_gather(shard)], lambda refs, target: [(refs[0], target.at[:, pl.ds(0, 2304)])] + [
            (refs[0].at[:, pl.ds(0, 256)], target.at[:, pl.ds(2304, 256)])], extra=256)

    def copies(refs, target):
        me = links.place()
        out = []
        for source, w, n in gathered.blocks(refs, 0, me):
            out.append((source(0, 384), window(target, w * 96, at_least(n, (0, 768, 1152, 1920)), 96, 384)))
        for source, w, n in gathered.blocks(refs, 1, me):
            for part, places in enumerate(((384, 2304, 1536, 2432), (512, 640, 1664, 1792))):
                out.append((source(384 + 128 * part, 128), window(target, w * 96, at_least(n, places), 96, 128)))
        return out

    return Weight(gathered.operands[0], copies, ((512, 2304), (1664, 2432)), 256)


def proj_operands(links, gathered, shard):
    if not links.boxed:
        return Weight([native_gather(shard)], lambda refs, target: [(refs[0], target.at[:, pl.ds(0, 768)])] + [
            (refs[0].at[:, pl.ds(0, 256)], target.at[:, pl.ds(768, 256)])], extra=256)

    def copies(refs, target):
        me = links.place()
        out = []
        for part, (col, places) in enumerate(((0, (0, 768, 384, 896)), (128, (128, 256, 512, 640)))):
            for source, w, n in gathered.blocks(refs, part, me):
                out.append((source(col, 128), window(target, w * 96, at_least(n, places), 96, 128)))
        return out

    return Weight(gathered.operands[0], copies, ((128, 768), (512, 896)), 256)


def up_block(shard, chunk):
    return jnp.concatenate(
        [shard[:, 384 * half + 128 * chunk : 384 * half + 128 * chunk + 128] for half in range(2)], axis=1
    )


def down_block(shard_t, chunk):
    piece = shard_t[:, 128 * chunk : 128 * chunk + 128]
    half = piece.shape[0] // 2
    return jnp.concatenate([piece[:half], piece[half:]], axis=1)


def chunk_copies(full, chunk):
    def slices(refs, target):
        return [
            (columns(refs[0], 384 * g + 128 * chunk, 128), columns(target, 128 * g, 128)) for g in range(8)
        ]

    return Weight([full], slices)


def up_operands(links, gathered, group, full, chunk):
    if not links.boxed:
        return chunk_copies(full, chunk)

    def copies(refs, target):
        me = links.place()
        return [
            (source(0, 256), window(target, w * 96, n * 256, 96, 256))
            for source, w, n in gathered.blocks(refs, 0, me)
        ]

    return Weight(gathered.operands[group], copies)


def down_operands(links, gathered, group, full, chunk):
    if not links.boxed:
        return chunk_copies(full, chunk)

    def copies(refs, target):
        me = links.place()
        return [
            (source(256 + 128 * half, 128), window(target, n * 192 + half * 96, w * 128, 96, 128))
            for source, w, n in gathered.blocks(refs, 1, me)
            for half in range(2)
        ]

    return Weight(gathered.operands[group], copies)


class Scatter:
    orders = (("x", "y"), ("y", "x"))

    def __init__(self, links, here, split):
        self.links, self.here, self.split = links, here, split
        self.pairs, self.flying, self.stage = [], [], 0

    def first(self, away, stay):
        shape = (self.links.x, self.links.z, self.links.y) + away.shape[2:]
        self.pairs.append((stay.reshape(shape), self.links.swap(away.reshape(shape), core=1)))
        self.flying.append(self.pairs[-1][1])

    def jobs(self, step, picks):
        if step == "second":
            return [
                ([(self.pairs[k], cols) for k, cols in part], order[0])
                for part, order in zip(picks, self.orders, strict=True)
            ]
        whole_of = [(t, (0, t[0].shape[-1])) for t in self.terms]
        if step == "third":
            return [([t], order[1]) for t, order in zip(whole_of, self.orders, strict=True)]
        if step == "fifth":
            return [([(self.terms[0], (0, self.terms[0][0].shape[-1]))], "z_low")]
        return [(whole_of, "z_high" if step == "halves" else "z")]

    def take(self, results, unit):
        self.sent = [v for r in results for v in r[1:]]
        self.terms = []
        axes = [(order[self.stage], 1) for order in self.orders] if self.stage < 2 else [("z", unit)]
        for (keep, *sent), (axis, step) in zip(results, axes, strict=True):
            self.terms.append([keep] + [self.links.swap(v, **{axis: d * step}) for d, v in enumerate(sent, 1)])
        self.stage += 1
        self.flying = [v for t in self.terms for v in t[1:]]

    def done(self, *wait):
        terms = tied(self.terms[0], wait)
        total = terms[0]
        for term in terms[1:]:
            total = total + term.astype(F32)
        return total.reshape(total.shape[-2:])


def exchange(links, wait, *items):
    jobs = [job for scatter, step, picks in items for job in scatter.jobs(step, picks)]
    group, cols = jobs[0][0][0]
    jobs[0][0][0] = ((after(group[0], *wait),) + tuple(group[1:]), cols)
    results = fold(links, jobs)
    for scatter, step, _ in items:
        count = 2 if step in ("second", "third") else 1
        scatter.take(results[:count], 2 if step == "halves" else 1)
        results = results[count:]


def all_tiles(here, away, stay):
    return jnp.where(
        here["core"] == 0, jnp.stack([stay, away], axis=1), jnp.stack([away, stay], axis=1)
    ).reshape((4,) + away.shape[1:])


def native_scatter(partial):
    low = lax.psum_scatter(partial.astype(BF16), "wide", scatter_dimension=0, tiled=True)
    return lax.psum_scatter(low, "narrow", scatter_dimension=1, tiled=True).astype(F32)


def qkv_home(here, block):
    even = here["n"] % 2 == 0
    main, side = block[:, :384], block[:, 384:]
    return jnp.where(
        even,
        jnp.concatenate([main, side[:, :192]], axis=1),
        jnp.concatenate([side[:, 64:], main], axis=1),
    )


def proj_home(here, block):
    return jnp.where(here["n"] % 2 == 0, block[:, :192], block[:, 64:])


def natural_qkv(tiles):
    tiles = tiles.reshape(4, 768, 640)
    out = []
    for n in range(4):
        main, side = tiles[n, :, :384], tiles[n, :, 384:]
        out += [main, side[:, :192]] if n % 2 == 0 else [side[:, 64:], main]
    return jnp.concatenate(out, axis=1)


def natural_proj(tiles):
    tiles = tiles.reshape(4, 768, 256)
    return jnp.concatenate([tiles[n, :, :192] if n % 2 == 0 else tiles[n, :, 64:] for n in range(4)], axis=1)


def natural_up(chunks):
    tiles = [t.reshape(4, 768, 2, 128) for t in chunks]
    return jnp.stack(tiles, axis=0).transpose(2, 1, 3, 0, 4).reshape(768, -1)


def natural_down(chunks):
    tiles = [t.reshape(4, 8, 96, 2, 128) for t in chunks]
    return jnp.stack(tiles, axis=0).transpose(2, 0, 5, 1, 4, 3).reshape(-1, 768)


def tree_sum(terms):
    while len(terms) > 1:
        terms = [terms[k] + terms[k + 1] for k in range(0, len(terms), 2)]
    return terms[0]


def sum_everywhere(links, here, away, stay, wait):
    if links.boxed:
        half = after(stay + links.swap(away, core=1), *wait)
        steps = [
            (axis, 1 << bit) for axis in ("z", "x", "y") for bit in range(links.size[axis].bit_length() - 1)
        ]
        for axis, step in sorted(steps, key=lambda s: s[0] == "z" and s[1] > 1):
            half = half + links.swap(half, **{axis: step})
        other = links.swap(half, core=1)
    else:
        first = jnp.where(here["core"] == 0, stay, away)
        second = jnp.where(here["core"] == 0, away, stay)
        return lax.psum(jnp.concatenate([first, second], axis=0), AXES)
    return jnp.where(
        here["core"] == 0, jnp.concatenate([half, other], axis=0), jnp.concatenate([other, half], axis=0)
    )


def whole(shape):
    return pl.BlockSpec(tuple(shape), lambda *_: (0,) * len(shape))


def kept(shape):
    return pl.BlockSpec(tuple(shape), lambda *_: (0,) * len(shape), pipeline_mode=pl.Buffered(1))


ANY = pl.BlockSpec(memory_space=pl.ANY)
FAR = pl.BlockSpec(memory_space=pltpu.HBM)
SCALARS = pl.BlockSpec(memory_space=pltpu.SMEM)


LIMITS = {"stack": 16, "arrange": 8, "fold": 24, "pack": 8, "prepare": 16, "bias": 16, "bias_back": 20, "project": 24, "attend": 18, "merge": 20, "feed": 28, "middle_back": 28, "attend_back": 22, "mixed_grad": 24, "start_back": 28}


def call(kernel, name, grid, ins, outs, scratch=(), flops=0, aliases=None):
    moved = sum(a.size * a.dtype.itemsize for a, *_ in ins)
    moved += sum(math.prod(s) * jnp.dtype(d).itemsize for s, d, *_ in outs)
    return pl.pallas_call(
        kernel,
        name=name,
        grid=grid,
        in_specs=[spec for _, spec, *_ in ins],
        out_specs=[spec for _, _, spec, *_ in outs],
        out_shape=[pltpu.HBM(s, d) if far else jax.ShapeDtypeStruct(s, d) for s, d, _, *far in outs],
        scratch_shapes=list(scratch),
        input_output_aliases=aliases or {},
        compiler_params=pltpu.CompilerParams(vmem_limit_bytes=LIMITS[name] * MIB),
        cost_estimate=pl.CostEstimate(flops=int(flops), bytes_accessed=int(moved), transcendentals=0),
    )(*[pltpu.with_memory_space_constraint(a, pltpu.HBM) if far else a for a, _, *far in ins])


def nn(a, b):
    return lax.dot_general(a, b, (((1,), (0,)), ((), ())), preferred_element_type=F32)


def nt(a, b):
    return lax.dot_general(a, b, (((1,), (1,)), ((), ())), preferred_element_type=F32)


def tn(a, b):
    return lax.dot_general(a, b, (((0,), (0,)), ((), ())), preferred_element_type=F32)


def arrange(blocks, split):
    rows, cols = blocks[0].shape
    count = len(blocks)

    def kernel(*refs):
        for k in range(count):
            refs[count][k] = refs[k][:, :split]
            refs[count + 1][k] = refs[k][:, split:]

    return call(
        kernel, "arrange", (),
        [(b, whole(b.shape)) for b in blocks],
        [((count, rows, part), BF16, whole((count, rows, part))) for part in (split, cols - split)],
    )


def stack(parts):
    flat = [v for part in parts for v in part]
    outs = [(sum(v.shape[0] for v in part), part[0].shape[1], part[0].shape[2]) for part in parts]

    def kernel(*refs):
        number = 0
        for k, part in enumerate(parts):
            at = 0
            for v in part:
                refs[len(flat) + k][at : at + v.shape[0]] = refs[number][...]
                at += v.shape[0]
                number += 1

    return call(
        kernel, "stack", (), [(v, whole(v.shape)) for v in flat], [(shape, BF16, whole(shape)) for shape in outs]
    )


def regroup(parts, groups, far):
    flat = [v for part in parts for v in part]
    count, rows = sum(v.shape[0] for v in parts[0]), parts[0][0].shape[1]
    outs = [(count, rows, sum(end - begin for begin, end in group)) for group in groups]

    def kernel(*refs):
        for out, group in zip(refs[len(flat) :], groups, strict=True):
            number, col = 0, 0
            for part, (begin, end) in zip(parts, group, strict=True):
                at = 0
                for v in part:
                    if end > begin:
                        out[at : at + v.shape[0], :, col : col + end - begin] = refs[number][:, :, begin:end]
                    at += v.shape[0]
                    number += 1
                col += end - begin

    return call(
        kernel, "stack", (), [(v, whole(v.shape)) for v in flat],
        [(shape, BF16, whole(shape), FAR) if far else (shape, BF16, whole(shape)) for shape in outs],
    )


def fold(links, jobs):
    arrays, index = [], {}
    for sources, _ in jobs:
        for group, _ in sources:
            for array in group:
                if id(array) not in index:
                    index[id(array)] = len(arrays)
                    arrays.append(array)
    dims = {"x": 0, "z": 1, "z_high": 1, "z_low": 1, "y": 2}
    size = dict(links.size, z_high=2, z_low=2)
    held = {"x": 1, "y": 1, "z": 1, "z_high": links.z // 2, "z_low": 1}
    outs = []
    for sources, axis in jobs:
        first = sources[0][0][0]
        cols = sum(part[1] - part[0] for _, part in sources)
        shape = tuple(held[axis] if k == dims[axis] else first.shape[k] for k in range(4)) + (cols,)
        outs += [(shape, F32 if d == 0 else BF16, whole(shape)) for d in range(size[axis])]

    def kernel(*refs):
        me = links.place()
        me["z_high"], me["z_low"] = me["z"] // 2, me["z"] % 2
        at_out = len(arrays)
        for sources, axis in jobs:
            for d in range(size[axis]):
                where = [slice(None)] * 4
                where[dims[axis]] = pl.ds((me[axis] ^ d) * held[axis], held[axis])
                col = 0
                for group, (begin, end) in sources:
                    picked = tuple(where) + (slice(begin, end),)
                    total = refs[index[id(group[0])]][picked].astype(F32)
                    for array in group[1:]:
                        total = total + refs[index[id(array)]][picked].astype(F32)
                    out = refs[at_out]
                    out[..., col : col + end - begin] = total.astype(out.dtype)
                    col += end - begin
                at_out += 1

    results = call(kernel, "fold", (), [(a, whole(a.shape)) for a in arrays], outs)
    out = []
    for _, axis in jobs:
        out.append(results[: size[axis]])
        results = results[size[axis] :]
    return out


def pack(links, table, heads, start_sums, middle_sums, halves, sum_fc2, hidden_sums):
    width = table.shape[1]

    def kernel(table_ref, start_ref, middle_ref, q0, v0, q1, v1, fc2_ref, a_ref, b_ref, c_ref, away_ref, stay_ref, all_s):
        all_s[...] = jnp.zeros_like(all_s)
        rows = [(table_ref, heads), (start_ref, 3), (middle_ref, 5)]
        at = 0
        for ref, count in rows:
            for k in range(count):
                all_s[(at + k) // 16, (at + k) % 16 : (at + k) % 16 + 1, :] = ref[k : k + 1, :]
            at += count
        for pair in ((q0, q1), (v0, v1)):
            for k, ref in enumerate(pair):
                all_s[at // 16, at % 16 : at % 16 + 1, k * 384 : k * 384 + 384] = ref[...]
            at += 1
        all_s[at // 16, at % 16 : at % 16 + 1, :] = fc2_ref[...]
        at += 1
        for k, ref in enumerate((a_ref, b_ref, c_ref)):
            all_s[(at + k) // 16, (at + k) % 16 : (at + k) % 16 + 1, :] = ref[:, 0:width]
            all_s[(at + 3) // 16, (at + 3) % 16 : (at + 3) % 16 + 1, k * 256 : k * 256 + 256] = ref[:, width : width + 256]
        c = lax.axis_index("narrow") % 2
        away_ref[...] = all_s[1 - c]
        stay_ref[...] = all_s[c]

    operands = [table, start_sums, middle_sums, *halves[0], *halves[1], sum_fc2, *hidden_sums]
    return call(
        kernel, "pack", (), [(a, whole(a.shape)) for a in operands],
        [((16, width), F32, whole((16, width)))] * 2, [pltpu.VMEM((2, 16, width), F32)],
    )


def norm(values):
    centre = jnp.mean(values, axis=-1, keepdims=True)
    centred = values - centre
    spread = jnp.mean(centred * centred, axis=-1, keepdims=True)
    scaling = lax.rsqrt(spread + EPSILON)
    return centred * scaling, scaling


def norm_back(grad, normed, scaling, gain):
    scaled = grad * gain
    first = jnp.mean(scaled, axis=-1, keepdims=True)
    second = jnp.mean(scaled * normed, axis=-1, keepdims=True)
    return (scaled - first - normed * second) * scaling


def banded(tall, body):
    if BAND >= tall:
        body(slice(0, tall), 0)
        return

    def step(k, carry):
        at = pl.multiple_of(k * BAND, 8)
        body(pl.ds(at, BAND), at)
        return carry

    lax.fori_loop(0, tall // BAND, step, 0)


def column_sum(values):
    return jnp.sum(values, axis=0, keepdims=True)


TOKEN, GAIN1, SHIFT1, GAMMA2, BIAS1, GAMMA1, GAIN2, SHIFT2, BIAS2 = range(9)


def row_of(ref, k):
    return ref[k : k + 1, :]


def masked_rows(image, sizes_ref, patterns_ref, tall):
    bound, group = 0, 0
    for k in range(sizes_ref.shape[0] - 1):
        bound = bound + sizes_ref[k]
        group = group + (image >= bound).astype(jnp.int32)
    columns_of = patterns_ref[...].T
    which = lax.broadcasted_iota(jnp.int32, columns_of.shape, 1) == group
    return jnp.sum(jnp.where(which, columns_of, 0.0), axis=1, keepdims=True)[0:tall] > 0.5


def first_image(images):
    return lax.axis_index(AXES) * images


def prepare(sizes, inputs, cotangent, group_sizes, mask_patterns, vectors):
    images, length, tall, width = sizes
    rows = images * tall
    groups, patches = mask_patterns.shape

    def kernel(x_ref, g_ref, sizes_ref, mask_ref, *refs):
        vector_refs, refs = refs[: len(vectors)], refs[len(vectors) :]
        h0_ref, n1_ref, g_out, df_ref, sum_ref, params_ref, patterns_ref, x_s, g_s, mask_s, sems, *vector_s = refs
        step = pl.program_id(0)

        @pl.when(step == 0)
        def _():
            x_s[...] = jnp.zeros_like(x_s)
            g_s[...] = jnp.zeros_like(g_s)
            sum_ref[...] = jnp.zeros_like(sum_ref)
            params_ref[...] = jnp.zeros_like(params_ref)
            patterns_ref[...] = jnp.zeros_like(patterns_ref)
            moves = [pltpu.make_async_copy(mask_ref, mask_s, sems.at[len(vectors)])]
            moves += [
                pltpu.make_async_copy(a, b, sems.at[k]) for k, (a, b) in enumerate(zip(vector_refs, vector_s, strict=True))
            ]
            for move in moves:
                move.start()
            for move in moves:
                move.wait()
            patterns_ref[0:groups, 1 : patches + 1] = mask_s[...].astype(F32)
            for k, ref in zip(vectors, vector_s, strict=True):
                params_ref[k : k + 1, :] = ref[...].reshape(1, width)

        x_s[0:length, :] = x_ref[0].astype(F32)
        g_s[0:length, :] = g_ref[0].astype(F32)
        masked = masked_rows(first_image(images) + step, sizes_ref, patterns_ref, tall)
        start = jnp.where(masked, row_of(params_ref, TOKEN), x_s[...])
        h0_ref[...] = start
        normed, _ = norm(start)
        n1_ref[...] = (normed * row_of(params_ref, GAIN1) + row_of(params_ref, SHIFT1)).astype(BF16)
        g = g_s[...]
        g_out[...] = g.astype(BF16)
        df = row_of(params_ref, GAMMA2) * g
        df_ref[...] = df.astype(BF16)
        sum_ref[...] += column_sum(df)

    image = pl.BlockSpec((1, length, width), lambda i: (i, 0, 0))
    band = pl.BlockSpec((tall, width), lambda i: (i, 0))
    return call(
        kernel, "prepare", (images,),
        [(inputs, image), (cotangent, image), (group_sizes, SCALARS), (mask_patterns, ANY, FAR)]
        + [(v, ANY, FAR) for v in vectors.values()],
        [((rows, width), F32, band), ((rows, width), BF16, band), ((rows, width), BF16, band, FAR),
         ((rows, width), BF16, band, FAR), ((1, width), F32, whole((1, width))), ((16, width), F32, whole((16, width))),
         ((8, 256), F32, whole((8, 256)))],
        [pltpu.VMEM((tall, width), F32), pltpu.VMEM((tall, width), F32), pltpu.VMEM(mask_patterns.shape, jnp.int32),
         pltpu.SemaphoreType.DMA((len(vectors) + 1,))] + [pltpu.VMEM((width,), F32) for _ in vectors],
        flops=rows * width * 40,
    )


def table_columns(grid_side, broad):
    side = 2 * grid_side - 1
    q = np.arange(broad)
    entry = (q // grid_side) * side + q % grid_side + grid_side - 1
    return jnp.asarray(np.where(q < side * grid_side, entry, -(1 << 20)).astype(np.int32)[None])


def three_parts(values):
    high = values.astype(BF16)
    rest = values - high.astype(F32)
    middle = rest.astype(BF16)
    return high, middle, (rest - middle.astype(F32)).astype(BF16)


def bias_kernel(table_t, entry, grid_side, tall, broad):
    heads = table_t.shape[0]
    length = grid_side * grid_side + 1
    wide = entry.shape[1]
    inner = (2 * grid_side - 1) ** 2

    def kernel(table_ref, entry_ref, out_ref, *halves):
        def put(at, count, values):
            for half, ref in enumerate(halves):
                ref[pl.ds(at, count), :] = values[:, 128 * half : 128 * half + 128]

        parts = jnp.concatenate(three_parts(table_ref[...]), axis=0)
        left, top, corner = (table_ref[:, inner + 1 : inner + 2], table_ref[:, inner : inner + 1],
                             table_ref[:, inner + 2 : inner + 3])
        lane = lax.broadcasted_iota(jnp.int32, (heads, broad), 1)

        def column(b, carry):
            which = lax.broadcasted_iota(jnp.int32, (table_ref.shape[1], wide), 0) + b
            select = jnp.where(which == entry_ref[...], 1.0, 0.0).astype(BF16)
            spread = nn(parts, select)
            spread = spread[:heads] + spread[heads : 2 * heads] + spread[2 * heads :]
            for a in range(grid_side):
                shift = (grid_side - 1 - a) * grid_side - 1
                moved = pltpu.roll(spread, (wide - shift) % wide, 1)[:, :broad]
                moved = jnp.where(lane == 0, top, moved)
                put(pl.multiple_of((1 + grid_side * a + b) * heads, 16), heads, moved)
            return carry

        lax.fori_loop(0, grid_side, column, 0)
        put(0, heads, jnp.where(lane == 0, corner, left))
        rest = (tall - length) * heads
        put(length * heads, rest, jnp.full((rest, broad), NEVER, F32))
        for h in range(out_ref.shape[0]):
            for half, ref in enumerate(halves):
                out_ref[h, :, 128 * half : 128 * half + 128] = ref[pl.ds(h, tall, stride=heads), :]

    return call(
        kernel, "bias", (),
        [(table_t, whole(table_t.shape)), (entry, whole(entry.shape))],
        [((12, tall, broad), F32, whole((12, tall, broad)))],
        [pltpu.VMEM((tall * heads, 128), F32)] * (broad // 128),
        flops=2 * 48 * 768 * wide * grid_side,
    )[0]


def bias_back_kernel(terms, entry, grid_side, width):
    count, tall, broad = terms.shape
    heads = 16
    wide = entry.shape[1]
    inner = (2 * grid_side - 1) ** 2
    length = grid_side * grid_side + 1

    def kernel(terms_ref, entry_ref, out_ref, *halves):
        def get(at, count):
            return jnp.concatenate([ref[pl.ds(at, count), :] for ref in halves], axis=1)

        lane = lax.broadcasted_iota(jnp.int32, (heads, broad), 1)
        inside = (lane >= 1) & (lane < length)
        for h in range(heads):
            values = terms_ref[h] if h < count else jnp.zeros((tall, broad), F32)
            for half, ref in enumerate(halves):
                ref[pl.ds(h, tall, stride=heads), :] = values[:, 128 * half : 128 * half + 128]

        def column(b, carry):
            total, edge = carry
            which = lax.broadcasted_iota(jnp.int32, (width, wide), 0) + b
            select = jnp.where(which == entry_ref[...], 1.0, 0.0).astype(BF16)
            spread = jnp.zeros((heads, wide), F32)
            for a in range(grid_side):
                shift = (grid_side - 1 - a) * grid_side - 1
                found = get(pl.multiple_of((1 + grid_side * a + b) * heads, 16), heads)
                edge = edge + jnp.where(lane == 0, found, 0.0)
                found = jnp.where(inside, found, 0.0)
                found = jnp.concatenate([found, jnp.zeros((heads, wide - broad), F32)], axis=1)
                spread = spread + pltpu.roll(found, shift % wide, 1)
            found = nt(jnp.concatenate(three_parts(spread), axis=0), select)
            total = total + found[:heads] + found[heads : 2 * heads] + found[2 * heads :]
            return total, edge

        total, edge = lax.fori_loop(
            0, grid_side, column, (jnp.zeros((heads, width), F32), jnp.zeros((heads, broad), F32))
        )
        first = get(0, heads)
        top = jnp.sum(edge, axis=1, keepdims=True)
        left = jnp.sum(jnp.where(inside, first, 0.0), axis=1, keepdims=True)
        corner = first[:, 0:1]
        place = lax.broadcasted_iota(jnp.int32, (heads, width), 1)
        total = jnp.where(place == inner, top, total)
        total = jnp.where(place == inner + 1, left, total)
        out_ref[...] = jnp.where(place == inner + 2, corner, total)

    return call(
        kernel, "bias_back", (),
        [(terms, whole(terms.shape)), (entry, whole(entry.shape))],
        [((heads, width), F32, whole((heads, width)))],
        [pltpu.VMEM((tall * heads, 128), F32)] * (broad // 128),
        flops=2 * 48 * 768 * wide * grid_side,
    )[0]


def project(sizes, first_low, weight, params, score_scale):
    images, length, tall, width = sizes
    rows = images * tall
    cols = 3 * width
    count = len(weight.operands)

    def kernel(*refs):
        n1_ref, params_ref = refs[:2]
        out_ref, w_s, sem = refs[2 + count :]
        step = pl.program_id(0)

        @pl.when(step == 0)
        def _():
            weight.fill(refs[2 : 2 + count], w_s, sem)
            weight.wait(w_s, sem)

        w = w_s[:, pl.ds(pl.multiple_of(step * width, 128), width)]
        scale = jnp.where(step == 0, score_scale, 1.0)
        out_ref[...] = ((nn(n1_ref[...], w) + params_ref[pl.ds(9 + step, 1), :]) * scale).astype(BF16)

    return call(
        kernel, "project", (cols // width,),
        [(first_low, kept((rows, width))), (params, kept(params.shape))] + [(a, ANY) for a in weight.operands],
        [((rows, cols), BF16, pl.BlockSpec((rows, width), lambda t: (0, t)))],
        [pltpu.VMEM((width, cols + weight.extra), BF16), pltpu.SemaphoreType.DMA],
        flops=2 * rows * width * cols,
    )[0]


def head_masks(tall):
    lane = lax.broadcasted_iota(jnp.int32, (tall, 128), 1)
    return [lane < 64, lane >= 64]


def attend(sizes, mixed, bias, first, pairs):
    images, length, tall, width = sizes
    rows = images * tall
    every = width // 128
    broad = bias.shape[2]

    def kernel(q_ref, k_ref, v_ref, bias_ref, out_ref, p_ref):
        masks = head_masks(tall)
        units = [(i, h) for i in range(images) for h in range(2)]
        scores, probs = [], []
        for i, h in units:
            q, k = q_ref[tall * i : tall * i + tall, :], k_ref[tall * i : tall * i + tall, :]
            scores.append(nt(k, jnp.where(masks[h], q, jnp.zeros_like(q))) + bias_ref[h, :, 0:tall])
        for (i, h), s in zip(units, scores, strict=True):
            e = jnp.exp(s - jnp.max(s, axis=0, keepdims=True))
            p = (e * (1.0 / jnp.sum(e, axis=0, keepdims=True))).astype(BF16)
            p_ref[h, i, :, 0:tall] = p
            probs.append(p)
        for i in range(images):
            vt = v_ref[tall * i : tall * i + tall, :].T
            out = [nn(vt[64 * h : 64 * h + 64, :], probs[2 * i + h]) for h in range(2)]
            out_ref[tall * i : tall * i + tall, :] = jnp.concatenate(out, axis=0).T.astype(BF16)

    def column(at):
        return pl.BlockSpec((rows, 128), lambda t: (0, at + t))

    return call(
        kernel, "attend", (pairs,),
        [(mixed, column(first)), (mixed, column(every + first)), (mixed, column(2 * every + first)),
         (bias, pl.BlockSpec((2, tall, broad), lambda t: (first + t, 0, 0)))],
        [((rows, 128 * pairs), BF16, column(0), FAR),
         ((2 * pairs, images, tall, broad), BF16,
          pl.BlockSpec((2, images, tall, broad), lambda t: (t, 0, 0, 0)), FAR)],
        flops=4 * rows * tall * 128 * pairs,
    )


def attend_back(sizes, mixed, probs, grad_out, score_scale, first, pairs, so_far):
    images, length, tall, width = sizes
    rows = images * tall
    every = width // 128
    broad = probs.shape[3]

    def kernel(q_ref, k_ref, v_ref, do_ref, p_ref, *refs):
        grad_ref, terms_ref, qb_ref, vb_ref = refs[-4:]
        masks = head_masks(tall)
        units = [(i, h) for i in range(images) for h in range(2)]

        def part(ref, i):
            return ref[tall * i : tall * i + tall, :]

        def own(value, h):
            return jnp.where(masks[h], value, jnp.zeros_like(value))

        grads = [nt(part(v_ref, i), own(part(do_ref, i), h)) for i, h in units]
        lows = []
        for (i, h), grad in zip(units, grads, strict=True):
            p = p_ref[h, i, :, 0:tall].astype(F32)
            t = p * grad
            lows.append((t - p * jnp.sum(t, axis=0, keepdims=True)).astype(BF16))
        for h in range(2):
            terms_ref[h, :, 0:tall] = sum(lows[2 * i + h].astype(F32) for i in range(images))
            terms_ref[h, :, tall:] = jnp.zeros((tall, broad - tall), F32)
        query_sum, value_sum = 0.0, 0.0
        for i in range(images):
            kt = part(k_ref, i).T
            dv = sum(nn(p_ref[h, i, :, 0:tall], own(part(do_ref, i), h)) for h in range(2))
            dk = sum(nn(lows[2 * i + h], own(part(q_ref, i), h)) for h in range(2))
            dq = jnp.concatenate(
                [nn(kt[64 * h : 64 * h + 64, :], lows[2 * i + h]) for h in range(2)], axis=0
            ).T * score_scale
            for number, grad in enumerate((dq, dk, dv)):
                grad_ref[number, tall * i : tall * i + tall, :] = grad.astype(BF16)
            query_sum += column_sum(dq)
            value_sum += column_sum(dv)
        qb_ref[...] = query_sum
        vb_ref[...] = value_sum

    def column(at):
        return pl.BlockSpec((rows, 128), lambda t: (0, at + t))

    one = pl.BlockSpec((1, 128), lambda t: (0, t))
    return call(
        kernel, "attend_back", (pairs,),
        [(mixed, column(first)), (mixed, column(every + first)), (mixed, column(2 * every + first)),
         (grad_out, column(first)),
         (probs, pl.BlockSpec((2, images, tall, broad), lambda t: (first + t, 0, 0, 0)), FAR)]
        + ([] if so_far is None else [(so_far, ANY)]),
        [((3, rows, width), BF16, pl.BlockSpec((3, rows, 128), lambda t: (0, 0, first + t)))]
        + [((2 * pairs, tall, broad), F32, pl.BlockSpec((2, tall, broad), lambda t: (t, 0, 0))),
           ((1, 128 * pairs), F32, one), ((1, 128 * pairs), F32, one)],
        flops=8 * rows * tall * 128 * pairs,
        aliases={} if so_far is None else {5: 0},
    )


def merge(sizes, attended, start, weight, params):
    images, length, tall, width = sizes
    rows = images * tall
    count = len(weight.operands)

    def kernel(*refs):
        att_refs, refs = refs[: len(attended)], refs[len(attended) :]
        h0_ref, params_ref = refs[:2]
        h1_ref, n2_ref, w_s, out_s, sem = refs[2 + count :]
        step = pl.program_id(0)

        @pl.when(step == 0)
        def _():
            weight.fill(refs[2 : 2 + count], w_s, sem)
            weight.wait(w_s, sem)
            part = width // len(attended)
            out_s[...] = sum(nn(r[...], w_s[part * k : part * k + part, 0:width]) for k, r in enumerate(att_refs))

        @pl.when(step > 0)
        def _():
            def body(at, first):
                out = out_s[pl.ds(pl.multiple_of((step - 1) * tall + first, 8), min(BAND, tall)), :]
                middle = h0_ref[at, :] + row_of(params_ref, GAMMA1) * (out + row_of(params_ref, BIAS1))
                h1_ref[at, :] = middle
                normed, _ = norm(middle)
                n2_ref[at, :] = (normed * row_of(params_ref, GAIN2) + row_of(params_ref, SHIFT2)).astype(BF16)

            banded(tall, body)

    band = pl.BlockSpec((tall, width), lambda i: (jnp.maximum(i - 1, 0), 0))
    return call(
        kernel, "merge", (images + 1,),
        [(a, kept(a.shape), FAR) for a in attended]
        + [(start, band), (params, kept(params.shape))]
        + [(a, ANY, FAR) for a in weight.operands],
        [((rows, width), F32, band), ((rows, width), BF16, band)],
        [pltpu.VMEM((width, width + weight.extra), BF16), pltpu.VMEM((rows, width), F32),
         pltpu.SemaphoreType.DMA],
        flops=2 * rows * width * width,
    )


def part_by_core(store, away_ref, stay_ref):
    c = lax.axis_index("narrow") % 2
    for x in range(2):
        away_ref[x] = store[2 * x + 1 - c]
        stay_ref[x] = store[2 * x + c]


def feed(sizes, second_low, down_low, up, down, bias, sums, last):
    images, length, tall, width = sizes
    rows = images * tall
    shared = up.operands[0] is down.operands[0]
    far = () if last else (FAR,)
    ups, downs = len(up.operands), 0 if shared else len(down.operands)
    carried = [] if sums is None else list(sums)

    def kernel(*refs):
        n2_ref, df_ref, bias_ref = refs[:3]
        rest = refs[3:]
        up_refs, rest = rest[:ups], rest[ups:]
        down_refs, rest = (up_refs if shared else rest[:downs]), rest[downs:]
        sum_refs, rest = rest[: len(carried)], rest[len(carried) :]
        f_ref, dn_ref, away_ref, stay_ref, gbias_ref, up_s, down_s, grad_s, sems = rest
        step = pl.program_id(0)

        @pl.when(step == 0)
        def _():
            up.fill(up_refs, up_s, sems.at[0])
            down.fill(down_refs, down_s, sems.at[1])
            if carried:
                pltpu.make_async_copy(sum_refs[0], f_ref, sems.at[2]).start()
                pltpu.make_async_copy(sum_refs[1], dn_ref, sems.at[3]).start()
            up.wait(up_s, sems.at[0])
            down.wait(down_s, sems.at[1])
            if not carried:
                f_ref[...] = jnp.zeros_like(f_ref)
                dn_ref[...] = jnp.zeros_like(dn_ref)

        at = pl.ds(pl.multiple_of(step * TILE, TILE), TILE)
        up_w, down_w = up_s[:, at], down_s[:, at]
        u = nn(n2_ref[...], up_w) + bias_ref[...]
        dz = nn(df_ref[...], down_w)
        bell = jnp.exp(-0.5 * u * u)
        below = 0.5 * (1.0 + lax.erf(u * ROOT_HALF))
        z = (u * below).astype(BF16)
        du = dz * (below + u * (DENSITY * bell))
        gbias_ref[...] = column_sum(du)
        du = du.astype(BF16)
        grad = tn(n2_ref[...], du).astype(BF16)
        for k in range(TILE // 256):
            grad_s[step * (TILE // 256) + k, :, :, 0:256] = grad[:, 256 * k : 256 * k + 256].reshape(8, 96, 256)
        grad = tn(df_ref[...], z).astype(BF16)
        for n in range(4):
            for w in range(TILE // 128):
                for half in range(2):
                    grad_s[n, step * (TILE // 128) + w, :, 256 + 128 * half : 384 + 128 * half] = grad[
                        192 * n + 96 * half : 192 * n + 96 * half + 96, 128 * w : 128 * w + 128
                    ]
        if carried:
            @pl.when(step == 0)
            def _():
                pltpu.make_async_copy(sum_refs[0], f_ref, sems.at[2]).wait()
                pltpu.make_async_copy(sum_refs[1], dn_ref, sems.at[3]).wait()

        f_ref[...] += nt(z, down_w)
        dn_ref[...] += nt(du, up_w)

        @pl.when(step == CHUNK // TILE - 1)
        def _():
            part_by_core(grad_s, away_ref, stay_ref)

    tile = pl.BlockSpec((1, TILE), lambda t: (0, t))
    full = whole((rows, width))
    shape = (2, 8, 96, 512)
    return call(
        kernel, "feed", (CHUNK // TILE,),
        [(second_low, kept((rows, width))), (down_low, kept((rows, width))), (bias, tile)]
        + [(a, ANY, FAR) for a in up.operands[:1]] + [(a, ANY) for a in up.operands[1:]]
        + [(a, ANY, FAR) for a in ([] if shared else down.operands) + carried],
        [((rows, width), F32, kept((rows, width)), *far), ((rows, width), F32, kept((rows, width)), *far),
         (shape, BF16, kept(shape)), (shape, BF16, kept(shape)), ((1, CHUNK), F32, tile)],
        [pltpu.VMEM((width, CHUNK), BF16), pltpu.VMEM((width, CHUNK), BF16), pltpu.VMEM((4, 8, 96, 512), BF16),
         pltpu.SemaphoreType.DMA((4,))],
        flops=12 * rows * width * CHUNK,
    )


def middle_back(sizes, attended, branch, grad_n2, middle, start, upstream, weight, params):
    images, length, tall, width = sizes
    rows = images * tall
    count = len(weight.operands)

    def kernel(*refs):
        att_refs, refs = refs[: len(attended)], refs[len(attended) :]
        f_ref, dn_ref, h1_ref, h0_ref, g_ref, params_ref = refs[:6]
        out_ref, dh_ref, do_ref, away_ref, stay_ref, sum_ref, w_s, da_s, grad_s, layer_s, sem = refs[6 + count :]
        step = pl.program_id(0)

        @pl.when(step == 0)
        def _():
            weight.fill(refs[6 : 6 + count], w_s, sem)
            sum_ref[...] = jnp.zeros_like(sum_ref)

        @pl.when(step < images)
        def _():
            def body(at, first):
                f = f_ref[at, :] + row_of(params_ref, BIAS2)
                h1 = h1_ref[at, :]
                g = g_ref[at, :].astype(F32)
                layer_s[at, :] = h1 + row_of(params_ref, GAMMA2) * f
                normed, scaling = norm(h1)
                dn = dn_ref[at, :]
                dh = g + norm_back(dn, normed, scaling, row_of(params_ref, GAIN2))
                dh_ref[at, :] = dh
                da = row_of(params_ref, GAMMA1) * dh
                sum_ref[0:1, :] += column_sum(g * f)
                sum_ref[1:2, :] += column_sum(dn * normed)
                sum_ref[2:3, :] += column_sum(dn)
                sum_ref[3:4, :] += column_sum(dh * (h1 - h0_ref[at, :]))
                sum_ref[4:5, :] += column_sum(da)
                da_s[pl.ds(pl.multiple_of(step * tall + first, 8), min(BAND, tall)), :] = da.astype(BF16)

            banded(tall, body)
            out_ref[0] = layer_s[0:length, :].astype(BF16)

        @pl.when(step == images)
        def _():
            sum_ref[3:4, :] = sum_ref[3:4, :] / row_of(params_ref, GAMMA1)
            weight.wait(w_s, sem)
            do_ref[...] = nt(da_s[...], w_s[:, 0:width]).astype(BF16)
            grad = jnp.concatenate([tn(r[...], da_s[...]) for r in att_refs], axis=0).astype(BF16)
            for n, at in enumerate((0, 128, 384, 512)):
                grad_s[n] = grad[:, at : at + 256].reshape(8, 96, 256)
            part_by_core(grad_s, away_ref, stay_ref)

    def at(i):
        return jnp.minimum(i, images - 1)

    band = pl.BlockSpec((tall, width), lambda i: (at(i), 0))
    shape = (2, 8, 96, 256)
    return call(
        kernel, "middle_back", (images + 1,),
        [(a, kept(a.shape), FAR) for a in attended]
        + [(a, band) for a in (branch, grad_n2, middle, start)] + [(a, band, FAR) for a in (upstream,)] + [(params, kept(params.shape))]
        + [(a, ANY, FAR) for a in weight.operands],
        [((images, length, width), BF16, pl.BlockSpec((1, length, width), lambda i: (at(i), 0, 0))),
         ((rows, width), F32, band), ((rows, width), BF16, whole((rows, width))),
         (shape, BF16, whole(shape)), (shape, BF16, whole(shape)), ((8, width), F32, whole((8, width)))],
        [pltpu.VMEM((width, width + weight.extra), BF16), pltpu.VMEM((rows, width), BF16),
         pltpu.VMEM((4, 8, 96, 256), BF16), pltpu.VMEM((tall, width), F32), pltpu.SemaphoreType.DMA],
        flops=4 * rows * width * width,
    )


def mixed_grad(sizes, first_low, grads):
    images, length, tall, width = sizes
    rows = images * tall

    def kernel(n1_ref, grad_ref, away_ref, stay_ref):
        step = pl.program_id(0)
        c = lax.axis_index("narrow") % 2
        n = 2 * (step % 2) + jnp.where(step < 2, 1 - c, c)
        main = grad_ref[at_least(n, (0, 1, 1, 2)), :, pl.ds(pl.multiple_of(at_least(n, (0, 0, 384, 384)), 128), 384)]
        side = grad_ref[at_least(n, (0, 0, 2, 2)), :, pl.ds(pl.multiple_of(at_least(n, (384, 512, 0, 128)), 128), 256)]
        main = tn(n1_ref[...], main).astype(BF16).reshape(8, 96, 384)
        side = tn(n1_ref[...], side).astype(BF16).reshape(8, 96, 256)
        for role, ref in enumerate((away_ref, stay_ref)):
            @pl.when(step // 2 == role)
            def _(ref=ref):
                ref[0, :, :, 0:384] = main
                ref[0, :, :, 384:640] = side

    shape = (2, 8, 96, 640)
    return call(
        kernel, "mixed_grad", (4,),
        [(first_low, kept((rows, width))), (grads, kept(grads.shape))],
        [(shape, BF16, pl.BlockSpec((1, 8, 96, 640), lambda t: (jnp.minimum(t, 1), 0, 0, 0))),
         (shape, BF16, pl.BlockSpec((1, 8, 96, 640), lambda t: (jnp.maximum(t - 2, 0), 0, 0, 0)))],
        flops=6 * rows * width * width,
    )


def start_back(sizes, grads, weight, start, grad_middle, group_sizes, patterns, params):
    images, length, tall, width = sizes
    rows = images * tall
    count = len(weight.operands)

    def kernel(*refs):
        grad_ref, h0_ref, dh_ref, sizes_ref, patterns_ref, params_ref = refs[:6]
        out_ref, sum_ref, w_s, dn_s, out_s, sem = refs[6 + count :]
        step = pl.program_id(0)

        @pl.when(step == 0)
        def _():
            weight.fill(refs[6 : 6 + count], w_s, sem)
            sum_ref[...] = jnp.zeros_like(sum_ref)
            dn_s[...] = jnp.zeros_like(dn_s)
            weight.wait(w_s, sem)

        @pl.when(step < 3)
        def _():
            dn_s[...] += nt(grad_ref[0], w_s[:, pl.ds(pl.multiple_of(step * width, 128), width)])

        @pl.when(step > 2)
        def _():
            masked = masked_rows(first_image(images) + step - 3, sizes_ref, patterns_ref, tall)

            def body(at, first):
                dn = dn_s[pl.ds(pl.multiple_of((step - 3) * tall + first, 8), min(BAND, tall)), :]
                normed, scaling = norm(h0_ref[at, :])
                dh = dh_ref[at, :] + norm_back(dn, normed, scaling, row_of(params_ref, GAIN1))
                out_s[at, :] = jnp.where(masked, 0.0, dh)
                sum_ref[0:1, :] += column_sum(dn * normed)
                sum_ref[1:2, :] += column_sum(dn)
                sum_ref[2:3, :] += column_sum(jnp.where(masked, dh, 0.0))

            banded(tall, body)
            out_ref[0] = out_s[0:length, :]

    def at(i):
        return jnp.maximum(i - 3, 0)

    band = pl.BlockSpec((tall, width), lambda i: (at(i), 0))
    return call(
        kernel, "start_back", (images + 3,),
        [(grads, pl.BlockSpec((1, rows, width), lambda i: (jnp.minimum(i, 2), 0, 0)))]
        + [(start, band), (grad_middle, band), (group_sizes, SCALARS), (patterns, kept(patterns.shape)),
           (params, kept(params.shape))]
        + [(a, ANY) for a in weight.operands],
        [((images, length, width), F32, pl.BlockSpec((1, length, width), lambda i: (at(i), 0, 0))),
         ((8, width), F32, whole((8, width)))],
        [pltpu.VMEM((width, 3 * width + weight.extra), BF16), pltpu.VMEM((rows, width), F32),
         pltpu.VMEM((tall, width), F32), pltpu.SemaphoreType.DMA],
        flops=6 * rows * width * width,
    )


def local(
    links,
    inputs,
    cotangent,
    group_sizes,
    mask_patterns,
    mask_token,
    norm1_gain,
    norm1_bias,
    qkv_weight,
    query_bias,
    value_bias,
    bias_table,
    proj_weight,
    proj_bias,
    gamma_attn,
    norm2_gain,
    norm2_bias,
    fc1_weight,
    fc1_bias,
    fc2_weight,
    fc2_bias,
    gamma_mlp,
):
    images, length, width = inputs.shape
    table_rows, heads = bias_table.shape
    grid_side = math.isqrt(length - 1)
    group_count = mask_patterns.shape[0]
    tall = -(-length // 8) * 8
    rows = images * tall
    hidden = fc1_bias.shape[0]
    chunks = hidden // CHUNK
    sizes = (images, length, tall, width)
    score_scale = (width // heads) ** (-0.5)
    here = links.place()

    vectors = {
        TOKEN: mask_token, GAIN1: norm1_gain, SHIFT1: norm1_bias, GAMMA2: gamma_mlp, BIAS1: proj_bias,
        GAMMA1: gamma_attn, GAIN2: norm2_gain, SHIFT2: norm2_bias, BIAS2: fc2_bias, 9: query_bias, 11: value_bias,
    }

    boxed = links.boxed
    fc2_t = fc2_weight.T
    if boxed:
        mix = Gather(links, qkv_block(here, qkv_weight), 384, [((0, 384), (0, 256))])
        side = align_side(here, proj_weight)
        near = Gather(
            links,
            jnp.concatenate(
                [side[:, :128], up_block(fc1_weight, 0), down_block(fc2_t, 0), side[:, 128:]], axis=1
            ),
            384,
            [((0, 128), (256, 384)), ((128, 384), (0, 256))],
        )
        far = Gather(
            links,
            jnp.concatenate(
                [up_block(fc1_weight, 1), up_block(fc1_weight, 2), down_block(fc2_t, 1), down_block(fc2_t, 2)],
                axis=1,
            ),
            512,
            [((0, 256), (0, 256)), ((256, 512), (256, 512))],
        )
        full_up = full_down = None
    else:
        mix = near = far = None
        full_up, full_down = native_gather(fc1_weight), native_gather(fc2_weight).T

    entry = table_columns(grid_side, 384)

    def behind(value, *exchanges):
        return after(value, *[v for e in exchanges for v in e.sent]) if boxed else value

    def met(value, *exchanges):
        return [value] + [v for e in exchanges for v in e.flying]

    if boxed:
        mix.first()
    start, first_low, upstream, down_low, sum_fc2, params, patterns = prepare(
        sizes, inputs, cotangent, group_sizes, mask_patterns, vectors
    )
    if boxed:
        gap = met(first_low, mix)
        mix.second(*gap)
        near.first(*gap)
    table_t = jnp.pad(after(bias_table, first_low).T, ((0, 16 - heads), (0, width - table_rows)))
    bias = bias_kernel(behind(table_t, mix), entry, grid_side, tall, 256)
    if boxed:
        mix.third(*met(bias, mix))
        mix.fourth(False, *met(bias, near))
        near.second(*mix.sent)
    qkv = qkv_operands(links, mix, qkv_weight)
    mixed = project(sizes, behind(first_low, near), qkv, params, score_scale)
    if boxed:
        gap = met(mixed, near)
        near.third(*gap)
        far.first(*gap)
    attended, probs = attend(sizes, behind(mixed, near), bias, 0, width // 128)
    if boxed:
        near.fourth(False, *met(attended, far))
        far.second(*near.sent)
    proj = proj_operands(links, near, proj_weight)
    middle, second_low = merge(sizes, [attended], behind(start, far), proj, params)
    if boxed:
        far.third(*met(second_low, far))

    fc1_groups = fc1_bias.reshape(8, chunks, 128)
    ups = [up_operands(links, near, 1, full_up, 0), None, None]
    downs = [down_operands(links, near, 1, full_down, 0), None, None]
    halves = [[(0, (0, 256))], [(0, (256, 512))]]
    sums, pairs_out, hidden_sums = None, [], []
    waves = [Scatter(links, here, 256), Scatter(links, here, 256), Scatter(links, here, 512)]
    second_here = behind(second_low, far)
    for k in range(chunks):
        branch, grad_n2, away, stay, hidden_sum = feed(
            sizes, second_here, down_low, ups[k], downs[k], fc1_groups[:, k].reshape(1, -1), sums, k == chunks - 1
        )
        if k == 0:
            if boxed:
                far.fourth(True, *met(away, far))
                waves[0].first(after(away, *far.sent), stay)
            ups[1:] = [up_operands(links, far, 0, full_up, 1), up_operands(links, far, 1, full_up, 2)]
            downs[1:] = [down_operands(links, far, 0, full_down, 1), down_operands(links, far, 1, full_down, 2)]
            second_here = second_low
        elif k == 1 and boxed:
            exchange(links, [away], (waves[0], "second", halves))
            waves[1].first(after(away, *waves[0].sent), stay)
            second_here = behind(second_low, waves[0])
        elif boxed:
            exchange(links, [away], (waves[0], "third", None), (waves[1], "second", halves))
            waves[2].first(after(away, *waves[1].sent), stay)
        sums = (branch, grad_n2)
        pairs_out.append((away, stay))
        hidden_sums.append(hidden_sum)

    layer_out, grad_middle, grad_att, proj_away, proj_stay, middle_sums = middle_back(
        sizes, [attended], behind(branch, waves[0], waves[1]), grad_n2, middle, start, upstream, proj, params
    )
    if boxed:
        exchange(links, [grad_att], (waves[0], "halves", None), (waves[1], "third", None))
        waves[2].first(after(proj_away, *waves[1].sent), proj_stay)

    back, grads = [], None
    for number, (first, pairs) in enumerate(((0, 3), (3, 3))):
        grad_here = behind(grad_att, *(waves[:2] if number == 0 else waves[1:]))
        grads, *rest = attend_back(sizes, mixed, probs, grad_here, score_scale, first, pairs, grads)
        back.append(rest)
        if boxed and number == 0:
            exchange(
                links, [grads], (waves[0], "fifth", None), (waves[1], "halves", None),
                (waves[2], "second", [[(1, (0, 256)), (0, (0, 128))], [(0, (128, 512))]]),
            )
    if boxed:
        gap_grads = met(grads, waves[0])
        exchange(links, gap_grads, (waves[1], "fifth", None), (waves[2], "third", None))
    mix_away, mix_stay = mixed_grad(sizes, behind(first_low, waves[2]), grads)
    last = Scatter(links, here, 384)
    terms = jnp.concatenate([b[0] for b in back], axis=0)
    if boxed:
        gap_mix = met(mix_away, waves[1])
        exchange(links, gap_mix, (waves[2], "halves", None))
        last.first(after(mix_away, *waves[2].sent), mix_stay)
    grad_table = bias_back_kernel(after(behind(terms, waves[2]), mix_away), entry, grid_side, width)
    if boxed:
        exchange(links, [grad_table], (last, "second", [[(0, (0, 384))], [(0, (384, 640))]]))
    input_grad, start_sums = start_back(
        sizes, grads, qkv, start, behind(grad_middle, last), group_sizes, patterns, params
    )
    small_away, small_stay = pack(
        links, grad_table, heads, start_sums, middle_sums, [b[1:] for b in back], sum_fc2, hidden_sums
    )
    if boxed:
        exchange(links, [start_sums], (last, "third", None))
        small_away = after(small_away, *last.sent, *waves[2].flying)
    small = sum_everywhere(links, here, small_away, small_stay, last.flying)
    if boxed:
        exchange(links, [], (last, "fourth", None), (waves[2], "fifth", None))
        grad_qkv = qkv_home(here, last.done())
        blocks = [waves[0].done(*gap_grads), waves[1].done(*gap_mix), waves[2].done()]
        grad_proj = proj_home(here, blocks[2][:, 0:256])
        up_parts = [blocks[0][:, 0:256], blocks[1][:, 0:256], blocks[2][:, 256:512]]
        down_parts = [blocks[0][:, 256:512], blocks[1][:, 256:512], blocks[2][:, 512:768]]
        grad_fc1 = jnp.concatenate(
            [up_parts[k][:, 128 * half : 128 * half + 128] for half in range(2) for k in range(chunks)], axis=1
        )
        grad_fc2 = jnp.concatenate(
            [jnp.concatenate([p[:, :128], p[:, 128:]], axis=0) for p in down_parts], axis=1
        ).T
    else:
        tiles = [all_tiles(here, *pair) for pair in pairs_out]
        grad_qkv = native_scatter(natural_qkv(all_tiles(here, mix_away, mix_stay)))
        grad_proj = native_scatter(natural_proj(all_tiles(here, proj_away, proj_stay)))
        grad_fc1 = native_scatter(natural_up([t[..., :256] for t in tiles]))
        grad_fc2 = native_scatter(natural_down([t[..., 256:] for t in tiles]))
    at = heads
    hidden_rows = [
        jnp.concatenate([small[at + 11 + k], small[at + 14, 256 * k : 256 * k + 256]]).reshape(8, 128) for k in range(chunks)
    ]
    sum_fc1 = jnp.stack(hidden_rows, axis=1).reshape(-1)
    return (
        layer_out,
        input_grad,
        small[at + 2],
        small[at],
        small[at + 1],
        grad_qkv,
        small[at + 8],
        small[at + 9],
        small[:heads, :table_rows].T,
        grad_proj,
        small[at + 7],
        small[at + 6],
        small[at + 4],
        small[at + 5],
        grad_fc1,
        sum_fc1,
        grad_fc2,
        small[at + 10],
        small[at + 3],
    )


def solution(mesh):
    images = P(AXES, None, None)
    both = P("wide", "narrow")
    same = P()
    links = Links(mesh.shape["wide"], mesh.shape["narrow"])
    return jax.shard_map(
        functools.partial(local, links),
        mesh=mesh,
        in_specs=(
            images, images, same, same, same, same, same, both, same, same, same, both, same, same,
            same, same, both, same, both, same, same,
        ),
        out_specs=(
            images, images, same, same, same, both, same, same, same, both, same, same, same, same,
            both, same, both, same, same,
        ),
        check_vma=False,
    )
```

```python
import functools
import math

import jax
import jax.numpy as jnp
import numpy as np
from jax import lax
from jax.experimental import pallas as pl
from jax.experimental.pallas import tpu as pltpu
from jax.sharding import PartitionSpec as P

EPSILON = 1e-06
ROOT_HALF = 0.7071067811865476
DENSITY = 0.3989422804014327
BF16 = jnp.bfloat16
F32 = jnp.float32
AXES = ("wide", "narrow")
TILE = 512
BAND = 200
CHUNK = 1024
NEVER = -1e30
MIB = 1 << 20


class Links:
    def __init__(self, wide, narrow):
        self.wide, self.narrow = wide, narrow
        self.y = 1 << ((wide.bit_length() - 1) // 2)
        self.z = wide // self.y
        self.x = narrow // 2
        self.size = {"z": self.z, "y": self.y, "x": self.x, "core": 2}
        self.unit = {"core": 1, "x": 2, "y": narrow, "z": narrow * self.y}
        self.boxed = (self.z, self.y, self.x) == (4, 2, 2)

    def place(self):
        w, n = lax.axis_index("wide"), lax.axis_index("narrow")
        return {"z": w // self.y, "y": w % self.y, "x": n // 2, "core": n % 2, "w": w, "n": n}

    def swap(self, value, **offsets):
        mask = sum(self.unit[axis] * offset for axis, offset in offsets.items())
        count = self.wide * self.narrow
        return lax.ppermute(value, AXES, [(k, k ^ mask) for k in range(count)])

    def others(self, value, axis):
        return [self.swap(value, **{axis: d}) for d in range(1, self.size[axis])]


def pick(value, axis, index, count):
    size = value.shape[axis] // count
    return lax.dynamic_slice_in_dim(value, index * size, size, axis)


def after(value, *others):
    return lax.optimization_barrier((value,) + others)[0]


def tied(values, wait):
    if not wait:
        return list(values)
    return list(lax.optimization_barrier(tuple(values) + tuple(wait)))[: len(values)]


def native_gather(shard):
    return lax.all_gather(
        lax.all_gather(shard, "narrow", axis=1, tiled=True), "wide", axis=0, tiled=True
    )


class Gather:
    orders = (("x", "y"), ("y", "x"))

    def __init__(self, links, block, split, groups):
        self.links, self.block, self.split, self.groups = links, block, split, groups

    def first(self, *wait):
        block = after(self.block, *wait) if wait else self.block
        self.sent = [block]
        self.steps = [block] + self.links.others(block, "z")
        self.flying = self.steps[1:]

    def second(self, *wait):
        parts = arrange([after(self.steps[0], *wait) if wait else self.steps[0]] + self.steps[1:], self.split)
        self.steps, self.sent = [], []
        for held, order in zip(parts, self.orders, strict=True):
            self.sent.append(held)
            self.steps.append([held] + self.links.others(held, order[0]))
        self.flying = [v for p in self.steps for v in p[1:]]

    def third(self, *wait):
        parts = stack([[after(self.steps[0][0], *wait)] + self.steps[0][1:], self.steps[1]])
        self.steps, self.sent = [], []
        for held, order in zip(parts, self.orders, strict=True):
            self.sent.append(held)
            self.steps.append([held] + self.links.others(held, order[1]))
        self.flying = [v for p in self.steps for v in p[1:]]

    def fourth(self, far, *wait):
        first = after(self.steps[0][0], *wait)
        self.operands = []
        held = regroup([[first] + self.steps[0][1:], self.steps[1]], self.groups, far)
        for number, array in enumerate(held):
            self.operands.append([array, self.links.swap(array, core=1)])
        self.sent = held
        self.flying = [pair[1] for pair in self.operands]

    def blocks(self, refs, number, me):
        links = self.links
        order = self.orders[number]
        out = []
        for core in range(2):
            for k in range(refs[core].shape[0]):
                at, rest = {}, k
                for axis in ("z",) + order:
                    at[axis] = me[axis] ^ (rest % links.size[axis])
                    rest //= links.size[axis]
                source = functools.partial(block_columns, refs[core], k)
                out.append((source, at["z"] * links.y + at["y"], at["x"] * 2 + (me["core"] ^ core)))
        return out


def block_columns(ref, k, col, broad):
    return ref.at[k, :, pl.ds(col, broad)]


def at_least(n, values):
    out = values[3]
    for k in (2, 1, 0):
        out = jnp.where(n == k, values[k], out)
    return out


def window(ref, row, col, tall, broad):
    if not isinstance(row, int):
        row = pl.multiple_of(row, 8)
    if not isinstance(col, int):
        col = pl.multiple_of(col, 128)
    return ref.at[pl.ds(row, tall), pl.ds(col, broad)]


def columns(ref, col, broad):
    return ref.at[:, pl.ds(col, broad)]


class Weight:
    def __init__(self, operands, copies, joints=(), extra=0):
        self.operands, self.copies, self.joints, self.extra = operands, copies, joints, extra

    def fill(self, refs, target, sem):
        for source, to in self.copies(refs, target):
            pltpu.make_async_copy(source, to, sem).start()

    def wait(self, target, sem):
        pltpu.make_async_copy(target, target, sem).wait()
        for here, there in self.joints:
            target[:, here : here + 128] += target[:, there : there + 128]


def align_side(here, side):
    zero = jnp.zeros((side.shape[0], 64), side.dtype)
    return jnp.where(
        here["n"] % 2 == 0,
        jnp.concatenate([side, zero], axis=1),
        jnp.concatenate([zero, side], axis=1),
    )


def qkv_block(here, shard):
    even = here["n"] % 2 == 0
    main = jnp.where(even, shard[:, :384], shard[:, 192:])
    return jnp.concatenate([main, align_side(here, jnp.where(even, shard[:, 384:], shard[:, :192]))], axis=1)


def qkv_operands(links, gathered, shard):
    if not links.boxed:
        return Weight([native_gather(shard)], lambda refs, target: [(refs[0], target.at[:, pl.ds(0, 2304)])] + [
            (refs[0].at[:, pl.ds(0, 256)], target.at[:, pl.ds(2304, 256)])], extra=256)

    def copies(refs, target):
        me = links.place()
        out = []
        for source, w, n in gathered.blocks(refs, 0, me):
            out.append((source(0, 384), window(target, w * 96, at_least(n, (0, 768, 1152, 1920)), 96, 384)))
        for source, w, n in gathered.blocks(refs, 1, me):
            for part, places in enumerate(((384, 2304, 1536, 2432), (512, 640, 1664, 1792))):
                out.append((source(384 + 128 * part, 128), window(target, w * 96, at_least(n, places), 96, 128)))
        return out

    return Weight(gathered.operands[0], copies, ((512, 2304), (1664, 2432)), 256)


def proj_operands(links, gathered, shard):
    if not links.boxed:
        return Weight([native_gather(shard)], lambda refs, target: [(refs[0], target.at[:, pl.ds(0, 768)])] + [
            (refs[0].at[:, pl.ds(0, 256)], target.at[:, pl.ds(768, 256)])], extra=256)

    def copies(refs, target):
        me = links.place()
        out = []
        for part, (col, places) in enumerate(((0, (0, 768, 384, 896)), (128, (128, 256, 512, 640)))):
            for source, w, n in gathered.blocks(refs, part, me):
                out.append((source(col, 128), window(target, w * 96, at_least(n, places), 96, 128)))
        return out

    return Weight(gathered.operands[0], copies, ((128, 768), (512, 896)), 256)


def up_block(shard, chunk):
    return jnp.concatenate(
        [shard[:, 384 * half + 128 * chunk : 384 * half + 128 * chunk + 128] for half in range(2)], axis=1
    )


def down_block(shard_t, chunk):
    piece = shard_t[:, 128 * chunk : 128 * chunk + 128]
    half = piece.shape[0] // 2
    return jnp.concatenate([piece[:half], piece[half:]], axis=1)


def chunk_copies(full, chunk):
    def slices(refs, target):
        return [
            (columns(refs[0], 384 * g + 128 * chunk, 128), columns(target, 128 * g, 128)) for g in range(8)
        ]

    return Weight([full], slices)


def up_operands(links, gathered, group, full, chunk):
    if not links.boxed:
        return chunk_copies(full, chunk)

    def copies(refs, target):
        me = links.place()
        return [
            (source(0, 256), window(target, w * 96, n * 256, 96, 256))
            for source, w, n in gathered.blocks(refs, 0, me)
        ]

    return Weight(gathered.operands[group], copies)


def down_operands(links, gathered, group, full, chunk):
    if not links.boxed:
        return chunk_copies(full, chunk)

    def copies(refs, target):
        me = links.place()
        return [
            (source(256 + 128 * half, 128), window(target, n * 192 + half * 96, w * 128, 96, 128))
            for source, w, n in gathered.blocks(refs, 1, me)
            for half in range(2)
        ]

    return Weight(gathered.operands[group], copies)


class Scatter:
    orders = (("x", "y"), ("y", "x"))

    def __init__(self, links, here, split):
        self.links, self.here, self.split = links, here, split
        self.pairs, self.flying, self.stage = [], [], 0

    def first(self, away, stay):
        shape = (self.links.x, self.links.z, self.links.y) + away.shape[2:]
        self.pairs.append((stay.reshape(shape), self.links.swap(away.reshape(shape), core=1)))
        self.flying.append(self.pairs[-1][1])

    def jobs(self, step, picks):
        if step == "second":
            return [
                ([(self.pairs[k], cols) for k, cols in part], order[0])
                for part, order in zip(picks, self.orders, strict=True)
            ]
        whole_of = [(t, (0, t[0].shape[-1])) for t in self.terms]
        if step == "third":
            return [([t], order[1]) for t, order in zip(whole_of, self.orders, strict=True)]
        if step == "fifth":
            return [([(self.terms[0], (0, self.terms[0][0].shape[-1]))], "z_low")]
        return [(whole_of, "z_high" if step == "halves" else "z")]

    def take(self, results, unit):
        self.sent = [v for r in results for v in r[1:]]
        self.terms = []
        axes = [(order[self.stage], 1) for order in self.orders] if self.stage < 2 else [("z", unit)]
        for (keep, *sent), (axis, step) in zip(results, axes, strict=True):
            self.terms.append([keep] + [self.links.swap(v, **{axis: d * step}) for d, v in enumerate(sent, 1)])
        self.stage += 1
        self.flying = [v for t in self.terms for v in t[1:]]

    def done(self, *wait):
        terms = tied(self.terms[0], wait)
        total = terms[0]
        for term in terms[1:]:
            total = total + term.astype(F32)
        return total.reshape(total.shape[-2:])


def exchange(links, wait, *items):
    jobs = [job for scatter, step, picks in items for job in scatter.jobs(step, picks)]
    group, cols = jobs[0][0][0]
    jobs[0][0][0] = ((after(group[0], *wait),) + tuple(group[1:]), cols)
    results = fold(links, jobs)
    for scatter, step, _ in items:
        count = 2 if step in ("second", "third") else 1
        scatter.take(results[:count], 2 if step == "halves" else 1)
        results = results[count:]


def all_tiles(here, away, stay):
    return jnp.where(
        here["core"] == 0, jnp.stack([stay, away], axis=1), jnp.stack([away, stay], axis=1)
    ).reshape((4,) + away.shape[1:])


def native_scatter(partial):
    low = lax.psum_scatter(partial.astype(BF16), "wide", scatter_dimension=0, tiled=True)
    return lax.psum_scatter(low, "narrow", scatter_dimension=1, tiled=True).astype(F32)


def qkv_home(here, block):
    even = here["n"] % 2 == 0
    main, side = block[:, :384], block[:, 384:]
    return jnp.where(
        even,
        jnp.concatenate([main, side[:, :192]], axis=1),
        jnp.concatenate([side[:, 64:], main], axis=1),
    )


def proj_home(here, block):
    return jnp.where(here["n"] % 2 == 0, block[:, :192], block[:, 64:])


def natural_qkv(tiles):
    tiles = tiles.reshape(4, 768, 640)
    out = []
    for n in range(4):
        main, side = tiles[n, :, :384], tiles[n, :, 384:]
        out += [main, side[:, :192]] if n % 2 == 0 else [side[:, 64:], main]
    return jnp.concatenate(out, axis=1)


def natural_proj(tiles):
    tiles = tiles.reshape(4, 768, 256)
    return jnp.concatenate([tiles[n, :, :192] if n % 2 == 0 else tiles[n, :, 64:] for n in range(4)], axis=1)


def natural_up(chunks):
    tiles = [t.reshape(4, 768, 2, 128) for t in chunks]
    return jnp.stack(tiles, axis=0).transpose(2, 1, 3, 0, 4).reshape(768, -1)


def natural_down(chunks):
    tiles = [t.reshape(4, 8, 96, 2, 128) for t in chunks]
    return jnp.stack(tiles, axis=0).transpose(2, 0, 5, 1, 4, 3).reshape(-1, 768)


def tree_sum(terms):
    while len(terms) > 1:
        terms = [terms[k] + terms[k + 1] for k in range(0, len(terms), 2)]
    return terms[0]


def sum_everywhere(links, here, away, stay, wait):
    if links.boxed:
        half = after(stay + links.swap(away, core=1), *wait)
        steps = [
            (axis, 1 << bit) for axis in ("z", "x", "y") for bit in range(links.size[axis].bit_length() - 1)
        ]
        for axis, step in sorted(steps, key=lambda s: s[0] == "z" and s[1] > 1):
            half = half + links.swap(half, **{axis: step})
        other = links.swap(half, core=1)
    else:
        first = jnp.where(here["core"] == 0, stay, away)
        second = jnp.where(here["core"] == 0, away, stay)
        return lax.psum(jnp.concatenate([first, second], axis=0), AXES)
    return jnp.where(
        here["core"] == 0, jnp.concatenate([half, other], axis=0), jnp.concatenate([other, half], axis=0)
    )


def whole(shape):
    return pl.BlockSpec(tuple(shape), lambda *_: (0,) * len(shape))


def kept(shape):
    return pl.BlockSpec(tuple(shape), lambda *_: (0,) * len(shape), pipeline_mode=pl.Buffered(1))


ANY = pl.BlockSpec(memory_space=pl.ANY)
FAR = pl.BlockSpec(memory_space=pltpu.HBM)
SCALARS = pl.BlockSpec(memory_space=pltpu.SMEM)


LIMITS = {"stack": 16, "arrange": 8, "fold": 24, "pack": 8, "prepare": 16, "bias": 16, "bias_back": 20, "project": 24, "attend": 18, "merge": 20, "feed": 28, "middle_back": 28, "attend_back": 22, "mixed_grad": 24, "start_back": 28}


def call(kernel, name, grid, ins, outs, scratch=(), flops=0, aliases=None):
    moved = sum(a.size * a.dtype.itemsize for a, *_ in ins)
    moved += sum(math.prod(s) * jnp.dtype(d).itemsize for s, d, *_ in outs)
    return pl.pallas_call(
        kernel,
        name=name,
        grid=grid,
        in_specs=[spec for _, spec, *_ in ins],
        out_specs=[spec for _, _, spec, *_ in outs],
        out_shape=[pltpu.HBM(s, d) if far else jax.ShapeDtypeStruct(s, d) for s, d, _, *far in outs],
        scratch_shapes=list(scratch),
        input_output_aliases=aliases or {},
        compiler_params=pltpu.CompilerParams(vmem_limit_bytes=LIMITS[name] * MIB),
        cost_estimate=pl.CostEstimate(flops=int(flops), bytes_accessed=int(moved), transcendentals=0),
    )(*[pltpu.with_memory_space_constraint(a, pltpu.HBM) if far else a for a, _, *far in ins])


def nn(a, b):
    return lax.dot_general(a, b, (((1,), (0,)), ((), ())), preferred_element_type=F32)


def nt(a, b):
    return lax.dot_general(a, b, (((1,), (1,)), ((), ())), preferred_element_type=F32)


def tn(a, b):
    return lax.dot_general(a, b, (((0,), (0,)), ((), ())), preferred_element_type=F32)


def arrange(blocks, split):
    rows, cols = blocks[0].shape
    count = len(blocks)

    def kernel(*refs):
        for k in range(count):
            refs[count][k] = refs[k][:, :split]
            refs[count + 1][k] = refs[k][:, split:]

    return call(
        kernel, "arrange", (),
        [(b, whole(b.shape)) for b in blocks],
        [((count, rows, part), BF16, whole((count, rows, part))) for part in (split, cols - split)],
    )


def stack(parts):
    flat = [v for part in parts for v in part]
    outs = [(sum(v.shape[0] for v in part), part[0].shape[1], part[0].shape[2]) for part in parts]

    def kernel(*refs):
        number = 0
        for k, part in enumerate(parts):
            at = 0
            for v in part:
                refs[len(flat) + k][at : at + v.shape[0]] = refs[number][...]
                at += v.shape[0]
                number += 1

    return call(
        kernel, "stack", (), [(v, whole(v.shape)) for v in flat], [(shape, BF16, whole(shape)) for shape in outs]
    )


def regroup(parts, groups, far):
    flat = [v for part in parts for v in part]
    count, rows = sum(v.shape[0] for v in parts[0]), parts[0][0].shape[1]
    outs = [(count, rows, sum(end - begin for begin, end in group)) for group in groups]

    def kernel(*refs):
        for out, group in zip(refs[len(flat) :], groups, strict=True):
            number, col = 0, 0
            for part, (begin, end) in zip(parts, group, strict=True):
                at = 0
                for v in part:
                    if end > begin:
                        out[at : at + v.shape[0], :, col : col + end - begin] = refs[number][:, :, begin:end]
                    at += v.shape[0]
                    number += 1
                col += end - begin

    return call(
        kernel, "stack", (), [(v, whole(v.shape)) for v in flat],
        [(shape, BF16, whole(shape), FAR) if far else (shape, BF16, whole(shape)) for shape in outs],
    )


def fold(links, jobs):
    arrays, index = [], {}
    for sources, _ in jobs:
        for group, _ in sources:
            for array in group:
                if id(array) not in index:
                    index[id(array)] = len(arrays)
                    arrays.append(array)
    dims = {"x": 0, "z": 1, "z_high": 1, "z_low": 1, "y": 2}
    size = dict(links.size, z_high=2, z_low=2)
    held = {"x": 1, "y": 1, "z": 1, "z_high": links.z // 2, "z_low": 1}
    outs = []
    for sources, axis in jobs:
        first = sources[0][0][0]
        cols = sum(part[1] - part[0] for _, part in sources)
        shape = tuple(held[axis] if k == dims[axis] else first.shape[k] for k in range(4)) + (cols,)
        outs += [(shape, F32 if d == 0 else BF16, whole(shape)) for d in range(size[axis])]

    def kernel(*refs):
        me = links.place()
        me["z_high"], me["z_low"] = me["z"] // 2, me["z"] % 2
        at_out = len(arrays)
        for sources, axis in jobs:
            for d in range(size[axis]):
                where = [slice(None)] * 4
                where[dims[axis]] = pl.ds((me[axis] ^ d) * held[axis], held[axis])
                col = 0
                for group, (begin, end) in sources:
                    picked = tuple(where) + (slice(begin, end),)
                    total = refs[index[id(group[0])]][picked].astype(F32)
                    for array in group[1:]:
                        total = total + refs[index[id(array)]][picked].astype(F32)
                    out = refs[at_out]
                    out[..., col : col + end - begin] = total.astype(out.dtype)
                    col += end - begin
                at_out += 1

    results = call(kernel, "fold", (), [(a, whole(a.shape)) for a in arrays], outs)
    out = []
    for _, axis in jobs:
        out.append(results[: size[axis]])
        results = results[size[axis] :]
    return out


def pack(links, table, heads, start_sums, middle_sums, halves, sum_fc2, hidden_sums):
    width = table.shape[1]

    def kernel(table_ref, start_ref, middle_ref, q0, v0, q1, v1, fc2_ref, a_ref, b_ref, c_ref, away_ref, stay_ref, all_s):
        all_s[...] = jnp.zeros_like(all_s)
        rows = [(table_ref, heads), (start_ref, 3), (middle_ref, 5)]
        at = 0
        for ref, count in rows:
            for k in range(count):
                all_s[(at + k) // 16, (at + k) % 16 : (at + k) % 16 + 1, :] = ref[k : k + 1, :]
            at += count
        for pair in ((q0, q1), (v0, v1)):
            for k, ref in enumerate(pair):
                all_s[at // 16, at % 16 : at % 16 + 1, k * 384 : k * 384 + 384] = ref[...]
            at += 1
        all_s[at // 16, at % 16 : at % 16 + 1, :] = fc2_ref[...]
        at += 1
        for k, ref in enumerate((a_ref, b_ref, c_ref)):
            all_s[(at + k) // 16, (at + k) % 16 : (at + k) % 16 + 1, :] = ref[:, 0:width]
            all_s[(at + 3) // 16, (at + 3) % 16 : (at + 3) % 16 + 1, k * 256 : k * 256 + 256] = ref[:, width : width + 256]
        c = lax.axis_index("narrow") % 2
        away_ref[...] = all_s[1 - c]
        stay_ref[...] = all_s[c]

    operands = [table, start_sums, middle_sums, *halves[0], *halves[1], sum_fc2, *hidden_sums]
    return call(
        kernel, "pack", (), [(a, whole(a.shape)) for a in operands],
        [((16, width), F32, whole((16, width)))] * 2, [pltpu.VMEM((2, 16, width), F32)],
    )


def norm(values):
    centre = jnp.mean(values, axis=-1, keepdims=True)
    centred = values - centre
    spread = jnp.mean(centred * centred, axis=-1, keepdims=True)
    scaling = lax.rsqrt(spread + EPSILON)
    return centred * scaling, scaling


def norm_back(grad, normed, scaling, gain):
    scaled = grad * gain
    first = jnp.mean(scaled, axis=-1, keepdims=True)
    second = jnp.mean(scaled * normed, axis=-1, keepdims=True)
    return (scaled - first - normed * second) * scaling


def banded(tall, body):
    if BAND >= tall:
        body(slice(0, tall), 0)
        return

    def step(k, carry):
        at = pl.multiple_of(k * BAND, 8)
        body(pl.ds(at, BAND), at)
        return carry

    lax.fori_loop(0, tall // BAND, step, 0)


def column_sum(values):
    return jnp.sum(values, axis=0, keepdims=True)


TOKEN, GAIN1, SHIFT1, GAMMA2, BIAS1, GAMMA1, GAIN2, SHIFT2, BIAS2 = range(9)


def row_of(ref, k):
    return ref[k : k + 1, :]


def masked_rows(image, sizes_ref, patterns_ref, tall):
    bound, group = 0, 0
    for k in range(sizes_ref.shape[0] - 1):
        bound = bound + sizes_ref[k]
        group = group + (image >= bound).astype(jnp.int32)
    columns_of = patterns_ref[...].T
    which = lax.broadcasted_iota(jnp.int32, columns_of.shape, 1) == group
    return jnp.sum(jnp.where(which, columns_of, 0.0), axis=1, keepdims=True)[0:tall] > 0.5


def first_image(images):
    return lax.axis_index(AXES) * images


def prepare(sizes, inputs, cotangent, group_sizes, mask_patterns, vectors):
    images, length, tall, width = sizes
    rows = images * tall
    groups, patches = mask_patterns.shape

    def kernel(x_ref, g_ref, sizes_ref, mask_ref, *refs):
        vector_refs, refs = refs[: len(vectors)], refs[len(vectors) :]
        h0_ref, n1_ref, g_out, df_ref, sum_ref, params_ref, patterns_ref, x_s, g_s, mask_s, sems, *vector_s = refs
        step = pl.program_id(0)

        @pl.when(step == 0)
        def _():
            x_s[...] = jnp.zeros_like(x_s)
            g_s[...] = jnp.zeros_like(g_s)
            sum_ref[...] = jnp.zeros_like(sum_ref)
            params_ref[...] = jnp.zeros_like(params_ref)
            patterns_ref[...] = jnp.zeros_like(patterns_ref)
            moves = [pltpu.make_async_copy(mask_ref, mask_s, sems.at[len(vectors)])]
            moves += [
                pltpu.make_async_copy(a, b, sems.at[k]) for k, (a, b) in enumerate(zip(vector_refs, vector_s, strict=True))
            ]
            for move in moves:
                move.start()
            for move in moves:
                move.wait()
            patterns_ref[0:groups, 1 : patches + 1] = mask_s[...].astype(F32)
            for k, ref in zip(vectors, vector_s, strict=True):
                params_ref[k : k + 1, :] = ref[...].reshape(1, width)

        x_s[0:length, :] = x_ref[0].astype(F32)
        g_s[0:length, :] = g_ref[0].astype(F32)
        masked = masked_rows(first_image(images) + step, sizes_ref, patterns_ref, tall)
        start = jnp.where(masked, row_of(params_ref, TOKEN), x_s[...])
        h0_ref[...] = start
        normed, _ = norm(start)
        n1_ref[...] = (normed * row_of(params_ref, GAIN1) + row_of(params_ref, SHIFT1)).astype(BF16)
        g = g_s[...]
        g_out[...] = g.astype(BF16)
        df = row_of(params_ref, GAMMA2) * g
        df_ref[...] = df.astype(BF16)
        sum_ref[...] += column_sum(df)

    image = pl.BlockSpec((1, length, width), lambda i: (i, 0, 0))
    band = pl.BlockSpec((tall, width), lambda i: (i, 0))
    return call(
        kernel, "prepare", (images,),
        [(inputs, image), (cotangent, image), (group_sizes, SCALARS), (mask_patterns, ANY, FAR)]
        + [(v, ANY, FAR) for v in vectors.values()],
        [((rows, width), F32, band), ((rows, width), BF16, band), ((rows, width), BF16, band, FAR),
         ((rows, width), BF16, band, FAR), ((1, width), F32, whole((1, width))), ((16, width), F32, whole((16, width))),
         ((8, 256), F32, whole((8, 256)))],
        [pltpu.VMEM((tall, width), F32), pltpu.VMEM((tall, width), F32), pltpu.VMEM(mask_patterns.shape, jnp.int32),
         pltpu.SemaphoreType.DMA((len(vectors) + 1,))] + [pltpu.VMEM((width,), F32) for _ in vectors],
        flops=rows * width * 40,
    )


def table_columns(grid_side, broad):
    side = 2 * grid_side - 1
    q = np.arange(broad)
    entry = (q // grid_side) * side + q % grid_side + grid_side - 1
    return jnp.asarray(np.where(q < side * grid_side, entry, -(1 << 20)).astype(np.int32)[None])


def three_parts(values):
    high = values.astype(BF16)
    rest = values - high.astype(F32)
    middle = rest.astype(BF16)
    return high, middle, (rest - middle.astype(F32)).astype(BF16)


def bias_kernel(table_t, entry, grid_side, tall, broad):
    heads = table_t.shape[0]
    length = grid_side * grid_side + 1
    wide = entry.shape[1]
    inner = (2 * grid_side - 1) ** 2

    def kernel(table_ref, entry_ref, out_ref, *halves):
        def put(at, count, values):
            for half, ref in enumerate(halves):
                ref[pl.ds(at, count), :] = values[:, 128 * half : 128 * half + 128]

        parts = jnp.concatenate(three_parts(table_ref[...]), axis=0)
        left, top, corner = (table_ref[:, inner + 1 : inner + 2], table_ref[:, inner : inner + 1],
                             table_ref[:, inner + 2 : inner + 3])
        lane = lax.broadcasted_iota(jnp.int32, (heads, broad), 1)

        def column(b, carry):
            which = lax.broadcasted_iota(jnp.int32, (table_ref.shape[1], wide), 0) + b
            select = jnp.where(which == entry_ref[...], 1.0, 0.0).astype(BF16)
            spread = nn(parts, select)
            spread = spread[:heads] + spread[heads : 2 * heads] + spread[2 * heads :]
            for a in range(grid_side):
                shift = (grid_side - 1 - a) * grid_side - 1
                moved = pltpu.roll(spread, (wide - shift) % wide, 1)[:, :broad]
                moved = jnp.where(lane == 0, top, moved)
                put(pl.multiple_of((1 + grid_side * a + b) * heads, 16), heads, moved)
            return carry

        lax.fori_loop(0, grid_side, column, 0)
        put(0, heads, jnp.where(lane == 0, corner, left))
        rest = (tall - length) * heads
        put(length * heads, rest, jnp.full((rest, broad), NEVER, F32))
        for h in range(out_ref.shape[0]):
            for half, ref in enumerate(halves):
                out_ref[h, :, 128 * half : 128 * half + 128] = ref[pl.ds(h, tall, stride=heads), :]

    return call(
        kernel, "bias", (),
        [(table_t, whole(table_t.shape)), (entry, whole(entry.shape))],
        [((12, tall, broad), F32, whole((12, tall, broad)))],
        [pltpu.VMEM((tall * heads, 128), F32)] * (broad // 128),
        flops=2 * 48 * 768 * wide * grid_side,
    )[0]


def bias_back_kernel(terms, entry, grid_side, width):
    count, tall, broad = terms.shape
    heads = 16
    wide = entry.shape[1]
    inner = (2 * grid_side - 1) ** 2
    length = grid_side * grid_side + 1

    def kernel(terms_ref, entry_ref, out_ref, *halves):
        def get(at, count):
            return jnp.concatenate([ref[pl.ds(at, count), :] for ref in halves], axis=1)

        lane = lax.broadcasted_iota(jnp.int32, (heads, broad), 1)
        inside = (lane >= 1) & (lane < length)
        for h in range(heads):
            values = terms_ref[h] if h < count else jnp.zeros((tall, broad), F32)
            for half, ref in enumerate(halves):
                ref[pl.ds(h, tall, stride=heads), :] = values[:, 128 * half : 128 * half + 128]

        def column(b, carry):
            total, edge = carry
            which = lax.broadcasted_iota(jnp.int32, (width, wide), 0) + b
            select = jnp.where(which == entry_ref[...], 1.0, 0.0).astype(BF16)
            spread = jnp.zeros((heads, wide), F32)
            for a in range(grid_side):
                shift = (grid_side - 1 - a) * grid_side - 1
                found = get(pl.multiple_of((1 + grid_side * a + b) * heads, 16), heads)
                edge = edge + jnp.where(lane == 0, found, 0.0)
                found = jnp.where(inside, found, 0.0)
                found = jnp.concatenate([found, jnp.zeros((heads, wide - broad), F32)], axis=1)
                spread = spread + pltpu.roll(found, shift % wide, 1)
            found = nt(jnp.concatenate(three_parts(spread), axis=0), select)
            total = total + found[:heads] + found[heads : 2 * heads] + found[2 * heads :]
            return total, edge

        total, edge = lax.fori_loop(
            0, grid_side, column, (jnp.zeros((heads, width), F32), jnp.zeros((heads, broad), F32))
        )
        first = get(0, heads)
        top = jnp.sum(edge, axis=1, keepdims=True)
        left = jnp.sum(jnp.where(inside, first, 0.0), axis=1, keepdims=True)
        corner = first[:, 0:1]
        place = lax.broadcasted_iota(jnp.int32, (heads, width), 1)
        total = jnp.where(place == inner, top, total)
        total = jnp.where(place == inner + 1, left, total)
        out_ref[...] = jnp.where(place == inner + 2, corner, total)

    return call(
        kernel, "bias_back", (),
        [(terms, whole(terms.shape)), (entry, whole(entry.shape))],
        [((heads, width), F32, whole((heads, width)))],
        [pltpu.VMEM((tall * heads, 128), F32)] * (broad // 128),
        flops=2 * 48 * 768 * wide * grid_side,
    )[0]


def project(sizes, first_low, weight, params, score_scale):
    images, length, tall, width = sizes
    rows = images * tall
    cols = 3 * width
    count = len(weight.operands)

    def kernel(*refs):
        n1_ref, params_ref = refs[:2]
        out_ref, w_s, sem = refs[2 + count :]
        step = pl.program_id(0)

        @pl.when(step == 0)
        def _():
            weight.fill(refs[2 : 2 + count], w_s, sem)
            weight.wait(w_s, sem)

        w = w_s[:, pl.ds(pl.multiple_of(step * width, 128), width)]
        scale = jnp.where(step == 0, score_scale, 1.0)
        out_ref[...] = ((nn(n1_ref[...], w) + params_ref[pl.ds(9 + step, 1), :]) * scale).astype(BF16)

    return call(
        kernel, "project", (cols // width,),
        [(first_low, kept((rows, width))), (params, kept(params.shape))] + [(a, ANY) for a in weight.operands],
        [((rows, cols), BF16, pl.BlockSpec((rows, width), lambda t: (0, t)))],
        [pltpu.VMEM((width, cols + weight.extra), BF16), pltpu.SemaphoreType.DMA],
        flops=2 * rows * width * cols,
    )[0]


def head_masks(tall):
    lane = lax.broadcasted_iota(jnp.int32, (tall, 128), 1)
    return [lane < 64, lane >= 64]


def attend(sizes, mixed, bias, first, pairs):
    images, length, tall, width = sizes
    rows = images * tall
    every = width // 128
    broad = bias.shape[2]

    def kernel(q_ref, k_ref, v_ref, bias_ref, out_ref, p_ref):
        masks = head_masks(tall)
        units = [(i, h) for i in range(images) for h in range(2)]
        scores, probs = [], []
        for i, h in units:
            q, k = q_ref[tall * i : tall * i + tall, :], k_ref[tall * i : tall * i + tall, :]
            scores.append(nt(k, jnp.where(masks[h], q, jnp.zeros_like(q))) + bias_ref[h, :, 0:tall])
        for (i, h), s in zip(units, scores, strict=True):
            e = jnp.exp(s - jnp.max(s, axis=0, keepdims=True))
            p = (e * (1.0 / jnp.sum(e, axis=0, keepdims=True))).astype(BF16)
            p_ref[h, i, :, 0:tall] = p
            probs.append(p)
        for i in range(images):
            vt = v_ref[tall * i : tall * i + tall, :].T
            out = [nn(vt[64 * h : 64 * h + 64, :], probs[2 * i + h]) for h in range(2)]
            out_ref[tall * i : tall * i + tall, :] = jnp.concatenate(out, axis=0).T.astype(BF16)

    def column(at):
        return pl.BlockSpec((rows, 128), lambda t: (0, at + t))

    return call(
        kernel, "attend", (pairs,),
        [(mixed, column(first)), (mixed, column(every + first)), (mixed, column(2 * every + first)),
         (bias, pl.BlockSpec((2, tall, broad), lambda t: (first + t, 0, 0)))],
        [((rows, 128 * pairs), BF16, column(0), FAR),
         ((2 * pairs, images, tall, broad), BF16,
          pl.BlockSpec((2, images, tall, broad), lambda t: (t, 0, 0, 0)), FAR)],
        flops=4 * rows * tall * 128 * pairs,
    )


def attend_back(sizes, mixed, probs, grad_out, score_scale, first, pairs, so_far):
    images, length, tall, width = sizes
    rows = images * tall
    every = width // 128
    broad = probs.shape[3]

    def kernel(q_ref, k_ref, v_ref, do_ref, p_ref, *refs):
        grad_ref, terms_ref, qb_ref, vb_ref = refs[-4:]
        masks = head_masks(tall)
        units = [(i, h) for i in range(images) for h in range(2)]

        def part(ref, i):
            return ref[tall * i : tall * i + tall, :]

        def own(value, h):
            return jnp.where(masks[h], value, jnp.zeros_like(value))

        grads = [nt(part(v_ref, i), own(part(do_ref, i), h)) for i, h in units]
        lows = []
        for (i, h), grad in zip(units, grads, strict=True):
            p = p_ref[h, i, :, 0:tall].astype(F32)
            t = p * grad
            lows.append((t - p * jnp.sum(t, axis=0, keepdims=True)).astype(BF16))
        for h in range(2):
            terms_ref[h, :, 0:tall] = sum(lows[2 * i + h].astype(F32) for i in range(images))
            terms_ref[h, :, tall:] = jnp.zeros((tall, broad - tall), F32)
        query_sum, value_sum = 0.0, 0.0
        for i in range(images):
            kt = part(k_ref, i).T
            dv = sum(nn(p_ref[h, i, :, 0:tall], own(part(do_ref, i), h)) for h in range(2))
            dk = sum(nn(lows[2 * i + h], own(part(q_ref, i), h)) for h in range(2))
            dq = jnp.concatenate(
                [nn(kt[64 * h : 64 * h + 64, :], lows[2 * i + h]) for h in range(2)], axis=0
            ).T * score_scale
            for number, grad in enumerate((dq, dk, dv)):
                grad_ref[number, tall * i : tall * i + tall, :] = grad.astype(BF16)
            query_sum += column_sum(dq)
            value_sum += column_sum(dv)
        qb_ref[...] = query_sum
        vb_ref[...] = value_sum

    def column(at):
        return pl.BlockSpec((rows, 128), lambda t: (0, at + t))

    one = pl.BlockSpec((1, 128), lambda t: (0, t))
    return call(
        kernel, "attend_back", (pairs,),
        [(mixed, column(first)), (mixed, column(every + first)), (mixed, column(2 * every + first)),
         (grad_out, column(first)),
         (probs, pl.BlockSpec((2, images, tall, broad), lambda t: (first + t, 0, 0, 0)), FAR)]
        + ([] if so_far is None else [(so_far, ANY)]),
        [((3, rows, width), BF16, pl.BlockSpec((3, rows, 128), lambda t: (0, 0, first + t)))]
        + [((2 * pairs, tall, broad), F32, pl.BlockSpec((2, tall, broad), lambda t: (t, 0, 0))),
           ((1, 128 * pairs), F32, one), ((1, 128 * pairs), F32, one)],
        flops=8 * rows * tall * 128 * pairs,
        aliases={} if so_far is None else {5: 0},
    )


def merge(sizes, attended, start, weight, params):
    images, length, tall, width = sizes
    rows = images * tall
    count = len(weight.operands)

    def kernel(*refs):
        att_refs, refs = refs[: len(attended)], refs[len(attended) :]
        h0_ref, params_ref = refs[:2]
        h1_ref, n2_ref, w_s, out_s, sem = refs[2 + count :]
        step = pl.program_id(0)

        @pl.when(step == 0)
        def _():
            weight.fill(refs[2 : 2 + count], w_s, sem)
            weight.wait(w_s, sem)
            part = width // len(attended)
            out_s[...] = sum(nn(r[...], w_s[part * k : part * k + part, 0:width]) for k, r in enumerate(att_refs))

        @pl.when(step > 0)
        def _():
            def body(at, first):
                out = out_s[pl.ds(pl.multiple_of((step - 1) * tall + first, 8), min(BAND, tall)), :]
                middle = h0_ref[at, :] + row_of(params_ref, GAMMA1) * (out + row_of(params_ref, BIAS1))
                h1_ref[at, :] = middle
                normed, _ = norm(middle)
                n2_ref[at, :] = (normed * row_of(params_ref, GAIN2) + row_of(params_ref, SHIFT2)).astype(BF16)

            banded(tall, body)

    band = pl.BlockSpec((tall, width), lambda i: (jnp.maximum(i - 1, 0), 0))
    return call(
        kernel, "merge", (images + 1,),
        [(a, kept(a.shape), FAR) for a in attended]
        + [(start, band), (params, kept(params.shape))]
        + [(a, ANY, FAR) for a in weight.operands],
        [((rows, width), F32, band), ((rows, width), BF16, band)],
        [pltpu.VMEM((width, width + weight.extra), BF16), pltpu.VMEM((rows, width), F32),
         pltpu.SemaphoreType.DMA],
        flops=2 * rows * width * width,
    )


def part_by_core(store, away_ref, stay_ref):
    c = lax.axis_index("narrow") % 2
    for x in range(2):
        away_ref[x] = store[2 * x + 1 - c]
        stay_ref[x] = store[2 * x + c]


def feed(sizes, second_low, down_low, up, down, bias, sums, last):
    images, length, tall, width = sizes
    rows = images * tall
    shared = up.operands[0] is down.operands[0]
    far = () if last else (FAR,)
    ups, downs = len(up.operands), 0 if shared else len(down.operands)
    carried = [] if sums is None else list(sums)

    def kernel(*refs):
        n2_ref, df_ref, bias_ref = refs[:3]
        rest = refs[3:]
        up_refs, rest = rest[:ups], rest[ups:]
        down_refs, rest = (up_refs if shared else rest[:downs]), rest[downs:]
        sum_refs, rest = rest[: len(carried)], rest[len(carried) :]
        f_ref, dn_ref, away_ref, stay_ref, gbias_ref, up_s, down_s, grad_s, sems = rest
        step = pl.program_id(0)

        @pl.when(step == 0)
        def _():
            up.fill(up_refs, up_s, sems.at[0])
            down.fill(down_refs, down_s, sems.at[1])
            if carried:
                pltpu.make_async_copy(sum_refs[0], f_ref, sems.at[2]).start()
                pltpu.make_async_copy(sum_refs[1], dn_ref, sems.at[3]).start()
            up.wait(up_s, sems.at[0])
            down.wait(down_s, sems.at[1])
            if not carried:
                f_ref[...] = jnp.zeros_like(f_ref)
                dn_ref[...] = jnp.zeros_like(dn_ref)

        at = pl.ds(pl.multiple_of(step * TILE, TILE), TILE)
        up_w, down_w = up_s[:, at], down_s[:, at]
        u = nn(n2_ref[...], up_w) + bias_ref[...]
        dz = nn(df_ref[...], down_w)
        bell = jnp.exp(-0.5 * u * u)
        below = 0.5 * (1.0 + lax.erf(u * ROOT_HALF))
        z = (u * below).astype(BF16)
        du = dz * (below + u * (DENSITY * bell))
        gbias_ref[...] = column_sum(du)
        du = du.astype(BF16)
        grad = tn(n2_ref[...], du).astype(BF16)
        for k in range(TILE // 256):
            grad_s[step * (TILE // 256) + k, :, :, 0:256] = grad[:, 256 * k : 256 * k + 256].reshape(8, 96, 256)
        grad = tn(df_ref[...], z).astype(BF16)
        for n in range(4):
            for w in range(TILE // 128):
                for half in range(2):
                    grad_s[n, step * (TILE // 128) + w, :, 256 + 128 * half : 384 + 128 * half] = grad[
                        192 * n + 96 * half : 192 * n + 96 * half + 96, 128 * w : 128 * w + 128
                    ]
        if carried:
            @pl.when(step == 0)
            def _():
                pltpu.make_async_copy(sum_refs[0], f_ref, sems.at[2]).wait()
                pltpu.make_async_copy(sum_refs[1], dn_ref, sems.at[3]).wait()

        f_ref[...] += nt(z, down_w)
        dn_ref[...] += nt(du, up_w)

        @pl.when(step == CHUNK // TILE - 1)
        def _():
            part_by_core(grad_s, away_ref, stay_ref)

    tile = pl.BlockSpec((1, TILE), lambda t: (0, t))
    full = whole((rows, width))
    shape = (2, 8, 96, 512)
    return call(
        kernel, "feed", (CHUNK // TILE,),
        [(second_low, kept((rows, width))), (down_low, kept((rows, width))), (bias, tile)]
        + [(a, ANY, FAR) for a in up.operands[:1]] + [(a, ANY) for a in up.operands[1:]]
        + [(a, ANY, FAR) for a in ([] if shared else down.operands) + carried],
        [((rows, width), F32, kept((rows, width)), *far), ((rows, width), F32, kept((rows, width)), *far),
         (shape, BF16, kept(shape)), (shape, BF16, kept(shape)), ((1, CHUNK), F32, tile)],
        [pltpu.VMEM((width, CHUNK), BF16), pltpu.VMEM((width, CHUNK), BF16), pltpu.VMEM((4, 8, 96, 512), BF16),
         pltpu.SemaphoreType.DMA((4,))],
        flops=12 * rows * width * CHUNK,
    )


def middle_back(sizes, attended, branch, grad_n2, middle, start, upstream, weight, params):
    images, length, tall, width = sizes
    rows = images * tall
    count = len(weight.operands)

    def kernel(*refs):
        att_refs, refs = refs[: len(attended)], refs[len(attended) :]
        f_ref, dn_ref, h1_ref, h0_ref, g_ref, params_ref = refs[:6]
        out_ref, dh_ref, do_ref, away_ref, stay_ref, sum_ref, w_s, da_s, grad_s, layer_s, sem = refs[6 + count :]
        step = pl.program_id(0)

        @pl.when(step == 0)
        def _():
            weight.fill(refs[6 : 6 + count], w_s, sem)
            sum_ref[...] = jnp.zeros_like(sum_ref)

        @pl.when(step < images)
        def _():
            def body(at, first):
                f = f_ref[at, :] + row_of(params_ref, BIAS2)
                h1 = h1_ref[at, :]
                g = g_ref[at, :].astype(F32)
                layer_s[at, :] = h1 + row_of(params_ref, GAMMA2) * f
                normed, scaling = norm(h1)
                dn = dn_ref[at, :]
                dh = g + norm_back(dn, normed, scaling, row_of(params_ref, GAIN2))
                dh_ref[at, :] = dh
                da = row_of(params_ref, GAMMA1) * dh
                sum_ref[0:1, :] += column_sum(g * f)
                sum_ref[1:2, :] += column_sum(dn * normed)
                sum_ref[2:3, :] += column_sum(dn)
                sum_ref[3:4, :] += column_sum(dh * (h1 - h0_ref[at, :]))
                sum_ref[4:5, :] += column_sum(da)
                da_s[pl.ds(pl.multiple_of(step * tall + first, 8), min(BAND, tall)), :] = da.astype(BF16)

            banded(tall, body)
            out_ref[0] = layer_s[0:length, :].astype(BF16)

        @pl.when(step == images)
        def _():
            sum_ref[3:4, :] = sum_ref[3:4, :] / row_of(params_ref, GAMMA1)
            weight.wait(w_s, sem)
            do_ref[...] = nt(da_s[...], w_s[:, 0:width]).astype(BF16)
            grad = jnp.concatenate([tn(r[...], da_s[...]) for r in att_refs], axis=0).astype(BF16)
            for n, at in enumerate((0, 128, 384, 512)):
                grad_s[n] = grad[:, at : at + 256].reshape(8, 96, 256)
            part_by_core(grad_s, away_ref, stay_ref)

    def at(i):
        return jnp.minimum(i, images - 1)

    band = pl.BlockSpec((tall, width), lambda i: (at(i), 0))
    shape = (2, 8, 96, 256)
    return call(
        kernel, "middle_back", (images + 1,),
        [(a, kept(a.shape), FAR) for a in attended]
        + [(a, band) for a in (branch, grad_n2, middle, start)] + [(a, band, FAR) for a in (upstream,)] + [(params, kept(params.shape))]
        + [(a, ANY, FAR) for a in weight.operands],
        [((images, length, width), BF16, pl.BlockSpec((1, length, width), lambda i: (at(i), 0, 0))),
         ((rows, width), F32, band), ((rows, width), BF16, whole((rows, width))),
         (shape, BF16, whole(shape)), (shape, BF16, whole(shape)), ((8, width), F32, whole((8, width)))],
        [pltpu.VMEM((width, width + weight.extra), BF16), pltpu.VMEM((rows, width), BF16),
         pltpu.VMEM((4, 8, 96, 256), BF16), pltpu.VMEM((tall, width), F32), pltpu.SemaphoreType.DMA],
        flops=4 * rows * width * width,
    )


def mixed_grad(sizes, first_low, grads):
    images, length, tall, width = sizes
    rows = images * tall

    def kernel(n1_ref, grad_ref, away_ref, stay_ref):
        step = pl.program_id(0)
        c = lax.axis_index("narrow") % 2
        n = 2 * (step % 2) + jnp.where(step < 2, 1 - c, c)
        main = grad_ref[at_least(n, (0, 1, 1, 2)), :, pl.ds(pl.multiple_of(at_least(n, (0, 0, 384, 384)), 128), 384)]
        side = grad_ref[at_least(n, (0, 0, 2, 2)), :, pl.ds(pl.multiple_of(at_least(n, (384, 512, 0, 128)), 128), 256)]
        main = tn(n1_ref[...], main).astype(BF16).reshape(8, 96, 384)
        side = tn(n1_ref[...], side).astype(BF16).reshape(8, 96, 256)
        for role, ref in enumerate((away_ref, stay_ref)):
            @pl.when(step // 2 == role)
            def _(ref=ref):
                ref[0, :, :, 0:384] = main
                ref[0, :, :, 384:640] = side

    shape = (2, 8, 96, 640)
    return call(
        kernel, "mixed_grad", (4,),
        [(first_low, kept((rows, width))), (grads, kept(grads.shape))],
        [(shape, BF16, pl.BlockSpec((1, 8, 96, 640), lambda t: (jnp.minimum(t, 1), 0, 0, 0))),
         (shape, BF16, pl.BlockSpec((1, 8, 96, 640), lambda t: (jnp.maximum(t - 2, 0), 0, 0, 0)))],
        flops=6 * rows * width * width,
    )


def start_back(sizes, grads, weight, start, grad_middle, group_sizes, patterns, params):
    images, length, tall, width = sizes
    rows = images * tall
    count = len(weight.operands)

    def kernel(*refs):
        grad_ref, h0_ref, dh_ref, sizes_ref, patterns_ref, params_ref = refs[:6]
        out_ref, sum_ref, w_s, dn_s, out_s, sem = refs[6 + count :]
        step = pl.program_id(0)

        @pl.when(step == 0)
        def _():
            weight.fill(refs[6 : 6 + count], w_s, sem)
            sum_ref[...] = jnp.zeros_like(sum_ref)
            dn_s[...] = jnp.zeros_like(dn_s)
            weight.wait(w_s, sem)

        @pl.when(step < 3)
        def _():
            dn_s[...] += nt(grad_ref[0], w_s[:, pl.ds(pl.multiple_of(step * width, 128), width)])

        @pl.when(step > 2)
        def _():
            masked = masked_rows(first_image(images) + step - 3, sizes_ref, patterns_ref, tall)

            def body(at, first):
                dn = dn_s[pl.ds(pl.multiple_of((step - 3) * tall + first, 8), min(BAND, tall)), :]
                normed, scaling = norm(h0_ref[at, :])
                dh = dh_ref[at, :] + norm_back(dn, normed, scaling, row_of(params_ref, GAIN1))
                out_s[at, :] = jnp.where(masked, 0.0, dh)
                sum_ref[0:1, :] += column_sum(dn * normed)
                sum_ref[1:2, :] += column_sum(dn)
                sum_ref[2:3, :] += column_sum(jnp.where(masked, dh, 0.0))

            banded(tall, body)
            out_ref[0] = out_s[0:length, :]

    def at(i):
        return jnp.maximum(i - 3, 0)

    band = pl.BlockSpec((tall, width), lambda i: (at(i), 0))
    return call(
        kernel, "start_back", (images + 3,),
        [(grads, pl.BlockSpec((1, rows, width), lambda i: (jnp.minimum(i, 2), 0, 0)))]
        + [(start, band), (grad_middle, band), (group_sizes, SCALARS), (patterns, kept(patterns.shape)),
           (params, kept(params.shape))]
        + [(a, ANY) for a in weight.operands],
        [((images, length, width), F32, pl.BlockSpec((1, length, width), lambda i: (at(i), 0, 0))),
         ((8, width), F32, whole((8, width)))],
        [pltpu.VMEM((width, 3 * width + weight.extra), BF16), pltpu.VMEM((rows, width), F32),
         pltpu.VMEM((tall, width), F32), pltpu.SemaphoreType.DMA],
        flops=6 * rows * width * width,
    )


def local(
    links,
    inputs,
    cotangent,
    group_sizes,
    mask_patterns,
    mask_token,
    norm1_gain,
    norm1_bias,
    qkv_weight,
    query_bias,
    value_bias,
    bias_table,
    proj_weight,
    proj_bias,
    gamma_attn,
    norm2_gain,
    norm2_bias,
    fc1_weight,
    fc1_bias,
    fc2_weight,
    fc2_bias,
    gamma_mlp,
):
    images, length, width = inputs.shape
    table_rows, heads = bias_table.shape
    grid_side = math.isqrt(length - 1)
    group_count = mask_patterns.shape[0]
    tall = -(-length // 8) * 8
    rows = images * tall
    hidden = fc1_bias.shape[0]
    chunks = hidden // CHUNK
    sizes = (images, length, tall, width)
    score_scale = (width // heads) ** (-0.5)
    here = links.place()

    vectors = {
        TOKEN: mask_token, GAIN1: norm1_gain, SHIFT1: norm1_bias, GAMMA2: gamma_mlp, BIAS1: proj_bias,
        GAMMA1: gamma_attn, GAIN2: norm2_gain, SHIFT2: norm2_bias, BIAS2: fc2_bias, 9: query_bias, 11: value_bias,
    }

    boxed = links.boxed
    fc2_t = fc2_weight.T
    if boxed:
        mix = Gather(links, qkv_block(here, qkv_weight), 384, [((0, 384), (0, 256))])
        side = align_side(here, proj_weight)
        near = Gather(
            links,
            jnp.concatenate(
                [side[:, :128], up_block(fc1_weight, 0), down_block(fc2_t, 0), side[:, 128:]], axis=1
            ),
            384,
            [((0, 128), (256, 384)), ((128, 384), (0, 256))],
        )
        far = Gather(
            links,
            jnp.concatenate(
                [up_block(fc1_weight, 1), up_block(fc1_weight, 2), down_block(fc2_t, 1), down_block(fc2_t, 2)],
                axis=1,
            ),
            512,
            [((0, 256), (0, 256)), ((256, 512), (256, 512))],
        )
        full_up = full_down = None
    else:
        mix = near = far = None
        full_up, full_down = native_gather(fc1_weight), native_gather(fc2_weight).T

    entry = table_columns(grid_side, 384)

    def behind(value, *exchanges):
        return after(value, *[v for e in exchanges for v in e.sent]) if boxed else value

    def met(value, *exchanges):
        return [value] + [v for e in exchanges for v in e.flying]

    if boxed:
        mix.first()
    start, first_low, upstream, down_low, sum_fc2, params, patterns = prepare(
        sizes, inputs, cotangent, group_sizes, mask_patterns, vectors
    )
    if boxed:
        gap = met(first_low, mix)
        mix.second(*gap)
        near.first(*gap)
    table_t = jnp.pad(after(bias_table, first_low).T, ((0, 16 - heads), (0, width - table_rows)))
    bias = bias_kernel(behind(table_t, mix), entry, grid_side, tall, 256)
    if boxed:
        mix.third(*met(bias, mix))
        mix.fourth(False, *met(bias, near))
        near.second(*mix.sent)
    qkv = qkv_operands(links, mix, qkv_weight)
    mixed = project(sizes, behind(first_low, near), qkv, params, score_scale)
    if boxed:
        gap = met(mixed, near)
        near.third(*gap)
        far.first(*gap)
    attended, probs = attend(sizes, behind(mixed, near), bias, 0, width // 128)
    if boxed:
        near.fourth(False, *met(attended, far))
        far.second(*near.sent)
    proj = proj_operands(links, near, proj_weight)
    middle, second_low = merge(sizes, [attended], behind(start, far), proj, params)
    if boxed:
        far.third(*met(second_low, far))

    fc1_groups = fc1_bias.reshape(8, chunks, 128)
    ups = [up_operands(links, near, 1, full_up, 0), None, None]
    downs = [down_operands(links, near, 1, full_down, 0), None, None]
    halves = [[(0, (0, 256))], [(0, (256, 512))]]
    sums, pairs_out, hidden_sums = None, [], []
    waves = [Scatter(links, here, 256), Scatter(links, here, 256), Scatter(links, here, 512)]
    second_here = behind(second_low, far)
    for k in range(chunks):
        branch, grad_n2, away, stay, hidden_sum = feed(
            sizes, second_here, down_low, ups[k], downs[k], fc1_groups[:, k].reshape(1, -1), sums, k == chunks - 1
        )
        if k == 0:
            if boxed:
                far.fourth(True, *met(away, far))
                waves[0].first(after(away, *far.sent), stay)
                exchange(links, [away], (waves[0], "second", halves))
            ups[1:] = [up_operands(links, far, 0, full_up, 1), up_operands(links, far, 1, full_up, 2)]
            downs[1:] = [down_operands(links, far, 0, full_down, 1), down_operands(links, far, 1, full_down, 2)]
            second_here = behind(second_low, waves[0])
        elif k == 1 and boxed:
            exchange(links, [away], (waves[0], "third", None))
            waves[1].first(after(away, *waves[0].sent), stay)
            second_here = behind(second_low, waves[0])
        elif boxed:
            exchange(links, [away], (waves[0], "halves", None), (waves[1], "second", halves))
            waves[2].first(after(away, *waves[1].sent), stay)
        sums = (branch, grad_n2)
        pairs_out.append((away, stay))
        hidden_sums.append(hidden_sum)

    layer_out, grad_middle, grad_att, proj_away, proj_stay, middle_sums = middle_back(
        sizes, [attended], behind(branch, waves[0], waves[1]), grad_n2, middle, start, upstream, proj, params
    )
    if boxed:
        exchange(links, [grad_att], (waves[0], "fifth", None), (waves[1], "third", None))
        waves[2].first(after(proj_away, *waves[1].sent), proj_stay)

    back, grads = [], None
    for number, (first, pairs) in enumerate(((0, 3), (3, 3))):
        grad_here = behind(grad_att, *(waves[:2] if number == 0 else waves[1:]))
        grads, *rest = attend_back(sizes, mixed, probs, grad_here, score_scale, first, pairs, grads)
        back.append(rest)
        if boxed and number == 0:
            exchange(
                links, met(grads, waves[0]), (waves[1], "halves", None),
                (waves[2], "second", [[(1, (0, 256)), (0, (0, 128))], [(0, (128, 512))]]),
            )
    if boxed:
        gap_grads = met(grads, waves[0])
        exchange(links, gap_grads, (waves[1], "fifth", None), (waves[2], "third", None))
    mix_away, mix_stay = mixed_grad(sizes, behind(first_low, waves[2]), grads)
    last = Scatter(links, here, 384)
    terms = jnp.concatenate([b[0] for b in back], axis=0)
    if boxed:
        gap_mix = met(mix_away, waves[1])
        exchange(links, gap_mix, (waves[2], "halves", None))
        last.first(after(mix_away, *waves[2].sent), mix_stay)
    grad_table = bias_back_kernel(after(behind(terms, waves[2]), mix_away), entry, grid_side, width)
    if boxed:
        exchange(links, [grad_table], (last, "second", [[(0, (0, 384))], [(0, (384, 640))]]))
    input_grad, start_sums = start_back(
        sizes, grads, qkv, start, behind(grad_middle, last), group_sizes, patterns, params
    )
    small_away, small_stay = pack(
        links, grad_table, heads, start_sums, middle_sums, [b[1:] for b in back], sum_fc2, hidden_sums
    )
    if boxed:
        exchange(links, [start_sums], (last, "third", None))
        small_away = after(small_away, *last.sent, *waves[2].flying)
    small = sum_everywhere(links, here, small_away, small_stay, last.flying)
    if boxed:
        exchange(links, [], (last, "fourth", None), (waves[2], "fifth", None))
        grad_qkv = qkv_home(here, last.done())
        blocks = [waves[0].done(*gap_grads), waves[1].done(*gap_mix), waves[2].done()]
        grad_proj = proj_home(here, blocks[2][:, 0:256])
        up_parts = [blocks[0][:, 0:256], blocks[1][:, 0:256], blocks[2][:, 256:512]]
        down_parts = [blocks[0][:, 256:512], blocks[1][:, 256:512], blocks[2][:, 512:768]]
        grad_fc1 = jnp.concatenate(
            [up_parts[k][:, 128 * half : 128 * half + 128] for half in range(2) for k in range(chunks)], axis=1
        )
        grad_fc2 = jnp.concatenate(
            [jnp.concatenate([p[:, :128], p[:, 128:]], axis=0) for p in down_parts], axis=1
        ).T
    else:
        tiles = [all_tiles(here, *pair) for pair in pairs_out]
        grad_qkv = native_scatter(natural_qkv(all_tiles(here, mix_away, mix_stay)))
        grad_proj = native_scatter(natural_proj(all_tiles(here, proj_away, proj_stay)))
        grad_fc1 = native_scatter(natural_up([t[..., :256] for t in tiles]))
        grad_fc2 = native_scatter(natural_down([t[..., 256:] for t in tiles]))
    at = heads
    hidden_rows = [
        jnp.concatenate([small[at + 11 + k], small[at + 14, 256 * k : 256 * k + 256]]).reshape(8, 128) for k in range(chunks)
    ]
    sum_fc1 = jnp.stack(hidden_rows, axis=1).reshape(-1)
    return (
        layer_out,
        input_grad,
        small[at + 2],
        small[at],
        small[at + 1],
        grad_qkv,
        small[at + 8],
        small[at + 9],
        small[:heads, :table_rows].T,
        grad_proj,
        small[at + 7],
        small[at + 6],
        small[at + 4],
        small[at + 5],
        grad_fc1,
        sum_fc1,
        grad_fc2,
        small[at + 10],
        small[at + 3],
    )


def solution(mesh):
    images = P(AXES, None, None)
    both = P("wide", "narrow")
    same = P()
    links = Links(mesh.shape["wide"], mesh.shape["narrow"])
    return jax.shard_map(
        functools.partial(local, links),
        mesh=mesh,
        in_specs=(
            images, images, same, same, same, same, same, both, same, same, same, both, same, same,
            same, same, both, same, both, same, same,
        ),
        out_specs=(
            images, images, same, same, same, both, same, same, same, both, same, same, same, same,
            both, same, both, same, same,
        ),
        check_vma=False,
    )
```
